32 devices in a mesh: replica: 4 (over z), shard: 8 (over y, x, core).
Axes of the slice: x: 2, y: 2, z: 4, core: 2. Of those that a mesh axis runs over, the one named last changes fastest.
Arguments:
- hidden_in: bfloat16 [4, 1024, 2048], P('replica', 'shard'), may hold values from -6 to 6
- cotangent: bfloat16 [4, 1024, 2048], P('replica', 'shard'), may hold values from -6 to 6
- doc_lengths: int32 [4, 4], P('replica'), may hold values from 1 to 512, 1024 in all within a row
- w_query: bfloat16 [2048, 2048], P('shard'), may hold values from -0.1875 to 0.1875
- w_key: bfloat16 [2048, 2048], P('shard'), may hold values from -0.1875 to 0.1875
- w_value: bfloat16 [2048, 2048], P('shard'), may hold values from -0.125 to 0.125
- w_out: bfloat16 [2048, 2048], P('shard'), may hold values from -0.5 to 0.5
- w_gate: bfloat16 [8192, 2048], P('shard'), may hold values from -0.125 to 0.125
- w_up: bfloat16 [8192, 2048], P('shard'), may hold values from -0.125 to 0.125
- w_down: bfloat16 [2048, 8192], P('shard'), may hold values from -0.125 to 0.125
Outputs:
- layer_out: bfloat16 [4, 1024, 2048], P('replica', 'shard')
- grad_in: float32 [4, 1024, 2048], P('replica', 'shard')
- grad_query: float32 [2048, 2048], P('shard')
- grad_key: float32 [2048, 2048], P('shard')
- grad_value: float32 [2048, 2048], P('shard')
- grad_out: float32 [2048, 2048], P('shard')
- grad_gate: float32 [8192, 2048], P('shard')
- grad_up: float32 [8192, 2048], P('shard')
- grad_down: float32 [2048, 8192], P('shard')
The draws below stay inside these ranges and needn't reach their ends.
Inputs may be any that keep to these rules, and one draw needn't show every extreme that they name: `doc_lengths`: the 4 lengths of a sequence add up to 1024; in every sequence the longest is exactly 512.
All inputs are finite; a program needn't handle non-finite values.
Results may differ from the reference program's by a relative error of at most 0.022.
Values may be sent and summed in bfloat16 or wider, within the bound.
A program may use at most 448 MiB of HBM per device.

```python
import math
import jax
import jax.numpy as jnp
import numpy as np
from jax import lax

D = 2048
FF = 8192
HEADS = 16
HEAD_DIM = 128
DOCS = 4
SEQS = 4
SEQ = 1024
MOST_DOC = 512


def level_of(stream_key, extent, cuts, low, high):
    loudness, own = 1.0, jax.random.fold_in(stream_key, 6)
    for position, parts in cuts:
        heights = jnp.exp(jax.random.uniform(jax.random.fold_in(own, position), (parts,), jnp.float32, low / len(cuts), high / len(cuts)))
        loudness = loudness * jnp.repeat(heights, extent[position] // parts).reshape([-1 if axis == position else 1 for axis in range(len(extent))])
    return loudness


def profile(number_of, total, limit, skew):
    portions = [(1 << 20) // math.isqrt(rank ** skew) + 1 for rank in range(2, number_of + 1)]
    rest, holding = total - limit - (number_of - 1), [1] * (number_of - 1)
    while rest > 0:
        candidates = [i for i in range(number_of - 1) if holding[i] < limit]
        mass, left = sum([portions[i] for i in candidates]), rest
        for i in candidates:
            addition = min(limit - holding[i], max(1, left * portions[i] // mass), rest)
            holding[i] = holding[i] + addition
            rest = rest - addition
    return np.array([limit] + holding)


def ragged(stream_key, number_of, total, most, lean):
    if number_of == 2:
        one = jax.random.randint(stream_key, (), max(1, total - most), min(most, total - 1) + 1)
        return jnp.stack([one, total - one])
    sizes = jnp.asarray(profile(number_of, total, most, lean), jnp.int32)
    pairs = (number_of - 1) // 2
    giver, sink = sizes[1:1 + 2 * pairs:2], sizes[2:2 + 2 * pairs:2]
    room = jnp.minimum(giver - 1, most - sink)
    shifted = jax.random.randint(jax.random.fold_in(stream_key, 1), (pairs,), 0, 1 << 20) % (room + 1)
    sizes = sizes.at[1:1 + 2 * pairs:2].set(giver - shifted).at[2:2 + 2 * pairs:2].set(sink + shifted)
    return sizes[jax.random.permutation(jax.random.fold_in(stream_key, 2), number_of)]


def centred(key, dims, scale, limit, shards=(), kind=jnp.bfloat16):
    gain = level_of(key, dims, shards, -0.22, 0.18) if shards else 1.0
    entries = jax.random.normal(key, dims, jnp.float32) * scale * gain
    return jnp.minimum(jnp.maximum(entries, -limit), limit).astype(kind)


def setup_inputs(seed: int = 0) -> dict:
    key_list = jax.random.split(jax.random.key(seed), 11)
    return {
        "hidden_in": centred(key_list[0], (SEQS, SEQ, D), 1.0, 6.0, ((0, 4), (1, 8))),
        "cotangent": centred(key_list[1], (SEQS, SEQ, D), 1.0, 6.0, ((0, 4), (1, 8))),
        "doc_lengths": jax.vmap(lambda own: ragged(own, DOCS, SEQ, MOST_DOC, 1))(jax.random.split(key_list[2], SEQS)).reshape((SEQS, DOCS)).astype(jnp.int32),
        "w_query": centred(key_list[3], (D, D), (D // 2) ** -0.5, 0.1875, ((0, 8),)),
        "w_key": centred(key_list[4], (D, D), (D // 2) ** -0.5, 0.1875, ((0, 8),)),
        "w_value": centred(key_list[5], (D, D), D ** -0.5, 0.125, ((0, 8),)),
        "w_out": centred(key_list[6], (D, D), (D // 16) ** -0.5, 0.5, ((0, 8),)),
        "w_gate": centred(key_list[7], (FF, D), D ** -0.5, 0.125, ((0, 8),)),
        "w_up": centred(key_list[8], (FF, D), D ** -0.5, 0.125, ((0, 8),)),
        "w_down": centred(key_list[9], (D, FF), (FF // 4) ** -0.5, 0.125, ((0, 8),)),
    }


@jax.custom_vjp
def low(v):
    return lax.optimization_barrier(v.astype(jnp.bfloat16)).astype(jnp.float32)

@jax.custom_vjp
def low_back(v):
    return v

def low_keep(v):
    return (low(v), None)

def low_pass(kept, grad):
    return (grad,)

def back_keep(v):
    return (v, None)

def back_low(kept, grad):
    return (low(grad),)
low.defvjp(low_keep, low_pass)
low_back.defvjp(back_keep, back_low)
epsilon = 1e-05
theta_base = 10000.0
masked = -1e+30

def normalize(values):
    center = values - lax.optimization_barrier(jnp.mean(values, axis=-1, keepdims=True))
    return center * lax.rsqrt(lax.optimization_barrier(jnp.mean(center * center, axis=-1, keepdims=True)) + epsilon)

def project(values, weight):
    return lax.dot_general(values, weight, (((1,), (1,)), ((), ())), precision=lax.Precision.HIGHEST)

def doc_layout(lengths, places):
    ends = jnp.cumsum(lengths).astype(jnp.int32)
    starts = ends - lengths
    segment = lax.optimization_barrier(jnp.sum((places[:, None] >= ends[None, :]).astype(jnp.int32), axis=1)).astype(jnp.int32)
    member = segment[:, None] == jnp.arange(lengths.shape[0], dtype=jnp.int32)[None, :]
    offset = places - lax.optimization_barrier(jnp.sum(jnp.where(member, starts[None, :], 0), axis=1)).astype(jnp.int32)
    return (segment, offset)

def rope_tables(offset):
    half = HEAD_DIM // 2
    freq = theta_base ** (-2.0 * jnp.arange(half, dtype=jnp.float32) / HEAD_DIM)
    angle = offset.astype(jnp.float32)[:, None] * freq[None, :]
    return (jnp.cos(angle)[:, None, :], jnp.sin(angle)[:, None, :])

def rotate(values, cosine, sine):
    half = values.shape[-1] // 2
    first = values[..., :half]
    second = values[..., half:]
    return jnp.concatenate([first * cosine - second * sine, second * cosine + first * sine], axis=-1)

def attend(query, keys, values, segment):
    length = query.shape[0]
    block_size = math.gcd(length, 512)
    places = jnp.arange(length, dtype=jnp.int32)
    factor = 1.0 / math.sqrt(HEAD_DIM)

    def one_block(items):
        query_block, seg_block, place_block = items
        scores = jnp.einsum('qhe,khe->hqk', query_block, keys, precision=lax.Precision.HIGHEST) * factor
        scores = low_back(scores)
        allowed = (seg_block[:, None] == segment[None, :]) & (places[None, :] <= place_block[:, None])
        scores = jnp.where(allowed[None], scores, masked)
        probs = low(jax.nn.softmax(scores, axis=-1))
        return jnp.einsum('hqk,khe->qhe', probs, values, precision=lax.Precision.HIGHEST)
    count = length // block_size
    outputs = lax.map(jax.checkpoint(one_block), (query.reshape(count, block_size, HEADS, HEAD_DIM), segment.reshape(count, block_size), places.reshape(count, block_size)))
    return outputs.reshape(length, HEADS * HEAD_DIM)

def layer(x, w_query, w_key, w_value, w_out, w_gate, w_up, w_down, segment, offset):
    length = x.shape[0]
    cosine, sine = rope_tables(offset)
    normed = low(normalize(x))
    query = low_back(project(normed, w_query)).reshape(length, HEADS, HEAD_DIM)
    keys = low_back(project(normed, w_key)).reshape(length, HEADS, HEAD_DIM)
    query_rot = low(rotate(query, cosine, sine))
    keys_rot = low(rotate(keys, cosine, sine))
    values = low(low_back(project(normed, w_value))).reshape(length, HEADS, HEAD_DIM)
    attn_out = low(low_back(attend(query_rot, keys_rot, values, segment)))
    middle = x + low_back(project(attn_out, w_out))
    normed_two = low(normalize(middle))
    gate = low_back(project(normed_two, w_gate))
    up_part = low_back(project(normed_two, w_up))
    hidden = low(jax.nn.silu(gate) * up_part)
    return middle + low_back(project(hidden, w_down))

def reference(hidden_in, cotangent, doc_lengths, w_query, w_key, w_value, w_out, w_gate, w_up, w_down):
    weights = (w_query.astype(jnp.float32), w_key.astype(jnp.float32), w_value.astype(jnp.float32), w_out.astype(jnp.float32), w_gate.astype(jnp.float32), w_up.astype(jnp.float32), w_down.astype(jnp.float32))
    zeros = tuple((jnp.zeros_like(weight) for weight in weights))

    def one_sequence(totals, items):
        values, cot, lengths = items
        segment, offset = doc_layout(lengths, jnp.arange(SEQ, dtype=jnp.int32))

        def forward(x, wq_f, wk_f, wv_f, wo_f, wg_f, wu_f, wd_f):
            return layer(x, wq_f, wk_f, wv_f, wo_f, wg_f, wu_f, wd_f, segment, offset)
        result, pullback = jax.vjp(forward, values.astype(jnp.float32), weights[0], weights[1], weights[2], weights[3], weights[4], weights[5], weights[6])
        grads = pullback(cot.astype(jnp.float32))
        totals = tuple((total + grad for total, grad in zip(totals, grads[1:])))
        return (totals, (result.astype(jnp.bfloat16), grads[0]))
    totals, (outputs, grad_in) = lax.scan(one_sequence, zeros, (hidden_in, cotangent, doc_lengths))
    return (outputs, grad_in, totals[0], totals[1], totals[2], totals[3], totals[4], totals[5], totals[6])
```

```python
import math

import jax
import jax.numpy as jnp
from jax import lax
from jax.sharding import PartitionSpec as P

HEAD_DIM = 128

epsilon = 1e-05
theta_base = 10000.0
masked = -1e30
BF = jnp.bfloat16
F32 = jnp.float32


def normalize(values):
    center = values - jnp.mean(values, axis=-1, keepdims=True)
    inverse = lax.rsqrt(jnp.mean(center * center, axis=-1, keepdims=True) + epsilon)
    return (center * inverse, inverse)


def norm_back(normed, inverse, grad):
    inner = (
        grad
        - jnp.mean(grad, axis=-1, keepdims=True)
        - normed * jnp.mean(grad * normed, axis=-1, keepdims=True)
    )
    return inverse * inner


def dot(a, b, ca, cb):
    return lax.dot_general(a, b, (((ca,), (cb,)), ((), ())), preferred_element_type=F32)


def doc_layout(lengths, places):
    ends = jnp.cumsum(lengths)
    starts = ends - lengths
    segment = jnp.sum((places[:, None] >= ends[None, :]).astype(jnp.int32), axis=1)
    member = segment[:, None] == jnp.arange(lengths.shape[0], dtype=jnp.int32)[None, :]
    offset = places - jnp.sum(jnp.where(member, starts[None, :], 0), axis=1)
    return (segment, offset)


def rope_tables(offset, head_dim):
    half = head_dim // 2
    freq = theta_base ** (-2.0 * jnp.arange(half, dtype=F32) / head_dim)
    angle = offset.astype(F32)[:, None] * freq[None, :]
    return (jnp.cos(angle)[None], jnp.sin(angle)[None])


def rotate(values, cosine, sine):
    half = values.shape[-1] // 2
    first = values[..., :half]
    second = values[..., half:]
    return jnp.concatenate(
        [first * cosine - second * sine, second * cosine + first * sine], axis=-1
    )


def split_heads(values):
    tokens, width = values.shape
    return jnp.transpose(values.reshape(tokens, width // HEAD_DIM, HEAD_DIM), (1, 0, 2))


def join_heads(values):
    heads, tokens, size = values.shape
    return jnp.transpose(values, (1, 0, 2)).reshape(tokens, heads * size)


def gather_tokens(values):
    return lax.all_gather(values, "shard", axis=0, tiled=True)


def scatter_tokens(partial):
    return lax.psum_scatter(
        partial.astype(BF), "shard", scatter_dimension=0, tiled=True
    ).astype(F32)


def rows_to_columns(weight):
    return lax.all_to_all(weight, "shard", split_axis=1, concat_axis=0, tiled=True)


def columns_to_rows(grad):
    return lax.all_to_all(grad, "shard", split_axis=0, concat_axis=1, tiled=True)


def replica_sum(part):
    replicas = lax.axis_size("replica")
    if replicas != 4:
        return lax.psum(part, "replica")
    place = lax.axis_index("replica")
    inner = (place == 1) | (place == 2)
    from_outer = lax.ppermute(part, "replica", [(0, 1), (3, 2)])
    half = part + from_outer
    other = lax.ppermute(half, "replica", [(1, 2), (2, 1)])
    total = half + other
    back = lax.ppermute(total, "replica", [(1, 0), (2, 3)])
    return jnp.where(inner, total, back)


def body(hidden_in, cotangent, doc_lengths, w_query, w_key, w_value, w_out, w_gate, w_up, w_down):
    x = hidden_in[0].astype(F32)
    dyb = cotangent[0]
    tokens_here = x.shape[0]
    groups = lax.axis_size("shard")
    seq_length = tokens_here * groups
    factor = 1.0 / math.sqrt(HEAD_DIM)
    places = jnp.arange(seq_length, dtype=jnp.int32)
    segment, offset = doc_layout(doc_lengths[0], places)
    cosine, sine = rope_tables(offset, HEAD_DIM)
    allowed = ((segment[:, None] == segment[None, :]) & (places[None, :] <= places[:, None]))[None]

    normed_one, inverse_one = normalize(x)
    n1 = gather_tokens(normed_one.astype(BF))
    w_out_columns = rows_to_columns(w_out)
    query = rotate(split_heads(dot(n1, w_query, 1, 1)), cosine, sine).astype(BF)
    keys = rotate(split_heads(dot(n1, w_key, 1, 1)), cosine, sine).astype(BF)
    values = split_heads(dot(n1, w_value, 1, 1)).astype(BF)
    scores = factor * jnp.einsum("hqe,hke->hqk", query, keys, preferred_element_type=F32)
    scores = jnp.where(allowed, scores, masked)
    top = jnp.max(scores, axis=-1, keepdims=True)
    weights = jnp.where(allowed, jnp.exp(scores - top), 0.0)
    total = jnp.sum(weights, axis=-1, keepdims=True)
    log_total = top + jnp.log(total)
    attn = jnp.einsum("hqk,hke->hqe", weights.astype(BF), values, preferred_element_type=F32) / total
    out_b = join_heads(attn).astype(BF)
    middle = x + scatter_tokens(dot(out_b, w_out_columns, 1, 1))

    normed_two, inverse_two = normalize(middle)
    n2 = gather_tokens(normed_two.astype(BF))
    dy_all = gather_tokens(dyb)
    w_down_columns = rows_to_columns(w_down)
    gate = dot(n2, w_gate, 1, 1)
    up = dot(n2, w_up, 1, 1)
    sigma = jax.nn.sigmoid(gate)
    silu = gate * sigma
    hidden = (silu * up).astype(BF)
    grad_down = columns_to_rows(replica_sum(dot(dy_all, hidden, 0, 0).astype(BF)))
    grad_hidden = dot(dy_all, w_down_columns, 1, 0)
    grad_gate_b = (grad_hidden * up * sigma * (1.0 + gate * (1.0 - sigma))).astype(BF)
    grad_up_b = (grad_hidden * silu).astype(BF)
    grad_gate = replica_sum(dot(grad_gate_b, n2, 0, 0).astype(BF))
    grad_up = replica_sum(dot(grad_up_b, n2, 0, 0).astype(BF))
    grad_normed_two = scatter_tokens(dot(grad_gate_b, w_gate, 1, 0) + dot(grad_up_b, w_up, 1, 0))
    mixed = scatter_tokens(dot(hidden, w_down_columns, 1, 1))
    layer_out = (middle + mixed).astype(BF)
    grad_middle = dyb.astype(F32) + norm_back(normed_two, inverse_two, grad_normed_two)

    grad_middle_all = gather_tokens(grad_middle.astype(BF))
    grad_out = columns_to_rows(replica_sum(dot(grad_middle_all, out_b, 0, 0).astype(BF)))
    grad_attn = split_heads(dot(grad_middle_all, w_out_columns, 1, 0)).astype(BF)
    delta = jnp.sum(grad_attn.astype(F32) * attn, axis=-1, keepdims=True)
    probs = jnp.where(allowed, jnp.exp(scores - log_total), 0.0)
    grad_probs = jnp.einsum("hqe,hke->hqk", grad_attn, values, preferred_element_type=F32)
    grad_scores = (probs * (grad_probs - delta)).astype(BF)
    query_grad = factor * jnp.einsum("hqk,hke->hqe", grad_scores, keys, preferred_element_type=F32)
    key_grad = factor * jnp.einsum("hqk,hqe->hke", grad_scores, query, preferred_element_type=F32)
    value_grad = jnp.einsum("hqk,hqe->hke", probs.astype(BF), grad_attn, preferred_element_type=F32)
    query_grad = join_heads(rotate(query_grad, cosine, -sine)).astype(BF)
    key_grad = join_heads(rotate(key_grad, cosine, -sine)).astype(BF)
    value_grad = join_heads(value_grad).astype(BF)
    grad_query = replica_sum(dot(query_grad, n1, 0, 0).astype(BF))
    grad_key = replica_sum(dot(key_grad, n1, 0, 0).astype(BF))
    grad_value = replica_sum(dot(value_grad, n1, 0, 0).astype(BF))
    grad_normed_one = scatter_tokens(
        dot(query_grad, w_query, 1, 0) + dot(key_grad, w_key, 1, 0) + dot(value_grad, w_value, 1, 0)
    )
    grad_in = grad_middle + norm_back(normed_one, inverse_one, grad_normed_one)
    return (
        layer_out[None],
        grad_in[None],
        grad_query.astype(F32),
        grad_key.astype(F32),
        grad_value.astype(F32),
        grad_out.astype(F32),
        grad_gate.astype(F32),
        grad_up.astype(F32),
        grad_down.astype(F32),
    )


def solution(mesh):
    rows = P("shard", None)
    tokens = P("replica", "shard", None)
    in_specs = (tokens, tokens, P("replica", None)) + (rows,) * 7
    out_specs = (tokens, tokens) + (rows,) * 7
    return jax.shard_map(body, mesh=mesh, in_specs=in_specs, out_specs=out_specs, check_vma=False)
```

```python
import math

import jax
import jax.numpy as jnp
from jax import lax
from jax.experimental import pallas as pl
from jax.experimental.pallas import tpu as pltpu
from jax.sharding import PartitionSpec as P

HEAD_DIM = 128

epsilon = 1e-05
theta_base = 10000.0
masked = -1e30
BF = jnp.bfloat16
F32 = jnp.float32


MESH = pl.DeviceIdType.MESH
VMEM = pltpu.VMEM


def whereabouts():
    place = lax.axis_index("shard")
    core, col, row = lax.rem(place, 2), lax.rem(place // 2, 2), place // 4
    return (
        place,
        place + 1 - 2 * core,
        place + 2 - 4 * col,
        place + 4 - 8 * row,
        place + 2 - 4 * col + 4 - 8 * row,
    )


def greet(devices):
    barrier = pltpu.get_barrier_semaphore()
    replica = lax.axis_index("replica")
    for device in devices:
        pl.semaphore_signal(barrier, inc=1, device_id=(replica, device), device_id_type=MESH)
    pl.semaphore_wait(barrier, len(devices))


def gather_kernel(block, out, own_sem, sent, came):
    replica = lax.axis_index("replica")
    me, mate, across, along, far = whereabouts()
    half = block.shape[0] // 2
    low, high, whole = pl.ds(0, half), pl.ds(half, half), pl.ds(0, 2 * half)

    def move(k, slot, rows, device, first=False):
        return pltpu.make_async_remote_copy(
            src_ref=block.at[rows] if first else out.at[slot, rows],
            dst_ref=out.at[slot, rows],
            send_sem=sent.at[k],
            recv_sem=came.at[k],
            device_id=(replica, device),
            device_id_type=MESH,
        )

    own = pltpu.make_async_copy(block, out.at[me], own_sem)
    own.start()
    greet((mate, across, along))
    sends = [
        move(1, me, low, across, True),
        move(3, me, high, along, True),
        move(0, me, whole, mate, True),
        move(2, me, high, across, True),
        move(4, me, low, along, True),
    ]
    for copy in sends:
        copy.start()
    plan = [
        (1, across, low, ((5, along), (6, mate))),
        (3, along, high, ((7, across), (8, mate))),
        (2, across, high, ((9, mate),)),
        (4, along, low, ((10, mate),)),
        (5, far, low, ((11, mate),)),
        (7, far, high, ((12, mate),)),
    ]
    for k, slot, rows, onward in plan:
        move(k, slot, rows, mate).wait_recv()
        for k2, device in onward:
            copy = move(k2, slot, rows, device)
            copy.start()
            sends.append(copy)
    there = whereabouts_of_mate()
    for k, slot, rows in (
        (0, mate, whole),
        (6, there[0], low),
        (8, there[1], high),
        (9, there[0], high),
        (10, there[1], low),
        (11, there[2], low),
        (12, there[2], high),
    ):
        move(k, slot, rows, mate).wait_recv()
    for copy in sends:
        copy.wait_send()
    own.wait()


def whereabouts_of_mate():
    me, mate, across, along, far = whereabouts()
    shift = mate - me
    return across + shift, along + shift, far + shift


def gather_tokens(values):
    groups = lax.axis_size("shard")
    if groups != 8 or lax.axis_size("replica") != 4:
        return lax.all_gather(values, "shard", axis=0, tiled=True)
    tokens, width = values.shape
    out = pl.pallas_call(
        gather_kernel,
        out_shape=jax.ShapeDtypeStruct((groups, tokens, width), values.dtype),
        in_specs=[pl.BlockSpec(memory_space=VMEM)],
        out_specs=pl.BlockSpec(memory_space=pl.ANY),
        scratch_shapes=[
            pltpu.SemaphoreType.DMA,
            pltpu.SemaphoreType.DMA((13,)),
            pltpu.SemaphoreType.DMA((13,)),
        ],
        compiler_params=pltpu.CompilerParams(collective_id=0, has_side_effects=True),
        name="gather_tokens",
    )(values)
    return out.reshape(groups * tokens, width)


def scatter_kernel(parts, out, pair, sums, by_far, by_side, sent, came):
    replica = lax.axis_index("replica")
    me, mate, across, along, far = whereabouts()
    shift = mate - me
    half = out.shape[0] // 2
    low, high = pl.ds(0, half), pl.ds(half, half)
    mine = (me, across, along, far)

    def move(k, src, dst, device):
        return pltpu.make_async_remote_copy(
            src_ref=src,
            dst_ref=dst,
            send_sem=sent.at[k],
            recv_sem=came.at[k],
            device_id=(replica, device),
            device_id_type=MESH,
        )

    greet((mate, across, along))
    swaps = {k: move(k, parts.at[mine[k] + shift], pair.at[k], mate) for k in (3, 1, 2, 0)}
    for k in (3, 1, 2, 0):
        swaps[k].start()
    far_low = move(4, sums.at[2, low], by_far.at[0], across)
    far_high = move(5, sums.at[2, high], by_far.at[1], along)
    across_low = move(6, sums.at[0, low], by_side.at[0, low], across)
    along_high = move(7, sums.at[1, high], by_side.at[1, high], along)
    along_low = move(8, sums.at[1, low], by_side.at[1, low], along)
    across_high = move(9, sums.at[0, high], by_side.at[0, high], across)

    def pair_sum(k):
        swaps[k].wait_recv()
        sums[k - 1] = (parts[mine[k]].astype(F32) + pair[k].astype(F32)).astype(BF)

    pair_sum(3)
    far_low.start()
    far_high.start()
    pair_sum(1)
    across_low.start()
    pair_sum(2)
    along_high.start()
    swaps[0].wait_recv()
    out[...] = parts[me].astype(F32) + pair[0].astype(F32)
    far_low.wait_recv()
    sums[1, low] = (sums[1, low].astype(F32) + by_far[0].astype(F32)).astype(BF)
    along_low.start()
    far_high.wait_recv()
    sums[0, high] = (sums[0, high].astype(F32) + by_far[1].astype(F32)).astype(BF)
    across_high.start()
    across_low.wait_recv()
    along_high.wait_recv()
    along_low.wait_recv()
    across_high.wait_recv()
    out[...] = out[...] + (by_side[0].astype(F32) + by_side[1].astype(F32))
    for copy in (*swaps.values(), far_low, far_high, across_low, along_high, along_low, across_high):
        copy.wait_send()


def scatter_tokens(partial):
    groups = lax.axis_size("shard")
    partial = partial.astype(BF)
    if groups != 8 or lax.axis_size("replica") != 4:
        return lax.psum_scatter(partial, "shard", scatter_dimension=0, tiled=True).astype(F32)
    tokens, width = partial.shape[0] // groups, partial.shape[1]
    return pl.pallas_call(
        scatter_kernel,
        out_shape=jax.ShapeDtypeStruct((tokens, width), F32),
        in_specs=[pl.BlockSpec(memory_space=VMEM)],
        out_specs=pl.BlockSpec(memory_space=VMEM),
        scratch_shapes=[
            pltpu.VMEM((4, tokens, width), BF),
            pltpu.VMEM((3, tokens, width), BF),
            pltpu.VMEM((2, tokens // 2, width), BF),
            pltpu.VMEM((2, tokens, width), BF),
            pltpu.SemaphoreType.DMA((10,)),
            pltpu.SemaphoreType.DMA((10,)),
        ],
        compiler_params=pltpu.CompilerParams(
            collective_id=1, has_side_effects=True, vmem_limit_bytes=40 * 1024 * 1024
        ),
        name="scatter_tokens",
    )(partial.reshape(groups, tokens, width))


def normalize(values):
    center = values - jnp.mean(values, axis=-1, keepdims=True)
    inverse = lax.rsqrt(jnp.mean(center * center, axis=-1, keepdims=True) + epsilon)
    return (center * inverse, inverse)


def norm_back(normed, inverse, grad):
    inner = (
        grad
        - jnp.mean(grad, axis=-1, keepdims=True)
        - normed * jnp.mean(grad * normed, axis=-1, keepdims=True)
    )
    return inverse * inner


def dot(a, b, ca, cb):
    return lax.dot_general(a, b, (((ca,), (cb,)), ((), ())), preferred_element_type=F32)


def doc_layout(lengths, places):
    ends = jnp.cumsum(lengths)
    starts = ends - lengths
    segment = jnp.sum((places[:, None] >= ends[None, :]).astype(jnp.int32), axis=1)
    member = segment[:, None] == jnp.arange(lengths.shape[0], dtype=jnp.int32)[None, :]
    offset = places - jnp.sum(jnp.where(member, starts[None, :], 0), axis=1)
    return (segment, offset)


def rope_tables(offset, head_dim):
    half = head_dim // 2
    freq = theta_base ** (-2.0 * jnp.arange(half, dtype=F32) / head_dim)
    angle = offset.astype(F32)[:, None] * freq[None, :]
    return (jnp.cos(angle)[None], jnp.sin(angle)[None])


def rotate(values, cosine, sine):
    half = values.shape[-1] // 2
    first = values[..., :half]
    second = values[..., half:]
    return jnp.concatenate(
        [first * cosine - second * sine, second * cosine + first * sine], axis=-1
    )


def split_heads(values):
    tokens, width = values.shape
    return jnp.transpose(values.reshape(tokens, width // HEAD_DIM, HEAD_DIM), (1, 0, 2))


def join_heads(values):
    heads, tokens, size = values.shape
    return jnp.transpose(values, (1, 0, 2)).reshape(tokens, heads * size)


def rows_to_columns(weight):
    return lax.all_to_all(weight, "shard", split_axis=1, concat_axis=0, tiled=True)


def columns_to_rows(grad):
    return lax.all_to_all(grad, "shard", split_axis=0, concat_axis=1, tiled=True)


def replica_sum(part):
    replicas = lax.axis_size("replica")
    if replicas != 4:
        return lax.psum(part, "replica")
    place = lax.axis_index("replica")
    inner = (place == 1) | (place == 2)
    from_outer = lax.ppermute(part, "replica", [(0, 1), (3, 2)])
    half = part + from_outer
    other = lax.ppermute(half, "replica", [(1, 2), (2, 1)])
    total = half + other
    back = lax.ppermute(total, "replica", [(1, 0), (2, 3)])
    return jnp.where(inner, total, back)


def body(hidden_in, cotangent, doc_lengths, w_query, w_key, w_value, w_out, w_gate, w_up, w_down):
    x = hidden_in[0].astype(F32)
    dyb = cotangent[0]
    tokens_here = x.shape[0]
    groups = lax.axis_size("shard")
    seq_length = tokens_here * groups
    factor = 1.0 / math.sqrt(HEAD_DIM)
    places = jnp.arange(seq_length, dtype=jnp.int32)
    segment, offset = doc_layout(doc_lengths[0], places)
    cosine, sine = rope_tables(offset, HEAD_DIM)
    allowed = ((segment[:, None] == segment[None, :]) & (places[None, :] <= places[:, None]))[None]

    normed_one, inverse_one = normalize(x)
    n1 = gather_tokens(normed_one.astype(BF))
    w_out_columns = rows_to_columns(w_out)
    query = rotate(split_heads(dot(n1, w_query, 1, 1)), cosine, sine).astype(BF)
    keys = rotate(split_heads(dot(n1, w_key, 1, 1)), cosine, sine).astype(BF)
    values = split_heads(dot(n1, w_value, 1, 1)).astype(BF)
    scores = factor * jnp.einsum("hqe,hke->hqk", query, keys, preferred_element_type=F32)
    scores = jnp.where(allowed, scores, masked)
    top = jnp.max(scores, axis=-1, keepdims=True)
    weights = jnp.where(allowed, jnp.exp(scores - top), 0.0)
    total = jnp.sum(weights, axis=-1, keepdims=True)
    log_total = top + jnp.log(total)
    attn = jnp.einsum("hqk,hke->hqe", weights.astype(BF), values, preferred_element_type=F32) / total
    out_b = join_heads(attn).astype(BF)
    middle = x + scatter_tokens(dot(out_b, w_out_columns, 1, 1))

    normed_two, inverse_two = normalize(middle)
    n2 = gather_tokens(normed_two.astype(BF))
    dy_all = gather_tokens(dyb)
    w_down_columns = rows_to_columns(w_down)
    gate = dot(n2, w_gate, 1, 1)
    up = dot(n2, w_up, 1, 1)
    sigma = jax.nn.sigmoid(gate)
    silu = gate * sigma
    hidden = (silu * up).astype(BF)
    grad_down = columns_to_rows(replica_sum(dot(dy_all, hidden, 0, 0).astype(BF)))
    grad_hidden = dot(dy_all, w_down_columns, 1, 0)
    grad_gate_b = (grad_hidden * up * sigma * (1.0 + gate * (1.0 - sigma))).astype(BF)
    grad_up_b = (grad_hidden * silu).astype(BF)
    grad_gate = replica_sum(dot(grad_gate_b, n2, 0, 0).astype(BF))
    grad_up = replica_sum(dot(grad_up_b, n2, 0, 0).astype(BF))
    grad_normed_two = scatter_tokens(dot(grad_gate_b, w_gate, 1, 0) + dot(grad_up_b, w_up, 1, 0))
    mixed = scatter_tokens(dot(hidden, w_down_columns, 1, 1))
    layer_out = (middle + mixed).astype(BF)
    grad_middle = dyb.astype(F32) + norm_back(normed_two, inverse_two, grad_normed_two)

    grad_middle_all = gather_tokens(grad_middle.astype(BF))
    grad_out = columns_to_rows(replica_sum(dot(grad_middle_all, out_b, 0, 0).astype(BF)))
    grad_attn = split_heads(dot(grad_middle_all, w_out_columns, 1, 0)).astype(BF)
    delta = jnp.sum(grad_attn.astype(F32) * attn, axis=-1, keepdims=True)
    probs = jnp.where(allowed, jnp.exp(scores - log_total), 0.0)
    grad_probs = jnp.einsum("hqe,hke->hqk", grad_attn, values, preferred_element_type=F32)
    grad_scores = (probs * (grad_probs - delta)).astype(BF)
    query_grad = factor * jnp.einsum("hqk,hke->hqe", grad_scores, keys, preferred_element_type=F32)
    key_grad = factor * jnp.einsum("hqk,hqe->hke", grad_scores, query, preferred_element_type=F32)
    value_grad = jnp.einsum("hqk,hqe->hke", probs.astype(BF), grad_attn, preferred_element_type=F32)
    query_grad = join_heads(rotate(query_grad, cosine, -sine)).astype(BF)
    key_grad = join_heads(rotate(key_grad, cosine, -sine)).astype(BF)
    value_grad = join_heads(value_grad).astype(BF)
    grad_query = replica_sum(dot(query_grad, n1, 0, 0).astype(BF))
    grad_key = replica_sum(dot(key_grad, n1, 0, 0).astype(BF))
    grad_value = replica_sum(dot(value_grad, n1, 0, 0).astype(BF))
    grad_normed_one = scatter_tokens(
        dot(query_grad, w_query, 1, 0) + dot(key_grad, w_key, 1, 0) + dot(value_grad, w_value, 1, 0)
    )
    grad_in = grad_middle + norm_back(normed_one, inverse_one, grad_normed_one)
    return (
        layer_out[None],
        grad_in[None],
        grad_query.astype(F32),
        grad_key.astype(F32),
        grad_value.astype(F32),
        grad_out.astype(F32),
        grad_gate.astype(F32),
        grad_up.astype(F32),
        grad_down.astype(F32),
    )


def solution(mesh):
    rows = P("shard", None)
    tokens = P("replica", "shard", None)
    in_specs = (tokens, tokens, P("replica", None)) + (rows,) * 7
    out_specs = (tokens, tokens) + (rows,) * 7
    return jax.shard_map(body, mesh=mesh, in_specs=in_specs, out_specs=out_specs, check_vma=False)
```

```python
import functools
import math

import jax
import jax.numpy as jnp
from jax import lax
from jax.experimental import pallas as pl
from jax.experimental.pallas import tpu as pltpu
from jax.sharding import PartitionSpec as P

HEAD_DIM = 128

epsilon = 1e-05
theta_base = 10000.0
masked = -1e30
BF = jnp.bfloat16
F32 = jnp.float32


MESH = pl.DeviceIdType.MESH
VMEM = pltpu.VMEM


def whereabouts():
    place = lax.axis_index("shard")
    core, col, row = lax.rem(place, 2), lax.rem(place // 2, 2), place // 4
    return (
        place,
        place + 1 - 2 * core,
        place + 2 - 4 * col,
        place + 4 - 8 * row,
        place + 2 - 4 * col + 4 - 8 * row,
    )


def greet(devices):
    barrier = pltpu.get_barrier_semaphore()
    replica = lax.axis_index("replica")
    for device in devices:
        pl.semaphore_signal(barrier, inc=1, device_id=(replica, device), device_id_type=MESH)
    pl.semaphore_wait(barrier, len(devices))


def gather_kernel(block, out, own_sem, sent, came):
    replica = lax.axis_index("replica")
    me, mate, across, along, far = whereabouts()
    half = block.shape[0] // 2
    low, high, whole = pl.ds(0, half), pl.ds(half, half), pl.ds(0, 2 * half)

    def move(k, slot, rows, device, first=False):
        return pltpu.make_async_remote_copy(
            src_ref=block.at[rows] if first else out.at[slot, rows],
            dst_ref=out.at[slot, rows],
            send_sem=sent.at[k],
            recv_sem=came.at[k],
            device_id=(replica, device),
            device_id_type=MESH,
        )

    own = pltpu.make_async_copy(block, out.at[me], own_sem)
    own.start()
    greet((mate, across, along))
    sends = [
        move(1, me, low, across, True),
        move(3, me, high, along, True),
        move(0, me, whole, mate, True),
        move(2, me, high, across, True),
        move(4, me, low, along, True),
    ]
    for copy in sends:
        copy.start()
    plan = [
        (1, across, low, ((5, along), (6, mate))),
        (3, along, high, ((7, across), (8, mate))),
        (2, across, high, ((9, mate),)),
        (4, along, low, ((10, mate),)),
        (5, far, low, ((11, mate),)),
        (7, far, high, ((12, mate),)),
    ]
    for k, slot, rows, onward in plan:
        move(k, slot, rows, mate).wait_recv()
        for k2, device in onward:
            copy = move(k2, slot, rows, device)
            copy.start()
            sends.append(copy)
    there = whereabouts_of_mate()
    for k, slot, rows in (
        (0, mate, whole),
        (6, there[0], low),
        (8, there[1], high),
        (9, there[0], high),
        (10, there[1], low),
        (11, there[2], low),
        (12, there[2], high),
    ):
        move(k, slot, rows, mate).wait_recv()
    for copy in sends:
        copy.wait_send()
    own.wait()


def whereabouts_of_mate():
    me, mate, across, along, far = whereabouts()
    shift = mate - me
    return across + shift, along + shift, far + shift


def gather_tokens(values):
    groups = lax.axis_size("shard")
    if groups != 8 or lax.axis_size("replica") != 4:
        return lax.all_gather(values, "shard", axis=0, tiled=True)
    tokens, width = values.shape
    out = pl.pallas_call(
        gather_kernel,
        out_shape=jax.ShapeDtypeStruct((groups, tokens, width), values.dtype),
        in_specs=[pl.BlockSpec(memory_space=VMEM)],
        out_specs=pl.BlockSpec(memory_space=pl.ANY),
        scratch_shapes=[
            pltpu.SemaphoreType.DMA,
            pltpu.SemaphoreType.DMA((13,)),
            pltpu.SemaphoreType.DMA((13,)),
        ],
        compiler_params=pltpu.CompilerParams(collective_id=0, has_side_effects=True),
        name="gather_tokens",
    )(values)
    return out.reshape(groups * tokens, width)


def scatter_kernel(parts, out, pair, sums, by_far, by_side, sent, came):
    replica = lax.axis_index("replica")
    me, mate, across, along, far = whereabouts()
    shift = mate - me
    half = out.shape[0] // 2
    low, high = pl.ds(0, half), pl.ds(half, half)
    mine = (me, across, along, far)

    def move(k, src, dst, device):
        return pltpu.make_async_remote_copy(
            src_ref=src,
            dst_ref=dst,
            send_sem=sent.at[k],
            recv_sem=came.at[k],
            device_id=(replica, device),
            device_id_type=MESH,
        )

    greet((mate, across, along))
    swaps = {k: move(k, parts.at[mine[k] + shift], pair.at[k], mate) for k in (3, 1, 2, 0)}
    for k in (3, 1, 2, 0):
        swaps[k].start()
    far_low = move(4, sums.at[2, low], by_far.at[0], across)
    far_high = move(5, sums.at[2, high], by_far.at[1], along)
    across_low = move(6, sums.at[0, low], by_side.at[0, low], across)
    along_high = move(7, sums.at[1, high], by_side.at[1, high], along)
    along_low = move(8, sums.at[1, low], by_side.at[1, low], along)
    across_high = move(9, sums.at[0, high], by_side.at[0, high], across)

    def pair_sum(k):
        swaps[k].wait_recv()
        sums[k - 1] = (parts[mine[k]].astype(F32) + pair[k].astype(F32)).astype(BF)

    pair_sum(3)
    far_low.start()
    far_high.start()
    pair_sum(1)
    across_low.start()
    pair_sum(2)
    along_high.start()
    swaps[0].wait_recv()
    out[...] = parts[me].astype(F32) + pair[0].astype(F32)
    far_low.wait_recv()
    sums[1, low] = (sums[1, low].astype(F32) + by_far[0].astype(F32)).astype(BF)
    along_low.start()
    far_high.wait_recv()
    sums[0, high] = (sums[0, high].astype(F32) + by_far[1].astype(F32)).astype(BF)
    across_high.start()
    across_low.wait_recv()
    along_high.wait_recv()
    along_low.wait_recv()
    across_high.wait_recv()
    out[...] = out[...] + (by_side[0].astype(F32) + by_side[1].astype(F32))
    for copy in (*swaps.values(), far_low, far_high, across_low, along_high, along_low, across_high):
        copy.wait_send()


def scatter_tokens(partial):
    groups = lax.axis_size("shard")
    partial = partial.astype(BF)
    if groups != 8 or lax.axis_size("replica") != 4:
        return lax.psum_scatter(partial, "shard", scatter_dimension=0, tiled=True).astype(F32)
    tokens, width = partial.shape[0] // groups, partial.shape[1]
    return pl.pallas_call(
        scatter_kernel,
        out_shape=jax.ShapeDtypeStruct((tokens, width), F32),
        in_specs=[pl.BlockSpec(memory_space=VMEM)],
        out_specs=pl.BlockSpec(memory_space=VMEM),
        scratch_shapes=[
            pltpu.VMEM((4, tokens, width), BF),
            pltpu.VMEM((3, tokens, width), BF),
            pltpu.VMEM((2, tokens // 2, width), BF),
            pltpu.VMEM((2, tokens, width), BF),
            pltpu.SemaphoreType.DMA((10,)),
            pltpu.SemaphoreType.DMA((10,)),
        ],
        compiler_params=pltpu.CompilerParams(
            collective_id=1, has_side_effects=True, vmem_limit_bytes=40 * 1024 * 1024
        ),
        name="scatter_tokens",
    )(partial.reshape(groups, tokens, width))


def tile_loop(rows, columns, size, step):
    across = columns // size

    def one(i, carry):
        step(
            pl.ds(pl.multiple_of((i // across) * size, size), size),
            pl.ds(pl.multiple_of(lax.rem(i, across) * size, size), size),
        )
        return carry

    lax.fori_loop(0, (rows // size) * across, one, 0)


def product(a, b, ca, cb):
    return lax.dot_general(a, b, (((ca,), (cb,)), ((), ())), preferred_element_type=F32)


def ffn_tile(normed, dy, w_gate, w_up, w_down, hidden, grad_gate, grad_up, rows, columns):
    gate = product(normed[rows, :], w_gate[columns, :], 1, 1)
    up = product(normed[rows, :], w_up[columns, :], 1, 1)
    grad = product(dy[rows, :], w_down[:, columns], 1, 0)
    sigma = 1.0 / (1.0 + jnp.exp(-gate))
    silu = gate * sigma
    hidden[rows, columns] = (silu * up).astype(BF)
    grad_gate[rows, columns] = (grad * up * sigma * (1.0 + gate * (1.0 - sigma))).astype(BF)
    grad_up[rows, columns] = (grad * silu).astype(BF)


def every_kernel(
    blocks, own_normed, dy_every, own_hidden, own_grad_gate, own_grad_up, w_gate, w_up, w_down,
    out_gate, out_up, out_down, landed,
    normed, dy, hidden, grad_gate, grad_up, down, load_sem, sent, came,
):
    replica = lax.axis_index("replica")
    replicas = blocks.shape[0]
    me, mate, across, along, far = whereabouts()
    shift = mate - me
    tokens = blocks.shape[1]
    half = tokens // 2
    low, high, whole = pl.ds(0, half), pl.ds(half, half), pl.ds(0, tokens)
    order = (me, mate, across, across + shift, along, along + shift, far, far + shift)
    size = 512

    def move(n, k, slot, rows, device, first=False):
        src = blocks.at[lax.rem(replica + n + 1, replicas), rows] if first else landed.at[n, slot, rows]
        return pltpu.make_async_remote_copy(
            src_ref=src,
            dst_ref=landed.at[n, slot, rows],
            send_sem=sent.at[n, k],
            recv_sem=came.at[n, k],
            device_id=(replica, device),
            device_id_type=MESH,
        )

    def sends_one(n):
        return [
            move(n, 1, me, low, across, True),
            move(n, 3, me, high, along, True),
            move(n, 0, me, whole, mate, True),
            move(n, 2, me, high, across, True),
            move(n, 4, me, low, along, True),
        ]

    def sends_two(n):
        return [
            move(n, 5, across, low, along),
            move(n, 7, along, high, across),
            move(n, 6, across, low, mate),
            move(n, 8, along, high, mate),
        ]

    def sends_three(n):
        return [move(n, 9, across, high, mate), move(n, 10, along, low, mate)]

    def sends_four(n):
        return [move(n, 11, far, low, mate), move(n, 12, far, high, mate)]

    def start_all(copies):
        for copy in copies:
            copy.start()

    def stage_two(n):
        move(n, 1, across, low, across).wait_recv()
        move(n, 3, along, high, along).wait_recv()
        start_all(sends_two(n))

    def stage_three(n):
        move(n, 2, across, high, across).wait_recv()
        move(n, 4, along, low, along).wait_recv()
        start_all(sends_three(n))

    def stage_four(n):
        move(n, 5, far, low, along).wait_recv()
        move(n, 7, far, high, across).wait_recv()
        start_all(sends_four(n))

    def finish(n):
        move(n, 0, mate, whole, mate).wait_recv()
        for k, slot, rows in (
            (6, across + shift, low),
            (8, along + shift, high),
            (9, across + shift, high),
            (10, along + shift, low),
            (11, far + shift, low),
            (12, far + shift, high),
        ):
            move(n, k, slot, rows, mate).wait_recv()
        for copy in sends_one(n) + sends_two(n) + sends_three(n) + sends_four(n):
            copy.wait_send()

    def dy_load(n, slot):
        source = dy_every.at[lax.rem(replica + n, replicas)]
        return pltpu.make_async_copy(source, dy.at[slot], load_sem.at[slot, 8])

    def normed_loads(n, slot):
        loads = []
        for i, device in enumerate(order):
            source = blocks.at[lax.rem(replica + n, replicas)] if i == 0 else landed.at[n - 1, device]
            rows = pl.ds(pl.multiple_of(device * tokens, tokens), tokens)
            loads.append(pltpu.make_async_copy(source, normed.at[slot, rows], load_sem.at[slot, i]))
        return loads

    first = [
        pltpu.make_async_copy(own_normed, normed.at[0], load_sem.at[0, 0]),
        pltpu.make_async_copy(own_hidden, hidden, load_sem.at[0, 1]),
        pltpu.make_async_copy(own_grad_gate, grad_gate, load_sem.at[0, 2]),
        pltpu.make_async_copy(own_grad_up, grad_up, load_sem.at[0, 3]),
        dy_load(0, 0),
    ]
    start_all(first)
    greet((mate, across, along))
    start_all(sends_one(0))
    for copy in first:
        copy.wait()

    def sequence(n, carry):
        slot = lax.rem(n, 2)
        more = n < replicas - 1

        def collect(out, left, right):
            def step(rows, columns):
                value = product(left[:, rows], right[:, columns], 0, 0)
                out[rows, columns] = jnp.where(n == 0, value, out[rows, columns] + value)

            tile_loop(out.shape[0], out.shape[1], size, step)

        @pl.when(more)
        def _():
            dy_load(n + 1, 1 - slot).start()

        @pl.when(n > 0)
        def _():
            tile_loop(
                normed.shape[1], w_gate.shape[0], size,
                functools.partial(
                    ffn_tile, normed.at[slot], dy.at[slot], w_gate, w_up, w_down,
                    hidden, grad_gate, grad_up,
                ),
            )

        @pl.when(more)
        def _():
            stage_two(n)

            @pl.when(n > 0)
            def _():
                stage_three(n)

        collect(out_gate, grad_gate, normed.at[slot])

        @pl.when(more)
        def _():
            @pl.when(n == 0)
            def _():
                stage_three(n)

            @pl.when(n > 0)
            def _():
                stage_four(n)

            @pl.when(n < replicas - 2)
            def _():
                start_all(sends_one(n + 1))

        collect(out_up, grad_up, normed.at[slot])

        @pl.when(more)
        def _():
            @pl.when(n == 0)
            def _():
                stage_four(n)

            finish(n)
            start_all(normed_loads(n + 1, 1 - slot))

        collect(down, dy.at[slot], hidden)

        @pl.when(more)
        def _():
            dy_load(n + 1, 1 - slot).wait()
            for copy in normed_loads(n + 1, 1 - slot):
                copy.wait()

        return carry

    lax.fori_loop(0, replicas, sequence, 0)
    rows = hidden.shape[0]
    for i, buffer in enumerate((hidden, grad_gate)):
        buffer[...] = down[i * rows : (i + 1) * rows, :].astype(BF)
        pltpu.make_async_copy(buffer, out_down.at[pl.ds(i * rows, rows)], load_sem.at[0, i]).start()
    for i, buffer in enumerate((hidden, grad_gate)):
        pltpu.make_async_copy(buffer, out_down.at[pl.ds(i * rows, rows)], load_sem.at[0, i]).wait()


def ffn_grads(blocks, n2, dy_every, own, w_gate, w_up, w_down_columns):
    replicas, tokens, width = blocks.shape
    sequence = n2.shape[0]
    groups = sequence // tokens
    columns = w_gate.shape[0]
    anywhere, vmem = pl.BlockSpec(memory_space=pl.ANY), pl.BlockSpec(memory_space=VMEM)
    out = pl.pallas_call(
        every_kernel,
        out_shape=(
            jax.ShapeDtypeStruct((columns, width), F32),
            jax.ShapeDtypeStruct((columns, width), F32),
            jax.ShapeDtypeStruct((width, columns), BF),
            jax.ShapeDtypeStruct((replicas - 1, groups, tokens, width), BF),
        ),
        in_specs=[anywhere] * 6 + [vmem] * 3,
        out_specs=(vmem, vmem, anywhere, anywhere),
        scratch_shapes=[
            pltpu.VMEM((2, sequence, width), BF),
            pltpu.VMEM((2, sequence, width), BF),
            pltpu.VMEM((sequence, columns), BF),
            pltpu.VMEM((sequence, columns), BF),
            pltpu.VMEM((sequence, columns), BF),
            pltpu.VMEM((width, columns), F32),
            pltpu.SemaphoreType.DMA((2, 9)),
            pltpu.SemaphoreType.DMA((replicas - 1, 13)),
            pltpu.SemaphoreType.DMA((replicas - 1, 13)),
        ],
        compiler_params=pltpu.CompilerParams(
            collective_id=2, has_side_effects=True, vmem_limit_bytes=67043328
        ),
        cost_estimate=pl.CostEstimate(
            flops=42 * sequence * width * columns, bytes_accessed=80 * 1024 * 1024, transcendentals=0
        ),
        name="ffn_grads",
    )(blocks, n2, dy_every, *own, w_gate, w_up, w_down_columns)
    return out[:3]


def normalize(values):
    center = values - jnp.mean(values, axis=-1, keepdims=True)
    inverse = lax.rsqrt(jnp.mean(center * center, axis=-1, keepdims=True) + epsilon)
    return (center * inverse, inverse)


def norm_back(normed, inverse, grad):
    inner = (
        grad
        - jnp.mean(grad, axis=-1, keepdims=True)
        - normed * jnp.mean(grad * normed, axis=-1, keepdims=True)
    )
    return inverse * inner


def dot(a, b, ca, cb):
    return lax.dot_general(a, b, (((ca,), (cb,)), ((), ())), preferred_element_type=F32)


def doc_layout(lengths, places):
    ends = jnp.cumsum(lengths)
    starts = ends - lengths
    segment = jnp.sum((places[:, None] >= ends[None, :]).astype(jnp.int32), axis=1)
    member = segment[:, None] == jnp.arange(lengths.shape[0], dtype=jnp.int32)[None, :]
    offset = places - jnp.sum(jnp.where(member, starts[None, :], 0), axis=1)
    return (segment, offset)


def rope_tables(offset, head_dim):
    half = head_dim // 2
    freq = theta_base ** (-2.0 * jnp.arange(half, dtype=F32) / head_dim)
    angle = offset.astype(F32)[:, None] * freq[None, :]
    return (jnp.cos(angle)[None], jnp.sin(angle)[None])


def rotate(values, cosine, sine):
    half = values.shape[-1] // 2
    first = values[..., :half]
    second = values[..., half:]
    return jnp.concatenate(
        [first * cosine - second * sine, second * cosine + first * sine], axis=-1
    )


def split_heads(values):
    tokens, width = values.shape
    return jnp.transpose(values.reshape(tokens, width // HEAD_DIM, HEAD_DIM), (1, 0, 2))


def join_heads(values):
    heads, tokens, size = values.shape
    return jnp.transpose(values, (1, 0, 2)).reshape(tokens, heads * size)


def rows_to_columns(weight):
    return lax.all_to_all(weight, "shard", split_axis=1, concat_axis=0, tiled=True)


def columns_to_rows(grad):
    return lax.all_to_all(grad, "shard", split_axis=0, concat_axis=1, tiled=True)


def ffn_parts(normed, dy, w_gate, w_up, w_down_columns):
    gate = dot(normed, w_gate, 1, 1)
    up = dot(normed, w_up, 1, 1)
    sigma = jax.nn.sigmoid(gate)
    silu = gate * sigma
    grad_hidden = dot(dy, w_down_columns, 1, 0)
    grad_gate = (grad_hidden * up * sigma * (1.0 + gate * (1.0 - sigma))).astype(BF)
    return (silu * up).astype(BF), grad_gate, (grad_hidden * silu).astype(BF)


def body(hidden_in, cotangent, doc_lengths, w_query, w_key, w_value, w_out, w_gate, w_up, w_down):
    x = hidden_in[0].astype(F32)
    dyb = cotangent[0]
    tokens_here = x.shape[0]
    groups = lax.axis_size("shard")
    seq_length = tokens_here * groups
    factor = 1.0 / math.sqrt(HEAD_DIM)
    places = jnp.arange(seq_length, dtype=jnp.int32)
    segment, offset = doc_layout(doc_lengths[0], places)
    cosine, sine = rope_tables(offset, HEAD_DIM)
    allowed = ((segment[:, None] == segment[None, :]) & (places[None, :] <= places[:, None]))[None]

    normed_one, inverse_one = normalize(x)
    n1 = gather_tokens(normed_one.astype(BF))
    w_out_columns = rows_to_columns(w_out)
    query = rotate(split_heads(dot(n1, w_query, 1, 1)), cosine, sine).astype(BF)
    keys = rotate(split_heads(dot(n1, w_key, 1, 1)), cosine, sine).astype(BF)
    values = split_heads(dot(n1, w_value, 1, 1)).astype(BF)
    scores = factor * jnp.einsum("hqe,hke->hqk", query, keys, preferred_element_type=F32)
    scores = jnp.where(allowed, scores, masked)
    top = jnp.max(scores, axis=-1, keepdims=True)
    weights = jnp.where(allowed, jnp.exp(scores - top), 0.0)
    total = jnp.sum(weights, axis=-1, keepdims=True)
    log_total = top + jnp.log(total)
    attn = jnp.einsum("hqk,hke->hqe", weights.astype(BF), values, preferred_element_type=F32) / total
    out_b = join_heads(attn).astype(BF)
    middle = x + scatter_tokens(dot(out_b, w_out_columns, 1, 1))

    normed_two, inverse_two = normalize(middle)
    normed_two_b = normed_two.astype(BF)
    n2 = gather_tokens(normed_two_b)
    dy_every = lax.all_gather(dyb, ("replica", "shard"), axis=0, tiled=True)
    dy_every = dy_every.reshape(-1, seq_length, x.shape[1])
    dy_all = lax.dynamic_index_in_dim(dy_every, lax.axis_index("replica"), 0, keepdims=False)
    w_down_columns = rows_to_columns(w_down)
    own = ffn_parts(n2, dy_all, w_gate, w_up, w_down_columns)
    hidden, grad_gate_b, grad_up_b = own
    grad_normed_two = scatter_tokens(dot(grad_gate_b, w_gate, 1, 0) + dot(grad_up_b, w_up, 1, 0))
    mixed = scatter_tokens(dot(hidden, w_down_columns, 1, 1))
    layer_out = (middle + mixed).astype(BF)
    grad_middle = dyb.astype(F32) + norm_back(normed_two, inverse_two, grad_normed_two)

    grad_middle_all = gather_tokens(grad_middle.astype(BF))
    grad_out = columns_to_rows(dot(grad_middle_all, out_b, 0, 0).astype(BF))
    grad_attn = split_heads(dot(grad_middle_all, w_out_columns, 1, 0)).astype(BF)
    delta = jnp.sum(grad_attn.astype(F32) * attn, axis=-1, keepdims=True)
    probs = jnp.where(allowed, jnp.exp(scores - log_total), 0.0)
    grad_probs = jnp.einsum("hqe,hke->hqk", grad_attn, values, preferred_element_type=F32)
    grad_scores = (probs * (grad_probs - delta)).astype(BF)
    query_grad = factor * jnp.einsum("hqk,hke->hqe", grad_scores, keys, preferred_element_type=F32)
    key_grad = factor * jnp.einsum("hqk,hqe->hke", grad_scores, query, preferred_element_type=F32)
    value_grad = jnp.einsum("hqk,hqe->hke", probs.astype(BF), grad_attn, preferred_element_type=F32)
    query_grad = join_heads(rotate(query_grad, cosine, -sine)).astype(BF)
    key_grad = join_heads(rotate(key_grad, cosine, -sine)).astype(BF)
    value_grad = join_heads(value_grad).astype(BF)
    grad_query = dot(query_grad, n1, 0, 0).astype(BF)
    grad_key = dot(key_grad, n1, 0, 0).astype(BF)
    grad_value = dot(value_grad, n1, 0, 0).astype(BF)
    grad_query, grad_key, grad_value, grad_out, n2 = lax.optimization_barrier(
        (grad_query, grad_key, grad_value, grad_out, n2)
    )
    grad_query, grad_key, grad_value, grad_out = lax.psum(
        (grad_query, grad_key, grad_value, grad_out), "replica"
    )
    grad_normed_one = scatter_tokens(
        dot(query_grad, w_query, 1, 0) + dot(key_grad, w_key, 1, 0) + dot(value_grad, w_value, 1, 0)
    )
    grad_in = grad_middle + norm_back(normed_one, inverse_one, grad_normed_one)
    if groups == 8 and lax.axis_size("replica") == 4:
        blocks = lax.all_gather(normed_two_b, "replica", axis=0)
        grad_gate, grad_up, grad_down = ffn_grads(
            blocks, n2, dy_every, own, w_gate, w_up, w_down_columns
        )
    else:
        n2_every = lax.all_gather(normed_two_b, ("replica", "shard"), axis=0, tiled=True)
        dy_every = dy_every.reshape(n2_every.shape)
        hidden, grad_gate_b, grad_up_b = ffn_parts(n2_every, dy_every, w_gate, w_up, w_down_columns)
        grad_down = dot(dy_every, hidden, 0, 0).astype(BF)
        grad_gate = dot(grad_gate_b, n2_every, 0, 0)
        grad_up = dot(grad_up_b, n2_every, 0, 0)
    grad_down = columns_to_rows(grad_down)
    return (
        layer_out[None],
        grad_in[None],
        grad_query.astype(F32),
        grad_key.astype(F32),
        grad_value.astype(F32),
        grad_out.astype(F32),
        grad_gate,
        grad_up,
        grad_down.astype(F32),
    )


def solution(mesh):
    rows = P("shard", None)
    tokens = P("replica", "shard", None)
    in_specs = (tokens, tokens, P("replica", None)) + (rows,) * 7
    out_specs = (tokens, tokens) + (rows,) * 7
    return jax.shard_map(body, mesh=mesh, in_specs=in_specs, out_specs=out_specs, check_vma=False)
```

```python
import functools
import math

import jax
import jax.numpy as jnp
from jax import lax
from jax.experimental import pallas as pl
from jax.experimental.pallas import tpu as pltpu
from jax.sharding import PartitionSpec as P

HEAD_DIM = 128

epsilon = 1e-05
theta_base = 10000.0
masked = -1e30
BF = jnp.bfloat16
F32 = jnp.float32
MESH = pl.DeviceIdType.MESH
VMEM = pltpu.VMEM


def normalize(values):
    center = values - jnp.mean(values, axis=-1, keepdims=True)
    inverse = lax.rsqrt(jnp.mean(center * center, axis=-1, keepdims=True) + epsilon)
    return (center * inverse, inverse)


def norm_back(normed, inverse, grad):
    inner = (
        grad
        - jnp.mean(grad, axis=-1, keepdims=True)
        - normed * jnp.mean(grad * normed, axis=-1, keepdims=True)
    )
    return inverse * inner


def dot(a, b, ca, cb):
    return lax.dot_general(a, b, (((ca,), (cb,)), ((), ())), preferred_element_type=F32)


def doc_layout(lengths, places):
    ends = jnp.cumsum(lengths)
    starts = ends - lengths
    segment = jnp.sum((places[:, None] >= ends[None, :]).astype(jnp.int32), axis=1)
    member = segment[:, None] == jnp.arange(lengths.shape[0], dtype=jnp.int32)[None, :]
    offset = places - jnp.sum(jnp.where(member, starts[None, :], 0), axis=1)
    return (segment, offset)


def rope_tables(offset, head_dim):
    half = head_dim // 2
    freq = theta_base ** (-2.0 * jnp.arange(half, dtype=F32) / head_dim)
    angle = offset.astype(F32)[:, None] * freq[None, :]
    return (jnp.cos(angle)[None], jnp.sin(angle)[None])


def rotate(values, cosine, sine):
    half = values.shape[-1] // 2
    first = values[..., :half]
    second = values[..., half:]
    return jnp.concatenate(
        [first * cosine - second * sine, second * cosine + first * sine], axis=-1
    )


def split_heads(values):
    tokens, width = values.shape
    return jnp.transpose(values.reshape(tokens, width // HEAD_DIM, HEAD_DIM), (1, 0, 2))


def join_heads(values):
    heads, tokens, size = values.shape
    return jnp.transpose(values, (1, 0, 2)).reshape(tokens, heads * size)


def whereabouts():
    place = lax.axis_index("shard")
    core, col, row = lax.rem(place, 2), lax.rem(place // 2, 2), place // 4
    across, along = place + 2 - 4 * col, place + 4 - 8 * row
    return place, place + 1 - 2 * core, across, along, across + 4 - 8 * row


def whereabouts_of_mate():
    me, mate, across, along, far = whereabouts()
    shift = mate - me
    return across + shift, along + shift, far + shift


def tile_loop(rows, columns, size, step, narrow=None):
    narrow = narrow or size
    across = columns // narrow

    def one(i, carry):
        step(
            pl.ds(pl.multiple_of((i // across) * size, size), size),
            pl.ds(pl.multiple_of(lax.rem(i, across) * narrow, narrow), narrow),
        )
        return carry

    lax.fori_loop(0, (rows // size) * across, one, 0)


def product(a, b, ca, cb):
    return lax.dot_general(a, b, (((ca,), (cb,)), ((), ())), preferred_element_type=F32)


def ffn_tile(normed, dy, w_gate, w_up, w_down, hidden, grad_gate, grad_up, rows, columns):
    gate = product(normed[rows, :], w_gate[columns, :], 1, 1)
    up = product(normed[rows, :], w_up[columns, :], 1, 1)
    grad = product(dy[rows, :], w_down[:, columns], 1, 0)
    sigma = 1.0 / (1.0 + jnp.exp(-gate))
    silu = gate * sigma
    hidden[rows, columns] = (silu * up).astype(BF)
    grad_gate[rows, columns] = (grad * up * sigma * (1.0 + gate * (1.0 - sigma))).astype(BF)
    grad_up[rows, columns] = (grad * silu).astype(BF)


def block_rows(slot, tokens, part=0):
    size = tokens // 2
    if part:
        return pl.ds(pl.multiple_of(slot * tokens + (part - 1) * size, size), size)
    return pl.ds(pl.multiple_of(slot * tokens, tokens), tokens)


class Gather:
    def __init__(self, block, out, sent, came):
        self.block, self.out, self.sent, self.came = block, out, sent, came
        self.tokens = block.shape[0]
        self.replica = lax.axis_index("replica")
        self.me, self.mate, self.across, self.along, self.far = whereabouts()
        self.sends = []

    def move(self, k, slot, part, device, first=False):
        tokens = self.tokens
        local = pl.ds((part - 1) * (tokens // 2) if part else 0, tokens // 2 if part else tokens)
        rows = block_rows(slot, tokens, part)
        return pltpu.make_async_remote_copy(
            src_ref=self.block.at[local] if first else self.out.at[rows],
            dst_ref=self.out.at[rows],
            send_sem=self.sent.at[k],
            recv_sem=self.came.at[k],
            device_id=(self.replica, device),
            device_id_type=MESH,
        )

    def start(self, *moves):
        for one in moves:
            copy = self.move(*one)
            copy.start()
            self.sends.append(copy)

    def came_in(self, *moves):
        for k, slot, part in moves:
            self.move(k, slot, part, self.mate).wait_recv()

    def one(self):
        me = self.me
        self.start(
            (1, me, 1, self.across, True),
            (3, me, 2, self.along, True),
            (0, me, 0, self.mate, True),
            (2, me, 2, self.across, True),
            (4, me, 1, self.along, True),
        )

    def two(self):
        self.came_in((1, self.across, 1))
        self.start((5, self.across, 1, self.along), (6, self.across, 1, self.mate))
        self.came_in((3, self.along, 2))
        self.start((7, self.along, 2, self.across), (8, self.along, 2, self.mate))

    def three(self):
        self.came_in((2, self.across, 2))
        self.start((9, self.across, 2, self.mate))
        self.came_in((4, self.along, 1))
        self.start((10, self.along, 1, self.mate))

    def four(self):
        self.came_in((5, self.far, 1))
        self.start((11, self.far, 1, self.mate))
        self.came_in((7, self.far, 2))
        self.start((12, self.far, 2, self.mate))

    def finish(self):
        across, along, far = whereabouts_of_mate()
        self.came_in(
            (0, self.mate, 0), (6, across, 1), (8, along, 2), (9, across, 2), (10, along, 1),
            (11, far, 1), (12, far, 2),
        )

    def drain(self):
        for copy in self.sends:
            copy.wait_send()


class Scatter:
    def __init__(self, parts, buffers, sent, came):
        self.parts = parts
        self.pair, self.sums, self.by_far, self.by_side = buffers
        self.sent, self.came = sent, came
        self.tokens = self.pair.shape[1]
        self.replica = lax.axis_index("replica")
        me, mate, across, along, far = whereabouts()
        self.mine, self.shift, self.mate = (me, across, along, far), mate - me, mate
        low, high = pl.ds(0, self.tokens // 2), pl.ds(self.tokens // 2, self.tokens // 2)
        self.low, self.high = low, high
        sums, by_far, by_side = self.sums, self.by_far, self.by_side
        self.swaps = [
            self.move(k, parts.at[block_rows(self.mine[k] + self.shift, self.tokens)], self.pair.at[k], mate)
            for k in range(4)
        ]
        self.far_low = self.move(4, sums.at[2, low], by_far.at[0], across)
        self.far_high = self.move(5, sums.at[2, high], by_far.at[1], along)
        self.across_low = self.move(6, sums.at[0, low], by_side.at[0, low], across)
        self.along_high = self.move(7, sums.at[1, high], by_side.at[1, high], along)
        self.along_low = self.move(8, sums.at[1, low], by_side.at[1, low], along)
        self.across_high = self.move(9, sums.at[0, high], by_side.at[0, high], across)

    def move(self, k, src, dst, device):
        return pltpu.make_async_remote_copy(
            src_ref=src,
            dst_ref=dst,
            send_sem=self.sent.at[k],
            recv_sem=self.came.at[k],
            device_id=(self.replica, device),
            device_id_type=MESH,
        )

    def swap(self, *which):
        for k in which:
            self.swaps[k].start()

    def pair_sum(self, k):
        self.swaps[k].wait_recv()
        own = self.parts[block_rows(self.mine[k], self.tokens), :].astype(F32)
        self.sums[k - 1] = (own + self.pair[k].astype(F32)).astype(BF)

    def send_far(self):
        self.pair_sum(3)
        self.far_low.start()
        self.far_high.start()

    def send_near(self):
        self.pair_sum(1)
        self.across_low.start()
        self.pair_sum(2)
        self.along_high.start()

    def send_rest(self):
        low, high, sums = self.low, self.high, self.sums
        self.far_low.wait_recv()
        sums[1, low] = (sums[1, low].astype(F32) + self.by_far[0].astype(F32)).astype(BF)
        self.along_low.start()
        self.far_high.wait_recv()
        sums[0, high] = (sums[0, high].astype(F32) + self.by_far[1].astype(F32)).astype(BF)
        self.across_high.start()

    def total(self):
        self.swaps[0].wait_recv()
        own = self.parts[block_rows(self.mine[0], self.tokens), :].astype(F32)
        own = own + self.pair[0].astype(F32)
        for copy in (self.across_low, self.along_high, self.along_low, self.across_high):
            copy.wait_recv()
        return own + (self.by_side[0].astype(F32) + self.by_side[1].astype(F32))

    def drain(self):
        for copy in (
            *self.swaps, self.far_low, self.far_high, self.across_low, self.along_high,
            self.along_low, self.across_high,
        ):
            copy.wait_send()


class Line:
    def __init__(self, own, slots, sent, came):
        self.own, self.slots, self.sent, self.came = own, slots, sent, came
        self.replica, self.me = lax.axis_index("replica"), lax.axis_index("shard")
        self.replicas = lax.axis_size("replica")

    def move(self, way, i, slot, first):
        target = self.replica + (1 if way == 0 else -1)
        return pltpu.make_async_remote_copy(
            src_ref=self.own if first else self.slots(slot),
            dst_ref=self.slots(slot),
            send_sem=self.sent.at[way, i],
            recv_sem=self.came.at[way, i],
            device_id=(target, self.me),
            device_id_type=MESH,
        )

    def source(self, way, i):
        return self.replica - i if way == 0 else self.replica + i

    def has(self, way, i):
        return self.replica >= i if way == 0 else self.replica + i < self.replicas

    def can_send(self, way):
        return self.replica + 1 < self.replicas if way == 0 else self.replica >= 1

    def start(self):
        for way in (0, 1):

            @pl.when(self.can_send(way))
            def _(way=way):
                self.move(way, 0, self.replica, True).start()

    def step(self, i):
        for way in (0, 1):

            @pl.when(self.has(way, i))
            def _(way=way):
                self.move(way, i - 1, self.source(way, i), False).wait_recv()
                if i < self.replicas - 1:

                    @pl.when(self.can_send(way))
                    def _():
                        self.move(way, i, self.source(way, i), False).start()

    def drain(self):
        for way in (0, 1):
            for i in range(self.replicas - 1):

                @pl.when(self.has(way, i) & self.can_send(way))
                def _(way=way, i=i):
                    self.move(way, i, self.source(way, i), i == 0).wait_send()


def rotate_head(values, cosine, sine):
    return values * cosine + pltpu.roll(values, values.shape[-1] // 2, 1) * sine


def head_scores(query, keys, start, first):
    rows, columns = query.shape[0], keys.shape[0]
    scores = product(query, keys, 1, 1) * (1.0 / math.sqrt(HEAD_DIM))
    key_place = lax.broadcasted_iota(jnp.int32, (rows, columns), 1)
    query_place = lax.broadcasted_iota(jnp.int32, (rows, columns), 0) + first
    allowed = (key_place <= query_place) & (key_place >= start)
    return jnp.where(allowed, scores, masked)


def front_kernel(
    n1_own, x_own, dy_own, start, cosine, sine, w_query, w_key, w_value, w_out, w_gate, w_up, w_down,
    n1_out, query_out, key_out, value_out, attn_out, attn_b_out, out_columns_out, down_parts,
    down_columns_out, hidden_out, grad_gate_out, grad_up_out, middle_out, n2_out, dy_out, lined,
    grad_out, grad_all_out,
    n1, n2, dy, query, key, value, attn, attn_b, out_columns, gate_w, up_w, down_w,
    hidden, grad_gate, grad_up, parts, pair, sums, by_far, by_side, middle, normed, n2_own, grad_own,
    load_sem, save_sem, gather_sent, gather_came, scatter_sent, scatter_came,
    swap_sent, swap_came, line_sent, line_came,
):
    replica = lax.axis_index("replica")
    replicas = lax.axis_size("replica")
    me = lax.axis_index("shard")
    groups = lax.axis_size("shard")
    tokens, width = n1_own.shape
    sequence = n1.shape[0]
    saves = []

    def save(src, dst):
        copy = pltpu.make_async_copy(src, dst, save_sem.at[len(saves)])
        copy.start()
        saves.append(copy)

    def exchange(which, source, target):
        copies = []
        for i in range(1, groups):
            device = lax.rem(me + i, groups)
            copies.append(
                pltpu.make_async_remote_copy(
                    src_ref=source(device),
                    dst_ref=target,
                    send_sem=swap_sent.at[which, i],
                    recv_sem=swap_came.at[which, i],
                    device_id=(replica, device),
                    device_id_type=MESH,
                )
            )
        return copies

    gate_load = pltpu.make_async_copy(w_gate, gate_w, load_sem.at[0])
    up_load = pltpu.make_async_copy(w_up, up_w, load_sem.at[1])
    gate_load.start()
    up_load.start()
    own_rows = block_rows(me, tokens)
    own_n1 = pltpu.make_async_copy(n1_own, n1.at[own_rows], load_sem.at[2])
    own_dy = pltpu.make_async_copy(dy_own, dy.at[own_rows], load_sem.at[3])
    own_n1.start()
    own_dy.start()

    barrier = pltpu.get_barrier_semaphore()
    for i in range(1, groups):
        device = lax.rem(me + i, groups)
        pl.semaphore_signal(barrier, inc=1, device_id=(replica, device), device_id_type=MESH)

    @pl.when(replica >= 1)
    def _():
        pl.semaphore_signal(barrier, inc=1, device_id=(replica - 1, me), device_id_type=MESH)

    @pl.when(replica + 1 < replicas)
    def _():
        pl.semaphore_signal(barrier, inc=1, device_id=(replica + 1, me), device_id_type=MESH)

    edge = (replica == 0) | (replica == replicas - 1)

    @pl.when(edge)
    def _():
        pl.semaphore_wait(barrier, groups)

    @pl.when(jnp.logical_not(edge))
    def _():
        pl.semaphore_wait(barrier, groups + 1)

    n1_gather = Gather(n1_own, n1, gather_sent.at[0], gather_came.at[0])
    dy_gather = Gather(dy_own, dy, gather_sent.at[1], gather_came.at[1])
    n2_gather = Gather(n2_own, n2, gather_sent.at[2], gather_came.at[2])
    grad_gather = Gather(grad_own, grad_all_out, gather_sent.at[3], gather_came.at[3])
    dy_line = Line(
        dy_own, lambda s: lined.at[s, pl.ds(tokens, tokens)], line_sent.at[0], line_came.at[0]
    )
    n2_line = Line(
        n2_own, lambda s: lined.at[s, pl.ds(0, tokens)], line_sent.at[1], line_came.at[1]
    )
    down_line = Line(
        down_parts.at[replica], lambda s: down_parts.at[s], line_sent.at[2], line_came.at[2]
    )
    buffers = (pair, sums, by_far, by_side)

    n1_gather.one()
    dy_line.start()
    n1_gather.two()
    n1_gather.three()
    wide = w_out.shape[0]
    mine = pl.ds(pl.multiple_of(me * wide, wide), wide)

    def out_block(device):
        return w_out.at[:, pl.ds(pl.multiple_of(device * wide, wide), wide)]

    out_swaps = exchange(0, out_block, out_columns.at[mine])
    for copy in out_swaps:
        copy.start()
    own_out = pltpu.make_async_copy(out_block(me), out_columns.at[mine], load_sem.at[4])
    own_out.start()
    part = down_parts.shape[2]

    def down_block(device):
        column = (device * replicas + replica) * part
        return w_down.at[:, pl.ds(pl.multiple_of(column, part), part)]

    down_swaps = exchange(1, down_block, down_parts.at[replica, mine])
    own_down = pltpu.make_async_copy(down_block(me), down_parts.at[replica, mine], load_sem.at[5])
    own_down.start()
    n1_gather.four()
    for copy in down_swaps:
        copy.start()
    own_n1.wait()
    n1_gather.finish()
    save(n1, n1_out)

    heads = query.shape[1] // HEAD_DIM
    for first in range(0, sequence, 512):
        rows = pl.ds(first, 512)
        for weight, target in ((w_query, query), (w_key, key), (w_value, value)):
            values = product(n1[rows, :], weight[...], 1, 1)
            for head in range(heads):
                lanes = pl.ds(head * HEAD_DIM, HEAD_DIM)
                piece = values[:, head * HEAD_DIM : (head + 1) * HEAD_DIM]
                if target is not value:
                    piece = rotate_head(piece, cosine[rows, :], sine[rows, :])
                target[rows, lanes] = piece.astype(BF)
    save(query, query_out)
    save(key, key_out)
    save(value, value_out)
    dy_line.step(1)
    for first in range(0, sequence, 256):
        rows = pl.ds(first, 256)
        upto = pl.ds(0, first + 256)
        for head in range(heads):
            lanes = pl.ds(head * HEAD_DIM, HEAD_DIM)
            scores = head_scores(query[rows, lanes], key[upto, lanes], start[rows, :], first)
            weights = jnp.exp(scores - jnp.max(scores, axis=-1, keepdims=True))
            total = jnp.sum(weights, axis=-1, keepdims=True)
            result = product(weights.astype(BF), value[upto, lanes], 1, 0) / total
            attn[rows, lanes] = result
            attn_b[rows, lanes] = result.astype(BF)
    save(attn, attn_out)
    save(attn_b, attn_b_out)
    dy_line.step(2)

    own_out.wait()
    for copy in out_swaps:
        copy.wait_recv()
    save(out_columns, out_columns_out)

    def spread(rows, columns):
        parts[rows, columns] = product(attn_b[rows, :], out_columns[columns, :], 1, 1).astype(BF)

    tile_loop(sequence, width, 512, spread)
    scatter = Scatter(parts, buffers, scatter_sent.at[0], scatter_came.at[0])
    scatter.swap(3, 1, 2, 0)
    scatter.send_far()
    scatter.send_near()
    own_down.wait()
    for copy in down_swaps:
        copy.wait_recv()
    down_line.start()
    scatter.send_rest()
    dy_line.step(3)
    middle[...] = x_own[...].astype(F32) + scatter.total()
    scatter.drain()
    save(middle, middle_out)
    center = middle[...] - jnp.mean(middle[...], axis=-1, keepdims=True)
    inverse = lax.rsqrt(jnp.mean(center * center, axis=-1, keepdims=True) + epsilon)
    normed[...] = center * inverse
    n2_own[...] = normed[...].astype(BF)
    n2_gather.one()
    own_n2 = pltpu.make_async_copy(n2_own, n2.at[own_rows], load_sem.at[6])
    own_n2.start()
    n2_gather.two()
    n2_gather.three()
    dy_gather.one()
    n2_gather.four()
    down_line.step(1)
    own_n2.wait()
    n2_gather.finish()
    save(n2, n2_out)
    dy_gather.two()
    dy_gather.three()
    dy_gather.four()
    down_line.step(2)
    own_dy.wait()
    dy_gather.finish()
    save(dy, dy_out)
    down_line.step(3)
    n2_line.start()
    down_loads = []
    for r in range(replicas):
        down_loads.append(
            pltpu.make_async_copy(
                down_parts.at[r], down_w.at[:, pl.ds(r * part, part)], load_sem.at[7 + r]
            )
        )
        down_loads[-1].start()
    gate_load.wait()
    up_load.wait()
    for copy in down_loads:
        copy.wait()
    save(down_w, down_columns_out)

    half = sequence // 2
    row = me // (groups // 2)
    back = Scatter(parts, buffers, scatter_sent.at[1], scatter_came.at[1])

    def feed(base):
        def forward(rows, columns):
            rows = pl.ds(pl.multiple_of(base, half), half)
            ffn_tile(n2, dy, gate_w, up_w, down_w, hidden, grad_gate, grad_up, rows, columns)

        tile_loop(512, gate_w.shape[0], 512, forward)

        def backward(rows, columns):
            rows = pl.ds(pl.multiple_of(base, half), half)
            value = product(grad_gate[rows, :], gate_w[:, columns], 1, 0)
            value = value + product(grad_up[rows, :], up_w[:, columns], 1, 0)
            parts[rows, columns] = value.astype(BF)

        tile_loop(512, width, 512, backward)

    feed((1 - row) * half)
    back.swap(3, 2)
    n2_line.step(1)
    back.send_far()
    feed(row * half)
    save(hidden, hidden_out)
    save(grad_gate, grad_gate_out)
    save(grad_up, grad_up_out)
    back.swap(1, 0)
    back.send_near()
    back.send_rest()
    n2_line.step(2)
    inner = back.total()
    back.drain()
    inner = (
        inner
        - jnp.mean(inner, axis=-1, keepdims=True)
        - normed[...] * jnp.mean(inner * normed[...], axis=-1, keepdims=True)
    )
    center = middle[...] - jnp.mean(middle[...], axis=-1, keepdims=True)
    inverse = lax.rsqrt(jnp.mean(center * center, axis=-1, keepdims=True) + epsilon)
    normed[...] = dy_own[...].astype(F32) + inverse * inner
    grad_own[...] = normed[...].astype(BF)
    grad_gather.one()
    save(normed, grad_out)
    save(grad_own, grad_all_out.at[own_rows])
    grad_gather.two()
    grad_gather.three()
    grad_gather.four()
    n2_line.step(3)
    grad_gather.finish()
    for copy in saves:
        copy.wait()
    for copy in out_swaps + down_swaps:
        copy.wait_send()
    for user in (n1_gather, n2_gather, dy_gather, grad_gather, dy_line, n2_line, down_line):
        user.drain()


def front(
    n1_own, x_own, dy_own, start, cosine, sine,
    w_query, w_key, w_value, w_out, w_gate, w_up, w_down,
):
    groups, replicas = lax.axis_size("shard"), lax.axis_size("replica")
    tokens, width = n1_own.shape
    sequence = tokens * groups
    wide, columns = w_query.shape[0], w_gate.shape[0]
    anywhere, vmem = pl.BlockSpec(memory_space=pl.ANY), pl.BlockSpec(memory_space=VMEM)

    def shape(dims, kind=BF):
        return jax.ShapeDtypeStruct(dims, kind)

    outs = (
        shape((sequence, width)),
        shape((sequence, wide)),
        shape((sequence, wide)),
        shape((sequence, wide)),
        shape((sequence, wide), F32),
        shape((sequence, wide)),
        shape((width, wide)),
        shape((replicas, width, columns // replicas)),
        shape((width, columns)),
        shape((sequence, columns)),
        shape((sequence, columns)),
        shape((sequence, columns)),
        shape((tokens, width), F32),
        shape((sequence, width)),
        shape((sequence, width)),
        shape((replicas, 2 * tokens, width)),
        shape((tokens, width), F32),
        shape((sequence, width)),
    )
    dma = pltpu.SemaphoreType.DMA
    return pl.pallas_call(
        front_kernel,
        out_shape=outs,
        in_specs=[vmem] * 9 + [anywhere] * 4,
        out_specs=(anywhere,) * len(outs),
        scratch_shapes=[
            pltpu.VMEM((sequence, width), BF),
            pltpu.VMEM((sequence, width), BF),
            pltpu.VMEM((sequence, width), BF),
            pltpu.VMEM((sequence, wide), BF),
            pltpu.VMEM((sequence, wide), BF),
            pltpu.VMEM((sequence, wide), BF),
            pltpu.VMEM((sequence, wide), F32),
            pltpu.VMEM((sequence, wide), BF),
            pltpu.VMEM((width, wide), BF),
            pltpu.VMEM((columns, width), BF),
            pltpu.VMEM((columns, width), BF),
            pltpu.VMEM((width, columns), BF),
            pltpu.VMEM((sequence, columns), BF),
            pltpu.VMEM((sequence, columns), BF),
            pltpu.VMEM((sequence, columns), BF),
            pltpu.VMEM((sequence, width), BF),
            pltpu.VMEM((4, tokens, width), BF),
            pltpu.VMEM((3, tokens, width), BF),
            pltpu.VMEM((2, tokens // 2, width), BF),
            pltpu.VMEM((2, tokens, width), BF),
            pltpu.VMEM((tokens, width), F32),
            pltpu.VMEM((tokens, width), F32),
            pltpu.VMEM((tokens, width), BF),
            pltpu.VMEM((tokens, width), BF),
            dma((7 + replicas,)),
            dma((20,)),
            dma((4, 13)),
            dma((4, 13)),
            dma((2, 10)),
            dma((2, 10)),
            dma((2, groups)),
            dma((2, groups)),
            dma((3, 2, replicas)),
            dma((3, 2, replicas)),
        ],
        compiler_params=pltpu.CompilerParams(
            collective_id=3, has_side_effects=True, vmem_limit_bytes=67043328
        ),
        cost_estimate=pl.CostEstimate(
            flops=12 * sequence * width * columns, bytes_accessed=64 * 1024 * 1024, transcendentals=0
        ),
        name="front",
    )(n1_own, x_own, dy_own, start, cosine, sine, w_query, w_key, w_value, w_out, w_gate, w_up, w_down)


def back_kernel(
    x_own, start, cosine, sine, hidden_in, down_in, grad_in, out_columns_in, attn_b_in, attn_in,
    query_in, key_in, value_in, n1_in, w_query, w_key, w_value, middle, grad_middle,
    layer_out, input_grad, attn_part,
    hidden, down_w, grad, out_columns, attn_b, attn, query, key, value, n1, weights,
    grad_attn, key_grad, value_grad, columns_grad, out_grad, rows_grad, parts,
    pair, sums, by_far, by_side, pair2, sums2, by_far2, by_side2,
    load_sem, save_sem, scatter_sent, scatter_came, swap_sent, swap_came,
):
    replica = lax.axis_index("replica")
    me = lax.axis_index("shard")
    groups = lax.axis_size("shard")
    sequence, width = n1.shape
    wide = query.shape[1]
    heads = wide // HEAD_DIM
    pairs = (
        (hidden_in, hidden), (down_in, down_w), (grad_in, grad), (out_columns_in, out_columns),
        (attn_b_in, attn_b), (attn_in, attn), (query_in, query), (key_in, key), (value_in, value),
        (n1_in, n1), (w_query, weights.at[pl.ds(0, wide)]), (w_key, weights.at[pl.ds(wide, wide)]),
        (w_value, weights.at[pl.ds(2 * wide, wide)]),
    )
    loads = [
        pltpu.make_async_copy(src, dst, load_sem.at[i]) for i, (src, dst) in enumerate(pairs)
    ]
    for copy in loads:
        copy.start()
    barrier = pltpu.get_barrier_semaphore()
    for i in range(1, groups):
        device = lax.rem(me + i, groups)
        pl.semaphore_signal(barrier, inc=1, device_id=(replica, device), device_id_type=MESH)
    pl.semaphore_wait(barrier, groups - 1)

    loads[0].wait()
    loads[1].wait()

    def mix(rows, columns):
        parts[rows, columns] = product(hidden[rows, :], down_w[columns, :], 1, 1).astype(BF)

    tile_loop(sequence, width, 512, mix)
    mixed = Scatter(parts, (pair, sums, by_far, by_side), scatter_sent.at[0], scatter_came.at[0])
    mixed.swap(3, 1, 2, 0)

    for copy in loads[2:6]:
        copy.wait()
    mixed.send_far()
    mixed.send_near()
    for first in range(0, width, 512):
        rows = pl.ds(first, 512)
        out_grad[rows, :] = product(grad[:, rows], attn_b[...], 0, 0).astype(BF)
    mine = pl.ds(pl.multiple_of(me * wide, wide), wide)
    out_rows = pl.ds(3 * wide, wide)
    swaps = []
    for i in range(1, groups):
        device = lax.rem(me + i, groups)
        swaps.append(
            pltpu.make_async_remote_copy(
                src_ref=out_grad.at[pl.ds(pl.multiple_of(device * wide, wide), wide)],
                dst_ref=attn_part.at[out_rows, mine],
                send_sem=swap_sent.at[i],
                recv_sem=swap_came.at[i],
                device_id=(replica, device),
                device_id_type=MESH,
            )
        )
        swaps[-1].start()
    own_swap = pltpu.make_async_copy(out_grad.at[mine], attn_part.at[out_rows, mine], save_sem.at[0])
    own_swap.start()
    for first in range(0, sequence, 512):
        rows = pl.ds(first, 512)
        grad_attn[rows, :] = product(grad[rows, :], out_columns[...], 1, 0).astype(BF)
    for copy in loads[6:]:
        copy.wait()
    mixed.send_rest()

    step = 256
    for first in range(sequence - step, -1, -step):
        rows = pl.ds(first, step)
        upto = pl.ds(0, first + step)
        for head in range(heads):
            lanes = pl.ds(head * HEAD_DIM, HEAD_DIM)
            query_piece, grad_piece = query[rows, lanes], grad_attn[rows, lanes]
            scores = head_scores(query_piece, key[upto, lanes], start[rows, :], first)
            probs = jnp.exp(scores - jnp.max(scores, axis=-1, keepdims=True))
            probs = probs / jnp.sum(probs, axis=-1, keepdims=True)
            delta = jnp.sum(grad_piece.astype(F32) * attn[rows, lanes], axis=-1, keepdims=True)
            grad_probs = product(grad_piece, value[upto, lanes], 1, 1)
            grad_scores = (probs * (grad_probs - delta)).astype(BF)
            query_grad = product(grad_scores, key[upto, lanes], 1, 0) * (1.0 / math.sqrt(HEAD_DIM))
            query_grad = rotate_head(query_grad, cosine[rows, :], -sine[rows, :])
            columns_grad[rows, lanes] = query_grad.astype(BF)
            key_part = product(grad_scores, query_piece, 0, 0)
            value_part = product(probs.astype(BF), grad_piece, 0, 0)
            if first == sequence - step:
                key_grad[:, lanes] = key_part
                value_grad[:, lanes] = value_part
            else:
                key_grad[upto, lanes] += key_part
                value_grad[upto, lanes] += value_part
    for head in range(heads):
        lanes = pl.ds(head * HEAD_DIM, HEAD_DIM)
        piece = key_grad[:, lanes] * (1.0 / math.sqrt(HEAD_DIM))
        piece = rotate_head(piece, cosine[...], -sine[...])
        columns_grad[:, pl.ds(wide + head * HEAD_DIM, HEAD_DIM)] = piece.astype(BF)
        columns_grad[:, pl.ds(2 * wide + head * HEAD_DIM, HEAD_DIM)] = value_grad[:, lanes].astype(BF)

    layer_out[...] = (middle[...] + mixed.total()).astype(BF)
    mixed.drain()

    def back(rows, columns):
        parts[rows, columns] = product(columns_grad[rows, :], weights[:, columns], 1, 0).astype(BF)

    tile_loop(sequence, width, 512, back)
    last = Scatter(parts, (pair2, sums2, by_far2, by_side2), scatter_sent.at[1], scatter_came.at[1])
    last.swap(3, 1, 2, 0)
    last.send_far()
    last.send_near()

    def collect(rows, columns):
        rows_grad[rows, columns] = product(columns_grad[:, rows], n1[:, columns], 0, 0).astype(BF)

    tile_loop(3 * wide, width, 256, collect, 512)
    rows_save = pltpu.make_async_copy(rows_grad, attn_part.at[pl.ds(0, 3 * wide)], save_sem.at[1])
    rows_save.start()
    last.send_rest()
    x = x_own[...].astype(F32)
    center = x - jnp.mean(x, axis=-1, keepdims=True)
    inverse = lax.rsqrt(jnp.mean(center * center, axis=-1, keepdims=True) + epsilon)
    inner = last.total()
    normed = center * inverse
    inner = (
        inner
        - jnp.mean(inner, axis=-1, keepdims=True)
        - normed * jnp.mean(inner * normed, axis=-1, keepdims=True)
    )
    input_grad[...] = grad_middle[...] + inverse * inner
    last.drain()
    for copy in swaps:
        copy.wait()
    own_swap.wait()
    rows_save.wait()


def back(x_own, start, cosine, sine, hidden, down, grad, out_columns, attn_b, attn, query, key, value, n1,
         w_query, w_key, w_value, middle, grad_middle):
    groups = lax.axis_size("shard")
    tokens, width = x_own.shape
    sequence = tokens * groups
    wide, columns = query.shape[1], hidden.shape[1]
    anywhere, vmem = pl.BlockSpec(memory_space=pl.ANY), pl.BlockSpec(memory_space=VMEM)
    dma = pltpu.SemaphoreType.DMA
    buffers = [
        pltpu.VMEM((4, tokens, width), BF),
        pltpu.VMEM((3, tokens, width), BF),
        pltpu.VMEM((2, tokens // 2, width), BF),
        pltpu.VMEM((2, tokens, width), BF),
    ]
    return pl.pallas_call(
        back_kernel,
        out_shape=(
            jax.ShapeDtypeStruct((tokens, width), BF),
            jax.ShapeDtypeStruct((tokens, width), F32),
            jax.ShapeDtypeStruct((4 * wide, width), BF),
        ),
        in_specs=[vmem] * 4 + [anywhere] * 13 + [vmem] * 2,
        out_specs=(vmem, vmem, anywhere),
        scratch_shapes=[
            pltpu.VMEM((sequence, columns), BF),
            pltpu.VMEM((width, columns), BF),
            pltpu.VMEM((sequence, width), BF),
            pltpu.VMEM((width, wide), BF),
            pltpu.VMEM((sequence, wide), BF),
            pltpu.VMEM((sequence, wide), F32),
            pltpu.VMEM((sequence, wide), BF),
            pltpu.VMEM((sequence, wide), BF),
            pltpu.VMEM((sequence, wide), BF),
            pltpu.VMEM((sequence, width), BF),
            pltpu.VMEM((3 * wide, width), BF),
            pltpu.VMEM((sequence, wide), BF),
            pltpu.VMEM((sequence, wide), F32),
            pltpu.VMEM((sequence, wide), F32),
            pltpu.VMEM((sequence, 3 * wide), BF),
            pltpu.VMEM((width, wide), BF),
            pltpu.VMEM((3 * wide, width), BF),
            pltpu.VMEM((sequence, width), BF),
            *buffers,
            *buffers,
            dma((13,)),
            dma((2,)),
            dma((2, 10)),
            dma((2, 10)),
            dma((groups,)),
            dma((groups,)),
        ],
        compiler_params=pltpu.CompilerParams(
            collective_id=4, has_side_effects=True, vmem_limit_bytes=67043328
        ),
        cost_estimate=pl.CostEstimate(
            flops=24 * sequence * width * wide, bytes_accessed=48 * 1024 * 1024, transcendentals=0
        ),
        name="back",
    )(x_own, start, cosine, sine, hidden, down, grad, out_columns, attn_b, attn, query, key, value, n1,
      w_query, w_key, w_value, middle, grad_middle)


def every_kernel(
    blocks, own_normed, own_dy, own_hidden, own_grad_gate, own_grad_up, attn_part,
    w_gate, w_up, w_down,
    out_gate, out_up, out_down, out_attn, landed,
    normed, dy, hidden, grad_gate, grad_up, down, first_sum, second_sum, stage,
    load_sem, sent, came, line_sent, line_came, line_own,
):
    replica = lax.axis_index("replica")
    replicas = blocks.shape[0]
    me, mate, across, along, far = whereabouts()
    shift = mate - me
    tokens = blocks.shape[1] // 2
    low, high, whole = pl.ds(0, tokens), pl.ds(tokens, tokens), pl.ds(0, 2 * tokens)
    order = (me, mate, across, across + shift, along, along + shift, far, far + shift)
    size = 512
    inner = (replica == 1) | (replica == 2)
    outer = (replica == 0) | (replica == 3)
    beside = replica + 1 - 2 * lax.rem(replica, 2)
    facing = 3 - replica
    chunks, depth = first_sum.shape[0], first_sum.shape[1]

    def piece(c):
        return pl.ds(c * depth, depth)

    def line_move(kind, c, src, dst, target):
        return pltpu.make_async_remote_copy(
            src_ref=src,
            dst_ref=dst,
            send_sem=line_sent.at[kind, c],
            recv_sem=line_came.at[kind, c],
            device_id=(target, me),
            device_id_type=MESH,
        )

    def inward(c):
        return line_move(0, c, attn_part.at[piece(c)], first_sum.at[c], beside)

    def middle(c):
        return line_move(1, c, first_sum.at[c], second_sum.at[c], facing)

    def outward(c):
        return line_move(2, c, second_sum.at[c], out_attn.at[piece(c)], beside)

    def keep(c):
        return pltpu.make_async_copy(second_sum.at[c], out_attn.at[piece(c)], line_own.at[c])

    def stage_load(c):
        return pltpu.make_async_copy(attn_part.at[piece(c)], stage, load_sem.at[2, 0])

    def half_sum(c):
        @pl.when(inner)
        def _():
            stage_load(c).wait()
            inward(c).wait_recv()
            first_sum[c] = (stage[...].astype(F32) + first_sum[c].astype(F32)).astype(BF)
            middle(c).start()
            if c + 1 < chunks:
                stage_load(c + 1).start()

    def full_sum(c):
        @pl.when(inner)
        def _():
            middle(c).wait_recv()
            second_sum[c] = (first_sum[c].astype(F32) + second_sum[c].astype(F32)).astype(BF)
            outward(c).start()
            keep(c).start()

    agenda = {
        (0, "up"): ((half_sum, 0),),
        (0, "down"): ((half_sum, 1), (full_sum, 0)),
        (1, "ffn"): ((half_sum, 2), (half_sum, 3), (full_sum, 1)),
        (1, "up"): ((half_sum, 4),),
        (1, "down"): ((full_sum, 2),),
        (2, "ffn"): ((half_sum, 5), (half_sum, 6), (full_sum, 3)),
        (2, "gate"): ((full_sum, 4),),
        (2, "up"): ((half_sum, 7),),
        (2, "down"): ((full_sum, 5),),
        (3, "ffn"): ((full_sum, 6),),
        (3, "gate"): ((full_sum, 7),),
    }

    def tick(n, phase):
        for (when, name), actions in agenda.items():
            if name == phase:

                @pl.when(n == when)
                def _(actions=actions):
                    for action, c in actions:
                        action(c)

    def move(n, k, slot, rows, device, first=False):
        src = blocks.at[lax.rem(replica + n + 1, replicas), rows] if first else landed.at[n, slot, rows]
        return pltpu.make_async_remote_copy(
            src_ref=src,
            dst_ref=landed.at[n, slot, rows],
            send_sem=sent.at[n, k],
            recv_sem=came.at[n, k],
            device_id=(replica, device),
            device_id_type=MESH,
        )

    def sends_one(n):
        return [
            move(n, 1, me, low, across, True),
            move(n, 3, me, high, along, True),
            move(n, 0, me, whole, mate, True),
            move(n, 2, me, high, across, True),
            move(n, 4, me, low, along, True),
        ]

    def sends_two(n):
        return [
            move(n, 5, across, low, along),
            move(n, 7, along, high, across),
            move(n, 6, across, low, mate),
            move(n, 8, along, high, mate),
        ]

    def sends_three(n):
        return [move(n, 9, across, high, mate), move(n, 10, along, low, mate)]

    def sends_four(n):
        return [move(n, 11, far, low, mate), move(n, 12, far, high, mate)]

    def start_all(copies):
        for copy in copies:
            copy.start()

    def stage_two(n):
        move(n, 1, across, low, across).wait_recv()
        move(n, 3, along, high, along).wait_recv()
        start_all(sends_two(n))

    def stage_three(n):
        move(n, 2, across, high, across).wait_recv()
        move(n, 4, along, low, along).wait_recv()
        start_all(sends_three(n))

    def stage_four(n):
        move(n, 5, far, low, along).wait_recv()
        move(n, 7, far, high, across).wait_recv()
        start_all(sends_four(n))

    def finish(n):
        move(n, 0, mate, whole, mate).wait_recv()
        for k, slot, rows in (
            (6, across + shift, low),
            (8, along + shift, high),
            (9, across + shift, high),
            (10, along + shift, low),
            (11, far + shift, low),
            (12, far + shift, high),
        ):
            move(n, k, slot, rows, mate).wait_recv()

    def drain(n):
        for copy in sends_one(n) + sends_two(n) + sends_three(n) + sends_four(n):
            copy.wait_send()

    def loads(n):
        normed_loads, dy_loads = [], []
        for i, device in enumerate(order):
            source = blocks.at[lax.rem(replica + n, replicas)] if i == 0 else landed.at[n - 1, device]
            rows = pl.ds(pl.multiple_of(device * tokens, tokens), tokens)
            normed_loads.append(pltpu.make_async_copy(source.at[low], normed.at[rows], load_sem.at[0, i]))
            dy_loads.append(pltpu.make_async_copy(source.at[high], dy.at[rows], load_sem.at[1, i]))
        return normed_loads, dy_loads

    first = [
        pltpu.make_async_copy(own_normed, normed, load_sem.at[0, 0]),
        pltpu.make_async_copy(own_hidden, hidden, load_sem.at[0, 1]),
        pltpu.make_async_copy(own_grad_gate, grad_gate, load_sem.at[0, 2]),
        pltpu.make_async_copy(own_grad_up, grad_up, load_sem.at[0, 3]),
        pltpu.make_async_copy(own_dy, dy, load_sem.at[1, 0]),
    ]
    start_all(first)
    barrier = pltpu.get_barrier_semaphore()
    for device in (mate, across, along):
        pl.semaphore_signal(barrier, inc=1, device_id=(replica, device), device_id_type=MESH)
    pl.semaphore_signal(barrier, inc=1, device_id=(beside, me), device_id_type=MESH)

    @pl.when(inner)
    def _():
        pl.semaphore_signal(barrier, inc=1, device_id=(facing, me), device_id_type=MESH)
        pl.semaphore_wait(barrier, 5)

    @pl.when(outer)
    def _():
        pl.semaphore_wait(barrier, 4)

    start_all(sends_one(0))

    @pl.when(outer)
    def _():
        start_all([inward(c) for c in range(chunks)])

    @pl.when(inner)
    def _():
        stage_load(0).start()

    for copy in first:
        copy.wait()

    def sequence(n, carry):
        more = n < replicas - 1

        def collect(out, left, right):
            def step(rows, columns):
                value = product(left[:, rows], right[:, columns], 0, 0)
                out[rows, columns] = jnp.where(n == 0, value, out[rows, columns] + value)

            tile_loop(out.shape[0], out.shape[1], size, step)

        @pl.when(n > 0)
        def _():
            tile_loop(
                normed.shape[0], w_gate.shape[0], size,
                functools.partial(
                    ffn_tile, normed, dy, w_gate, w_up, w_down, hidden, grad_gate, grad_up
                ),
                256,
            )

        @pl.when(more & (n > 0))
        def _():
            stage_two(n)

        tick(n, "ffn")
        collect(out_gate, grad_gate, normed)

        @pl.when(more)
        def _():
            @pl.when(n == 0)
            def _():
                stage_two(n)

            @pl.when(n > 0)
            def _():
                stage_three(n)

        tick(n, "gate")
        collect(out_up, grad_up, normed)

        @pl.when(more)
        def _():
            @pl.when(n == 0)
            def _():
                stage_three(n)

            stage_four(n)

            @pl.when(n < replicas - 2)
            def _():
                start_all(sends_one(n + 1))

        tick(n, "up")

        @pl.when(more)
        def _():
            finish(n)
            start_all(loads(n + 1)[0])

        collect(down, dy, hidden)

        @pl.when(more)
        def _():
            start_all(loads(n + 1)[1])

        tick(n, "down")

        @pl.when(more)
        def _():
            normed_loads, dy_loads = loads(n + 1)
            for copy in normed_loads + dy_loads:
                copy.wait()
            drain(n)

        return carry

    lax.fori_loop(0, replicas, sequence, 0)
    rows = hidden.shape[0]
    for i, buffer in enumerate((hidden, grad_gate)):
        buffer[...] = down[i * rows : (i + 1) * rows, :].astype(BF)
        pltpu.make_async_copy(buffer, out_down.at[pl.ds(i * rows, rows)], load_sem.at[0, i]).start()

    @pl.when(outer)
    def _():
        for c in range(chunks):
            inward(c).wait_send()
            outward(c).wait_recv()

    @pl.when(inner)
    def _():
        for c in range(chunks):
            middle(c).wait_send()
            outward(c).wait_send()
            keep(c).wait()

    for i, buffer in enumerate((hidden, grad_gate)):
        pltpu.make_async_copy(buffer, out_down.at[pl.ds(i * rows, rows)], load_sem.at[0, i]).wait()


def ffn_grads(blocks, n2, dy_all, own, attn_part, w_gate, w_up, w_down_columns):
    replicas, tokens, width = blocks.shape
    tokens = tokens // 2
    sequence = n2.shape[0]
    groups = sequence // tokens
    columns = w_gate.shape[0]
    chunks = 8
    depth = attn_part.shape[0] // chunks
    anywhere, vmem = pl.BlockSpec(memory_space=pl.ANY), pl.BlockSpec(memory_space=VMEM)
    out = pl.pallas_call(
        every_kernel,
        out_shape=(
            jax.ShapeDtypeStruct((columns, width), F32),
            jax.ShapeDtypeStruct((columns, width), F32),
            jax.ShapeDtypeStruct((width, columns), BF),
            jax.ShapeDtypeStruct(attn_part.shape, BF),
            jax.ShapeDtypeStruct((replicas - 1, groups, 2 * tokens, width), BF),
        ),
        in_specs=[anywhere] * 7 + [vmem] * 3,
        out_specs=(vmem, vmem, anywhere, anywhere, anywhere),
        scratch_shapes=[
            pltpu.VMEM((sequence, width), BF),
            pltpu.VMEM((sequence, width), BF),
            pltpu.VMEM((sequence, columns), BF),
            pltpu.VMEM((sequence, columns), BF),
            pltpu.VMEM((sequence, columns), BF),
            pltpu.VMEM((width, columns), F32),
            pltpu.VMEM((chunks, depth, width), BF),
            pltpu.VMEM((chunks, depth, width), BF),
            pltpu.VMEM((depth, width), BF),
            pltpu.SemaphoreType.DMA((3, 8)),
            pltpu.SemaphoreType.DMA((replicas - 1, 13)),
            pltpu.SemaphoreType.DMA((replicas - 1, 13)),
            pltpu.SemaphoreType.DMA((3, chunks)),
            pltpu.SemaphoreType.DMA((3, chunks)),
            pltpu.SemaphoreType.DMA((chunks,)),
        ],
        compiler_params=pltpu.CompilerParams(
            collective_id=2, has_side_effects=True, vmem_limit_bytes=67043328
        ),
        cost_estimate=pl.CostEstimate(
            flops=42 * sequence * width * columns, bytes_accessed=80 * 1024 * 1024, transcendentals=0
        ),
        name="ffn_grads",
    )(blocks, n2, dy_all, *own, attn_part, w_gate, w_up, w_down_columns)
    return out[:4]


def gather_tokens(values):
    return lax.all_gather(values, "shard", axis=0, tiled=True)


def scatter_tokens(partial):
    return lax.psum_scatter(
        partial.astype(BF), "shard", scatter_dimension=0, tiled=True
    ).astype(F32)


def rows_to_columns(weight):
    return lax.all_to_all(weight, "shard", split_axis=1, concat_axis=0, tiled=True)


def columns_to_rows(grad):
    return lax.all_to_all(grad, "shard", split_axis=0, concat_axis=1, tiled=True)


def replica_sum(part):
    return lax.psum(part.astype(BF), "replica")


def general_body(hidden_in, cotangent, doc_lengths, w_query, w_key, w_value, w_out, w_gate, w_up, w_down):
    x = hidden_in[0].astype(F32)
    dyb = cotangent[0]
    tokens_here = x.shape[0]
    groups = lax.axis_size("shard")
    seq_length = tokens_here * groups
    factor = 1.0 / math.sqrt(HEAD_DIM)
    places = jnp.arange(seq_length, dtype=jnp.int32)
    segment, offset = doc_layout(doc_lengths[0], places)
    cosine, sine = rope_tables(offset, HEAD_DIM)
    allowed = ((segment[:, None] == segment[None, :]) & (places[None, :] <= places[:, None]))[None]

    normed_one, inverse_one = normalize(x)
    n1 = gather_tokens(normed_one.astype(BF))
    w_out_columns = rows_to_columns(w_out)
    query = rotate(split_heads(dot(n1, w_query, 1, 1)), cosine, sine).astype(BF)
    keys = rotate(split_heads(dot(n1, w_key, 1, 1)), cosine, sine).astype(BF)
    values = split_heads(dot(n1, w_value, 1, 1)).astype(BF)
    scores = factor * jnp.einsum("hqe,hke->hqk", query, keys, preferred_element_type=F32)
    scores = jnp.where(allowed, scores, masked)
    top = jnp.max(scores, axis=-1, keepdims=True)
    weights = jnp.where(allowed, jnp.exp(scores - top), 0.0)
    total = jnp.sum(weights, axis=-1, keepdims=True)
    log_total = top + jnp.log(total)
    attn = jnp.einsum("hqk,hke->hqe", weights.astype(BF), values, preferred_element_type=F32) / total
    out_b = join_heads(attn).astype(BF)
    middle = x + scatter_tokens(dot(out_b, w_out_columns, 1, 1))

    normed_two, inverse_two = normalize(middle)
    n2 = gather_tokens(normed_two.astype(BF))
    dy_all = gather_tokens(dyb)
    w_down_columns = rows_to_columns(w_down)
    gate = dot(n2, w_gate, 1, 1)
    up = dot(n2, w_up, 1, 1)
    sigma = jax.nn.sigmoid(gate)
    silu = gate * sigma
    hidden = (silu * up).astype(BF)
    grad_down = columns_to_rows(replica_sum(dot(dy_all, hidden, 0, 0)))
    grad_hidden = dot(dy_all, w_down_columns, 1, 0)
    grad_gate_b = (grad_hidden * up * sigma * (1.0 + gate * (1.0 - sigma))).astype(BF)
    grad_up_b = (grad_hidden * silu).astype(BF)
    grad_gate = replica_sum(dot(grad_gate_b, n2, 0, 0).astype(BF))
    grad_up = replica_sum(dot(grad_up_b, n2, 0, 0).astype(BF))
    grad_normed_two = scatter_tokens(dot(grad_gate_b, w_gate, 1, 0) + dot(grad_up_b, w_up, 1, 0))
    mixed = scatter_tokens(dot(hidden, w_down_columns, 1, 1))
    layer_out = (middle + mixed).astype(BF)
    grad_middle = dyb.astype(F32) + norm_back(normed_two, inverse_two, grad_normed_two)

    grad_middle_all = gather_tokens(grad_middle.astype(BF))
    grad_out = columns_to_rows(replica_sum(dot(grad_middle_all, out_b, 0, 0).astype(BF)))
    grad_attn = split_heads(dot(grad_middle_all, w_out_columns, 1, 0)).astype(BF)
    delta = jnp.sum(grad_attn.astype(F32) * attn, axis=-1, keepdims=True)
    probs = jnp.where(allowed, jnp.exp(scores - log_total), 0.0)
    grad_probs = jnp.einsum("hqe,hke->hqk", grad_attn, values, preferred_element_type=F32)
    grad_scores = (probs * (grad_probs - delta)).astype(BF)
    query_grad = factor * jnp.einsum("hqk,hke->hqe", grad_scores, keys, preferred_element_type=F32)
    key_grad = factor * jnp.einsum("hqk,hqe->hke", grad_scores, query, preferred_element_type=F32)
    value_grad = jnp.einsum("hqk,hqe->hke", probs.astype(BF), grad_attn, preferred_element_type=F32)
    query_grad = join_heads(rotate(query_grad, cosine, -sine)).astype(BF)
    key_grad = join_heads(rotate(key_grad, cosine, -sine)).astype(BF)
    value_grad = join_heads(value_grad).astype(BF)
    grad_query = replica_sum(dot(query_grad, n1, 0, 0).astype(BF))
    grad_key = replica_sum(dot(key_grad, n1, 0, 0).astype(BF))
    grad_value = replica_sum(dot(value_grad, n1, 0, 0).astype(BF))
    grad_normed_one = scatter_tokens(
        dot(query_grad, w_query, 1, 0) + dot(key_grad, w_key, 1, 0) + dot(value_grad, w_value, 1, 0)
    )
    grad_in = grad_middle + norm_back(normed_one, inverse_one, grad_normed_one)
    return (
        layer_out[None],
        grad_in[None],
        grad_query.astype(F32),
        grad_key.astype(F32),
        grad_value.astype(F32),
        grad_out.astype(F32),
        grad_gate.astype(F32),
        grad_up.astype(F32),
        grad_down.astype(F32),
    )


def body(hidden_in, cotangent, doc_lengths, w_query, w_key, w_value, w_out, w_gate, w_up, w_down):
    x_own, dy_own = hidden_in[0], cotangent[0]
    sequence = x_own.shape[0] * lax.axis_size("shard")
    places = jnp.arange(sequence, dtype=jnp.int32)
    offset = doc_layout(doc_lengths[0], places)[1]
    cosine, sine = rope_tables(offset, HEAD_DIM)
    cosine = jnp.concatenate([cosine[0], cosine[0]], axis=-1)
    sine = jnp.concatenate([-sine[0], sine[0]], axis=-1)
    start = (places - offset)[:, None]
    n1_own = normalize(x_own.astype(F32))[0].astype(BF)
    (
        n1, query, key, value, attn, attn_b, out_columns, _, down_columns,
        hidden, grad_gate_b, grad_up_b, middle, n2, dy, blocks, grad_middle, grad_all,
    ) = front(
        n1_own, x_own, dy_own, start, cosine, sine, w_query, w_key, w_value, w_out, w_gate, w_up, w_down
    )
    layer_out, grad_in, attn_part = back(
        x_own, start, cosine, sine, hidden, down_columns, grad_all, out_columns, attn_b, attn,
        query, key, value, n1, w_query, w_key, w_value, middle, grad_middle,
    )
    grad_gate, grad_up, grad_down, attn_sum = ffn_grads(
        blocks, n2, dy, (hidden, grad_gate_b, grad_up_b), attn_part, w_gate, w_up, down_columns
    )
    grad_query, grad_key, grad_value, grad_out = jnp.split(attn_sum.astype(F32), 4, axis=0)
    return (
        layer_out[None],
        grad_in[None],
        grad_query,
        grad_key,
        grad_value,
        grad_out,
        grad_gate,
        grad_up,
        columns_to_rows(grad_down).astype(F32),
    )


def solution(mesh):
    rows = P("shard", None)
    tokens = P("replica", "shard", None)
    in_specs = (tokens, tokens, P("replica", None)) + (rows,) * 7
    out_specs = (tokens, tokens) + (rows,) * 7
    local = body if mesh.shape["shard"] == 8 and mesh.shape["replica"] == 4 else general_body
    return jax.shard_map(local, mesh=mesh, in_specs=in_specs, out_specs=out_specs, check_vma=False)
```

```python
import functools
import math

import jax
import jax.numpy as jnp
import numpy as np
from jax import lax
from jax.experimental import pallas as pl
from jax.experimental.pallas import tpu as pltpu
from jax.sharding import PartitionSpec as P

HEAD_DIM = 128

epsilon = 1e-05
theta_base = 10000.0
masked = -1e30
BF = jnp.bfloat16
F32 = jnp.float32
MESH = pl.DeviceIdType.MESH
VMEM = pltpu.VMEM


def normalize(values):
    center = values - jnp.mean(values, axis=-1, keepdims=True)
    inverse = lax.rsqrt(jnp.mean(center * center, axis=-1, keepdims=True) + epsilon)
    return (center * inverse, inverse)


def norm_back(normed, inverse, grad):
    inner = (
        grad
        - jnp.mean(grad, axis=-1, keepdims=True)
        - normed * jnp.mean(grad * normed, axis=-1, keepdims=True)
    )
    return inverse * inner


def dot(a, b, ca, cb):
    return lax.dot_general(a, b, (((ca,), (cb,)), ((), ())), preferred_element_type=F32)


def doc_layout(lengths, places):
    ends = jnp.cumsum(lengths)
    starts = ends - lengths
    segment = jnp.sum((places[:, None] >= ends[None, :]).astype(jnp.int32), axis=1)
    member = segment[:, None] == jnp.arange(lengths.shape[0], dtype=jnp.int32)[None, :]
    offset = places - jnp.sum(jnp.where(member, starts[None, :], 0), axis=1)
    return (segment, offset)


def rope_tables(offset, head_dim):
    half = head_dim // 2
    freq = theta_base ** (-2.0 * jnp.arange(half, dtype=F32) / head_dim)
    angle = offset.astype(F32)[:, None] * freq[None, :]
    return (jnp.cos(angle)[None], jnp.sin(angle)[None])


def rotate(values, cosine, sine):
    half = values.shape[-1] // 2
    first = values[..., :half]
    second = values[..., half:]
    return jnp.concatenate(
        [first * cosine - second * sine, second * cosine + first * sine], axis=-1
    )


def split_heads(values):
    tokens, width = values.shape
    return jnp.transpose(values.reshape(tokens, width // HEAD_DIM, HEAD_DIM), (1, 0, 2))


def join_heads(values):
    heads, tokens, size = values.shape
    return jnp.transpose(values, (1, 0, 2)).reshape(tokens, heads * size)


def whereabouts():
    place = lax.axis_index("shard")
    core, col, row = lax.rem(place, 2), lax.rem(place // 2, 2), place // 4
    across, along = place + 2 - 4 * col, place + 4 - 8 * row
    return place, place + 1 - 2 * core, across, along, across + 4 - 8 * row


def whereabouts_of_mate():
    me, mate, across, along, far = whereabouts()
    shift = mate - me
    return across + shift, along + shift, far + shift


def tile_loop(rows, columns, size, step, narrow=None):
    narrow = narrow or size
    across = columns // narrow

    def one(i, carry):
        step(
            pl.ds(pl.multiple_of((i // across) * size, size), size),
            pl.ds(pl.multiple_of(lax.rem(i, across) * narrow, narrow), narrow),
        )
        return carry

    lax.fori_loop(0, (rows // size) * across, one, 0)


def product(a, b, ca, cb):
    return lax.dot_general(a, b, (((ca,), (cb,)), ((), ())), preferred_element_type=F32)


def ffn_tile(normed, dy, w_gate, w_up, w_down, hidden, grad_gate, grad_up, rows, columns):
    gate = product(normed[rows, :], w_gate[columns, :], 1, 1)
    up = product(normed[rows, :], w_up[columns, :], 1, 1)
    grad = product(dy[rows, :], w_down[:, columns], 1, 0)
    sigma = 1.0 / (1.0 + jnp.exp(-gate))
    silu = gate * sigma
    hidden[rows, columns] = (silu * up).astype(BF)
    grad_gate[rows, columns] = (grad * up * sigma * (1.0 + gate * (1.0 - sigma))).astype(BF)
    grad_up[rows, columns] = (grad * silu).astype(BF)


def block_rows(slot, tokens, part=0):
    size = tokens // 2
    if part:
        return pl.ds(pl.multiple_of(slot * tokens + (part - 1) * size, size), size)
    return pl.ds(pl.multiple_of(slot * tokens, tokens), tokens)


class Gather:
    def __init__(self, block, out, sent, came):
        self.block, self.out, self.sent, self.came = block, out, sent, came
        self.tokens = block.shape[0]
        self.replica = lax.axis_index("replica")
        self.me, self.mate, self.across, self.along, self.far = whereabouts()
        self.sends = []

    def move(self, k, slot, part, device, first=False):
        tokens = self.tokens
        local = pl.ds((part - 1) * (tokens // 2) if part else 0, tokens // 2 if part else tokens)
        rows = block_rows(slot, tokens, part)
        return pltpu.make_async_remote_copy(
            src_ref=self.block.at[local] if first else self.out.at[rows],
            dst_ref=self.out.at[rows],
            send_sem=self.sent.at[k],
            recv_sem=self.came.at[k],
            device_id=(self.replica, device),
            device_id_type=MESH,
        )

    def start(self, *moves):
        for one in moves:
            self.move(*one).start()
            self.sends.append(one)

    def came_in(self, *moves):
        for k, slot, part in moves:
            self.move(k, slot, part, self.mate).wait_recv()

    def one(self):
        me = self.me
        self.start(
            (1, me, 1, self.across, True),
            (3, me, 2, self.along, True),
            (0, me, 0, self.mate, True),
            (2, me, 2, self.across, True),
            (4, me, 1, self.along, True),
        )

    def two(self):
        self.came_in((1, self.across, 1))
        self.start((5, self.across, 1, self.along), (6, self.across, 1, self.mate))
        self.came_in((3, self.along, 2))
        self.start((7, self.along, 2, self.across), (8, self.along, 2, self.mate))

    def three(self):
        self.came_in((2, self.across, 2))
        self.start((9, self.across, 2, self.mate))
        self.came_in((4, self.along, 1))
        self.start((10, self.along, 1, self.mate))

    def four(self):
        self.came_in((5, self.far, 1))
        self.start((11, self.far, 1, self.mate))
        self.came_in((7, self.far, 2))
        self.start((12, self.far, 2, self.mate))

    def finish(self):
        across, along, far = whereabouts_of_mate()
        self.came_in(
            (0, self.mate, 0), (6, across, 1), (8, along, 2), (9, across, 2), (10, along, 1),
            (11, far, 1), (12, far, 2),
        )

    def drain(self):
        for one in self.sends:
            self.move(*one).wait_send()


class Scatter:
    def __init__(self, parts, buffers, sent, came):
        self.parts = parts
        self.pair, self.sums, self.by_far, self.by_side = buffers
        self.sent, self.came = sent, came
        self.tokens = self.pair.shape[1]
        self.replica = lax.axis_index("replica")
        me, mate, across, along, far = whereabouts()
        self.mine, self.shift, self.mate = (me, across, along, far), mate - me, mate
        low, high = pl.ds(0, self.tokens // 2), pl.ds(self.tokens // 2, self.tokens // 2)
        self.low, self.high = low, high
        sums, by_far, by_side = self.sums, self.by_far, self.by_side
        self.swaps = [
            self.move(k, parts.at[block_rows(self.mine[k] + self.shift, self.tokens)], self.pair.at[k], mate)
            for k in range(4)
        ]
        self.far_low = self.move(4, sums.at[2, low], by_far.at[0], across)
        self.far_high = self.move(5, sums.at[2, high], by_far.at[1], along)
        self.across_low = self.move(6, sums.at[0, low], by_side.at[0, low], across)
        self.along_high = self.move(7, sums.at[1, high], by_side.at[1, high], along)
        self.along_low = self.move(8, sums.at[1, low], by_side.at[1, low], along)
        self.across_high = self.move(9, sums.at[0, high], by_side.at[0, high], across)

    def move(self, k, src, dst, device):
        return pltpu.make_async_remote_copy(
            src_ref=src,
            dst_ref=dst,
            send_sem=self.sent.at[k],
            recv_sem=self.came.at[k],
            device_id=(self.replica, device),
            device_id_type=MESH,
        )

    def swap(self, *which):
        for k in which:
            self.swaps[k].start()

    def pair_sum(self, k):
        self.swaps[k].wait_recv()
        own = self.parts[block_rows(self.mine[k], self.tokens), :].astype(F32)
        self.sums[k - 1] = (own + self.pair[k].astype(F32)).astype(BF)

    def send_far(self):
        self.pair_sum(3)
        self.far_low.start()
        self.far_high.start()

    def send_near(self):
        self.pair_sum(1)
        self.across_low.start()
        self.pair_sum(2)
        self.along_high.start()

    def send_rest(self):
        low, high, sums = self.low, self.high, self.sums
        self.far_low.wait_recv()
        sums[1, low] = (sums[1, low].astype(F32) + self.by_far[0].astype(F32)).astype(BF)
        self.along_low.start()
        self.far_high.wait_recv()
        sums[0, high] = (sums[0, high].astype(F32) + self.by_far[1].astype(F32)).astype(BF)
        self.across_high.start()

    def total(self):
        self.swaps[0].wait_recv()
        own = self.parts[block_rows(self.mine[0], self.tokens), :].astype(F32)
        own = own + self.pair[0].astype(F32)
        for copy in (self.across_low, self.along_high, self.along_low, self.across_high):
            copy.wait_recv()
        return own + (self.by_side[0].astype(F32) + self.by_side[1].astype(F32))

    def drain(self):
        for copy in (
            *self.swaps, self.far_low, self.far_high, self.across_low, self.along_high,
            self.along_low, self.across_high,
        ):
            copy.wait_send()


class Line:
    def __init__(self, own, slots, sent, came):
        self.own, self.slots, self.sent, self.came = own, slots, sent, came
        self.replica, self.me = lax.axis_index("replica"), lax.axis_index("shard")
        self.replicas = lax.axis_size("replica")

    def move(self, way, i, slot, first):
        target = self.replica + (1 if way == 0 else -1)
        return pltpu.make_async_remote_copy(
            src_ref=self.own if first else self.slots(slot),
            dst_ref=self.slots(slot),
            send_sem=self.sent.at[way, i],
            recv_sem=self.came.at[way, i],
            device_id=(target, self.me),
            device_id_type=MESH,
        )

    def source(self, way, i):
        return self.replica - i if way == 0 else self.replica + i

    def has(self, way, i):
        return self.replica >= i if way == 0 else self.replica + i < self.replicas

    def can_send(self, way):
        return self.replica + 1 < self.replicas if way == 0 else self.replica >= 1

    def start(self):
        for way in (0, 1):

            @pl.when(self.can_send(way))
            def _(way=way):
                self.move(way, 0, self.replica, True).start()

    def step(self, i):
        for way in (0, 1):

            @pl.when(self.has(way, i))
            def _(way=way):
                self.move(way, i - 1, self.source(way, i), False).wait_recv()
                if i < self.replicas - 1:

                    @pl.when(self.can_send(way))
                    def _():
                        self.move(way, i, self.source(way, i), False).start()

    def drain(self):
        for way in (0, 1):
            for i in range(self.replicas - 1):

                @pl.when(self.has(way, i) & self.can_send(way))
                def _(way=way, i=i):
                    self.move(way, i, self.source(way, i), i == 0).wait_send()


def rotate_head(values, cosine, sine):
    return values * cosine + pltpu.roll(values, values.shape[-1] // 2, 1) * sine


def key_reach(first, step, sequence):
    low = max(0, (first + 1 - sequence // 2) // 128 * 128)
    return low, pl.ds(low, first + step - low)


def allowed_bias(start, first, step, low):
    shape = (step, first + step - low)
    key_place = lax.broadcasted_iota(jnp.int32, shape, 1) + low
    query_place = lax.broadcasted_iota(jnp.int32, shape, 0) + first
    return jnp.where((key_place <= query_place) & (key_place >= start), 0.0, masked)


def head_scores(query, keys, bias):
    return product(query, keys, 1, 1) * (1.0 / math.sqrt(HEAD_DIM)) + bias


def fill_tables(lengths, frequency, cosine, sine, start):
    shape = start.shape
    place = lax.broadcasted_iota(jnp.int32, shape, 0)
    begin = jnp.zeros(shape, jnp.int32)
    end = 0
    for i in range(lengths.shape[1] - 1):
        end = end + lengths[0, i]
        begin = jnp.where(place >= end, end, begin)
    start[...] = begin
    angle = (place - begin).astype(F32) * frequency[...]
    lane = lax.broadcasted_iota(jnp.int32, shape, 1)
    cosine[...] = jnp.cos(angle)
    sine[...] = jnp.where(lane < shape[1] // 2, -1.0, 1.0) * jnp.sin(angle)


def front_kernel(
    lengths, frequency, x_own, dy_own, w_query, w_key, w_value, w_out, w_gate, w_up, w_down,
    n1_out, query_out, key_out, value_out, attn_out, attn_b_out, out_columns_out, down_parts,
    down_columns_out, hidden_out, grad_gate_out, grad_up_out, middle_out, n2_out, dy_out, lined,
    grad_out, grad_all_out, next_out, cosine_out, sine_out, start_out,
    n1, n2, dy, query, key, value, attn, attn_b, out_columns, gate_w, up_w, down_w,
    hidden, grad_gate, grad_up, parts, pair, sums, by_far, by_side, middle, normed, n2_own, grad_own, n1_own, cosine, sine, start,
    load_sem, save_sem, gather_sent, gather_came, scatter_sent, scatter_came,
    swap_sent, swap_came, line_sent, line_came,
):
    replica = lax.axis_index("replica")
    replicas = lax.axis_size("replica")
    me = lax.axis_index("shard")
    groups = lax.axis_size("shard")
    tokens, width = x_own.shape
    sequence = n1.shape[0]
    saves = []

    def save(src, dst):
        copy = pltpu.make_async_copy(src, dst, save_sem.at[len(saves)])
        copy.start()
        saves.append(copy)

    def exchange(which, source, target):
        copies = []
        for i in range(1, groups):
            device = lax.rem(me + i, groups)
            copies.append(
                pltpu.make_async_remote_copy(
                    src_ref=source(device),
                    dst_ref=target,
                    send_sem=swap_sent.at[which, i],
                    recv_sem=swap_came.at[which, i],
                    device_id=(replica, device),
                    device_id_type=MESH,
                )
            )
        return copies

    gate_load = pltpu.make_async_copy(w_gate, gate_w, load_sem.at[0])
    up_load = pltpu.make_async_copy(w_up, up_w, load_sem.at[1])
    gate_load.start()
    up_load.start()
    own_rows = block_rows(me, tokens)
    x = x_own[...].astype(F32)
    center = x - jnp.mean(x, axis=-1, keepdims=True)
    inverse = lax.rsqrt(jnp.mean(center * center, axis=-1, keepdims=True) + epsilon)
    n1_own[...] = (center * inverse).astype(BF)
    own_n1 = pltpu.make_async_copy(n1_own, n1.at[own_rows], load_sem.at[2])
    own_dy = pltpu.make_async_copy(dy_own, dy.at[own_rows], load_sem.at[3])
    own_n1.start()
    own_dy.start()

    barrier = pltpu.get_barrier_semaphore()
    for i in range(1, groups):
        device = lax.rem(me + i, groups)
        pl.semaphore_signal(barrier, inc=1, device_id=(replica, device), device_id_type=MESH)

    @pl.when(replica >= 1)
    def _():
        pl.semaphore_signal(barrier, inc=1, device_id=(replica - 1, me), device_id_type=MESH)

    @pl.when(replica + 1 < replicas)
    def _():
        pl.semaphore_signal(barrier, inc=1, device_id=(replica + 1, me), device_id_type=MESH)

    edge = (replica == 0) | (replica == replicas - 1)

    @pl.when(edge)
    def _():
        pl.semaphore_wait(barrier, groups)

    @pl.when(jnp.logical_not(edge))
    def _():
        pl.semaphore_wait(barrier, groups + 1)

    n1_gather = Gather(n1_own, n1, gather_sent.at[0], gather_came.at[0])
    dy_gather = Gather(dy_own, dy, gather_sent.at[1], gather_came.at[1])
    n2_gather = Gather(n2_own, n2, gather_sent.at[2], gather_came.at[2])
    grad_gather = Gather(grad_own, grad_all_out, gather_sent.at[3], gather_came.at[3])
    dy_line = Line(
        dy_own, lambda s: lined.at[s, pl.ds(tokens, tokens)], line_sent.at[0], line_came.at[0]
    )
    n2_line = Line(
        n2_own, lambda s: lined.at[s, pl.ds(0, tokens)], line_sent.at[1], line_came.at[1]
    )
    down_line = Line(
        down_parts.at[replica], lambda s: down_parts.at[s], line_sent.at[2], line_came.at[2]
    )
    buffers = (pair, sums, by_far, by_side)

    n1_gather.one()
    dy_line.start()
    fill_tables(lengths, frequency, cosine, sine, start)
    save(cosine, cosine_out)
    save(sine, sine_out)
    save(start, start_out)
    n1_gather.two()
    n1_gather.three()
    wide = w_out.shape[0]
    mine = pl.ds(pl.multiple_of(me * wide, wide), wide)
    part = down_parts.shape[2]

    def down_block(device):
        column = (device * replicas + replica) * part
        return w_down.at[:, pl.ds(pl.multiple_of(column, part), part)]

    def out_block(device):
        return w_out.at[:, pl.ds(pl.multiple_of(device * wide, wide), wide)]

    down_swaps = exchange(1, down_block, down_parts.at[replica, mine])
    out_swaps = exchange(0, out_block, out_columns.at[mine])
    own_down = pltpu.make_async_copy(down_block(me), down_parts.at[replica, mine], load_sem.at[5])
    own_down.start()
    own_out = pltpu.make_async_copy(out_block(me), out_columns.at[mine], load_sem.at[4])
    own_out.start()
    for copy in down_swaps + out_swaps:
        copy.start()
    n1_gather.four()
    own_n1.wait()
    n1_gather.finish()
    dy_gather.one()
    save(n1, n1_out)

    heads = query.shape[1] // HEAD_DIM
    for first in range(0, sequence, 512):
        rows = pl.ds(first, 512)
        for weight, target in ((w_query, query), (w_key, key), (w_value, value)):
            values = product(n1[rows, :], weight[...], 1, 1)
            for head in range(heads):
                lanes = pl.ds(head * HEAD_DIM, HEAD_DIM)
                piece = values[:, head * HEAD_DIM : (head + 1) * HEAD_DIM]
                if target is not value:
                    piece = rotate_head(piece, cosine[rows, :], sine[rows, :])
                target[rows, lanes] = piece.astype(BF)
    save(query, query_out)
    save(key, key_out)
    save(value, value_out)
    dy_line.step(1)
    own_down.wait()
    for copy in down_swaps:
        copy.wait_recv()
    down_line.start()
    step = 256
    for first in range(0, sequence, step):
        rows = pl.ds(first, step)
        low, reach = key_reach(first, step, sequence)
        bias = allowed_bias(start[rows, 0:1], first, step, low)
        for head in range(heads):
            lanes = pl.ds(head * HEAD_DIM, HEAD_DIM)
            scores = head_scores(query[rows, lanes], key[reach, lanes], bias)
            weights = jnp.exp(scores - jnp.max(scores, axis=-1, keepdims=True))
            total = jnp.sum(weights, axis=-1, keepdims=True)
            result = product(weights.astype(BF), value[reach, lanes], 1, 0) / total
            attn[rows, lanes] = result
            attn_b[rows, lanes] = result.astype(BF)
    save(attn, attn_out)
    save(attn_b, attn_b_out)
    dy_line.step(2)
    dy_gather.two()

    own_out.wait()
    for copy in out_swaps:
        copy.wait_recv()
    save(out_columns, out_columns_out)

    def spread(rows, columns):
        parts[rows, columns] = product(attn_b[rows, :], out_columns[columns, :], 1, 1).astype(BF)

    tile_loop(sequence, width, 512, spread)
    scatter = Scatter(parts, buffers, scatter_sent.at[0], scatter_came.at[0])
    scatter.swap(3, 1, 2, 0)
    scatter.send_far()
    scatter.send_near()
    dy_gather.three()
    dy_line.step(3)
    scatter.send_rest()
    middle[...] = x_own[...].astype(F32) + scatter.total()
    scatter.drain()
    save(middle, middle_out)
    center = middle[...] - jnp.mean(middle[...], axis=-1, keepdims=True)
    inverse = lax.rsqrt(jnp.mean(center * center, axis=-1, keepdims=True) + epsilon)
    normed[...] = center * inverse
    n2_own[...] = normed[...].astype(BF)
    n2_gather.one()
    own_n2 = pltpu.make_async_copy(n2_own, n2.at[own_rows], load_sem.at[6])
    own_n2.start()
    dy_gather.four()
    down_line.step(1)
    n2_gather.two()
    n2_gather.three()
    n2_gather.four()
    own_n2.wait()
    n2_gather.finish()
    save(n2, n2_out)
    own_dy.wait()
    dy_gather.finish()
    save(dy, dy_out)
    down_line.step(2)
    down_line.step(3)
    next_dy = lined.at[lax.rem(replica + 1, replicas), pl.ds(tokens, tokens)]
    next_gather = Gather(next_dy, next_out, gather_sent.at[4], gather_came.at[4])
    next_gather.one()
    save(next_dy, next_out.at[own_rows])
    n2_line.start()
    down_loads = []
    for r in range(replicas):
        down_loads.append(
            pltpu.make_async_copy(
                down_parts.at[r], down_w.at[:, pl.ds(r * part, part)], load_sem.at[7 + r]
            )
        )
        down_loads[-1].start()
    gate_load.wait()
    up_load.wait()
    for copy in down_loads:
        copy.wait()
    save(down_w, down_columns_out)

    half = sequence // 2
    row = me // (groups // 2)
    back = Scatter(parts, buffers, scatter_sent.at[1], scatter_came.at[1])

    def feed(base):
        def forward(rows, columns):
            rows = pl.ds(pl.multiple_of(base, half), half)
            ffn_tile(n2, dy, gate_w, up_w, down_w, hidden, grad_gate, grad_up, rows, columns)

        tile_loop(512, gate_w.shape[0], 512, forward)

        def backward(rows, columns):
            rows = pl.ds(pl.multiple_of(base, half), half)
            value = product(grad_gate[rows, :], gate_w[:, columns], 1, 0)
            value = value + product(grad_up[rows, :], up_w[:, columns], 1, 0)
            parts[rows, columns] = value.astype(BF)

        tile_loop(512, width, 512, backward)

    feed((1 - row) * half)
    back.swap(3, 2)
    next_gather.two()
    n2_line.step(1)
    back.send_far()
    feed(row * half)
    save(hidden, hidden_out)
    save(grad_gate, grad_gate_out)
    save(grad_up, grad_up_out)
    back.swap(1, 0)
    next_gather.three()
    back.send_near()
    back.send_rest()
    next_gather.four()
    n2_line.step(2)
    inner = back.total()
    back.drain()
    inner = (
        inner
        - jnp.mean(inner, axis=-1, keepdims=True)
        - normed[...] * jnp.mean(inner * normed[...], axis=-1, keepdims=True)
    )
    center = middle[...] - jnp.mean(middle[...], axis=-1, keepdims=True)
    inverse = lax.rsqrt(jnp.mean(center * center, axis=-1, keepdims=True) + epsilon)
    normed[...] = dy_own[...].astype(F32) + inverse * inner
    grad_own[...] = normed[...].astype(BF)
    grad_gather.one()
    save(normed, grad_out)
    save(grad_own, grad_all_out.at[own_rows])
    grad_gather.two()
    grad_gather.three()
    grad_gather.four()
    n2_line.step(3)
    grad_gather.finish()
    next_gather.finish()
    for copy in saves:
        copy.wait()
    for copy in out_swaps + down_swaps:
        copy.wait_send()
    for user in (n1_gather, n2_gather, dy_gather, grad_gather, next_gather, dy_line, n2_line, down_line):
        user.drain()


def front(lengths, frequency, x_own, dy_own, w_query, w_key, w_value, w_out, w_gate, w_up, w_down):
    groups, replicas = lax.axis_size("shard"), lax.axis_size("replica")
    tokens, width = x_own.shape
    sequence = tokens * groups
    wide, columns = w_query.shape[0], w_gate.shape[0]
    anywhere, vmem = pl.BlockSpec(memory_space=pl.ANY), pl.BlockSpec(memory_space=VMEM)

    def shape(dims, kind=BF):
        return jax.ShapeDtypeStruct(dims, kind)

    outs = (
        shape((sequence, width)),
        shape((sequence, wide)),
        shape((sequence, wide)),
        shape((sequence, wide)),
        shape((sequence, wide), F32),
        shape((sequence, wide)),
        shape((width, wide)),
        shape((replicas, width, columns // replicas)),
        shape((width, columns)),
        shape((sequence, columns)),
        shape((sequence, columns)),
        shape((sequence, columns)),
        shape((tokens, width), F32),
        shape((sequence, width)),
        shape((sequence, width)),
        shape((replicas, 2 * tokens, width)),
        shape((tokens, width), F32),
        shape((sequence, width)),
        shape((sequence, width)),
        shape((sequence, HEAD_DIM), F32),
        shape((sequence, HEAD_DIM), F32),
        shape((sequence, HEAD_DIM), jnp.int32),
    )
    dma = pltpu.SemaphoreType.DMA
    return pl.pallas_call(
        front_kernel,
        out_shape=outs,
        in_specs=[pl.BlockSpec(memory_space=pltpu.SMEM)] + [vmem] * 6 + [anywhere] * 4,
        out_specs=(anywhere,) * len(outs),
        scratch_shapes=[
            pltpu.VMEM((sequence, width), BF),
            pltpu.VMEM((sequence, width), BF),
            pltpu.VMEM((sequence, width), BF),
            pltpu.VMEM((sequence, wide), BF),
            pltpu.VMEM((sequence, wide), BF),
            pltpu.VMEM((sequence, wide), BF),
            pltpu.VMEM((sequence, wide), F32),
            pltpu.VMEM((sequence, wide), BF),
            pltpu.VMEM((width, wide), BF),
            pltpu.VMEM((columns, width), BF),
            pltpu.VMEM((columns, width), BF),
            pltpu.VMEM((width, columns), BF),
            pltpu.VMEM((sequence, columns), BF),
            pltpu.VMEM((sequence, columns), BF),
            pltpu.VMEM((sequence, columns), BF),
            pltpu.VMEM((sequence, width), BF),
            pltpu.VMEM((4, tokens, width), BF),
            pltpu.VMEM((3, tokens, width), BF),
            pltpu.VMEM((2, tokens // 2, width), BF),
            pltpu.VMEM((2, tokens, width), BF),
            pltpu.VMEM((tokens, width), F32),
            pltpu.VMEM((tokens, width), F32),
            pltpu.VMEM((tokens, width), BF),
            pltpu.VMEM((tokens, width), BF),
            pltpu.VMEM((tokens, width), BF),
            pltpu.VMEM((sequence, HEAD_DIM), F32),
            pltpu.VMEM((sequence, HEAD_DIM), F32),
            pltpu.VMEM((sequence, HEAD_DIM), jnp.int32),
            dma((7 + replicas,)),
            dma((24,)),
            dma((5, 13)),
            dma((5, 13)),
            dma((2, 10)),
            dma((2, 10)),
            dma((2, groups)),
            dma((2, groups)),
            dma((3, 2, replicas)),
            dma((3, 2, replicas)),
        ],
        compiler_params=pltpu.CompilerParams(
            collective_id=3, has_side_effects=True, vmem_limit_bytes=67043328
        ),
        cost_estimate=pl.CostEstimate(
            flops=12 * sequence * width * columns, bytes_accessed=64 * 1024 * 1024, transcendentals=0
        ),
        name="front",
    )(lengths, frequency, x_own, dy_own, w_query, w_key, w_value, w_out, w_gate, w_up, w_down)


def back_kernel(
    x_own, start, cosine, sine, hidden_in, down_in, grad_in, out_columns_in, attn_b_in, attn_in,
    query_in, key_in, value_in, n1_in, w_query, w_key, w_value, lined, middle, grad_middle,
    layer_out, input_grad, attn_part, next_out,
    hidden, down_w, grad, out_columns, attn_b, attn, query, key, value, n1, weights,
    grad_attn, key_grad, value_grad, columns_grad, out_grad, rows_grad, parts,
    pair, sums, by_far, by_side, pair2, sums2, by_far2, by_side2,
    load_sem, save_sem, scatter_sent, scatter_came, swap_sent, swap_came,
    gather_sent, gather_came,
):
    replica = lax.axis_index("replica")
    me = lax.axis_index("shard")
    groups = lax.axis_size("shard")
    sequence, width = n1.shape
    wide = query.shape[1]
    heads = wide // HEAD_DIM
    pairs = (
        (hidden_in, hidden), (down_in, down_w), (grad_in, grad), (out_columns_in, out_columns),
        (attn_b_in, attn_b), (attn_in, attn), (query_in, query), (key_in, key), (value_in, value),
        (n1_in, n1), (w_query, weights.at[pl.ds(0, wide)]), (w_key, weights.at[pl.ds(wide, wide)]),
        (w_value, weights.at[pl.ds(2 * wide, wide)]),
    )
    loads = [
        pltpu.make_async_copy(src, dst, load_sem.at[i]) for i, (src, dst) in enumerate(pairs)
    ]
    for copy in loads:
        copy.start()
    barrier = pltpu.get_barrier_semaphore()
    for i in range(1, groups):
        device = lax.rem(me + i, groups)
        pl.semaphore_signal(barrier, inc=1, device_id=(replica, device), device_id_type=MESH)
    pl.semaphore_wait(barrier, groups - 1)

    loads[0].wait()
    loads[1].wait()

    def mix(rows, columns):
        parts[rows, columns] = product(hidden[rows, :], down_w[columns, :], 1, 1).astype(BF)

    tile_loop(sequence, width, 512, mix)
    mixed = Scatter(parts, (pair, sums, by_far, by_side), scatter_sent.at[0], scatter_came.at[0])
    mixed.swap(3, 1, 2, 0)

    for copy in loads[2:6]:
        copy.wait()
    mixed.send_far()
    mixed.send_near()
    for first in range(0, width, 512):
        rows = pl.ds(first, 512)
        out_grad[rows, :] = product(grad[:, rows], attn_b[...], 0, 0).astype(BF)
    mine = pl.ds(pl.multiple_of(me * wide, wide), wide)
    out_rows = pl.ds(3 * wide, wide)
    swaps = []
    for i in range(1, groups):
        device = lax.rem(me + i, groups)
        swaps.append(
            pltpu.make_async_remote_copy(
                src_ref=out_grad.at[pl.ds(pl.multiple_of(device * wide, wide), wide)],
                dst_ref=attn_part.at[out_rows, mine],
                send_sem=swap_sent.at[i],
                recv_sem=swap_came.at[i],
                device_id=(replica, device),
                device_id_type=MESH,
            )
        )
        swaps[-1].start()
    own_swap = pltpu.make_async_copy(out_grad.at[mine], attn_part.at[out_rows, mine], save_sem.at[0])
    own_swap.start()
    tokens = x_own.shape[0]
    replicas = lax.axis_size("replica")
    next_dy = lined.at[lax.rem(replica + 2, replicas), pl.ds(tokens, tokens)]
    next_gather = Gather(next_dy, next_out, gather_sent, gather_came)
    next_gather.one()
    own_next = pltpu.make_async_copy(next_dy, next_out.at[block_rows(me, tokens)], save_sem.at[2])
    own_next.start()
    for first in range(0, sequence, 512):
        rows = pl.ds(first, 512)
        grad_attn[rows, :] = product(grad[rows, :], out_columns[...], 1, 0).astype(BF)
    for copy in loads[6:]:
        copy.wait()
    mixed.send_rest()

    step = 256
    for first in range(sequence - step, -1, -step):
        if first == sequence - 2 * step:
            next_gather.two()
        if first == 0:
            next_gather.three()
        rows = pl.ds(first, step)
        low, upto = key_reach(first, step, sequence)
        bias = allowed_bias(start[rows, 0:1], first, step, low)
        for head in range(heads):
            lanes = pl.ds(head * HEAD_DIM, HEAD_DIM)
            query_piece, grad_piece = query[rows, lanes], grad_attn[rows, lanes]
            scores = head_scores(query_piece, key[upto, lanes], bias)
            probs = jnp.exp(scores - jnp.max(scores, axis=-1, keepdims=True))
            probs = probs / jnp.sum(probs, axis=-1, keepdims=True)
            delta = jnp.sum(grad_piece.astype(F32) * attn[rows, lanes], axis=-1, keepdims=True)
            grad_probs = product(grad_piece, value[upto, lanes], 1, 1)
            grad_scores = (probs * (grad_probs - delta)).astype(BF)
            query_grad = product(grad_scores, key[upto, lanes], 1, 0) * (1.0 / math.sqrt(HEAD_DIM))
            query_grad = rotate_head(query_grad, cosine[rows, :], -sine[rows, :])
            columns_grad[rows, lanes] = query_grad.astype(BF)
            key_part = product(grad_scores, query_piece, 0, 0)
            value_part = product(probs.astype(BF), grad_piece, 0, 0)
            if first == sequence - step:
                key_grad[upto, lanes] = key_part
                value_grad[upto, lanes] = value_part
                if low:
                    key_grad[pl.ds(0, low), lanes] = jnp.zeros((low, HEAD_DIM), F32)
                    value_grad[pl.ds(0, low), lanes] = jnp.zeros((low, HEAD_DIM), F32)
            else:
                key_grad[upto, lanes] += key_part
                value_grad[upto, lanes] += value_part
    for head in range(heads):
        lanes = pl.ds(head * HEAD_DIM, HEAD_DIM)
        piece = key_grad[:, lanes] * (1.0 / math.sqrt(HEAD_DIM))
        piece = rotate_head(piece, cosine[...], -sine[...])
        columns_grad[:, pl.ds(wide + head * HEAD_DIM, HEAD_DIM)] = piece.astype(BF)
        columns_grad[:, pl.ds(2 * wide + head * HEAD_DIM, HEAD_DIM)] = value_grad[:, lanes].astype(BF)

    next_gather.four()
    layer_out[...] = (middle[...] + mixed.total()).astype(BF)
    mixed.drain()

    def back(rows, columns):
        parts[rows, columns] = product(columns_grad[rows, :], weights[:, columns], 1, 0).astype(BF)

    tile_loop(sequence, width, 512, back)
    last = Scatter(parts, (pair2, sums2, by_far2, by_side2), scatter_sent.at[1], scatter_came.at[1])
    last.swap(3, 1, 2, 0)
    last.send_far()
    last.send_near()

    def collect(rows, columns):
        rows_grad[rows, columns] = product(columns_grad[:, rows], n1[:, columns], 0, 0).astype(BF)

    tile_loop(3 * wide, width, 256, collect, 512)
    rows_save = pltpu.make_async_copy(rows_grad, attn_part.at[pl.ds(0, 3 * wide)], save_sem.at[1])
    rows_save.start()
    last.send_rest()
    x = x_own[...].astype(F32)
    center = x - jnp.mean(x, axis=-1, keepdims=True)
    inverse = lax.rsqrt(jnp.mean(center * center, axis=-1, keepdims=True) + epsilon)
    inner = last.total()
    normed = center * inverse
    inner = (
        inner
        - jnp.mean(inner, axis=-1, keepdims=True)
        - normed * jnp.mean(inner * normed, axis=-1, keepdims=True)
    )
    input_grad[...] = grad_middle[...] + inverse * inner
    last.drain()
    for copy in swaps:
        copy.wait()
    own_swap.wait()
    rows_save.wait()
    own_next.wait()
    next_gather.finish()
    next_gather.drain()


def back(x_own, start, cosine, sine, hidden, down, grad, out_columns, attn_b, attn, query, key, value, n1,
         w_query, w_key, w_value, lined, middle, grad_middle):
    groups = lax.axis_size("shard")
    tokens, width = x_own.shape
    sequence = tokens * groups
    wide, columns = query.shape[1], hidden.shape[1]
    anywhere, vmem = pl.BlockSpec(memory_space=pl.ANY), pl.BlockSpec(memory_space=VMEM)
    dma = pltpu.SemaphoreType.DMA
    buffers = [
        pltpu.VMEM((4, tokens, width), BF),
        pltpu.VMEM((3, tokens, width), BF),
        pltpu.VMEM((2, tokens // 2, width), BF),
        pltpu.VMEM((2, tokens, width), BF),
    ]
    return pl.pallas_call(
        back_kernel,
        out_shape=(
            jax.ShapeDtypeStruct((tokens, width), BF),
            jax.ShapeDtypeStruct((tokens, width), F32),
            jax.ShapeDtypeStruct((4 * wide, width), BF),
            jax.ShapeDtypeStruct((sequence, width), BF),
        ),
        in_specs=[vmem] * 4 + [anywhere] * 14 + [vmem] * 2,
        out_specs=(vmem, vmem, anywhere, anywhere),
        scratch_shapes=[
            pltpu.VMEM((sequence, columns), BF),
            pltpu.VMEM((width, columns), BF),
            pltpu.VMEM((sequence, width), BF),
            pltpu.VMEM((width, wide), BF),
            pltpu.VMEM((sequence, wide), BF),
            pltpu.VMEM((sequence, wide), F32),
            pltpu.VMEM((sequence, wide), BF),
            pltpu.VMEM((sequence, wide), BF),
            pltpu.VMEM((sequence, wide), BF),
            pltpu.VMEM((sequence, width), BF),
            pltpu.VMEM((3 * wide, width), BF),
            pltpu.VMEM((sequence, wide), BF),
            pltpu.VMEM((sequence, wide), F32),
            pltpu.VMEM((sequence, wide), F32),
            pltpu.VMEM((sequence, 3 * wide), BF),
            pltpu.VMEM((width, wide), BF),
            pltpu.VMEM((3 * wide, width), BF),
            pltpu.VMEM((sequence, width), BF),
            *buffers,
            *buffers,
            dma((13,)),
            dma((3,)),
            dma((2, 10)),
            dma((2, 10)),
            dma((groups,)),
            dma((groups,)),
            dma((13,)),
            dma((13,)),
        ],
        compiler_params=pltpu.CompilerParams(
            collective_id=4, has_side_effects=True, vmem_limit_bytes=67043328
        ),
        cost_estimate=pl.CostEstimate(
            flops=24 * sequence * width * wide, bytes_accessed=48 * 1024 * 1024, transcendentals=0
        ),
        name="back",
    )(x_own, start, cosine, sine, hidden, down, grad, out_columns, attn_b, attn, query, key, value, n1,
      w_query, w_key, w_value, lined, middle, grad_middle)


def every_kernel(
    lined, own_normed, own_dy, dy_one, dy_two, own_hidden, own_grad_gate, own_grad_up, attn_part,
    w_gate, w_up, w_down,
    out_gate, out_up, out_down, out_attn, landed, kept,
    normed, dy, hidden, grad_gate, grad_up, gate_w, up_w, down_w, down, first_sum, second_sum, stage,
    load_sem, keep_sem, gather_sent, gather_came, line_sent, line_came, line_own, swap_sent, swap_came,
):
    replica = lax.axis_index("replica")
    replicas = lax.axis_size("replica")
    me = lax.axis_index("shard")
    groups = lax.axis_size("shard")
    tokens = lined.shape[1] // 2
    sequence, width = normed.shape
    columns = hidden.shape[1]
    own_rows = block_rows(me, tokens)
    inner = (replica == 1) | (replica == 2)
    outer = (replica == 0) | (replica == 3)
    beside = replica + 1 - 2 * lax.rem(replica, 2)
    facing = 3 - replica
    chunks, depth = first_sum.shape[0], first_sum.shape[1]

    def piece(c):
        return pl.ds(c * depth, depth)

    def line_move(kind, c, src, dst, target):
        return pltpu.make_async_remote_copy(
            src_ref=src,
            dst_ref=dst,
            send_sem=line_sent.at[kind, c],
            recv_sem=line_came.at[kind, c],
            device_id=(target, me),
            device_id_type=MESH,
        )

    def inward(c):
        return line_move(0, c, attn_part.at[piece(c)], first_sum.at[c], beside)

    def middle(c):
        return line_move(1, c, first_sum.at[c], second_sum.at[c], facing)

    def outward(c):
        return line_move(2, c, second_sum.at[c], out_attn.at[piece(c)], beside)

    def keep(c):
        return pltpu.make_async_copy(second_sum.at[c], out_attn.at[piece(c)], line_own.at[c])

    def stage_load(c):
        return pltpu.make_async_copy(attn_part.at[piece(c)], stage, keep_sem.at[2, 0])

    def half_sums(*which):
        @pl.when(inner)
        def _():
            for c in which:
                stage_load(c).wait()
                inward(c).wait_recv()
                first_sum[c] = (stage[...].astype(F32) + first_sum[c].astype(F32)).astype(BF)
                middle(c).start()
                if c + 1 < chunks:
                    stage_load(c + 1).start()

    def full_sums(*which):
        @pl.when(inner)
        def _():
            for c in which:
                middle(c).wait_recv()
                second_sum[c] = (first_sum[c].astype(F32) + second_sum[c].astype(F32)).astype(BF)
                outward(c).start()
                keep(c).start()

    def other(n):
        return lined.at[lax.rem(replica + n, replicas)]

    gathers = [
        Gather(other(n).at[pl.ds(0, tokens)], landed.at[n - 1], gather_sent.at[n - 1], gather_came.at[n - 1])
        for n in range(1, 4)
    ]
    gathers.append(
        Gather(other(3).at[pl.ds(tokens, tokens)], landed.at[3], gather_sent.at[3], gather_came.at[3])
    )

    def normed_loads(n, target, base):
        copies = []
        for i in range(groups):
            device = lax.rem(me + i, groups)
            rows = block_rows(device, tokens)
            source = other(n).at[pl.ds(0, tokens)] if i == 0 else landed.at[n - 1, rows]
            copies.append(pltpu.make_async_copy(source, target.at[rows], load_sem.at[base, i]))
        return copies

    def dy_loads(n):
        if n < 3:
            return [pltpu.make_async_copy(dy_one if n == 1 else dy_two, dy, load_sem.at[1, 0])]
        copies = []
        for i in range(groups):
            device = lax.rem(me + i, groups)
            rows = block_rows(device, tokens)
            source = other(n).at[pl.ds(tokens, tokens)] if i == 0 else landed.at[3, rows]
            copies.append(pltpu.make_async_copy(source, dy.at[rows], load_sem.at[1, i]))
        return copies

    def keeps(n):
        return [
            pltpu.make_async_copy(grad_gate, kept.at[n - 1, 0], keep_sem.at[0, n]),
            pltpu.make_async_copy(grad_up, kept.at[n - 1, 1], keep_sem.at[1, n]),
        ]

    def start_all(copies):
        for copy in copies:
            copy.start()

    def wait_all(copies):
        for copy in copies:
            copy.wait()

    first = [
        pltpu.make_async_copy(own_normed, normed, load_sem.at[0, 0]),
        pltpu.make_async_copy(own_grad_gate, grad_gate, load_sem.at[0, 1]),
        pltpu.make_async_copy(own_grad_up, grad_up, load_sem.at[0, 2]),
        pltpu.make_async_copy(own_hidden, hidden, load_sem.at[1, 1]),
        pltpu.make_async_copy(own_dy, dy, load_sem.at[1, 0]),
    ]
    weights = [
        pltpu.make_async_copy(w_gate, gate_w, load_sem.at[2, 0]),
        pltpu.make_async_copy(w_up, up_w, load_sem.at[2, 1]),
        pltpu.make_async_copy(w_down, down_w, load_sem.at[2, 2]),
    ]
    start_all(first + weights)
    barrier = pltpu.get_barrier_semaphore()
    for i in range(1, groups):
        device = lax.rem(me + i, groups)
        pl.semaphore_signal(barrier, inc=1, device_id=(replica, device), device_id_type=MESH)
    pl.semaphore_signal(barrier, inc=1, device_id=(beside, me), device_id_type=MESH)

    @pl.when(inner)
    def _():
        pl.semaphore_signal(barrier, inc=1, device_id=(facing, me), device_id_type=MESH)
        pl.semaphore_wait(barrier, groups + 1)

    @pl.when(outer)
    def _():
        pl.semaphore_wait(barrier, groups)

    gathers[0].one()

    @pl.when(outer)
    def _():
        start_all([inward(c) for c in range(chunks)])

    @pl.when(inner)
    def _():
        stage_load(0).start()

    def collect(out, left, right, add):
        def step(rows, cols):
            value = product(left[:, rows], right[:, cols], 0, 0)
            if add is None:
                out[rows, cols] = value
            elif add is True:
                out[rows, cols] += value

        tile_loop(out.shape[0], out.shape[1], 512, step)

    wait_all(first[:3])
    collect(out_gate, grad_gate, normed, None)
    gathers[0].two()
    collect(out_up, grad_up, normed, None)
    gathers[0].three()
    gathers[1].one()
    gathers[0].four()
    gathers[0].finish()
    start_all(normed_loads(1, normed, 0))
    wait_all(first[3:])
    collect(down, dy, hidden, None)
    start_all(dy_loads(1))
    half_sums(0)
    wait_all(weights)
    wait_all(normed_loads(1, normed, 0))
    wait_all(dy_loads(1))

    near, further, last_normed, last_dy = gathers
    agenda = {
        (1, 1): (further.two,),
        (1, 3): (further.three, last_dy.one, lambda: half_sums(1)),
        (1, 5): (further.four,),
        (1, 7): (further.finish, lambda: full_sums(0)),
        (2, 0): (last_dy.two,),
        (2, 2): (last_dy.three, last_normed.one),
        (2, 3): (lambda: half_sums(3),),
        (2, 4): (last_dy.four,),
        (2, 6): (last_normed.two, lambda: full_sums(2)),
        (2, 7): (last_dy.finish,),
        (3, 1): (lambda: half_sums(5),),
        (3, 5): (lambda: full_sums(4),),
        (3, 7): (lambda: half_sums(6),),
    }

    def after_down(n):
        if n == 1:
            half_sums(2)
            full_sums(1)
        else:
            last_normed.three()
            half_sums(4)
            full_sums(3)
            last_normed.four()
            last_normed.finish()
            start_all(normed_loads(3, normed, 0))
        start_all(dy_loads(n + 1))
        wait_all(keeps(n))
        wait_all(normed_loads(n + 1, normed, 0))
        wait_all(dy_loads(n + 1))

    def sequence_step(n, carry):
        narrow = 256
        across = columns // narrow

        def one_tile(i, carry):
            ffn_tile(
                normed, dy, gate_w, up_w, down_w, hidden, grad_gate, grad_up,
                pl.ds(pl.multiple_of((i // across) * 512, 512), 512),
                pl.ds(pl.multiple_of(lax.rem(i, across) * narrow, narrow), narrow),
            )
            for (when, tile), actions in agenda.items():

                @pl.when((n == when) & (i == tile))
                def _(actions=actions):
                    for action in actions:
                        action()

            return carry

        lax.fori_loop(0, (sequence // 512) * across, one_tile, 0)
        for k in (1, 2):

            @pl.when(n == k)
            def _(k=k):
                start_all(keeps(k))
                if k == 1:
                    start_all(normed_loads(2, normed, 0))

        @pl.when(n < 3)
        def _():
            collect(down, dy, hidden, True)

        for k in (1, 2):

            @pl.when(n == k)
            def _(k=k):
                after_down(k)

        return carry

    lax.fori_loop(1, 4, sequence_step, 0)

    wide = width // groups
    core = lax.rem(me, 2)
    _, mate, across_device, along_device, far_device = whereabouts()

    def down_move(send_index, recv_index, row, sender, device):
        return pltpu.make_async_remote_copy(
            src_ref=down_w.at[pl.ds(pl.multiple_of(row, wide), wide)],
            dst_ref=out_down.at[:, pl.ds(pl.multiple_of(sender * columns, columns), columns)],
            send_sem=swap_sent.at[send_index],
            recv_sem=swap_came.at[recv_index],
            device_id=(replica, device),
            device_id_type=MESH,
        )

    swaps, arrivals = [], []
    for i, device in enumerate((far_device, across_device, along_device, me)):
        chip = device // 2
        rows = pl.ds(pl.multiple_of(chip * 2 * wide, 2 * wide), 2 * wide)

        def finish_down(j, carry, rows=rows):
            cols = pl.ds(pl.multiple_of(j * 512, 512), 512)
            down[rows, cols] += product(dy[:, rows], hidden[:, cols], 0, 0)
            return carry

        lax.fori_loop(0, columns // 512, finish_down, 0)
        down_w[i * 2 * wide : (i + 1) * 2 * wide, :] = down[rows, :].astype(BF)
        for k in range(2):
            if i < 3:
                row, peer = (2 * i + k) * wide, chip * 2 + k
                swaps.append(down_move(2 * i + k, 2 * i + core, row, me, peer))
                swaps[-1].start()
                arrivals.append(down_move(2 * i + k, 2 * i + k, row, peer, peer))
    swaps.append(down_move(6, 6, (6 + lax.rem(mate, 2)) * wide, me, mate))
    swaps[-1].start()
    arrivals.append(down_move(6, 6, 6 * wide, mate, mate))
    own_slab = pltpu.make_async_copy(
        down_w.at[pl.ds(pl.multiple_of((6 + core) * wide, wide), wide)],
        out_down.at[:, pl.ds(pl.multiple_of(me * columns, columns), columns)],
        keep_sem.at[2, 1],
    )
    own_slab.start()
    half_sums(7)
    full_sums(5)
    one_gate, one_up = up_w.at[:, pl.ds(0, columns)], up_w.at[:, pl.ds(columns, columns)]
    one_loads = normed_loads(1, gate_w, 2) + [
        pltpu.make_async_copy(kept.at[0, 0], one_gate, keep_sem.at[0, 0]),
        pltpu.make_async_copy(kept.at[0, 1], one_up, keep_sem.at[1, 0]),
    ]
    two_loads = normed_loads(2, dy, 0)
    two_gate = pltpu.make_async_copy(kept.at[1, 0], grad_gate, keep_sem.at[0, 3])
    two_up = pltpu.make_async_copy(kept.at[1, 1], grad_up, keep_sem.at[1, 3])
    start_all(one_loads + two_loads)
    collect(out_gate, grad_gate, normed, True)
    two_gate.start()
    full_sums(6)
    collect(out_up, grad_up, normed, True)
    two_up.start()
    wait_all(one_loads)
    collect(out_gate, one_gate, gate_w, True)
    full_sums(7)
    collect(out_up, one_up, gate_w, True)
    wait_all(two_loads)
    two_gate.wait()
    two_up.wait()
    collect(out_gate, grad_gate, dy, True)
    collect(out_up, grad_up, dy, True)

    @pl.when(outer)
    def _():
        for c in range(chunks):
            inward(c).wait_send()
            outward(c).wait_recv()

    @pl.when(inner)
    def _():
        for c in range(chunks):
            middle(c).wait_send()
            outward(c).wait_send()
            keep(c).wait()

    for copy in swaps:
        copy.wait_send()
    for copy in arrivals:
        copy.wait_recv()
    own_slab.wait()
    for gather in gathers:
        gather.drain()


def ffn_grads(lined, n2, dy_all, dy_one, dy_two, own, attn_part, w_gate, w_up, w_down_columns):
    replicas, tokens, width = lined.shape
    tokens = tokens // 2
    sequence = n2.shape[0]
    groups = sequence // tokens
    columns = w_gate.shape[0]
    chunks = 8
    depth = attn_part.shape[0] // chunks
    anywhere, vmem = pl.BlockSpec(memory_space=pl.ANY), pl.BlockSpec(memory_space=VMEM)
    dma = pltpu.SemaphoreType.DMA
    out = pl.pallas_call(
        every_kernel,
        out_shape=(
            jax.ShapeDtypeStruct((columns, width), F32),
            jax.ShapeDtypeStruct((columns, width), F32),
            jax.ShapeDtypeStruct((width // groups, columns * groups), BF),
            jax.ShapeDtypeStruct(attn_part.shape, BF),
            jax.ShapeDtypeStruct((replicas, sequence, width), BF),
            jax.ShapeDtypeStruct((2, 2, sequence, columns), BF),
        ),
        in_specs=[anywhere] * 12,
        out_specs=(vmem, vmem, anywhere, anywhere, anywhere, anywhere),
        scratch_shapes=[
            pltpu.VMEM((sequence, width), BF),
            pltpu.VMEM((sequence, width), BF),
            pltpu.VMEM((sequence, columns), BF),
            pltpu.VMEM((sequence, columns), BF),
            pltpu.VMEM((sequence, columns), BF),
            pltpu.VMEM((columns, width), BF),
            pltpu.VMEM((columns, width), BF),
            pltpu.VMEM((width, columns), BF),
            pltpu.VMEM((width, columns), F32),
            pltpu.VMEM((chunks, depth, width), BF),
            pltpu.VMEM((chunks, depth, width), BF),
            pltpu.VMEM((depth, width), BF),
            dma((3, groups)),
            dma((3, 4)),
            dma((4, 13)),
            dma((4, 13)),
            dma((3, chunks)),
            dma((3, chunks)),
            dma((chunks,)),
            dma((groups,)),
            dma((groups,)),
        ],
        compiler_params=pltpu.CompilerParams(
            collective_id=2, has_side_effects=True, vmem_limit_bytes=67043328
        ),
        cost_estimate=pl.CostEstimate(
            flops=42 * sequence * width * columns, bytes_accessed=80 * 1024 * 1024, transcendentals=0
        ),
        name="ffn_grads",
    )(lined, n2, dy_all, dy_one, dy_two, *own, attn_part, w_gate, w_up, w_down_columns)
    return out[:4]


def gather_tokens(values):
    return lax.all_gather(values, "shard", axis=0, tiled=True)


def scatter_tokens(partial):
    return lax.psum_scatter(
        partial.astype(BF), "shard", scatter_dimension=0, tiled=True
    ).astype(F32)


def rows_to_columns(weight):
    return lax.all_to_all(weight, "shard", split_axis=1, concat_axis=0, tiled=True)


def columns_to_rows(grad):
    return lax.all_to_all(grad, "shard", split_axis=0, concat_axis=1, tiled=True)


def replica_sum(part):
    return lax.psum(part.astype(BF), "replica")


def general_body(hidden_in, cotangent, doc_lengths, w_query, w_key, w_value, w_out, w_gate, w_up, w_down):
    x = hidden_in[0].astype(F32)
    dyb = cotangent[0]
    tokens_here = x.shape[0]
    groups = lax.axis_size("shard")
    seq_length = tokens_here * groups
    factor = 1.0 / math.sqrt(HEAD_DIM)
    places = jnp.arange(seq_length, dtype=jnp.int32)
    segment, offset = doc_layout(doc_lengths[0], places)
    cosine, sine = rope_tables(offset, HEAD_DIM)
    allowed = ((segment[:, None] == segment[None, :]) & (places[None, :] <= places[:, None]))[None]

    normed_one, inverse_one = normalize(x)
    n1 = gather_tokens(normed_one.astype(BF))
    w_out_columns = rows_to_columns(w_out)
    query = rotate(split_heads(dot(n1, w_query, 1, 1)), cosine, sine).astype(BF)
    keys = rotate(split_heads(dot(n1, w_key, 1, 1)), cosine, sine).astype(BF)
    values = split_heads(dot(n1, w_value, 1, 1)).astype(BF)
    scores = factor * jnp.einsum("hqe,hke->hqk", query, keys, preferred_element_type=F32)
    scores = jnp.where(allowed, scores, masked)
    top = jnp.max(scores, axis=-1, keepdims=True)
    weights = jnp.where(allowed, jnp.exp(scores - top), 0.0)
    total = jnp.sum(weights, axis=-1, keepdims=True)
    log_total = top + jnp.log(total)
    attn = jnp.einsum("hqk,hke->hqe", weights.astype(BF), values, preferred_element_type=F32) / total
    out_b = join_heads(attn).astype(BF)
    middle = x + scatter_tokens(dot(out_b, w_out_columns, 1, 1))

    normed_two, inverse_two = normalize(middle)
    n2 = gather_tokens(normed_two.astype(BF))
    dy_all = gather_tokens(dyb)
    w_down_columns = rows_to_columns(w_down)
    gate = dot(n2, w_gate, 1, 1)
    up = dot(n2, w_up, 1, 1)
    sigma = jax.nn.sigmoid(gate)
    silu = gate * sigma
    hidden = (silu * up).astype(BF)
    grad_down = columns_to_rows(replica_sum(dot(dy_all, hidden, 0, 0)))
    grad_hidden = dot(dy_all, w_down_columns, 1, 0)
    grad_gate_b = (grad_hidden * up * sigma * (1.0 + gate * (1.0 - sigma))).astype(BF)
    grad_up_b = (grad_hidden * silu).astype(BF)
    grad_gate = replica_sum(dot(grad_gate_b, n2, 0, 0).astype(BF))
    grad_up = replica_sum(dot(grad_up_b, n2, 0, 0).astype(BF))
    grad_normed_two = scatter_tokens(dot(grad_gate_b, w_gate, 1, 0) + dot(grad_up_b, w_up, 1, 0))
    mixed = scatter_tokens(dot(hidden, w_down_columns, 1, 1))
    layer_out = (middle + mixed).astype(BF)
    grad_middle = dyb.astype(F32) + norm_back(normed_two, inverse_two, grad_normed_two)

    grad_middle_all = gather_tokens(grad_middle.astype(BF))
    grad_out = columns_to_rows(replica_sum(dot(grad_middle_all, out_b, 0, 0).astype(BF)))
    grad_attn = split_heads(dot(grad_middle_all, w_out_columns, 1, 0)).astype(BF)
    delta = jnp.sum(grad_attn.astype(F32) * attn, axis=-1, keepdims=True)
    probs = jnp.where(allowed, jnp.exp(scores - log_total), 0.0)
    grad_probs = jnp.einsum("hqe,hke->hqk", grad_attn, values, preferred_element_type=F32)
    grad_scores = (probs * (grad_probs - delta)).astype(BF)
    query_grad = factor * jnp.einsum("hqk,hke->hqe", grad_scores, keys, preferred_element_type=F32)
    key_grad = factor * jnp.einsum("hqk,hqe->hke", grad_scores, query, preferred_element_type=F32)
    value_grad = jnp.einsum("hqk,hqe->hke", probs.astype(BF), grad_attn, preferred_element_type=F32)
    query_grad = join_heads(rotate(query_grad, cosine, -sine)).astype(BF)
    key_grad = join_heads(rotate(key_grad, cosine, -sine)).astype(BF)
    value_grad = join_heads(value_grad).astype(BF)
    grad_query = replica_sum(dot(query_grad, n1, 0, 0).astype(BF))
    grad_key = replica_sum(dot(key_grad, n1, 0, 0).astype(BF))
    grad_value = replica_sum(dot(value_grad, n1, 0, 0).astype(BF))
    grad_normed_one = scatter_tokens(
        dot(query_grad, w_query, 1, 0) + dot(key_grad, w_key, 1, 0) + dot(value_grad, w_value, 1, 0)
    )
    grad_in = grad_middle + norm_back(normed_one, inverse_one, grad_normed_one)
    return (
        layer_out[None],
        grad_in[None],
        grad_query.astype(F32),
        grad_key.astype(F32),
        grad_value.astype(F32),
        grad_out.astype(F32),
        grad_gate.astype(F32),
        grad_up.astype(F32),
        grad_down.astype(F32),
    )


def body(hidden_in, cotangent, doc_lengths, w_query, w_key, w_value, w_out, w_gate, w_up, w_down):
    x_own, dy_own = hidden_in[0], cotangent[0]
    half = HEAD_DIM // 2
    frequency = theta_base ** (-2.0 * (np.arange(HEAD_DIM) % half) / HEAD_DIM)
    (
        n1, query, key, value, attn, attn_b, out_columns, _, down_columns,
        hidden, grad_gate_b, grad_up_b, middle, n2, dy, lined, grad_middle, grad_all, dy_one,
        cosine, sine, start,
    ) = front(
        doc_lengths, jnp.asarray(frequency[None], F32), x_own, dy_own,
        w_query, w_key, w_value, w_out, w_gate, w_up, w_down,
    )
    layer_out, grad_in, attn_part, dy_two = back(
        x_own, start, cosine, sine, hidden, down_columns, grad_all, out_columns, attn_b, attn,
        query, key, value, n1, w_query, w_key, w_value, lined, middle, grad_middle,
    )
    grad_gate, grad_up, grad_down, attn_sum = ffn_grads(
        lined, n2, dy, dy_one, dy_two, (hidden, grad_gate_b, grad_up_b), attn_part, w_gate, w_up, down_columns
    )
    grad_query, grad_key, grad_value, grad_out = jnp.split(attn_sum.astype(F32), 4, axis=0)
    return (
        layer_out[None],
        grad_in[None],
        grad_query,
        grad_key,
        grad_value,
        grad_out,
        grad_gate,
        grad_up,
        grad_down.astype(F32),
    )


def solution(mesh):
    rows = P("shard", None)
    tokens = P("replica", "shard", None)
    in_specs = (tokens, tokens, P("replica", None)) + (rows,) * 7
    out_specs = (tokens, tokens) + (rows,) * 7
    local = body if mesh.shape["shard"] == 8 and mesh.shape["replica"] == 4 else general_body
    return jax.shard_map(local, mesh=mesh, in_specs=in_specs, out_specs=out_specs, check_vma=False)
```

```python
import functools
import math

import jax
import jax.numpy as jnp
import numpy as np
from jax import lax
from jax.experimental import pallas as pl
from jax.experimental.pallas import tpu as pltpu
from jax.sharding import PartitionSpec as P

HEAD_DIM = 128

epsilon = 1e-05
theta_base = 10000.0
masked = -1e30
BF = jnp.bfloat16
F32 = jnp.float32
MESH = pl.DeviceIdType.MESH
VMEM = pltpu.VMEM


def normalize(values):
    center = values - jnp.mean(values, axis=-1, keepdims=True)
    inverse = lax.rsqrt(jnp.mean(center * center, axis=-1, keepdims=True) + epsilon)
    return (center * inverse, inverse)


def norm_back(normed, inverse, grad):
    inner = (
        grad
        - jnp.mean(grad, axis=-1, keepdims=True)
        - normed * jnp.mean(grad * normed, axis=-1, keepdims=True)
    )
    return inverse * inner


def dot(a, b, ca, cb):
    return lax.dot_general(a, b, (((ca,), (cb,)), ((), ())), preferred_element_type=F32)


def doc_layout(lengths, places):
    ends = jnp.cumsum(lengths)
    starts = ends - lengths
    segment = jnp.sum((places[:, None] >= ends[None, :]).astype(jnp.int32), axis=1)
    member = segment[:, None] == jnp.arange(lengths.shape[0], dtype=jnp.int32)[None, :]
    offset = places - jnp.sum(jnp.where(member, starts[None, :], 0), axis=1)
    return (segment, offset)


def rope_tables(offset, head_dim):
    half = head_dim // 2
    freq = theta_base ** (-2.0 * jnp.arange(half, dtype=F32) / head_dim)
    angle = offset.astype(F32)[:, None] * freq[None, :]
    return (jnp.cos(angle)[None], jnp.sin(angle)[None])


def rotate(values, cosine, sine):
    half = values.shape[-1] // 2
    first = values[..., :half]
    second = values[..., half:]
    return jnp.concatenate(
        [first * cosine - second * sine, second * cosine + first * sine], axis=-1
    )


def split_heads(values):
    tokens, width = values.shape
    return jnp.transpose(values.reshape(tokens, width // HEAD_DIM, HEAD_DIM), (1, 0, 2))


def join_heads(values):
    heads, tokens, size = values.shape
    return jnp.transpose(values, (1, 0, 2)).reshape(tokens, heads * size)


def whereabouts():
    place = lax.axis_index("shard")
    core, col, row = lax.rem(place, 2), lax.rem(place // 2, 2), place // 4
    across, along = place + 2 - 4 * col, place + 4 - 8 * row
    return place, place + 1 - 2 * core, across, along, across + 4 - 8 * row


def whereabouts_of_mate():
    me, mate, across, along, far = whereabouts()
    shift = mate - me
    return across + shift, along + shift, far + shift


def tile_loop(rows, columns, size, step, narrow=None):
    narrow = narrow or size
    across = columns // narrow

    def one(i, carry):
        step(
            pl.ds(pl.multiple_of((i // across) * size, size), size),
            pl.ds(pl.multiple_of(lax.rem(i, across) * narrow, narrow), narrow),
        )
        return carry

    lax.fori_loop(0, (rows // size) * across, one, 0)


def product(a, b, ca, cb):
    return lax.dot_general(a, b, (((ca,), (cb,)), ((), ())), preferred_element_type=F32)


def ffn_tile(normed, dy, w_gate, w_up, w_down, hidden, grad_gate, grad_up, rows, columns):
    gate = product(normed[rows, :], w_gate[columns, :], 1, 1)
    up = product(normed[rows, :], w_up[columns, :], 1, 1)
    grad = product(dy[rows, :], w_down[:, columns], 1, 0)
    sigma = 0.5 + 0.5 * jnp.tanh(0.5 * gate)
    silu = gate * sigma
    hidden[rows, columns] = (silu * up).astype(BF)
    grad_gate[rows, columns] = (grad * (up * (sigma + silu * (1.0 - sigma)))).astype(BF)
    grad_up[rows, columns] = (grad * silu).astype(BF)


def block_rows(slot, tokens, part=0):
    size = tokens // 2
    if part:
        return pl.ds(pl.multiple_of(slot * tokens + (part - 1) * size, size), size)
    return pl.ds(pl.multiple_of(slot * tokens, tokens), tokens)


class Gather:
    def __init__(self, block, out, sent, came):
        self.block, self.out, self.sent, self.came = block, out, sent, came
        self.tokens = block.shape[0]
        self.replica = lax.axis_index("replica")
        self.me, self.mate, self.across, self.along, self.far = whereabouts()
        self.sends = []

    def move(self, k, slot, part, device, first=False):
        tokens = self.tokens
        local = pl.ds((part - 1) * (tokens // 2) if part else 0, tokens // 2 if part else tokens)
        rows = block_rows(slot, tokens, part)
        return pltpu.make_async_remote_copy(
            src_ref=self.block.at[local] if first else self.out.at[rows],
            dst_ref=self.out.at[rows],
            send_sem=self.sent.at[k],
            recv_sem=self.came.at[k],
            device_id=(self.replica, device),
            device_id_type=MESH,
        )

    def start(self, *moves):
        for one in moves:
            self.move(*one).start()
            self.sends.append(one)

    def came_in(self, *moves):
        for k, slot, part in moves:
            self.move(k, slot, part, self.mate).wait_recv()

    def one(self):
        me = self.me
        self.start(
            (1, me, 1, self.across, True),
            (3, me, 2, self.along, True),
            (0, me, 0, self.mate, True),
            (2, me, 2, self.across, True),
            (4, me, 1, self.along, True),
        )

    def two(self):
        self.came_in((1, self.across, 1))
        self.start((5, self.across, 1, self.along), (6, self.across, 1, self.mate))
        self.came_in((3, self.along, 2))
        self.start((7, self.along, 2, self.across), (8, self.along, 2, self.mate))

    def three(self):
        self.came_in((2, self.across, 2))
        self.start((9, self.across, 2, self.mate))
        self.came_in((4, self.along, 1))
        self.start((10, self.along, 1, self.mate))

    def four(self):
        self.came_in((5, self.far, 1))
        self.start((11, self.far, 1, self.mate))
        self.came_in((7, self.far, 2))
        self.start((12, self.far, 2, self.mate))

    def finish(self):
        across, along, far = whereabouts_of_mate()
        self.came_in(
            (0, self.mate, 0), (6, across, 1), (8, along, 2), (9, across, 2), (10, along, 1),
            (11, far, 1), (12, far, 2),
        )

    def drain(self):
        for one in self.sends:
            self.move(*one).wait_send()


class Scatter:
    def __init__(self, parts, buffers, sent, came):
        self.parts = parts
        self.pair, self.sums, self.by_far, self.by_side = buffers
        self.sent, self.came = sent, came
        self.tokens = self.pair.shape[1]
        self.replica = lax.axis_index("replica")
        me, mate, across, along, far = whereabouts()
        self.mine, self.shift, self.mate = (me, across, along, far), mate - me, mate
        low, high = pl.ds(0, self.tokens // 2), pl.ds(self.tokens // 2, self.tokens // 2)
        self.low, self.high = low, high
        sums, by_far, by_side = self.sums, self.by_far, self.by_side
        self.swaps = [
            self.move(k, parts.at[block_rows(self.mine[k] + self.shift, self.tokens)], self.pair.at[k], mate)
            for k in range(4)
        ]
        self.far_low = self.move(4, sums.at[2, low], by_far.at[0], across)
        self.far_high = self.move(5, sums.at[2, high], by_far.at[1], along)
        self.across_low = self.move(6, sums.at[0, low], by_side.at[0, low], across)
        self.along_high = self.move(7, sums.at[1, high], by_side.at[1, high], along)
        self.along_low = self.move(8, sums.at[1, low], by_side.at[1, low], along)
        self.across_high = self.move(9, sums.at[0, high], by_side.at[0, high], across)

    def move(self, k, src, dst, device):
        return pltpu.make_async_remote_copy(
            src_ref=src,
            dst_ref=dst,
            send_sem=self.sent.at[k],
            recv_sem=self.came.at[k],
            device_id=(self.replica, device),
            device_id_type=MESH,
        )

    def swap(self, *which):
        for k in which:
            self.swaps[k].start()

    def pair_sum(self, k):
        self.swaps[k].wait_recv()
        own = self.parts[block_rows(self.mine[k], self.tokens), :].astype(F32)
        self.sums[k - 1] = (own + self.pair[k].astype(F32)).astype(BF)

    def send_far(self):
        self.pair_sum(3)
        self.far_low.start()
        self.far_high.start()

    def send_near(self):
        self.pair_sum(1)
        self.across_low.start()
        self.pair_sum(2)
        self.along_high.start()

    def send_rest(self):
        low, high, sums = self.low, self.high, self.sums
        self.far_low.wait_recv()
        sums[1, low] = (sums[1, low].astype(F32) + self.by_far[0].astype(F32)).astype(BF)
        self.along_low.start()
        self.far_high.wait_recv()
        sums[0, high] = (sums[0, high].astype(F32) + self.by_far[1].astype(F32)).astype(BF)
        self.across_high.start()

    def total(self):
        self.swaps[0].wait_recv()
        own = self.parts[block_rows(self.mine[0], self.tokens), :].astype(F32)
        own = own + self.pair[0].astype(F32)
        for copy in (self.across_low, self.along_high, self.along_low, self.across_high):
            copy.wait_recv()
        return own + (self.by_side[0].astype(F32) + self.by_side[1].astype(F32))

    def drain(self):
        for copy in (
            *self.swaps, self.far_low, self.far_high, self.across_low, self.along_high,
            self.along_low, self.across_high,
        ):
            copy.wait_send()


class Line:
    def __init__(self, own, slots, sent, came):
        self.own, self.slots, self.sent, self.came = own, slots, sent, came
        self.replica, self.me = lax.axis_index("replica"), lax.axis_index("shard")
        self.replicas = lax.axis_size("replica")

    def move(self, way, i, slot, first):
        target = self.replica + (1 if way == 0 else -1)
        return pltpu.make_async_remote_copy(
            src_ref=self.own if first else self.slots(slot),
            dst_ref=self.slots(slot),
            send_sem=self.sent.at[way, i],
            recv_sem=self.came.at[way, i],
            device_id=(target, self.me),
            device_id_type=MESH,
        )

    def source(self, way, i):
        return self.replica - i if way == 0 else self.replica + i

    def has(self, way, i):
        return self.replica >= i if way == 0 else self.replica + i < self.replicas

    def can_send(self, way):
        return self.replica + 1 < self.replicas if way == 0 else self.replica >= 1

    def start(self):
        for way in (0, 1):

            @pl.when(self.can_send(way))
            def _(way=way):
                self.move(way, 0, self.replica, True).start()

    def step(self, i):
        for way in (0, 1):

            @pl.when(self.has(way, i))
            def _(way=way):
                self.move(way, i - 1, self.source(way, i), False).wait_recv()
                if i < self.replicas - 1:

                    @pl.when(self.can_send(way))
                    def _():
                        self.move(way, i, self.source(way, i), False).start()

    def drain(self):
        for way in (0, 1):
            for i in range(self.replicas - 1):

                @pl.when(self.has(way, i) & self.can_send(way))
                def _(way=way, i=i):
                    self.move(way, i, self.source(way, i), i == 0).wait_send()


def rotate_head(values, cosine, sine):
    return values * cosine + pltpu.roll(values, values.shape[-1] // 2, 1) * sine


def key_reach(first, step, sequence):
    low = max(0, (first + 1 - sequence // 2) // 128 * 128)
    return low, pl.ds(low, first + step - low)


def allowed_bias(start, first, step, low):
    shape = (step, first + step - low)
    key_place = lax.broadcasted_iota(jnp.int32, shape, 1) + low
    query_place = lax.broadcasted_iota(jnp.int32, shape, 0) + first
    return jnp.where((key_place <= query_place) & (key_place >= start), 0.0, masked)


def head_scores(query, keys, bias):
    return product(query, keys, 1, 1) * (1.0 / math.sqrt(HEAD_DIM)) + bias


def fill_tables(lengths, frequency, cosine, sine, start):
    shape = start.shape
    place = lax.broadcasted_iota(jnp.int32, shape, 0)
    begin = jnp.zeros(shape, jnp.int32)
    end = 0
    for i in range(lengths.shape[1] - 1):
        end = end + lengths[0, i]
        begin = jnp.where(place >= end, end, begin)
    start[...] = begin
    angle = (place - begin).astype(F32) * frequency[...]
    lane = lax.broadcasted_iota(jnp.int32, shape, 1)
    cosine[...] = jnp.cos(angle)
    sine[...] = jnp.where(lane < shape[1] // 2, -1.0, 1.0) * jnp.sin(angle)


def front_kernel(
    lengths, frequency, x_own, dy_own, w_query, w_key, w_value, w_out, w_gate, w_up, w_down,
    n1_out, query_out, key_out, value_out, attn_out, attn_b_out, out_columns_out, down_parts,
    down_columns_out, hidden_out, grad_gate_out, grad_up_out, middle_out, n2_out, dy_out, lined,
    grad_out, grad_all_out, next_out, cosine_out, sine_out, start_out,
    n1, n2, dy, query, key, value, attn, attn_b, out_columns, gate_w, up_w, down_w,
    hidden, grad_gate, grad_up, parts, pair, sums, by_far, by_side, middle, normed, n2_own, grad_own, n1_own, cosine, sine, start,
    load_sem, save_sem, gather_sent, gather_came, scatter_sent, scatter_came,
    swap_sent, swap_came, line_sent, line_came,
):
    replica = lax.axis_index("replica")
    replicas = lax.axis_size("replica")
    me = lax.axis_index("shard")
    groups = lax.axis_size("shard")
    tokens, width = x_own.shape
    sequence = n1.shape[0]
    saves = []

    def save(src, dst):
        copy = pltpu.make_async_copy(src, dst, save_sem.at[len(saves)])
        copy.start()
        saves.append(copy)

    def exchange(which, source, target):
        copies = []
        for i in range(1, groups):
            device = lax.rem(me + i, groups)
            copies.append(
                pltpu.make_async_remote_copy(
                    src_ref=source(device),
                    dst_ref=target,
                    send_sem=swap_sent.at[which, i],
                    recv_sem=swap_came.at[which, i],
                    device_id=(replica, device),
                    device_id_type=MESH,
                )
            )
        return copies

    gate_load = pltpu.make_async_copy(w_gate, gate_w, load_sem.at[0])
    up_load = pltpu.make_async_copy(w_up, up_w, load_sem.at[1])
    gate_load.start()
    up_load.start()
    own_rows = block_rows(me, tokens)
    x = x_own[...].astype(F32)
    center = x - jnp.mean(x, axis=-1, keepdims=True)
    inverse = lax.rsqrt(jnp.mean(center * center, axis=-1, keepdims=True) + epsilon)
    n1_own[...] = (center * inverse).astype(BF)
    own_n1 = pltpu.make_async_copy(n1_own, n1.at[own_rows], load_sem.at[2])
    own_dy = pltpu.make_async_copy(dy_own, dy.at[own_rows], load_sem.at[3])
    own_n1.start()
    own_dy.start()

    barrier = pltpu.get_barrier_semaphore()
    for i in range(1, groups):
        device = lax.rem(me + i, groups)
        pl.semaphore_signal(barrier, inc=1, device_id=(replica, device), device_id_type=MESH)

    @pl.when(replica >= 1)
    def _():
        pl.semaphore_signal(barrier, inc=1, device_id=(replica - 1, me), device_id_type=MESH)

    @pl.when(replica + 1 < replicas)
    def _():
        pl.semaphore_signal(barrier, inc=1, device_id=(replica + 1, me), device_id_type=MESH)

    edge = (replica == 0) | (replica == replicas - 1)

    @pl.when(edge)
    def _():
        pl.semaphore_wait(barrier, groups)

    @pl.when(jnp.logical_not(edge))
    def _():
        pl.semaphore_wait(barrier, groups + 1)

    n1_gather = Gather(n1_own, n1, gather_sent.at[0], gather_came.at[0])
    dy_gather = Gather(dy_own, dy, gather_sent.at[1], gather_came.at[1])
    n2_gather = Gather(n2_own, n2, gather_sent.at[2], gather_came.at[2])
    grad_gather = Gather(grad_own, grad_all_out, gather_sent.at[3], gather_came.at[3])
    dy_line = Line(
        dy_own, lambda s: lined.at[s, pl.ds(tokens, tokens)], line_sent.at[0], line_came.at[0]
    )
    n2_line = Line(
        n2_own, lambda s: lined.at[s, pl.ds(0, tokens)], line_sent.at[1], line_came.at[1]
    )
    down_line = Line(
        down_parts.at[replica], lambda s: down_parts.at[s], line_sent.at[2], line_came.at[2]
    )
    buffers = (pair, sums, by_far, by_side)

    n1_gather.one()
    dy_line.start()
    fill_tables(lengths, frequency, cosine, sine, start)
    save(cosine, cosine_out)
    save(sine, sine_out)
    save(start, start_out)
    n1_gather.two()
    n1_gather.three()
    wide = w_out.shape[0]
    mine = pl.ds(pl.multiple_of(me * wide, wide), wide)
    part = down_parts.shape[2]

    def down_block(device):
        column = (device * replicas + replica) * part
        return w_down.at[:, pl.ds(pl.multiple_of(column, part), part)]

    def out_block(device):
        return w_out.at[:, pl.ds(pl.multiple_of(device * wide, wide), wide)]

    down_swaps = exchange(1, down_block, down_parts.at[replica, mine])
    out_swaps = exchange(0, out_block, out_columns.at[mine])
    own_down = pltpu.make_async_copy(down_block(me), down_parts.at[replica, mine], load_sem.at[5])
    own_down.start()
    own_out = pltpu.make_async_copy(out_block(me), out_columns.at[mine], load_sem.at[4])
    own_out.start()
    for copy in down_swaps + out_swaps:
        copy.start()
    n1_gather.four()
    own_n1.wait()
    n1_gather.finish()
    save(n1, n1_out)

    heads = query.shape[1] // HEAD_DIM
    for first in range(0, sequence, 512):
        rows = pl.ds(first, 512)
        for weight, target in ((w_query, query), (w_key, key), (w_value, value)):
            values = product(n1[rows, :], weight[...], 1, 1)
            for head in range(heads):
                lanes = pl.ds(head * HEAD_DIM, HEAD_DIM)
                piece = values[:, head * HEAD_DIM : (head + 1) * HEAD_DIM]
                if target is not value:
                    piece = rotate_head(piece, cosine[rows, :], sine[rows, :])
                target[rows, lanes] = piece.astype(BF)
    save(query, query_out)
    save(key, key_out)
    save(value, value_out)
    dy_line.step(1)
    own_down.wait()
    for copy in down_swaps:
        copy.wait_recv()
    down_line.start()
    step = 256
    for first in range(0, sequence, step):
        rows = pl.ds(first, step)
        low, reach = key_reach(first, step, sequence)
        bias = allowed_bias(start[rows, 0:1], first, step, low)
        for head in range(heads):
            lanes = pl.ds(head * HEAD_DIM, HEAD_DIM)
            scores = head_scores(query[rows, lanes], key[reach, lanes], bias)
            weights = jnp.exp(scores - jnp.max(scores, axis=-1, keepdims=True))
            total = jnp.sum(weights, axis=-1, keepdims=True)
            result = product(weights.astype(BF), value[reach, lanes], 1, 0) / total
            attn[rows, lanes] = result
            attn_b[rows, lanes] = result.astype(BF)
    save(attn, attn_out)
    save(attn_b, attn_b_out)
    dy_line.step(2)

    own_out.wait()
    for copy in out_swaps:
        copy.wait_recv()
    save(out_columns, out_columns_out)

    def spread(rows, columns):
        parts[rows, columns] = product(attn_b[rows, :], out_columns[columns, :], 1, 1).astype(BF)

    tile_loop(sequence, width, 512, spread)
    scatter = Scatter(parts, buffers, scatter_sent.at[0], scatter_came.at[0])
    scatter.swap(3, 1, 2, 0)
    scatter.send_far()
    scatter.send_near()
    dy_line.step(3)
    scatter.send_rest()
    middle[...] = x_own[...].astype(F32) + scatter.total()
    scatter.drain()
    save(middle, middle_out)
    center = middle[...] - jnp.mean(middle[...], axis=-1, keepdims=True)
    inverse = lax.rsqrt(jnp.mean(center * center, axis=-1, keepdims=True) + epsilon)
    normed[...] = center * inverse
    n2_own[...] = normed[...].astype(BF)
    n2_gather.one()
    own_n2 = pltpu.make_async_copy(n2_own, n2.at[own_rows], load_sem.at[6])
    own_n2.start()
    down_line.step(1)
    n2_gather.two()
    n2_gather.three()
    dy_gather.one()
    n2_gather.four()
    own_n2.wait()
    n2_gather.finish()
    save(n2, n2_out)
    gate_load.wait()
    up_load.wait()
    half = sequence // 2
    row = me // (groups // 2)

    def feed_forward(base):
        def forward(rows, columns):
            rows = pl.ds(pl.multiple_of(base, half), half)
            gate = product(n2[rows, :], gate_w[columns, :], 1, 1)
            up = product(n2[rows, :], up_w[columns, :], 1, 1)
            sigma = 0.5 + 0.5 * jnp.tanh(0.5 * gate)
            silu = gate * sigma
            hidden[rows, columns] = (silu * up).astype(BF)
            grad_gate[rows, columns] = (up * (sigma + silu * (1.0 - sigma))).astype(BF)
            grad_up[rows, columns] = silu.astype(BF)

        tile_loop(half, gate_w.shape[0], half, forward, 256)

    feed_forward((1 - row) * half)
    dy_gather.two()
    down_line.step(2)
    dy_gather.three()
    feed_forward(row * half)
    dy_gather.four()
    own_dy.wait()
    dy_gather.finish()
    save(dy, dy_out)
    save(hidden, hidden_out)
    down_line.step(3)
    next_place = replica + 2 - 4 * (replica // 2)
    next_dy = lined.at[next_place, pl.ds(tokens, tokens)]
    next_gather = Gather(next_dy, next_out, gather_sent.at[4], gather_came.at[4])
    next_gather.one()
    save(next_dy, next_out.at[own_rows])
    n2_line.start()
    down_loads = []
    for r in range(replicas):
        down_loads.append(
            pltpu.make_async_copy(
                down_parts.at[r], down_w.at[:, pl.ds(r * part, part)], load_sem.at[7 + r]
            )
        )
        down_loads[-1].start()
    for copy in down_loads:
        copy.wait()
    save(down_w, down_columns_out)

    back = Scatter(parts, buffers, scatter_sent.at[1], scatter_came.at[1])

    def feed(base):
        def grads(rows, columns):
            rows = pl.ds(pl.multiple_of(base, half), half)
            grad = product(dy[rows, :], down_w[:, columns], 1, 0)
            grad_gate[rows, columns] = (grad * grad_gate[rows, columns].astype(F32)).astype(BF)
            grad_up[rows, columns] = (grad * grad_up[rows, columns].astype(F32)).astype(BF)

        tile_loop(half, gate_w.shape[0], half, grads)

        def backward(rows, columns):
            rows = pl.ds(pl.multiple_of(base, half), half)
            value = product(grad_gate[rows, :], gate_w[:, columns], 1, 0)
            value = value + product(grad_up[rows, :], up_w[:, columns], 1, 0)
            parts[rows, columns] = value.astype(BF)

        tile_loop(half, width, half, backward)

    feed((1 - row) * half)
    back.swap(3, 2)
    next_gather.two()
    n2_line.step(1)
    back.send_far()
    feed(row * half)
    save(grad_gate, grad_gate_out)
    save(grad_up, grad_up_out)
    back.swap(1, 0)
    next_gather.three()
    back.send_near()
    back.send_rest()
    next_gather.four()
    n2_line.step(2)
    inner = back.total()
    back.drain()
    inner = (
        inner
        - jnp.mean(inner, axis=-1, keepdims=True)
        - normed[...] * jnp.mean(inner * normed[...], axis=-1, keepdims=True)
    )
    center = middle[...] - jnp.mean(middle[...], axis=-1, keepdims=True)
    inverse = lax.rsqrt(jnp.mean(center * center, axis=-1, keepdims=True) + epsilon)
    normed[...] = dy_own[...].astype(F32) + inverse * inner
    grad_own[...] = normed[...].astype(BF)
    grad_gather.one()
    save(normed, grad_out)
    save(grad_own, grad_all_out.at[own_rows])
    grad_gather.two()
    grad_gather.three()
    grad_gather.four()
    n2_line.step(3)
    grad_gather.finish()
    next_gather.finish()
    for copy in saves:
        copy.wait()
    for copy in out_swaps + down_swaps:
        copy.wait_send()
    for user in (n1_gather, n2_gather, dy_gather, grad_gather, next_gather, dy_line, n2_line, down_line):
        user.drain()


def front(lengths, frequency, x_own, dy_own, w_query, w_key, w_value, w_out, w_gate, w_up, w_down):
    groups, replicas = lax.axis_size("shard"), lax.axis_size("replica")
    tokens, width = x_own.shape
    sequence = tokens * groups
    wide, columns = w_query.shape[0], w_gate.shape[0]
    anywhere, vmem = pl.BlockSpec(memory_space=pl.ANY), pl.BlockSpec(memory_space=VMEM)

    def shape(dims, kind=BF):
        return jax.ShapeDtypeStruct(dims, kind)

    outs = (
        shape((sequence, width)),
        shape((sequence, wide)),
        shape((sequence, wide)),
        shape((sequence, wide)),
        shape((sequence, wide), F32),
        shape((sequence, wide)),
        shape((width, wide)),
        shape((replicas, width, columns // replicas)),
        shape((width, columns)),
        shape((sequence, columns)),
        shape((sequence, columns)),
        shape((sequence, columns)),
        shape((tokens, width), F32),
        shape((sequence, width)),
        shape((sequence, width)),
        shape((replicas, 2 * tokens, width)),
        shape((tokens, width), F32),
        shape((sequence, width)),
        shape((sequence, width)),
        shape((sequence, HEAD_DIM), F32),
        shape((sequence, HEAD_DIM), F32),
        shape((sequence, HEAD_DIM), jnp.int32),
    )
    dma = pltpu.SemaphoreType.DMA
    return pl.pallas_call(
        front_kernel,
        out_shape=outs,
        in_specs=[pl.BlockSpec(memory_space=pltpu.SMEM)] + [vmem] * 6 + [anywhere] * 4,
        out_specs=(anywhere,) * len(outs),
        scratch_shapes=[
            pltpu.VMEM((sequence, width), BF),
            pltpu.VMEM((sequence, width), BF),
            pltpu.VMEM((sequence, width), BF),
            pltpu.VMEM((sequence, wide), BF),
            pltpu.VMEM((sequence, wide), BF),
            pltpu.VMEM((sequence, wide), BF),
            pltpu.VMEM((sequence, wide), F32),
            pltpu.VMEM((sequence, wide), BF),
            pltpu.VMEM((width, wide), BF),
            pltpu.VMEM((columns, width), BF),
            pltpu.VMEM((columns, width), BF),
            pltpu.VMEM((width, columns), BF),
            pltpu.VMEM((sequence, columns), BF),
            pltpu.VMEM((sequence, columns), BF),
            pltpu.VMEM((sequence, columns), BF),
            pltpu.VMEM((sequence, width), BF),
            pltpu.VMEM((4, tokens, width), BF),
            pltpu.VMEM((3, tokens, width), BF),
            pltpu.VMEM((2, tokens // 2, width), BF),
            pltpu.VMEM((2, tokens, width), BF),
            pltpu.VMEM((tokens, width), F32),
            pltpu.VMEM((tokens, width), F32),
            pltpu.VMEM((tokens, width), BF),
            pltpu.VMEM((tokens, width), BF),
            pltpu.VMEM((tokens, width), BF),
            pltpu.VMEM((sequence, HEAD_DIM), F32),
            pltpu.VMEM((sequence, HEAD_DIM), F32),
            pltpu.VMEM((sequence, HEAD_DIM), jnp.int32),
            dma((7 + replicas,)),
            dma((24,)),
            dma((5, 13)),
            dma((5, 13)),
            dma((2, 10)),
            dma((2, 10)),
            dma((2, groups)),
            dma((2, groups)),
            dma((3, 2, replicas)),
            dma((3, 2, replicas)),
        ],
        compiler_params=pltpu.CompilerParams(
            collective_id=3, has_side_effects=True, vmem_limit_bytes=67043328
        ),
        cost_estimate=pl.CostEstimate(
            flops=12 * sequence * width * columns, bytes_accessed=64 * 1024 * 1024, transcendentals=0
        ),
        name="front",
    )(lengths, frequency, x_own, dy_own, w_query, w_key, w_value, w_out, w_gate, w_up, w_down)


def back_kernel(
    x_own, start, cosine, sine, hidden_in, down_in, grad_in, out_columns_in, attn_b_in, attn_in,
    query_in, key_in, value_in, n1_in, w_query, w_key, w_value, dy, middle, grad_middle,
    layer_out, input_grad, attn_part, next_half,
    hidden, down_w, grad, out_columns, attn_b, attn, query, key, value, n1, weights,
    grad_attn, key_grad, value_grad, columns_grad, out_grad, rows_grad, parts,
    pair, sums, by_far, by_side, pair2, sums2, by_far2, by_side2,
    load_sem, save_sem, scatter_sent, scatter_came, swap_sent, swap_came,
    pair_sem,
):
    replica = lax.axis_index("replica")
    me = lax.axis_index("shard")
    groups = lax.axis_size("shard")
    sequence, width = n1.shape
    wide = query.shape[1]
    heads = wide // HEAD_DIM
    pairs = (
        (hidden_in, hidden), (down_in, down_w), (grad_in, grad), (out_columns_in, out_columns),
        (attn_b_in, attn_b), (attn_in, attn), (query_in, query), (key_in, key), (value_in, value),
        (n1_in, n1), (w_query, weights.at[pl.ds(0, wide)]), (w_key, weights.at[pl.ds(wide, wide)]),
        (w_value, weights.at[pl.ds(2 * wide, wide)]),
    )
    loads = [
        pltpu.make_async_copy(src, dst, load_sem.at[i]) for i, (src, dst) in enumerate(pairs)
    ]
    for copy in loads:
        copy.start()
    barrier = pltpu.get_barrier_semaphore()
    for i in range(1, groups):
        device = lax.rem(me + i, groups)
        pl.semaphore_signal(barrier, inc=1, device_id=(replica, device), device_id_type=MESH)
    beside = replica + 1 - 2 * lax.rem(replica, 2)
    pl.semaphore_signal(barrier, inc=1, device_id=(beside, me), device_id_type=MESH)
    pl.semaphore_wait(barrier, groups)
    half = sequence // 2
    next_copy = pltpu.make_async_remote_copy(
        src_ref=dy.at[pl.ds(pl.multiple_of(lax.rem(me, 2) * half, half), half)],
        dst_ref=next_half,
        send_sem=pair_sem.at[0],
        recv_sem=pair_sem.at[1],
        device_id=(beside, me),
        device_id_type=MESH,
    )
    next_copy.start()

    loads[0].wait()
    loads[1].wait()

    def mix(rows, columns):
        parts[rows, columns] = product(hidden[rows, :], down_w[columns, :], 1, 1).astype(BF)

    tile_loop(sequence, width, 512, mix)
    mixed = Scatter(parts, (pair, sums, by_far, by_side), scatter_sent.at[0], scatter_came.at[0])
    mixed.swap(3, 1, 2, 0)

    for copy in loads[2:6]:
        copy.wait()
    mixed.send_far()
    mixed.send_near()
    for first in range(0, width, 512):
        rows = pl.ds(first, 512)
        out_grad[rows, :] = product(grad[:, rows], attn_b[...], 0, 0).astype(BF)
    mine = pl.ds(pl.multiple_of(me * wide, wide), wide)
    out_rows = pl.ds(3 * wide, wide)
    swaps = []
    for i in range(1, groups):
        device = lax.rem(me + i, groups)
        swaps.append(
            pltpu.make_async_remote_copy(
                src_ref=out_grad.at[pl.ds(pl.multiple_of(device * wide, wide), wide)],
                dst_ref=attn_part.at[out_rows, mine],
                send_sem=swap_sent.at[i],
                recv_sem=swap_came.at[i],
                device_id=(replica, device),
                device_id_type=MESH,
            )
        )
        swaps[-1].start()
    own_swap = pltpu.make_async_copy(out_grad.at[mine], attn_part.at[out_rows, mine], save_sem.at[0])
    own_swap.start()
    for first in range(0, sequence, 512):
        rows = pl.ds(first, 512)
        grad_attn[rows, :] = product(grad[rows, :], out_columns[...], 1, 0).astype(BF)
    for copy in loads[6:]:
        copy.wait()
    mixed.send_rest()

    step = 256
    for first in range(sequence - step, -1, -step):
        rows = pl.ds(first, step)
        low, upto = key_reach(first, step, sequence)
        bias = allowed_bias(start[rows, 0:1], first, step, low)
        for head in range(heads):
            lanes = pl.ds(head * HEAD_DIM, HEAD_DIM)
            query_piece, grad_piece = query[rows, lanes], grad_attn[rows, lanes]
            scores = head_scores(query_piece, key[upto, lanes], bias)
            probs = jnp.exp(scores - jnp.max(scores, axis=-1, keepdims=True))
            probs = probs / jnp.sum(probs, axis=-1, keepdims=True)
            delta = jnp.sum(grad_piece.astype(F32) * attn[rows, lanes], axis=-1, keepdims=True)
            grad_probs = product(grad_piece, value[upto, lanes], 1, 1)
            grad_scores = (probs * (grad_probs - delta)).astype(BF)
            query_grad = product(grad_scores, key[upto, lanes], 1, 0) * (1.0 / math.sqrt(HEAD_DIM))
            query_grad = rotate_head(query_grad, cosine[rows, :], -sine[rows, :])
            columns_grad[rows, lanes] = query_grad.astype(BF)
            key_part = product(grad_scores, query_piece, 0, 0)
            value_part = product(probs.astype(BF), grad_piece, 0, 0)
            if first == sequence - step:
                key_grad[upto, lanes] = key_part
                value_grad[upto, lanes] = value_part
                if low:
                    key_grad[pl.ds(0, low), lanes] = jnp.zeros((low, HEAD_DIM), F32)
                    value_grad[pl.ds(0, low), lanes] = jnp.zeros((low, HEAD_DIM), F32)
            else:
                key_grad[upto, lanes] += key_part
                value_grad[upto, lanes] += value_part
    for head in range(heads):
        lanes = pl.ds(head * HEAD_DIM, HEAD_DIM)
        piece = key_grad[:, lanes] * (1.0 / math.sqrt(HEAD_DIM))
        piece = rotate_head(piece, cosine[...], -sine[...])
        columns_grad[:, pl.ds(wide + head * HEAD_DIM, HEAD_DIM)] = piece.astype(BF)
        columns_grad[:, pl.ds(2 * wide + head * HEAD_DIM, HEAD_DIM)] = value_grad[:, lanes].astype(BF)

    layer_out[...] = (middle[...] + mixed.total()).astype(BF)
    mixed.drain()

    def back(rows, columns):
        parts[rows, columns] = product(columns_grad[rows, :], weights[:, columns], 1, 0).astype(BF)

    tile_loop(sequence, width, 512, back)
    last = Scatter(parts, (pair2, sums2, by_far2, by_side2), scatter_sent.at[1], scatter_came.at[1])
    last.swap(3, 1, 2, 0)
    last.send_far()
    last.send_near()

    def collect(rows, columns):
        rows_grad[rows, columns] = product(columns_grad[:, rows], n1[:, columns], 0, 0).astype(BF)

    tile_loop(3 * wide, width, 256, collect, 512)
    rows_save = pltpu.make_async_copy(rows_grad, attn_part.at[pl.ds(0, 3 * wide)], save_sem.at[1])
    rows_save.start()
    last.send_rest()
    x = x_own[...].astype(F32)
    center = x - jnp.mean(x, axis=-1, keepdims=True)
    inverse = lax.rsqrt(jnp.mean(center * center, axis=-1, keepdims=True) + epsilon)
    inner = last.total()
    normed = center * inverse
    inner = (
        inner
        - jnp.mean(inner, axis=-1, keepdims=True)
        - normed * jnp.mean(inner * normed, axis=-1, keepdims=True)
    )
    input_grad[...] = grad_middle[...] + inverse * inner
    last.drain()
    for copy in swaps:
        copy.wait()
    own_swap.wait()
    rows_save.wait()
    next_copy.wait()


def back(x_own, start, cosine, sine, hidden, down, grad, out_columns, attn_b, attn, query, key, value, n1,
         w_query, w_key, w_value, dy, middle, grad_middle):
    groups = lax.axis_size("shard")
    tokens, width = x_own.shape
    sequence = tokens * groups
    wide, columns = query.shape[1], hidden.shape[1]
    anywhere, vmem = pl.BlockSpec(memory_space=pl.ANY), pl.BlockSpec(memory_space=VMEM)
    dma = pltpu.SemaphoreType.DMA
    buffers = [
        pltpu.VMEM((4, tokens, width), BF),
        pltpu.VMEM((3, tokens, width), BF),
        pltpu.VMEM((2, tokens // 2, width), BF),
        pltpu.VMEM((2, tokens, width), BF),
    ]
    return pl.pallas_call(
        back_kernel,
        out_shape=(
            jax.ShapeDtypeStruct((tokens, width), BF),
            jax.ShapeDtypeStruct((tokens, width), F32),
            jax.ShapeDtypeStruct((4 * wide, width), BF),
            jax.ShapeDtypeStruct((sequence // 2, width), BF),
        ),
        in_specs=[vmem] * 4 + [anywhere] * 14 + [vmem] * 2,
        out_specs=(vmem, vmem, anywhere, anywhere),
        scratch_shapes=[
            pltpu.VMEM((sequence, columns), BF),
            pltpu.VMEM((width, columns), BF),
            pltpu.VMEM((sequence, width), BF),
            pltpu.VMEM((width, wide), BF),
            pltpu.VMEM((sequence, wide), BF),
            pltpu.VMEM((sequence, wide), F32),
            pltpu.VMEM((sequence, wide), BF),
            pltpu.VMEM((sequence, wide), BF),
            pltpu.VMEM((sequence, wide), BF),
            pltpu.VMEM((sequence, width), BF),
            pltpu.VMEM((3 * wide, width), BF),
            pltpu.VMEM((sequence, wide), BF),
            pltpu.VMEM((sequence, wide), F32),
            pltpu.VMEM((sequence, wide), F32),
            pltpu.VMEM((sequence, 3 * wide), BF),
            pltpu.VMEM((width, wide), BF),
            pltpu.VMEM((3 * wide, width), BF),
            pltpu.VMEM((sequence, width), BF),
            *buffers,
            *buffers,
            dma((13,)),
            dma((2,)),
            dma((2, 10)),
            dma((2, 10)),
            dma((groups,)),
            dma((groups,)),
            dma((2,)),
        ],
        compiler_params=pltpu.CompilerParams(
            collective_id=4, has_side_effects=True, vmem_limit_bytes=67043328
        ),
        cost_estimate=pl.CostEstimate(
            flops=24 * sequence * width * wide, bytes_accessed=48 * 1024 * 1024, transcendentals=0
        ),
        name="back",
    )(x_own, start, cosine, sine, hidden, down, grad, out_columns, attn_b, attn, query, key, value, n1,
      w_query, w_key, w_value, dy, middle, grad_middle)


def every_kernel(
    lined, own_normed, own_dy, next_half, dy_two, own_hidden, own_grad_gate, own_grad_up, attn_part,
    w_gate, w_up, w_down,
    gate_out, up_out, out_down, out_attn, landed, kept, next_other,
    normed, dy, hidden, grad_gate, grad_up, gate_w, up_w, down_w, down, out_gate, out_up, first_sum, second_sum, stage,
    load_sem, keep_sem, gather_sent, gather_came, line_sent, line_came, line_own, swap_sent, swap_came,
    out_sem,
):
    replica = lax.axis_index("replica")
    replicas = lax.axis_size("replica")
    me = lax.axis_index("shard")
    groups = lax.axis_size("shard")
    tokens = lined.shape[1] // 2
    sequence, width = normed.shape
    columns = hidden.shape[1]
    own_rows = block_rows(me, tokens)
    inner = (replica == 1) | (replica == 2)
    outer = (replica == 0) | (replica == 3)
    beside = replica + 1 - 2 * lax.rem(replica, 2)
    facing = 3 - replica
    chunks, depth = first_sum.shape[0], first_sum.shape[1]

    def piece(c):
        return pl.ds(c * depth, depth)

    def line_move(kind, c, src, dst, target):
        return pltpu.make_async_remote_copy(
            src_ref=src,
            dst_ref=dst,
            send_sem=line_sent.at[kind, c],
            recv_sem=line_came.at[kind, c],
            device_id=(target, me),
            device_id_type=MESH,
        )

    def inward(c):
        return line_move(0, c, attn_part.at[piece(c)], first_sum.at[c], beside)

    def middle(c):
        return line_move(1, c, first_sum.at[c], second_sum.at[c], facing)

    def outward(c):
        return line_move(2, c, second_sum.at[c], out_attn.at[piece(c)], beside)

    def keep(c):
        return pltpu.make_async_copy(second_sum.at[c], out_attn.at[piece(c)], line_own.at[c])

    def stage_load(c):
        return pltpu.make_async_copy(attn_part.at[piece(c)], stage, keep_sem.at[2, 0])

    def half_sums(*which):
        @pl.when(inner)
        def _():
            for c in which:
                stage_load(c).wait()
                inward(c).wait_recv()
                first_sum[c] = (stage[...].astype(F32) + first_sum[c].astype(F32)).astype(BF)
                middle(c).start()
                if c + 1 < chunks:
                    stage_load(c + 1).start()

    def full_sums(*which):
        @pl.when(inner)
        def _():
            for c in which:
                middle(c).wait_recv()
                second_sum[c] = (first_sum[c].astype(F32) + second_sum[c].astype(F32)).astype(BF)
                outward(c).start()
                keep(c).start()

    def other(n):
        return lined.at[(beside, replica + 2 - 4 * (replica // 2), facing)[n - 1]]

    core = lax.rem(me, 2)
    mate = me + 1 - 2 * core
    next_copy = pltpu.make_async_remote_copy(
        src_ref=next_half,
        dst_ref=next_other,
        send_sem=swap_sent.at[7],
        recv_sem=swap_came.at[7],
        device_id=(replica, mate),
        device_id_type=MESH,
    )

    gathers = [
        Gather(other(n).at[pl.ds(0, tokens)], landed.at[n - 1], gather_sent.at[n - 1], gather_came.at[n - 1])
        for n in range(1, 4)
    ]
    gathers.append(
        Gather(other(3).at[pl.ds(tokens, tokens)], landed.at[3], gather_sent.at[3], gather_came.at[3])
    )

    def normed_loads(n, target, base):
        copies = []
        for i in range(groups):
            device = lax.rem(me + i, groups)
            rows = block_rows(device, tokens)
            source = other(n).at[pl.ds(0, tokens)] if i == 0 else landed.at[n - 1, rows]
            copies.append(pltpu.make_async_copy(source, target.at[rows], load_sem.at[base, i]))
        return copies

    def dy_loads(n):
        if n == 1:
            half = sequence // 2
            mine = dy.at[pl.ds(pl.multiple_of(core * half, half), half)]
            others = dy.at[pl.ds(pl.multiple_of((1 - core) * half, half), half)]
            return [
                pltpu.make_async_copy(next_half, mine, load_sem.at[1, 0]),
                pltpu.make_async_copy(next_other, others, load_sem.at[1, 1]),
            ]
        if n == 2:
            return [pltpu.make_async_copy(dy_two, dy, load_sem.at[1, 0])]
        copies = []
        for i in range(groups):
            device = lax.rem(me + i, groups)
            rows = block_rows(device, tokens)
            source = other(n).at[pl.ds(tokens, tokens)] if i == 0 else landed.at[3, rows]
            copies.append(pltpu.make_async_copy(source, dy.at[rows], load_sem.at[1, i]))
        return copies

    def keeps(n):
        return [
            pltpu.make_async_copy(grad_gate, kept.at[n - 1, 0], keep_sem.at[0, n]),
            pltpu.make_async_copy(grad_up, kept.at[n - 1, 1], keep_sem.at[1, n]),
        ]

    def start_all(copies):
        for copy in copies:
            copy.start()

    def wait_all(copies):
        for copy in copies:
            copy.wait()

    first = [
        pltpu.make_async_copy(own_normed, normed, load_sem.at[0, 0]),
        pltpu.make_async_copy(own_grad_gate, grad_gate, load_sem.at[0, 1]),
        pltpu.make_async_copy(own_grad_up, grad_up, load_sem.at[0, 2]),
        pltpu.make_async_copy(own_hidden, hidden, load_sem.at[1, 1]),
        pltpu.make_async_copy(own_dy, dy, load_sem.at[1, 0]),
    ]
    weights = [
        pltpu.make_async_copy(w_gate, gate_w, load_sem.at[2, 0]),
        pltpu.make_async_copy(w_up, up_w, load_sem.at[2, 1]),
        pltpu.make_async_copy(w_down, down_w, load_sem.at[2, 2]),
    ]
    start_all(first + weights)
    barrier = pltpu.get_barrier_semaphore()
    for i in range(1, groups):
        device = lax.rem(me + i, groups)
        pl.semaphore_signal(barrier, inc=1, device_id=(replica, device), device_id_type=MESH)
    pl.semaphore_signal(barrier, inc=1, device_id=(beside, me), device_id_type=MESH)

    @pl.when(inner)
    def _():
        pl.semaphore_signal(barrier, inc=1, device_id=(facing, me), device_id_type=MESH)
        pl.semaphore_wait(barrier, groups + 1)

    @pl.when(outer)
    def _():
        pl.semaphore_wait(barrier, groups)

    gathers[0].one()
    next_copy.start()

    @pl.when(outer)
    def _():
        start_all([inward(c) for c in range(chunks)])

    @pl.when(inner)
    def _():
        stage_load(0).start()

    def collect(out, left, right, add):
        def step(rows, cols):
            value = product(left[:, rows], right[:, cols], 0, 0)
            if add is None:
                out[rows, cols] = value
            elif add is True:
                out[rows, cols] += value

        tile_loop(out.shape[0], out.shape[1], 512, step)

    wait_all(first[:3])
    collect(out_gate, grad_gate, normed, None)
    gathers[0].two()
    collect(out_up, grad_up, normed, None)
    gathers[0].three()
    gathers[1].one()
    gathers[0].four()
    gathers[0].finish()
    start_all(normed_loads(1, normed, 0))
    next_copy.wait()
    wait_all(first[3:])
    collect(down, dy, hidden, None)
    start_all(dy_loads(1))
    half_sums(0)
    wait_all(weights)
    wait_all(normed_loads(1, normed, 0))
    wait_all(dy_loads(1))

    near, further, last_normed, last_dy = gathers
    agenda = {
        (1, 1): (further.two,),
        (1, 3): (further.three, last_dy.one, lambda: half_sums(1)),
        (1, 5): (further.four,),
        (1, 7): (further.finish, lambda: full_sums(0)),
        (2, 0): (last_dy.two,),
        (2, 2): (last_dy.three, last_normed.one),
        (2, 3): (lambda: half_sums(3),),
        (2, 4): (last_dy.four,),
        (2, 6): (last_normed.two, lambda: full_sums(2)),
        (2, 7): (last_dy.finish,),
        (3, 1): (lambda: half_sums(5),),
        (3, 5): (lambda: full_sums(4),),
        (3, 7): (lambda: half_sums(6),),
    }

    def after_down(n):
        if n == 1:
            half_sums(2)
            full_sums(1)
        else:
            last_normed.three()
            half_sums(4)
            full_sums(3)
            last_normed.four()
            last_normed.finish()
            start_all(normed_loads(3, normed, 0))
        start_all(dy_loads(n + 1))
        wait_all(keeps(n))
        wait_all(normed_loads(n + 1, normed, 0))
        wait_all(dy_loads(n + 1))

    def sequence_step(n, carry):
        narrow = 256
        across = columns // narrow

        def one_tile(i, carry):
            ffn_tile(
                normed, dy, gate_w, up_w, down_w, hidden, grad_gate, grad_up,
                pl.ds(pl.multiple_of((i // across) * 512, 512), 512),
                pl.ds(pl.multiple_of(lax.rem(i, across) * narrow, narrow), narrow),
            )
            for (when, tile), actions in agenda.items():

                @pl.when((n == when) & (i == tile))
                def _(actions=actions):
                    for action in actions:
                        action()

            return carry

        lax.fori_loop(0, (sequence // 512) * across, one_tile, 0)
        for k in (1, 2):

            @pl.when(n == k)
            def _(k=k):
                start_all(keeps(k))
                if k == 1:
                    start_all(normed_loads(2, normed, 0))

        @pl.when(n < 3)
        def _():
            collect(down, dy, hidden, True)

        for k in (1, 2):

            @pl.when(n == k)
            def _(k=k):
                after_down(k)

        return carry

    lax.fori_loop(1, 4, sequence_step, 0)
    one_gate, one_up = up_w.at[:, pl.ds(0, columns)], up_w.at[:, pl.ds(columns, columns)]
    one_loads = normed_loads(1, gate_w, 2) + [
        pltpu.make_async_copy(kept.at[0, 0], one_gate, keep_sem.at[0, 0]),
        pltpu.make_async_copy(kept.at[0, 1], one_up, keep_sem.at[1, 0]),
    ]
    start_all(one_loads)

    wide = width // groups
    _, _, across_device, along_device, far_device = whereabouts()

    def down_move(send_index, recv_index, row, sender, device):
        return pltpu.make_async_remote_copy(
            src_ref=down_w.at[pl.ds(pl.multiple_of(row, wide), wide)],
            dst_ref=out_down.at[:, pl.ds(pl.multiple_of(sender * columns, columns), columns)],
            send_sem=swap_sent.at[send_index],
            recv_sem=swap_came.at[recv_index],
            device_id=(replica, device),
            device_id_type=MESH,
        )

    swaps, arrivals = [], []
    for i, device in enumerate((far_device, across_device, along_device, me)):
        chip = device // 2
        rows = pl.ds(pl.multiple_of(chip * 2 * wide, 2 * wide), 2 * wide)

        def finish_down(j, carry, rows=rows):
            cols = pl.ds(pl.multiple_of(j * 512, 512), 512)
            down[rows, cols] += product(dy[:, rows], hidden[:, cols], 0, 0)
            return carry

        lax.fori_loop(0, columns // 512, finish_down, 0)
        down_w[i * 2 * wide : (i + 1) * 2 * wide, :] = down[rows, :].astype(BF)
        for k in range(2):
            if i < 3:
                row, peer = (2 * i + k) * wide, chip * 2 + k
                swaps.append(down_move(2 * i + k, 2 * i + core, row, me, peer))
                swaps[-1].start()
                arrivals.append(down_move(2 * i + k, 2 * i + k, row, peer, peer))
    swaps.append(down_move(6, 6, (6 + lax.rem(mate, 2)) * wide, me, mate))
    swaps[-1].start()
    arrivals.append(down_move(6, 6, 6 * wide, mate, mate))
    own_slab = pltpu.make_async_copy(
        down_w.at[pl.ds(pl.multiple_of((6 + core) * wide, wide), wide)],
        out_down.at[:, pl.ds(pl.multiple_of(me * columns, columns), columns)],
        keep_sem.at[2, 1],
    )
    own_slab.start()
    two_gate = pltpu.make_async_copy(kept.at[1, 0], hidden, keep_sem.at[0, 3])
    two_gate.start()
    half_sums(7)
    full_sums(5)
    wait_all(one_loads)
    two_loads = normed_loads(2, dy, 0)
    start_all(two_loads)

    def collect_pair(out, *pairs):
        def step(rows, cols):
            value = product(pairs[0][0][:, rows], pairs[0][1][:, cols], 0, 0)
            for left, right in pairs[1:]:
                value = value + product(left[:, rows], right[:, cols], 0, 0)
            out[rows, cols] += value

        tile_loop(out.shape[0], out.shape[1], 512, step)

    collect_pair(out_gate, (grad_gate, normed), (one_gate, gate_w))
    full_sums(6)
    wait_all(two_loads)
    two_gate.wait()
    collect_pair(out_gate, (hidden, dy))
    gate_save = pltpu.make_async_copy(out_gate, gate_out, out_sem.at[0])
    gate_save.start()
    two_up = pltpu.make_async_copy(kept.at[1, 1], grad_gate, keep_sem.at[1, 3])
    two_up.start()
    full_sums(7)
    collect_pair(out_up, (grad_up, normed), (one_up, gate_w))
    two_up.wait()
    up_saves = []
    for i in range(out_up.shape[0] // 512):
        rows = pl.ds(i * 512, 512)

        def last_up(j, carry, rows=rows):
            cols = pl.ds(pl.multiple_of(j * 512, 512), 512)
            out_up[rows, cols] += product(grad_gate[:, rows], dy[:, cols], 0, 0)
            return carry

        lax.fori_loop(0, width // 512, last_up, 0)
        up_saves.append(pltpu.make_async_copy(out_up.at[rows], up_out.at[rows], out_sem.at[1 + i]))
        up_saves[-1].start()

    @pl.when(outer)
    def _():
        for c in range(chunks):
            inward(c).wait_send()
            outward(c).wait_recv()

    @pl.when(inner)
    def _():
        for c in range(chunks):
            middle(c).wait_send()
            outward(c).wait_send()
            keep(c).wait()

    for copy in swaps:
        copy.wait_send()
    for copy in arrivals:
        copy.wait_recv()
    own_slab.wait()
    gate_save.wait()
    wait_all(up_saves)
    for gather in gathers:
        gather.drain()


def ffn_grads(lined, n2, dy_all, next_half, dy_two, own, attn_part, w_gate, w_up, w_down_columns):
    replicas, tokens, width = lined.shape
    tokens = tokens // 2
    sequence = n2.shape[0]
    groups = sequence // tokens
    columns = w_gate.shape[0]
    chunks = 8
    depth = attn_part.shape[0] // chunks
    anywhere = pl.BlockSpec(memory_space=pl.ANY)
    dma = pltpu.SemaphoreType.DMA
    out = pl.pallas_call(
        every_kernel,
        out_shape=(
            jax.ShapeDtypeStruct((columns, width), F32),
            jax.ShapeDtypeStruct((columns, width), F32),
            jax.ShapeDtypeStruct((width // groups, columns * groups), BF),
            jax.ShapeDtypeStruct(attn_part.shape, BF),
            jax.ShapeDtypeStruct((replicas, sequence, width), BF),
            jax.ShapeDtypeStruct((2, 2, sequence, columns), BF),
            jax.ShapeDtypeStruct(next_half.shape, BF),
        ),
        in_specs=[anywhere] * 12,
        out_specs=(anywhere,) * 7,
        scratch_shapes=[
            pltpu.VMEM((sequence, width), BF),
            pltpu.VMEM((sequence, width), BF),
            pltpu.VMEM((sequence, columns), BF),
            pltpu.VMEM((sequence, columns), BF),
            pltpu.VMEM((sequence, columns), BF),
            pltpu.VMEM((columns, width), BF),
            pltpu.VMEM((columns, width), BF),
            pltpu.VMEM((width, columns), BF),
            pltpu.VMEM((width, columns), F32),
            pltpu.VMEM((columns, width), F32),
            pltpu.VMEM((columns, width), F32),
            pltpu.VMEM((chunks, depth, width), BF),
            pltpu.VMEM((chunks, depth, width), BF),
            pltpu.VMEM((depth, width), BF),
            dma((3, groups)),
            dma((3, 4)),
            dma((4, 13)),
            dma((4, 13)),
            dma((3, chunks)),
            dma((3, chunks)),
            dma((chunks,)),
            dma((groups,)),
            dma((groups,)),
            dma((1 + columns // 512,)),
        ],
        compiler_params=pltpu.CompilerParams(
            collective_id=2, has_side_effects=True, vmem_limit_bytes=67043328
        ),
        cost_estimate=pl.CostEstimate(
            flops=42 * sequence * width * columns, bytes_accessed=80 * 1024 * 1024, transcendentals=0
        ),
        name="ffn_grads",
    )(lined, n2, dy_all, next_half, dy_two, *own, attn_part, w_gate, w_up, w_down_columns)
    return out[:4]


def gather_tokens(values):
    return lax.all_gather(values, "shard", axis=0, tiled=True)


def scatter_tokens(partial):
    return lax.psum_scatter(
        partial.astype(BF), "shard", scatter_dimension=0, tiled=True
    ).astype(F32)


def rows_to_columns(weight):
    return lax.all_to_all(weight, "shard", split_axis=1, concat_axis=0, tiled=True)


def columns_to_rows(grad):
    return lax.all_to_all(grad, "shard", split_axis=0, concat_axis=1, tiled=True)


def replica_sum(part):
    return lax.psum(part.astype(BF), "replica")


def general_body(hidden_in, cotangent, doc_lengths, w_query, w_key, w_value, w_out, w_gate, w_up, w_down):
    x = hidden_in[0].astype(F32)
    dyb = cotangent[0]
    tokens_here = x.shape[0]
    groups = lax.axis_size("shard")
    seq_length = tokens_here * groups
    factor = 1.0 / math.sqrt(HEAD_DIM)
    places = jnp.arange(seq_length, dtype=jnp.int32)
    segment, offset = doc_layout(doc_lengths[0], places)
    cosine, sine = rope_tables(offset, HEAD_DIM)
    allowed = ((segment[:, None] == segment[None, :]) & (places[None, :] <= places[:, None]))[None]

    normed_one, inverse_one = normalize(x)
    n1 = gather_tokens(normed_one.astype(BF))
    w_out_columns = rows_to_columns(w_out)
    query = rotate(split_heads(dot(n1, w_query, 1, 1)), cosine, sine).astype(BF)
    keys = rotate(split_heads(dot(n1, w_key, 1, 1)), cosine, sine).astype(BF)
    values = split_heads(dot(n1, w_value, 1, 1)).astype(BF)
    scores = factor * jnp.einsum("hqe,hke->hqk", query, keys, preferred_element_type=F32)
    scores = jnp.where(allowed, scores, masked)
    top = jnp.max(scores, axis=-1, keepdims=True)
    weights = jnp.where(allowed, jnp.exp(scores - top), 0.0)
    total = jnp.sum(weights, axis=-1, keepdims=True)
    log_total = top + jnp.log(total)
    attn = jnp.einsum("hqk,hke->hqe", weights.astype(BF), values, preferred_element_type=F32) / total
    out_b = join_heads(attn).astype(BF)
    middle = x + scatter_tokens(dot(out_b, w_out_columns, 1, 1))

    normed_two, inverse_two = normalize(middle)
    n2 = gather_tokens(normed_two.astype(BF))
    dy_all = gather_tokens(dyb)
    w_down_columns = rows_to_columns(w_down)
    gate = dot(n2, w_gate, 1, 1)
    up = dot(n2, w_up, 1, 1)
    sigma = jax.nn.sigmoid(gate)
    silu = gate * sigma
    hidden = (silu * up).astype(BF)
    grad_down = columns_to_rows(replica_sum(dot(dy_all, hidden, 0, 0)))
    grad_hidden = dot(dy_all, w_down_columns, 1, 0)
    grad_gate_b = (grad_hidden * up * sigma * (1.0 + gate * (1.0 - sigma))).astype(BF)
    grad_up_b = (grad_hidden * silu).astype(BF)
    grad_gate = replica_sum(dot(grad_gate_b, n2, 0, 0).astype(BF))
    grad_up = replica_sum(dot(grad_up_b, n2, 0, 0).astype(BF))
    grad_normed_two = scatter_tokens(dot(grad_gate_b, w_gate, 1, 0) + dot(grad_up_b, w_up, 1, 0))
    mixed = scatter_tokens(dot(hidden, w_down_columns, 1, 1))
    layer_out = (middle + mixed).astype(BF)
    grad_middle = dyb.astype(F32) + norm_back(normed_two, inverse_two, grad_normed_two)

    grad_middle_all = gather_tokens(grad_middle.astype(BF))
    grad_out = columns_to_rows(replica_sum(dot(grad_middle_all, out_b, 0, 0).astype(BF)))
    grad_attn = split_heads(dot(grad_middle_all, w_out_columns, 1, 0)).astype(BF)
    delta = jnp.sum(grad_attn.astype(F32) * attn, axis=-1, keepdims=True)
    probs = jnp.where(allowed, jnp.exp(scores - log_total), 0.0)
    grad_probs = jnp.einsum("hqe,hke->hqk", grad_attn, values, preferred_element_type=F32)
    grad_scores = (probs * (grad_probs - delta)).astype(BF)
    query_grad = factor * jnp.einsum("hqk,hke->hqe", grad_scores, keys, preferred_element_type=F32)
    key_grad = factor * jnp.einsum("hqk,hqe->hke", grad_scores, query, preferred_element_type=F32)
    value_grad = jnp.einsum("hqk,hqe->hke", probs.astype(BF), grad_attn, preferred_element_type=F32)
    query_grad = join_heads(rotate(query_grad, cosine, -sine)).astype(BF)
    key_grad = join_heads(rotate(key_grad, cosine, -sine)).astype(BF)
    value_grad = join_heads(value_grad).astype(BF)
    grad_query = replica_sum(dot(query_grad, n1, 0, 0).astype(BF))
    grad_key = replica_sum(dot(key_grad, n1, 0, 0).astype(BF))
    grad_value = replica_sum(dot(value_grad, n1, 0, 0).astype(BF))
    grad_normed_one = scatter_tokens(
        dot(query_grad, w_query, 1, 0) + dot(key_grad, w_key, 1, 0) + dot(value_grad, w_value, 1, 0)
    )
    grad_in = grad_middle + norm_back(normed_one, inverse_one, grad_normed_one)
    return (
        layer_out[None],
        grad_in[None],
        grad_query.astype(F32),
        grad_key.astype(F32),
        grad_value.astype(F32),
        grad_out.astype(F32),
        grad_gate.astype(F32),
        grad_up.astype(F32),
        grad_down.astype(F32),
    )


def body(hidden_in, cotangent, doc_lengths, w_query, w_key, w_value, w_out, w_gate, w_up, w_down):
    x_own, dy_own = hidden_in[0], cotangent[0]
    half = HEAD_DIM // 2
    frequency = theta_base ** (-2.0 * (np.arange(HEAD_DIM) % half) / HEAD_DIM)
    (
        n1, query, key, value, attn, attn_b, out_columns, _, down_columns,
        hidden, grad_gate_b, grad_up_b, middle, n2, dy, lined, grad_middle, grad_all, dy_two,
        cosine, sine, start,
    ) = front(
        doc_lengths, jnp.asarray(frequency[None], F32), x_own, dy_own,
        w_query, w_key, w_value, w_out, w_gate, w_up, w_down,
    )
    layer_out, grad_in, attn_part, next_half = back(
        x_own, start, cosine, sine, hidden, down_columns, grad_all, out_columns, attn_b, attn,
        query, key, value, n1, w_query, w_key, w_value, dy, middle, grad_middle,
    )
    grad_gate, grad_up, grad_down, attn_sum = ffn_grads(
        lined, n2, dy, next_half, dy_two, (hidden, grad_gate_b, grad_up_b), attn_part, w_gate, w_up, down_columns
    )
    grad_query, grad_key, grad_value, grad_out = jnp.split(attn_sum.astype(F32), 4, axis=0)
    return (
        layer_out[None],
        grad_in[None],
        grad_query,
        grad_key,
        grad_value,
        grad_out,
        grad_gate,
        grad_up,
        grad_down.astype(F32),
    )


def solution(mesh):
    rows = P("shard", None)
    tokens = P("replica", "shard", None)
    in_specs = (tokens, tokens, P("replica", None)) + (rows,) * 7
    out_specs = (tokens, tokens) + (rows,) * 7
    local = body if mesh.shape["shard"] == 8 and mesh.shape["replica"] == 4 else general_body
    return jax.shard_map(local, mesh=mesh, in_specs=in_specs, out_specs=out_specs, check_vma=False)
```

```python
import functools
import math

import jax
import jax.numpy as jnp
import numpy as np
from jax import lax
from jax.experimental import pallas as pl
from jax.experimental.pallas import tpu as pltpu
from jax.sharding import PartitionSpec as P

HEAD_DIM = 128

epsilon = 1e-05
theta_base = 10000.0
masked = -1e30
BF = jnp.bfloat16
F32 = jnp.float32
MESH = pl.DeviceIdType.MESH
VMEM = pltpu.VMEM


def normalize(values):
    center = values - jnp.mean(values, axis=-1, keepdims=True)
    inverse = lax.rsqrt(jnp.mean(center * center, axis=-1, keepdims=True) + epsilon)
    return (center * inverse, inverse)


def norm_back(normed, inverse, grad):
    inner = (
        grad
        - jnp.mean(grad, axis=-1, keepdims=True)
        - normed * jnp.mean(grad * normed, axis=-1, keepdims=True)
    )
    return inverse * inner


def dot(a, b, ca, cb):
    return lax.dot_general(a, b, (((ca,), (cb,)), ((), ())), preferred_element_type=F32)


def doc_layout(lengths, places):
    ends = jnp.cumsum(lengths)
    starts = ends - lengths
    segment = jnp.sum((places[:, None] >= ends[None, :]).astype(jnp.int32), axis=1)
    member = segment[:, None] == jnp.arange(lengths.shape[0], dtype=jnp.int32)[None, :]
    offset = places - jnp.sum(jnp.where(member, starts[None, :], 0), axis=1)
    return (segment, offset)


def rope_tables(offset, head_dim):
    half = head_dim // 2
    freq = theta_base ** (-2.0 * jnp.arange(half, dtype=F32) / head_dim)
    angle = offset.astype(F32)[:, None] * freq[None, :]
    return (jnp.cos(angle)[None], jnp.sin(angle)[None])


def rotate(values, cosine, sine):
    half = values.shape[-1] // 2
    first = values[..., :half]
    second = values[..., half:]
    return jnp.concatenate(
        [first * cosine - second * sine, second * cosine + first * sine], axis=-1
    )


def split_heads(values):
    tokens, width = values.shape
    return jnp.transpose(values.reshape(tokens, width // HEAD_DIM, HEAD_DIM), (1, 0, 2))


def join_heads(values):
    heads, tokens, size = values.shape
    return jnp.transpose(values, (1, 0, 2)).reshape(tokens, heads * size)


def whereabouts():
    place = lax.axis_index("shard")
    core, col, row = lax.rem(place, 2), lax.rem(place // 2, 2), place // 4
    across, along = place + 2 - 4 * col, place + 4 - 8 * row
    return place, place + 1 - 2 * core, across, along, across + 4 - 8 * row


def whereabouts_of_mate():
    me, mate, across, along, far = whereabouts()
    shift = mate - me
    return across + shift, along + shift, far + shift


def tile_loop(rows, columns, size, step, narrow=None):
    narrow = narrow or size
    across = columns // narrow

    def one(i, carry):
        step(
            pl.ds(pl.multiple_of((i // across) * size, size), size),
            pl.ds(pl.multiple_of(lax.rem(i, across) * narrow, narrow), narrow),
        )
        return carry

    lax.fori_loop(0, (rows // size) * across, one, 0)


def product(a, b, ca, cb):
    return lax.dot_general(a, b, (((ca,), (cb,)), ((), ())), preferred_element_type=F32)


def ffn_tile(normed, dy, w_gate, w_up, w_down, hidden, grad_gate, grad_up, rows, columns):
    gate = product(normed[rows, :], w_gate[columns, :], 1, 1)
    up = product(normed[rows, :], w_up[columns, :], 1, 1)
    grad = product(dy[rows, :], w_down[:, columns], 1, 0)
    sigma = 0.5 + 0.5 * jnp.tanh(0.5 * gate)
    silu = gate * sigma
    hidden[rows, columns] = (silu * up).astype(BF)
    grad_gate[rows, columns] = (grad * (up * (sigma + silu * (1.0 - sigma)))).astype(BF)
    grad_up[rows, columns] = (grad * silu).astype(BF)


def block_rows(slot, tokens, part=0):
    size = tokens // 2
    if part:
        return pl.ds(pl.multiple_of(slot * tokens + (part - 1) * size, size), size)
    return pl.ds(pl.multiple_of(slot * tokens, tokens), tokens)


class Gather:
    def __init__(self, block, out, sent, came):
        self.block, self.out, self.sent, self.came = block, out, sent, came
        self.tokens = block.shape[0]
        self.replica = lax.axis_index("replica")
        self.me, self.mate, self.across, self.along, self.far = whereabouts()
        self.sends = []

    def move(self, k, slot, part, device, first=False):
        tokens = self.tokens
        local = pl.ds((part - 1) * (tokens // 2) if part else 0, tokens // 2 if part else tokens)
        rows = block_rows(slot, tokens, part)
        return pltpu.make_async_remote_copy(
            src_ref=self.block.at[local] if first else self.out.at[rows],
            dst_ref=self.out.at[rows],
            send_sem=self.sent.at[k],
            recv_sem=self.came.at[k],
            device_id=(self.replica, device),
            device_id_type=MESH,
        )

    def start(self, *moves):
        for one in moves:
            self.move(*one).start()
            self.sends.append(one)

    def came_in(self, *moves):
        for k, slot, part in moves:
            self.move(k, slot, part, self.mate).wait_recv()

    def firsts(self):
        me = self.me
        return (
            (1, me, 1, self.across, True),
            (3, me, 2, self.along, True),
            (0, me, 0, self.mate, True),
            (2, me, 2, self.across, True),
            (4, me, 1, self.along, True),
        )

    def one(self):
        self.start(*self.firsts())

    def two(self):
        self.came_in((1, self.across, 1))
        self.start((5, self.across, 1, self.along), (6, self.across, 1, self.mate))
        self.came_in((3, self.along, 2))
        self.start((7, self.along, 2, self.across), (8, self.along, 2, self.mate))

    def three(self):
        self.came_in((2, self.across, 2))
        self.start((9, self.across, 2, self.mate))
        self.came_in((4, self.along, 1))
        self.start((10, self.along, 1, self.mate))

    def four(self):
        self.came_in((5, self.far, 1))
        self.start((11, self.far, 1, self.mate))
        self.came_in((7, self.far, 2))
        self.start((12, self.far, 2, self.mate))

    def finish(self):
        across, along, far = whereabouts_of_mate()
        self.came_in(
            (0, self.mate, 0), (6, across, 1), (8, along, 2), (9, across, 2), (10, along, 1),
            (11, far, 1), (12, far, 2),
        )

    def drain(self):
        for one in self.sends:
            self.move(*one).wait_send()


class Scatter:
    def __init__(self, parts, buffers, sent, came):
        self.parts = parts
        self.pair, self.sums, self.by_far, self.by_side = buffers
        self.sent, self.came = sent, came
        self.tokens = self.pair.shape[1]
        self.replica = lax.axis_index("replica")
        me, mate, across, along, far = whereabouts()
        self.mine, self.shift, self.mate = (me, across, along, far), mate - me, mate
        low, high = pl.ds(0, self.tokens // 2), pl.ds(self.tokens // 2, self.tokens // 2)
        self.low, self.high = low, high
        sums, by_far, by_side = self.sums, self.by_far, self.by_side
        self.swaps = [
            self.move(k, parts.at[block_rows(self.mine[k] + self.shift, self.tokens)], self.pair.at[k], mate)
            for k in range(4)
        ]
        self.far_low = self.move(4, sums.at[2, low], by_far.at[0], across)
        self.far_high = self.move(5, sums.at[2, high], by_far.at[1], along)
        self.across_low = self.move(6, sums.at[0, low], by_side.at[0, low], across)
        self.along_high = self.move(7, sums.at[1, high], by_side.at[1, high], along)
        self.along_low = self.move(8, sums.at[1, low], by_side.at[1, low], along)
        self.across_high = self.move(9, sums.at[0, high], by_side.at[0, high], across)

    def move(self, k, src, dst, device):
        return pltpu.make_async_remote_copy(
            src_ref=src,
            dst_ref=dst,
            send_sem=self.sent.at[k],
            recv_sem=self.came.at[k],
            device_id=(self.replica, device),
            device_id_type=MESH,
        )

    def swap(self, *which):
        for k in which:
            self.swaps[k].start()

    def pair_sum(self, k):
        self.swaps[k].wait_recv()
        own = self.parts[block_rows(self.mine[k], self.tokens), :].astype(F32)
        self.sums[k - 1] = (own + self.pair[k].astype(F32)).astype(BF)

    def send_far(self):
        self.pair_sum(3)
        self.far_low.start()
        self.far_high.start()

    def send_near(self):
        self.pair_sum(1)
        self.across_low.start()
        self.pair_sum(2)
        self.along_high.start()

    def send_rest(self):
        low, high, sums = self.low, self.high, self.sums
        self.far_low.wait_recv()
        sums[1, low] = (sums[1, low].astype(F32) + self.by_far[0].astype(F32)).astype(BF)
        self.along_low.start()
        self.far_high.wait_recv()
        sums[0, high] = (sums[0, high].astype(F32) + self.by_far[1].astype(F32)).astype(BF)
        self.across_high.start()

    def total(self):
        self.swaps[0].wait_recv()
        own = self.parts[block_rows(self.mine[0], self.tokens), :].astype(F32)
        own = own + self.pair[0].astype(F32)
        for copy in (self.across_low, self.along_high, self.along_low, self.across_high):
            copy.wait_recv()
        return own + (self.by_side[0].astype(F32) + self.by_side[1].astype(F32))

    def drain(self):
        for copy in (
            *self.swaps, self.far_low, self.far_high, self.across_low, self.along_high,
            self.along_low, self.across_high,
        ):
            copy.wait_send()


class Line:
    def __init__(self, own, slots, sent, came):
        self.own, self.slots, self.sent, self.came = own, slots, sent, came
        self.replica, self.me = lax.axis_index("replica"), lax.axis_index("shard")
        self.replicas = lax.axis_size("replica")

    def move(self, way, i, slot, first):
        target = self.replica + (1 if way == 0 else -1)
        return pltpu.make_async_remote_copy(
            src_ref=self.own if first else self.slots(slot),
            dst_ref=self.slots(slot),
            send_sem=self.sent.at[way, i],
            recv_sem=self.came.at[way, i],
            device_id=(target, self.me),
            device_id_type=MESH,
        )

    def source(self, way, i):
        return self.replica - i if way == 0 else self.replica + i

    def has(self, way, i):
        return self.replica >= i if way == 0 else self.replica + i < self.replicas

    def can_send(self, way):
        return self.replica + 1 < self.replicas if way == 0 else self.replica >= 1

    def start(self):
        for way in (0, 1):

            @pl.when(self.can_send(way))
            def _(way=way):
                self.move(way, 0, self.replica, True).start()

    def step(self, i):
        for way in (0, 1):

            @pl.when(self.has(way, i))
            def _(way=way):
                self.move(way, i - 1, self.source(way, i), False).wait_recv()
                if i < self.replicas - 1:

                    @pl.when(self.can_send(way))
                    def _():
                        self.move(way, i, self.source(way, i), False).start()

    def drain(self):
        for way in (0, 1):
            for i in range(self.replicas - 1):

                @pl.when(self.has(way, i) & self.can_send(way))
                def _(way=way, i=i):
                    self.move(way, i, self.source(way, i), i == 0).wait_send()


class Hop:
    def __init__(self, k, source, landing, sent, came):
        self.k, self.source, self.landing, self.sent, self.came = k, source, landing, sent, came
        self.replica, self.me = lax.axis_index("replica"), lax.axis_index("shard")
        self.replicas = lax.axis_size("replica")

    def move(self, way):
        return pltpu.make_async_remote_copy(
            src_ref=self.source(way),
            dst_ref=self.landing.at[way],
            send_sem=self.sent.at[way],
            recv_sem=self.came.at[way],
            device_id=(self.replica + (1 if way == 0 else -1), self.me),
            device_id_type=MESH,
        )

    def sends(self, way):
        last = self.replicas - 1
        if way == 0:
            return (self.replica >= self.k - 1) & (self.replica < last)
        return (self.replica <= self.replicas - self.k) & (self.replica > 0)

    def receives(self, way):
        return self.replica >= self.k if way == 0 else self.replica < self.replicas - self.k

    def start(self):
        for way in (0, 1):

            @pl.when(self.sends(way))
            def _(way=way):
                self.move(way).start()

    def arrive(self):
        for way in (0, 1):

            @pl.when(self.receives(way))
            def _(way=way):
                self.move(way).wait_recv()

    def drain(self):
        for way in (0, 1):

            @pl.when(self.sends(way))
            def _(way=way):
                self.move(way).wait_send()


def greet_all(barrier):
    replica, replicas = lax.axis_index("replica"), lax.axis_size("replica")
    me, groups = lax.axis_index("shard"), lax.axis_size("shard")
    for i in range(1, groups):
        device = lax.rem(me + i, groups)
        pl.semaphore_signal(barrier, inc=1, device_id=(replica, device), device_id_type=MESH)

    @pl.when(replica >= 1)
    def _():
        pl.semaphore_signal(barrier, inc=1, device_id=(replica - 1, me), device_id_type=MESH)

    @pl.when(replica + 1 < replicas)
    def _():
        pl.semaphore_signal(barrier, inc=1, device_id=(replica + 1, me), device_id_type=MESH)

    edge = (replica == 0) | (replica == replicas - 1)

    @pl.when(edge)
    def _():
        pl.semaphore_wait(barrier, groups)

    @pl.when(jnp.logical_not(edge))
    def _():
        pl.semaphore_wait(barrier, groups + 1)


def rotate_head(values, cosine, sine):
    return values * cosine + pltpu.roll(values, values.shape[-1] // 2, 1) * sine


def key_reach(first, step, sequence):
    low = max(0, (first + 1 - sequence // 2) // 128 * 128)
    return low, pl.ds(low, first + step - low)


def allowed_bias(start, first, step, low):
    shape = (step, first + step - low)
    key_place = lax.broadcasted_iota(jnp.int32, shape, 1) + low
    query_place = lax.broadcasted_iota(jnp.int32, shape, 0) + first
    return jnp.where((key_place <= query_place) & (key_place >= start), 0.0, masked)


def head_scores(query, keys, bias):
    return product(query, keys, 1, 1) * (1.0 / math.sqrt(HEAD_DIM)) + bias


def fill_tables(lengths, frequency, cosine, sine, start):
    shape = start.shape
    place = lax.broadcasted_iota(jnp.int32, shape, 0)
    begin = jnp.zeros(shape, jnp.int32)
    end = 0
    for i in range(lengths.shape[1] - 1):
        end = end + lengths[0, i]
        begin = jnp.where(place >= end, end, begin)
    start[...] = begin
    angle = (place - begin).astype(F32) * frequency[...]
    lane = lax.broadcasted_iota(jnp.int32, shape, 1)
    cosine[...] = jnp.cos(angle)
    sine[...] = jnp.where(lane < shape[1] // 2, -1.0, 1.0) * jnp.sin(angle)


def front_kernel(
    lengths, frequency, x_own, dy_own, w_query, w_key, w_value, w_out, w_gate, w_up, w_down,
    n1_out, query_out, key_out, value_out, attn_out, attn_b_out, out_columns_out, down_parts,
    down_columns_out, hidden_out, grad_gate_out, grad_up_out, middle_out, n2_out, dy_out, n2_hopped,
    grad_out, grad_all_out, dy_hopped, cosine_out, sine_out, start_out,
    n1, n2, dy, query, key, value, attn, attn_b, out_columns, gate_w, up_w, down_w,
    hidden, grad_gate, grad_up, parts, pair, sums, by_far, by_side, middle, normed, n2_own, grad_own, n1_own, cosine, sine, start,
    load_sem, save_sem, gather_sent, gather_came, scatter_sent, scatter_came,
    swap_sent, swap_came, line_sent, line_came, down_sent, down_came,
):
    replica = lax.axis_index("replica")
    replicas = lax.axis_size("replica")
    me = lax.axis_index("shard")
    groups = lax.axis_size("shard")
    tokens, width = x_own.shape
    sequence = n1.shape[0]
    saves = []

    def save(src, dst):
        copy = pltpu.make_async_copy(src, dst, save_sem.at[len(saves)])
        copy.start()
        saves.append(copy)

    def exchange(which, source, target):
        copies = []
        for i in range(1, groups):
            device = lax.rem(me + i, groups)
            copies.append(
                pltpu.make_async_remote_copy(
                    src_ref=source(device),
                    dst_ref=target,
                    send_sem=swap_sent.at[which, i],
                    recv_sem=swap_came.at[which, i],
                    device_id=(replica, device),
                    device_id_type=MESH,
                )
            )
        return copies

    gate_load = pltpu.make_async_copy(w_gate, gate_w, load_sem.at[0])
    up_load = pltpu.make_async_copy(w_up, up_w, load_sem.at[1])
    gate_load.start()
    up_load.start()
    own_rows = block_rows(me, tokens)
    x = x_own[...].astype(F32)
    center = x - jnp.mean(x, axis=-1, keepdims=True)
    inverse = lax.rsqrt(jnp.mean(center * center, axis=-1, keepdims=True) + epsilon)
    n1_own[...] = (center * inverse).astype(BF)
    own_n1 = pltpu.make_async_copy(n1_own, n1.at[own_rows], load_sem.at[2])
    own_dy = pltpu.make_async_copy(dy_own, dy.at[own_rows], load_sem.at[3])
    own_n1.start()
    own_dy.start()

    greet_all(pltpu.get_barrier_semaphore())
    n1_gather = Gather(n1_own, n1, gather_sent.at[0], gather_came.at[0])
    dy_gather = Gather(dy_own, dy, gather_sent.at[1], gather_came.at[1])
    n2_gather = Gather(n2_own, n2, gather_sent.at[2], gather_came.at[2])
    grad_gather = Gather(grad_own, grad_all_out, gather_sent.at[3], gather_came.at[3])
    half = sequence // 2
    dy_half = dy.at[pl.ds(pl.multiple_of(lax.rem(me, 2) * half, half), half)]
    n2_hop = Hop(1, lambda way: n2_own, n2_hopped, line_sent.at[0], line_came.at[0])
    dy_hop = Hop(1, lambda way: dy_half, dy_hopped, line_sent.at[1], line_came.at[1])
    down_line = Line(
        down_parts.at[replica], lambda s: down_parts.at[s], down_sent, down_came
    )
    buffers = (pair, sums, by_far, by_side)

    n1_gather.one()
    fill_tables(lengths, frequency, cosine, sine, start)
    save(cosine, cosine_out)
    save(sine, sine_out)
    save(start, start_out)
    n1_gather.two()
    n1_gather.three()
    wide = w_out.shape[0]
    mine = pl.ds(pl.multiple_of(me * wide, wide), wide)
    part = down_parts.shape[2]

    def down_block(device):
        column = (device * replicas + replica) * part
        return w_down.at[:, pl.ds(pl.multiple_of(column, part), part)]

    def out_block(device):
        return w_out.at[:, pl.ds(pl.multiple_of(device * wide, wide), wide)]

    down_swaps = exchange(1, down_block, down_parts.at[replica, mine])
    out_swaps = exchange(0, out_block, out_columns.at[mine])
    own_down = pltpu.make_async_copy(down_block(me), down_parts.at[replica, mine], load_sem.at[5])
    own_down.start()
    own_out = pltpu.make_async_copy(out_block(me), out_columns.at[mine], load_sem.at[4])
    own_out.start()
    for copy in down_swaps + out_swaps:
        copy.start()
    n1_gather.four()
    own_n1.wait()
    n1_gather.finish()
    save(n1, n1_out)

    heads = query.shape[1] // HEAD_DIM
    for first in range(0, sequence, 512):
        rows = pl.ds(first, 512)
        for weight, target in ((w_query, query), (w_key, key), (w_value, value)):
            values = product(n1[rows, :], weight[...], 1, 1)
            for head in range(heads):
                lanes = pl.ds(head * HEAD_DIM, HEAD_DIM)
                piece = values[:, head * HEAD_DIM : (head + 1) * HEAD_DIM]
                if target is not value:
                    piece = rotate_head(piece, cosine[rows, :], sine[rows, :])
                target[rows, lanes] = piece.astype(BF)
    save(query, query_out)
    save(key, key_out)
    save(value, value_out)
    own_down.wait()
    for copy in down_swaps:
        copy.wait_recv()
    down_line.start()
    step = 256
    for first in range(0, sequence, step):
        rows = pl.ds(first, step)
        low, reach = key_reach(first, step, sequence)
        bias = allowed_bias(start[rows, 0:1], first, step, low)
        for head in range(heads):
            lanes = pl.ds(head * HEAD_DIM, HEAD_DIM)
            scores = head_scores(query[rows, lanes], key[reach, lanes], bias)
            weights = jnp.exp(scores - jnp.max(scores, axis=-1, keepdims=True))
            total = jnp.sum(weights, axis=-1, keepdims=True)
            result = product(weights.astype(BF), value[reach, lanes], 1, 0) / total
            attn[rows, lanes] = result
            attn_b[rows, lanes] = result.astype(BF)
    save(attn, attn_out)
    save(attn_b, attn_b_out)

    own_out.wait()
    for copy in out_swaps:
        copy.wait_recv()
    save(out_columns, out_columns_out)

    def spread(rows, columns):
        parts[rows, columns] = product(attn_b[rows, :], out_columns[columns, :], 1, 1).astype(BF)

    tile_loop(sequence, width, 512, spread)
    scatter = Scatter(parts, buffers, scatter_sent.at[0], scatter_came.at[0])
    scatter.swap(3, 1, 2, 0)
    scatter.send_far()
    scatter.send_near()
    down_line.step(1)
    scatter.send_rest()
    middle[...] = x_own[...].astype(F32) + scatter.total()
    scatter.drain()
    save(middle, middle_out)
    center = middle[...] - jnp.mean(middle[...], axis=-1, keepdims=True)
    inverse = lax.rsqrt(jnp.mean(center * center, axis=-1, keepdims=True) + epsilon)
    normed[...] = center * inverse
    n2_own[...] = normed[...].astype(BF)
    n2_gather.one()
    own_n2 = pltpu.make_async_copy(n2_own, n2.at[own_rows], load_sem.at[6])
    own_n2.start()
    n2_gather.two()
    n2_gather.three()
    dy_gather.one()
    down_line.step(2)
    n2_hop.start()
    n2_gather.four()
    own_n2.wait()
    n2_gather.finish()
    save(n2, n2_out)
    gate_load.wait()
    up_load.wait()
    row = me // (groups // 2)

    def feed_forward(base):
        def forward(rows, columns):
            rows = pl.ds(pl.multiple_of(base, half), half)
            gate = product(n2[rows, :], gate_w[columns, :], 1, 1)
            up = product(n2[rows, :], up_w[columns, :], 1, 1)
            sigma = 0.5 + 0.5 * jnp.tanh(0.5 * gate)
            silu = gate * sigma
            hidden[rows, columns] = (silu * up).astype(BF)
            grad_gate[rows, columns] = (up * (sigma + silu * (1.0 - sigma))).astype(BF)
            grad_up[rows, columns] = silu.astype(BF)

        tile_loop(half, gate_w.shape[0], half, forward, 256)

    feed_forward((1 - row) * half)
    dy_gather.two()
    dy_gather.three()
    feed_forward(row * half)
    dy_gather.four()
    own_dy.wait()
    dy_gather.finish()
    save(dy, dy_out)
    save(hidden, hidden_out)
    dy_hop.start()
    down_line.step(3)
    down_loads = []
    for r in range(replicas):
        down_loads.append(
            pltpu.make_async_copy(
                down_parts.at[r], down_w.at[:, pl.ds(r * part, part)], load_sem.at[7 + r]
            )
        )
        down_loads[-1].start()
    for copy in down_loads:
        copy.wait()
    save(down_w, down_columns_out)

    back = Scatter(parts, buffers, scatter_sent.at[1], scatter_came.at[1])

    def feed(base):
        def grads(rows, columns):
            rows = pl.ds(pl.multiple_of(base, half), half)
            grad = product(dy[rows, :], down_w[:, columns], 1, 0)
            grad_gate[rows, columns] = (grad * grad_gate[rows, columns].astype(F32)).astype(BF)
            grad_up[rows, columns] = (grad * grad_up[rows, columns].astype(F32)).astype(BF)

        tile_loop(half, gate_w.shape[0], half, grads)

        def backward(rows, columns):
            rows = pl.ds(pl.multiple_of(base, half), half)
            value = product(grad_gate[rows, :], gate_w[:, columns], 1, 0)
            value = value + product(grad_up[rows, :], up_w[:, columns], 1, 0)
            parts[rows, columns] = value.astype(BF)

        tile_loop(half, width, half, backward)

    feed((1 - row) * half)
    back.swap(3, 2)
    back.send_far()
    feed(row * half)
    save(grad_gate, grad_gate_out)
    save(grad_up, grad_up_out)
    back.swap(1, 0)
    back.send_near()
    back.send_rest()
    inner = back.total()
    back.drain()
    inner = (
        inner
        - jnp.mean(inner, axis=-1, keepdims=True)
        - normed[...] * jnp.mean(inner * normed[...], axis=-1, keepdims=True)
    )
    center = middle[...] - jnp.mean(middle[...], axis=-1, keepdims=True)
    inverse = lax.rsqrt(jnp.mean(center * center, axis=-1, keepdims=True) + epsilon)
    normed[...] = dy_own[...].astype(F32) + inverse * inner
    grad_own[...] = normed[...].astype(BF)
    grad_gather.one()
    save(normed, grad_out)
    save(grad_own, grad_all_out.at[own_rows])
    grad_gather.two()
    grad_gather.three()
    grad_gather.four()
    grad_gather.finish()
    n2_hop.arrive()
    dy_hop.arrive()
    for copy in saves:
        copy.wait()
    for copy in out_swaps + down_swaps:
        copy.wait_send()
    for user in (n1_gather, n2_gather, dy_gather, grad_gather, down_line, n2_hop, dy_hop):
        user.drain()


def front(lengths, frequency, x_own, dy_own, w_query, w_key, w_value, w_out, w_gate, w_up, w_down):
    groups, replicas = lax.axis_size("shard"), lax.axis_size("replica")
    tokens, width = x_own.shape
    sequence = tokens * groups
    wide, columns = w_query.shape[0], w_gate.shape[0]
    anywhere, vmem = pl.BlockSpec(memory_space=pl.ANY), pl.BlockSpec(memory_space=VMEM)

    def shape(dims, kind=BF):
        return jax.ShapeDtypeStruct(dims, kind)

    outs = (
        shape((sequence, width)),
        shape((sequence, wide)),
        shape((sequence, wide)),
        shape((sequence, wide)),
        shape((sequence, wide), F32),
        shape((sequence, wide)),
        shape((width, wide)),
        shape((replicas, width, columns // replicas)),
        shape((width, columns)),
        shape((sequence, columns)),
        shape((sequence, columns)),
        shape((sequence, columns)),
        shape((tokens, width), F32),
        shape((sequence, width)),
        shape((sequence, width)),
        shape((2, tokens, width)),
        shape((tokens, width), F32),
        shape((sequence, width)),
        shape((2, sequence // 2, width)),
        shape((sequence, HEAD_DIM), F32),
        shape((sequence, HEAD_DIM), F32),
        shape((sequence, HEAD_DIM), jnp.int32),
    )
    dma = pltpu.SemaphoreType.DMA
    return pl.pallas_call(
        front_kernel,
        out_shape=outs,
        in_specs=[pl.BlockSpec(memory_space=pltpu.SMEM)] + [vmem] * 6 + [anywhere] * 4,
        out_specs=(anywhere,) * len(outs),
        scratch_shapes=[
            pltpu.VMEM((sequence, width), BF),
            pltpu.VMEM((sequence, width), BF),
            pltpu.VMEM((sequence, width), BF),
            pltpu.VMEM((sequence, wide), BF),
            pltpu.VMEM((sequence, wide), BF),
            pltpu.VMEM((sequence, wide), BF),
            pltpu.VMEM((sequence, wide), F32),
            pltpu.VMEM((sequence, wide), BF),
            pltpu.VMEM((width, wide), BF),
            pltpu.VMEM((columns, width), BF),
            pltpu.VMEM((columns, width), BF),
            pltpu.VMEM((width, columns), BF),
            pltpu.VMEM((sequence, columns), BF),
            pltpu.VMEM((sequence, columns), BF),
            pltpu.VMEM((sequence, columns), BF),
            pltpu.VMEM((sequence, width), BF),
            pltpu.VMEM((4, tokens, width), BF),
            pltpu.VMEM((3, tokens, width), BF),
            pltpu.VMEM((2, tokens // 2, width), BF),
            pltpu.VMEM((2, tokens, width), BF),
            pltpu.VMEM((tokens, width), F32),
            pltpu.VMEM((tokens, width), F32),
            pltpu.VMEM((tokens, width), BF),
            pltpu.VMEM((tokens, width), BF),
            pltpu.VMEM((tokens, width), BF),
            pltpu.VMEM((sequence, HEAD_DIM), F32),
            pltpu.VMEM((sequence, HEAD_DIM), F32),
            pltpu.VMEM((sequence, HEAD_DIM), jnp.int32),
            dma((7 + replicas,)),
            dma((24,)),
            dma((4, 13)),
            dma((4, 13)),
            dma((2, 10)),
            dma((2, 10)),
            dma((2, groups)),
            dma((2, groups)),
            dma((2, 2)),
            dma((2, 2)),
            dma((2, replicas)),
            dma((2, replicas)),
        ],
        compiler_params=pltpu.CompilerParams(
            collective_id=3, has_side_effects=True, vmem_limit_bytes=67043328
        ),
        cost_estimate=pl.CostEstimate(
            flops=12 * sequence * width * columns, bytes_accessed=64 * 1024 * 1024, transcendentals=0
        ),
        name="front",
    )(lengths, frequency, x_own, dy_own, w_query, w_key, w_value, w_out, w_gate, w_up, w_down)


def back_kernel(
    x_own, start, cosine, sine, hidden_in, down_in, grad_in, out_columns_in, attn_b_in, attn_in,
    query_in, key_in, value_in, n1_in, w_query, w_key, w_value, n2_near, dy_near, middle, grad_middle,
    layer_out, input_grad, attn_part, out_grad_out, n2_hopped, dy_hopped,
    hidden, down_w, grad, out_columns, attn_b, attn, query, key, value, n1, weights,
    grad_attn, key_grad, value_grad, columns_grad, out_grad, rows_grad, parts,
    pair, sums, by_far, by_side, pair2, sums2, by_far2, by_side2,
    load_sem, save_sem, scatter_sent, scatter_came, line_sent, line_came,
):
    sequence, width = n1.shape
    wide = query.shape[1]
    heads = wide // HEAD_DIM
    pairs = (
        (hidden_in, hidden), (down_in, down_w), (grad_in, grad), (out_columns_in, out_columns),
        (attn_b_in, attn_b), (attn_in, attn), (query_in, query), (key_in, key), (value_in, value),
        (n1_in, n1), (w_query, weights.at[pl.ds(0, wide)]), (w_key, weights.at[pl.ds(wide, wide)]),
        (w_value, weights.at[pl.ds(2 * wide, wide)]),
    )
    loads = [
        pltpu.make_async_copy(src, dst, load_sem.at[i]) for i, (src, dst) in enumerate(pairs)
    ]
    for copy in loads:
        copy.start()
    greet_all(pltpu.get_barrier_semaphore())
    hops = (
        Hop(2, lambda way: n2_near.at[way], n2_hopped, line_sent.at[0], line_came.at[0]),
        Hop(2, lambda way: dy_near.at[way], dy_hopped, line_sent.at[1], line_came.at[1]),
    )
    for hop in hops:
        hop.start()
    loads[0].wait()
    loads[1].wait()

    def mix(rows, columns):
        parts[rows, columns] = product(hidden[rows, :], down_w[columns, :], 1, 1).astype(BF)

    tile_loop(sequence, width, 512, mix)
    mixed = Scatter(parts, (pair, sums, by_far, by_side), scatter_sent.at[0], scatter_came.at[0])
    mixed.swap(3, 1, 2, 0)

    for copy in loads[2:6]:
        copy.wait()
    mixed.send_far()
    mixed.send_near()
    for first in range(0, width, 512):
        rows = pl.ds(first, 512)
        out_grad[rows, :] = product(grad[:, rows], attn_b[...], 0, 0).astype(BF)
    out_save = pltpu.make_async_copy(out_grad, out_grad_out, save_sem.at[0])
    out_save.start()
    for first in range(0, sequence, 512):
        rows = pl.ds(first, 512)
        grad_attn[rows, :] = product(grad[rows, :], out_columns[...], 1, 0).astype(BF)
    for copy in loads[6:]:
        copy.wait()
    mixed.send_rest()

    step = 256
    for first in range(sequence - step, -1, -step):
        rows = pl.ds(first, step)
        low, upto = key_reach(first, step, sequence)
        bias = allowed_bias(start[rows, 0:1], first, step, low)
        for head in range(heads):
            lanes = pl.ds(head * HEAD_DIM, HEAD_DIM)
            query_piece, grad_piece = query[rows, lanes], grad_attn[rows, lanes]
            scores = head_scores(query_piece, key[upto, lanes], bias)
            probs = jnp.exp(scores - jnp.max(scores, axis=-1, keepdims=True))
            probs = probs / jnp.sum(probs, axis=-1, keepdims=True)
            delta = jnp.sum(grad_piece.astype(F32) * attn[rows, lanes], axis=-1, keepdims=True)
            grad_probs = product(grad_piece, value[upto, lanes], 1, 1)
            grad_scores = (probs * (grad_probs - delta)).astype(BF)
            query_grad = product(grad_scores, key[upto, lanes], 1, 0) * (1.0 / math.sqrt(HEAD_DIM))
            query_grad = rotate_head(query_grad, cosine[rows, :], -sine[rows, :])
            columns_grad[rows, lanes] = query_grad.astype(BF)
            key_part = product(grad_scores, query_piece, 0, 0)
            value_part = product(probs.astype(BF), grad_piece, 0, 0)
            if first == sequence - step:
                key_grad[upto, lanes] = key_part
                value_grad[upto, lanes] = value_part
                if low:
                    key_grad[pl.ds(0, low), lanes] = jnp.zeros((low, HEAD_DIM), F32)
                    value_grad[pl.ds(0, low), lanes] = jnp.zeros((low, HEAD_DIM), F32)
            else:
                key_grad[upto, lanes] += key_part
                value_grad[upto, lanes] += value_part
    for head in range(heads):
        lanes = pl.ds(head * HEAD_DIM, HEAD_DIM)
        piece = key_grad[:, lanes] * (1.0 / math.sqrt(HEAD_DIM))
        piece = rotate_head(piece, cosine[...], -sine[...])
        columns_grad[:, pl.ds(wide + head * HEAD_DIM, HEAD_DIM)] = piece.astype(BF)
        columns_grad[:, pl.ds(2 * wide + head * HEAD_DIM, HEAD_DIM)] = value_grad[:, lanes].astype(BF)

    layer_out[...] = (middle[...] + mixed.total()).astype(BF)
    mixed.drain()

    def back(rows, columns):
        parts[rows, columns] = product(columns_grad[rows, :], weights[:, columns], 1, 0).astype(BF)

    tile_loop(sequence, width, 512, back)
    last = Scatter(parts, (pair2, sums2, by_far2, by_side2), scatter_sent.at[1], scatter_came.at[1])
    last.swap(3, 1, 2, 0)
    last.send_far()
    last.send_near()

    def collect(rows, columns):
        rows_grad[rows, columns] = product(columns_grad[:, rows], n1[:, columns], 0, 0).astype(BF)

    tile_loop(3 * wide, width, 256, collect, 512)
    rows_save = pltpu.make_async_copy(rows_grad, attn_part, save_sem.at[1])
    rows_save.start()
    last.send_rest()
    x = x_own[...].astype(F32)
    center = x - jnp.mean(x, axis=-1, keepdims=True)
    inverse = lax.rsqrt(jnp.mean(center * center, axis=-1, keepdims=True) + epsilon)
    inner = last.total()
    normed = center * inverse
    inner = (
        inner
        - jnp.mean(inner, axis=-1, keepdims=True)
        - normed * jnp.mean(inner * normed, axis=-1, keepdims=True)
    )
    input_grad[...] = grad_middle[...] + inverse * inner
    last.drain()
    out_save.wait()
    rows_save.wait()
    for hop in hops:
        hop.arrive()
        hop.drain()


def back(x_own, start, cosine, sine, hidden, down, grad, out_columns, attn_b, attn, query, key, value, n1,
         w_query, w_key, w_value, n2_near, dy_near, middle, grad_middle):
    groups = lax.axis_size("shard")
    tokens, width = x_own.shape
    sequence = tokens * groups
    wide, columns = query.shape[1], hidden.shape[1]
    anywhere, vmem = pl.BlockSpec(memory_space=pl.ANY), pl.BlockSpec(memory_space=VMEM)
    dma = pltpu.SemaphoreType.DMA
    buffers = [
        pltpu.VMEM((4, tokens, width), BF),
        pltpu.VMEM((3, tokens, width), BF),
        pltpu.VMEM((2, tokens // 2, width), BF),
        pltpu.VMEM((2, tokens, width), BF),
    ]
    return pl.pallas_call(
        back_kernel,
        out_shape=(
            jax.ShapeDtypeStruct((tokens, width), BF),
            jax.ShapeDtypeStruct((tokens, width), F32),
            jax.ShapeDtypeStruct((3 * wide, width), BF),
            jax.ShapeDtypeStruct((width, wide), BF),
            jax.ShapeDtypeStruct(n2_near.shape, BF),
            jax.ShapeDtypeStruct(dy_near.shape, BF),
        ),
        in_specs=[vmem] * 4 + [anywhere] * 15 + [vmem] * 2,
        out_specs=(vmem, vmem) + (anywhere,) * 4,
        scratch_shapes=[
            pltpu.VMEM((sequence, columns), BF),
            pltpu.VMEM((width, columns), BF),
            pltpu.VMEM((sequence, width), BF),
            pltpu.VMEM((width, wide), BF),
            pltpu.VMEM((sequence, wide), BF),
            pltpu.VMEM((sequence, wide), F32),
            pltpu.VMEM((sequence, wide), BF),
            pltpu.VMEM((sequence, wide), BF),
            pltpu.VMEM((sequence, wide), BF),
            pltpu.VMEM((sequence, width), BF),
            pltpu.VMEM((3 * wide, width), BF),
            pltpu.VMEM((sequence, wide), BF),
            pltpu.VMEM((sequence, wide), F32),
            pltpu.VMEM((sequence, wide), F32),
            pltpu.VMEM((sequence, 3 * wide), BF),
            pltpu.VMEM((width, wide), BF),
            pltpu.VMEM((3 * wide, width), BF),
            pltpu.VMEM((sequence, width), BF),
            *buffers,
            *buffers,
            dma((13,)),
            dma((2,)),
            dma((2, 10)),
            dma((2, 10)),
            dma((2, 2)),
            dma((2, 2)),
        ],
        compiler_params=pltpu.CompilerParams(
            collective_id=4, has_side_effects=True, vmem_limit_bytes=67043328
        ),
        cost_estimate=pl.CostEstimate(
            flops=24 * sequence * width * wide, bytes_accessed=48 * 1024 * 1024, transcendentals=0
        ),
        name="back",
    )(x_own, start, cosine, sine, hidden, down, grad, out_columns, attn_b, attn, query, key, value, n1,
      w_query, w_key, w_value, n2_near, dy_near, middle, grad_middle)


def every_kernel(
    n2_one, n2_two, dy_one, dy_two, own_normed, own_dy, own_hidden, own_grad_gate, own_grad_up,
    attn_part, out_part,
    w_gate, w_up, w_down,
    gate_out, up_out, out_down, out_attn, landed, kept, dy_other,
    out_rows, n2_three, dy_three,
    normed, dy, hidden, grad_gate, grad_up, gate_w, up_w, down_w, down, out_gate, out_up, first_sum, second_sum, stage,
    load_sem, keep_sem, gather_sent, gather_came, line_sent, line_came, line_own, swap_sent, swap_came,
    out_sem, pair_sem, out_swap_sem, hop_sent, hop_came,
):
    replica = lax.axis_index("replica")
    replicas = lax.axis_size("replica")
    me = lax.axis_index("shard")
    groups = lax.axis_size("shard")
    tokens = n2_one.shape[1]
    sequence, width = normed.shape
    half = sequence // 2
    columns = hidden.shape[1]
    own_rows = block_rows(me, tokens)
    inner = (replica == 1) | (replica == 2)
    outer = (replica == 0) | (replica == 3)
    beside = replica + 1 - 2 * lax.rem(replica, 2)
    facing = 3 - replica
    chunks, depth = first_sum.shape[0], first_sum.shape[1]

    def piece(c):
        return pl.ds(c * depth, depth)

    def line_move(kind, c, src, dst, target):
        return pltpu.make_async_remote_copy(
            src_ref=src,
            dst_ref=dst,
            send_sem=line_sent.at[kind, c],
            recv_sem=line_came.at[kind, c],
            device_id=(target, me),
            device_id_type=MESH,
        )

    attn_chunks = attn_part.shape[0] // depth

    def own_chunk(c):
        return attn_part.at[piece(c)] if c < attn_chunks else out_rows.at[piece(c - attn_chunks)]

    def inward(c):
        return line_move(0, c, own_chunk(c), first_sum.at[c], beside)

    def middle(c):
        return line_move(1, c, first_sum.at[c], second_sum.at[c], facing)

    def outward(c):
        return line_move(2, c, second_sum.at[c], out_attn.at[piece(c)], beside)

    def keep(c):
        return pltpu.make_async_copy(second_sum.at[c], out_attn.at[piece(c)], line_own.at[c])

    def stage_load(c):
        return pltpu.make_async_copy(own_chunk(c), stage, keep_sem.at[2, 0])

    def half_sums(*which):
        @pl.when(inner)
        def _():
            for c in which:
                stage_load(c).wait()
                inward(c).wait_recv()
                first_sum[c] = (stage[...].astype(F32) + first_sum[c].astype(F32)).astype(BF)
                middle(c).start()
                if c + 1 < chunks:
                    stage_load(c + 1).start()

    def full_sums(*which):
        @pl.when(inner)
        def _():
            for c in which:
                middle(c).wait_recv()
                second_sum[c] = (first_sum[c].astype(F32) + second_sum[c].astype(F32)).astype(BF)
                outward(c).start()
                keep(c).start()

    core = lax.rem(me, 2)
    mate = me + 1 - 2 * core
    low_side, high_side = 1 - lax.rem(replica, 2), 1 - replica // 2
    hops = (
        Hop(3, lambda way: n2_two.at[way], n2_three, hop_sent.at[0], hop_came.at[0]),
        Hop(3, lambda way: dy_two.at[way], dy_three, hop_sent.at[1], hop_came.at[1]),
    )
    n2_blocks = {1: n2_one.at[low_side], 2: n2_two.at[high_side]}
    dy_halves = {1: dy_one.at[low_side], 2: dy_two.at[high_side]}
    roles = ((inner, n2_one.at[high_side], dy_one.at[high_side]), (outer, n2_three.at[high_side], dy_three.at[high_side]))

    def gather_of(n, block):
        return Gather(block, landed.at[n - 1], gather_sent.at[n - 1], gather_came.at[n - 1])

    gathers = [gather_of(1, n2_blocks[1]), gather_of(2, n2_blocks[2]), gather_of(3, roles[0][1])]

    def last_one():
        hops[0].arrive()
        for role, block, _ in roles:

            @pl.when(role)
            def _(block=block):
                gather_of(3, block).one()

        gather = gathers[2]
        gather.sends.extend(gather.firsts())

    def pair_copy(n, source):
        return pltpu.make_async_remote_copy(
            src_ref=source,
            dst_ref=dy_other.at[n - 1],
            send_sem=pair_sem.at[0, n - 1],
            recv_sem=pair_sem.at[1, n - 1],
            device_id=(replica, mate),
            device_id_type=MESH,
        )

    def last_pair():
        hops[1].arrive()
        for role, _, source in roles:

            @pl.when(role)
            def _(source=source):
                pair_copy(3, source).start()

    def normed_loads(n, target, base, block=None):
        copies = []
        for i in range(groups):
            device = lax.rem(me + i, groups)
            rows = block_rows(device, tokens)
            source = (n2_blocks[n] if block is None else block) if i == 0 else landed.at[n - 1, rows]
            copies.append(pltpu.make_async_copy(source, target.at[rows], load_sem.at[base, i]))
        return copies

    def dy_loads(n, source=None):
        mine = dy.at[pl.ds(pl.multiple_of(core * half, half), half)]
        others = dy.at[pl.ds(pl.multiple_of((1 - core) * half, half), half)]
        return [
            pltpu.make_async_copy(dy_halves[n] if source is None else source, mine, load_sem.at[1, 0]),
            pltpu.make_async_copy(dy_other.at[n - 1], others, load_sem.at[1, 1]),
        ]

    wide = width // groups

    def out_move(i):
        device = lax.rem(me + i, groups)
        return pltpu.make_async_remote_copy(
            src_ref=out_part.at[pl.ds(pl.multiple_of(device * wide, wide), wide)],
            dst_ref=out_rows.at[:, pl.ds(pl.multiple_of(me * wide, wide), wide)],
            send_sem=out_swap_sem.at[0, i],
            recv_sem=out_swap_sem.at[1, i],
            device_id=(replica, device),
            device_id_type=MESH,
        )

    own_out = pltpu.make_async_copy(
        out_part.at[pl.ds(pl.multiple_of(me * wide, wide), wide)],
        out_rows.at[:, pl.ds(pl.multiple_of(me * wide, wide), wide)],
        out_swap_sem.at[0, 0],
    )

    def out_ready():
        own_out.wait()
        for i in range(1, groups):
            out_move(i).wait_recv()

        @pl.when(outer)
        def _():
            start_all([inward(c) for c in range(attn_chunks, chunks)])

    def keeps(n):
        return [
            pltpu.make_async_copy(grad_gate, kept.at[n - 1, 0], keep_sem.at[0, n]),
            pltpu.make_async_copy(grad_up, kept.at[n - 1, 1], keep_sem.at[1, n]),
        ]

    def start_all(copies):
        for copy in copies:
            copy.start()

    def wait_all(copies):
        for copy in copies:
            copy.wait()

    first = [
        pltpu.make_async_copy(own_normed, normed, load_sem.at[0, 0]),
        pltpu.make_async_copy(own_grad_gate, grad_gate, load_sem.at[0, 1]),
        pltpu.make_async_copy(own_grad_up, grad_up, load_sem.at[0, 2]),
        pltpu.make_async_copy(own_hidden, hidden, load_sem.at[1, 1]),
        pltpu.make_async_copy(own_dy, dy, load_sem.at[1, 0]),
    ]
    weights = [
        pltpu.make_async_copy(w_gate, gate_w, load_sem.at[2, 0]),
        pltpu.make_async_copy(w_up, up_w, load_sem.at[2, 1]),
        pltpu.make_async_copy(w_down, down_w, load_sem.at[2, 2]),
    ]
    start_all(first + weights)
    barrier = pltpu.get_barrier_semaphore()
    for i in range(1, groups):
        device = lax.rem(me + i, groups)
        pl.semaphore_signal(barrier, inc=1, device_id=(replica, device), device_id_type=MESH)
    pl.semaphore_signal(barrier, inc=1, device_id=(beside, me), device_id_type=MESH)

    @pl.when(inner)
    def _():
        pl.semaphore_signal(barrier, inc=1, device_id=(facing, me), device_id_type=MESH)
        pl.semaphore_wait(barrier, groups + 1)

    @pl.when(outer)
    def _():
        pl.semaphore_wait(barrier, groups)

    gathers[0].one()
    pair_copy(1, dy_halves[1]).start()
    pair_copy(2, dy_halves[2]).start()
    own_out.start()
    for hop in hops:
        hop.start()

    @pl.when(outer)
    def _():
        start_all([inward(c) for c in range(attn_chunks)])

    @pl.when(inner)
    def _():
        stage_load(0).start()

    def collect(out, left, right, add):
        def step(rows, cols):
            value = product(left[:, rows], right[:, cols], 0, 0)
            if add is None:
                out[rows, cols] = value
            elif add is True:
                out[rows, cols] += value

        tile_loop(out.shape[0], out.shape[1], 512, step)

    wait_all(first[:3])
    collect(out_gate, grad_gate, normed, None)
    gathers[0].two()
    collect(out_up, grad_up, normed, None)
    gathers[0].three()
    for i in range(1, groups):
        out_move(i).start()
    gathers[1].one()
    gathers[0].four()
    gathers[0].finish()
    start_all(normed_loads(1, normed, 0))
    pair_copy(1, dy_halves[1]).wait()
    pair_copy(2, dy_halves[2]).wait()
    wait_all(first[3:])
    collect(down, dy, hidden, None)
    start_all(dy_loads(1))
    half_sums(0)
    wait_all(weights)
    wait_all(normed_loads(1, normed, 0))
    wait_all(dy_loads(1))

    near, further, last_normed = gathers
    agenda = {
        (1, 0): (out_ready,),
        (1, 1): (further.two,),
        (1, 3): (further.three, lambda: half_sums(1)),
        (1, 5): (further.four,),
        (1, 7): (further.finish, lambda: full_sums(0)),
        (2, 0): (last_one,),
        (2, 2): (lambda: half_sums(3),),
        (2, 3): (last_normed.two,),
        (2, 4): (last_pair,),
        (2, 5): (last_normed.three,),
        (2, 6): (lambda: full_sums(2),),
        (2, 7): (last_normed.four,),
        (3, 1): (lambda: half_sums(5),),
        (3, 5): (lambda: full_sums(4),),
        (3, 7): (lambda: half_sums(6),),
    }

    def after_down(n):
        wait_all(keeps(n))
        if n == 1:
            half_sums(2)
            full_sums(1)
            start_all(dy_loads(2))
            wait_all(normed_loads(2, normed, 0))
            wait_all(dy_loads(2))
        else:
            half_sums(4)
            full_sums(3)
            for role, block, source in roles:

                @pl.when(role)
                def _(block=block, source=source):
                    pair_copy(3, source).wait()
                    start_all(dy_loads(3, source))
                    wait_all(normed_loads(3, normed, 0, block))
                    wait_all(dy_loads(3, source))

    def sequence_step(n, carry):
        narrow = 256
        across = columns // narrow

        def one_tile(i, carry):
            ffn_tile(
                normed, dy, gate_w, up_w, down_w, hidden, grad_gate, grad_up,
                pl.ds(pl.multiple_of((i // across) * 512, 512), 512),
                pl.ds(pl.multiple_of(lax.rem(i, across) * narrow, narrow), narrow),
            )
            for (when, tile), actions in agenda.items():

                @pl.when((n == when) & (i == tile))
                def _(actions=actions):
                    for action in actions:
                        action()

            return carry

        lax.fori_loop(0, (sequence // 512) * across, one_tile, 0)
        for k in (1, 2):

            @pl.when(n == k)
            def _(k=k):
                start_all(keeps(k))
                if k == 1:
                    start_all(normed_loads(2, normed, 0))
                else:
                    last_normed.finish()
                    for role, block, _ in roles:

                        @pl.when(role)
                        def _(block=block):
                            start_all(normed_loads(3, normed, 0, block))

        @pl.when(n < 3)
        def _():
            collect(down, dy, hidden, True)

        for k in (1, 2):

            @pl.when(n == k)
            def _(k=k):
                after_down(k)

        return carry

    lax.fori_loop(1, 4, sequence_step, 0)
    one_gate, one_up = up_w.at[:, pl.ds(0, columns)], up_w.at[:, pl.ds(columns, columns)]
    one_loads = normed_loads(1, gate_w, 2) + [
        pltpu.make_async_copy(kept.at[0, 0], one_gate, keep_sem.at[0, 0]),
        pltpu.make_async_copy(kept.at[0, 1], one_up, keep_sem.at[1, 0]),
    ]
    start_all(one_loads)

    wide = width // groups
    _, _, across_device, along_device, far_device = whereabouts()

    def down_move(send_index, recv_index, row, sender, device):
        return pltpu.make_async_remote_copy(
            src_ref=down_w.at[pl.ds(pl.multiple_of(row, wide), wide)],
            dst_ref=out_down.at[:, pl.ds(pl.multiple_of(sender * columns, columns), columns)],
            send_sem=swap_sent.at[send_index],
            recv_sem=swap_came.at[recv_index],
            device_id=(replica, device),
            device_id_type=MESH,
        )

    swaps, arrivals = [], []
    for i, device in enumerate((far_device, across_device, along_device, me)):
        chip = device // 2
        rows = pl.ds(pl.multiple_of(chip * 2 * wide, 2 * wide), 2 * wide)

        def finish_down(j, carry, rows=rows):
            cols = pl.ds(pl.multiple_of(j * 512, 512), 512)
            down[rows, cols] += product(dy[:, rows], hidden[:, cols], 0, 0)
            return carry

        lax.fori_loop(0, columns // 512, finish_down, 0)
        down_w[i * 2 * wide : (i + 1) * 2 * wide, :] = down[rows, :].astype(BF)
        for k in range(2):
            if i < 3:
                row, peer = (2 * i + k) * wide, chip * 2 + k
                swaps.append(down_move(2 * i + k, 2 * i + core, row, me, peer))
                swaps[-1].start()
                arrivals.append(down_move(2 * i + k, 2 * i + k, row, peer, peer))
    swaps.append(down_move(6, 6, (6 + lax.rem(mate, 2)) * wide, me, mate))
    swaps[-1].start()
    arrivals.append(down_move(6, 6, 6 * wide, mate, mate))
    own_slab = pltpu.make_async_copy(
        down_w.at[pl.ds(pl.multiple_of((6 + core) * wide, wide), wide)],
        out_down.at[:, pl.ds(pl.multiple_of(me * columns, columns), columns)],
        keep_sem.at[2, 1],
    )
    own_slab.start()
    two_gate = pltpu.make_async_copy(kept.at[1, 0], hidden, keep_sem.at[0, 3])
    two_gate.start()
    half_sums(7)
    full_sums(5)
    wait_all(one_loads)
    two_loads = normed_loads(2, dy, 0)
    start_all(two_loads)

    def collect_pair(out, *pairs):
        def step(rows, cols):
            value = product(pairs[0][0][:, rows], pairs[0][1][:, cols], 0, 0)
            for left, right in pairs[1:]:
                value = value + product(left[:, rows], right[:, cols], 0, 0)
            out[rows, cols] += value

        tile_loop(out.shape[0], out.shape[1], 512, step)

    collect_pair(out_gate, (grad_gate, normed), (one_gate, gate_w))
    full_sums(6)
    wait_all(two_loads)
    two_gate.wait()
    collect_pair(out_gate, (hidden, dy))
    gate_save = pltpu.make_async_copy(out_gate, gate_out, out_sem.at[0])
    gate_save.start()
    two_up = pltpu.make_async_copy(kept.at[1, 1], grad_gate, keep_sem.at[1, 3])
    two_up.start()
    full_sums(7)
    collect_pair(out_up, (grad_up, normed), (one_up, gate_w))
    two_up.wait()
    up_saves = []
    for i in range(out_up.shape[0] // 512):
        rows = pl.ds(i * 512, 512)

        def last_up(j, carry, rows=rows):
            cols = pl.ds(pl.multiple_of(j * 512, 512), 512)
            out_up[rows, cols] += product(grad_gate[:, rows], dy[:, cols], 0, 0)
            return carry

        lax.fori_loop(0, width // 512, last_up, 0)
        up_saves.append(pltpu.make_async_copy(out_up.at[rows], up_out.at[rows], out_sem.at[1 + i]))
        up_saves[-1].start()

    @pl.when(outer)
    def _():
        for c in range(chunks):
            inward(c).wait_send()
            outward(c).wait_recv()

    @pl.when(inner)
    def _():
        for c in range(chunks):
            middle(c).wait_send()
            outward(c).wait_send()
            keep(c).wait()

    for copy in swaps:
        copy.wait_send()
    for copy in arrivals:
        copy.wait_recv()
    own_slab.wait()
    for i in range(1, groups):
        out_move(i).wait_send()
    for hop in hops:
        hop.drain()
    gate_save.wait()
    wait_all(up_saves)
    for gather in gathers:
        gather.drain()


def ffn_grads(n2_one, n2_two, dy_one, dy_two, n2, dy_all, own, attn_part, out_part, w_gate, w_up, w_down_columns):
    _, tokens, width = n2_one.shape
    sequence = n2.shape[0]
    groups = sequence // tokens
    columns = w_gate.shape[0]
    chunks = 8
    attn_rows = attn_part.shape[0] + out_part.shape[1]
    depth = attn_rows // chunks
    anywhere = pl.BlockSpec(memory_space=pl.ANY)
    dma = pltpu.SemaphoreType.DMA
    out = pl.pallas_call(
        every_kernel,
        out_shape=(
            jax.ShapeDtypeStruct((columns, width), F32),
            jax.ShapeDtypeStruct((columns, width), F32),
            jax.ShapeDtypeStruct((width // groups, columns * groups), BF),
            jax.ShapeDtypeStruct((attn_rows, width), BF),
            jax.ShapeDtypeStruct((3, sequence, width), BF),
            jax.ShapeDtypeStruct((2, 2, sequence, columns), BF),
            jax.ShapeDtypeStruct((3, sequence // 2, width), BF),
            jax.ShapeDtypeStruct((out_part.shape[1], width), BF),
            jax.ShapeDtypeStruct(n2_two.shape, BF),
            jax.ShapeDtypeStruct(dy_two.shape, BF),
        ),
        in_specs=[anywhere] * 14,
        out_specs=(anywhere,) * 10,
        scratch_shapes=[
            pltpu.VMEM((sequence, width), BF),
            pltpu.VMEM((sequence, width), BF),
            pltpu.VMEM((sequence, columns), BF),
            pltpu.VMEM((sequence, columns), BF),
            pltpu.VMEM((sequence, columns), BF),
            pltpu.VMEM((columns, width), BF),
            pltpu.VMEM((columns, width), BF),
            pltpu.VMEM((width, columns), BF),
            pltpu.VMEM((width, columns), F32),
            pltpu.VMEM((columns, width), F32),
            pltpu.VMEM((columns, width), F32),
            pltpu.VMEM((chunks, depth, width), BF),
            pltpu.VMEM((chunks, depth, width), BF),
            pltpu.VMEM((depth, width), BF),
            dma((3, groups)),
            dma((3, 4)),
            dma((3, 13)),
            dma((3, 13)),
            dma((3, chunks)),
            dma((3, chunks)),
            dma((chunks,)),
            dma((groups,)),
            dma((groups,)),
            dma((1 + columns // 512,)),
            dma((2, 3)),
            dma((2, groups)),
            dma((2, 2)),
            dma((2, 2)),
        ],
        compiler_params=pltpu.CompilerParams(
            collective_id=2, has_side_effects=True, vmem_limit_bytes=67043328
        ),
        cost_estimate=pl.CostEstimate(
            flops=42 * sequence * width * columns, bytes_accessed=80 * 1024 * 1024, transcendentals=0
        ),
        name="ffn_grads",
    )(n2_one, n2_two, dy_one, dy_two, n2, dy_all, *own, attn_part, out_part, w_gate, w_up, w_down_columns)
    return out[:4]


def gather_tokens(values):
    return lax.all_gather(values, "shard", axis=0, tiled=True)


def scatter_tokens(partial):
    return lax.psum_scatter(
        partial.astype(BF), "shard", scatter_dimension=0, tiled=True
    ).astype(F32)


def rows_to_columns(weight):
    return lax.all_to_all(weight, "shard", split_axis=1, concat_axis=0, tiled=True)


def columns_to_rows(grad):
    return lax.all_to_all(grad, "shard", split_axis=0, concat_axis=1, tiled=True)


def replica_sum(part):
    return lax.psum(part.astype(BF), "replica")


def general_body(hidden_in, cotangent, doc_lengths, w_query, w_key, w_value, w_out, w_gate, w_up, w_down):
    x = hidden_in[0].astype(F32)
    dyb = cotangent[0]
    tokens_here = x.shape[0]
    groups = lax.axis_size("shard")
    seq_length = tokens_here * groups
    factor = 1.0 / math.sqrt(HEAD_DIM)
    places = jnp.arange(seq_length, dtype=jnp.int32)
    segment, offset = doc_layout(doc_lengths[0], places)
    cosine, sine = rope_tables(offset, HEAD_DIM)
    allowed = ((segment[:, None] == segment[None, :]) & (places[None, :] <= places[:, None]))[None]

    normed_one, inverse_one = normalize(x)
    n1 = gather_tokens(normed_one.astype(BF))
    w_out_columns = rows_to_columns(w_out)
    query = rotate(split_heads(dot(n1, w_query, 1, 1)), cosine, sine).astype(BF)
    keys = rotate(split_heads(dot(n1, w_key, 1, 1)), cosine, sine).astype(BF)
    values = split_heads(dot(n1, w_value, 1, 1)).astype(BF)
    scores = factor * jnp.einsum("hqe,hke->hqk", query, keys, preferred_element_type=F32)
    scores = jnp.where(allowed, scores, masked)
    top = jnp.max(scores, axis=-1, keepdims=True)
    weights = jnp.where(allowed, jnp.exp(scores - top), 0.0)
    total = jnp.sum(weights, axis=-1, keepdims=True)
    log_total = top + jnp.log(total)
    attn = jnp.einsum("hqk,hke->hqe", weights.astype(BF), values, preferred_element_type=F32) / total
    out_b = join_heads(attn).astype(BF)
    middle = x + scatter_tokens(dot(out_b, w_out_columns, 1, 1))

    normed_two, inverse_two = normalize(middle)
    n2 = gather_tokens(normed_two.astype(BF))
    dy_all = gather_tokens(dyb)
    w_down_columns = rows_to_columns(w_down)
    gate = dot(n2, w_gate, 1, 1)
    up = dot(n2, w_up, 1, 1)
    sigma = jax.nn.sigmoid(gate)
    silu = gate * sigma
    hidden = (silu * up).astype(BF)
    grad_down = columns_to_rows(replica_sum(dot(dy_all, hidden, 0, 0)))
    grad_hidden = dot(dy_all, w_down_columns, 1, 0)
    grad_gate_b = (grad_hidden * up * sigma * (1.0 + gate * (1.0 - sigma))).astype(BF)
    grad_up_b = (grad_hidden * silu).astype(BF)
    grad_gate = replica_sum(dot(grad_gate_b, n2, 0, 0).astype(BF))
    grad_up = replica_sum(dot(grad_up_b, n2, 0, 0).astype(BF))
    grad_normed_two = scatter_tokens(dot(grad_gate_b, w_gate, 1, 0) + dot(grad_up_b, w_up, 1, 0))
    mixed = scatter_tokens(dot(hidden, w_down_columns, 1, 1))
    layer_out = (middle + mixed).astype(BF)
    grad_middle = dyb.astype(F32) + norm_back(normed_two, inverse_two, grad_normed_two)

    grad_middle_all = gather_tokens(grad_middle.astype(BF))
    grad_out = columns_to_rows(replica_sum(dot(grad_middle_all, out_b, 0, 0).astype(BF)))
    grad_attn = split_heads(dot(grad_middle_all, w_out_columns, 1, 0)).astype(BF)
    delta = jnp.sum(grad_attn.astype(F32) * attn, axis=-1, keepdims=True)
    probs = jnp.where(allowed, jnp.exp(scores - log_total), 0.0)
    grad_probs = jnp.einsum("hqe,hke->hqk", grad_attn, values, preferred_element_type=F32)
    grad_scores = (probs * (grad_probs - delta)).astype(BF)
    query_grad = factor * jnp.einsum("hqk,hke->hqe", grad_scores, keys, preferred_element_type=F32)
    key_grad = factor * jnp.einsum("hqk,hqe->hke", grad_scores, query, preferred_element_type=F32)
    value_grad = jnp.einsum("hqk,hqe->hke", probs.astype(BF), grad_attn, preferred_element_type=F32)
    query_grad = join_heads(rotate(query_grad, cosine, -sine)).astype(BF)
    key_grad = join_heads(rotate(key_grad, cosine, -sine)).astype(BF)
    value_grad = join_heads(value_grad).astype(BF)
    grad_query = replica_sum(dot(query_grad, n1, 0, 0).astype(BF))
    grad_key = replica_sum(dot(key_grad, n1, 0, 0).astype(BF))
    grad_value = replica_sum(dot(value_grad, n1, 0, 0).astype(BF))
    grad_normed_one = scatter_tokens(
        dot(query_grad, w_query, 1, 0) + dot(key_grad, w_key, 1, 0) + dot(value_grad, w_value, 1, 0)
    )
    grad_in = grad_middle + norm_back(normed_one, inverse_one, grad_normed_one)
    return (
        layer_out[None],
        grad_in[None],
        grad_query.astype(F32),
        grad_key.astype(F32),
        grad_value.astype(F32),
        grad_out.astype(F32),
        grad_gate.astype(F32),
        grad_up.astype(F32),
        grad_down.astype(F32),
    )


def body(hidden_in, cotangent, doc_lengths, w_query, w_key, w_value, w_out, w_gate, w_up, w_down):
    x_own, dy_own = hidden_in[0], cotangent[0]
    half = HEAD_DIM // 2
    frequency = theta_base ** (-2.0 * (np.arange(HEAD_DIM) % half) / HEAD_DIM)
    (
        n1, query, key, value, attn, attn_b, out_columns, _, down_columns,
        hidden, grad_gate_b, grad_up_b, middle, n2, dy, n2_one, grad_middle, grad_all, dy_one,
        cosine, sine, start,
    ) = front(
        doc_lengths, jnp.asarray(frequency[None], F32), x_own, dy_own,
        w_query, w_key, w_value, w_out, w_gate, w_up, w_down,
    )
    layer_out, grad_in, attn_part, out_part, n2_two, dy_two = back(
        x_own, start, cosine, sine, hidden, down_columns, grad_all, out_columns, attn_b, attn,
        query, key, value, n1, w_query, w_key, w_value, n2_one, dy_one, middle, grad_middle,
    )
    grad_gate, grad_up, grad_down, attn_sum = ffn_grads(
        n2_one, n2_two, dy_one, dy_two, n2, dy, (hidden, grad_gate_b, grad_up_b),
        attn_part, out_part, w_gate, w_up, down_columns,
    )
    grad_query, grad_key, grad_value, grad_out = jnp.split(attn_sum.astype(F32), 4, axis=0)
    return (
        layer_out[None],
        grad_in[None],
        grad_query,
        grad_key,
        grad_value,
        grad_out,
        grad_gate,
        grad_up,
        grad_down.astype(F32),
    )


def solution(mesh):
    rows = P("shard", None)
    tokens = P("replica", "shard", None)
    in_specs = (tokens, tokens, P("replica", None)) + (rows,) * 7
    out_specs = (tokens, tokens) + (rows,) * 7
    local = body if mesh.shape["shard"] == 8 and mesh.shape["replica"] == 4 else general_body
    return jax.shard_map(local, mesh=mesh, in_specs=in_specs, out_specs=out_specs, check_vma=False)
```

```python
import functools
import math

import jax
import jax.numpy as jnp
import numpy as np
from jax import lax
from jax.experimental import pallas as pl
from jax.experimental.pallas import tpu as pltpu
from jax.sharding import PartitionSpec as P

HEAD_DIM = 128

epsilon = 1e-05
theta_base = 10000.0
masked = -1e30
BF = jnp.bfloat16
F32 = jnp.float32
MESH = pl.DeviceIdType.MESH
VMEM = pltpu.VMEM


def normalize(values):
    center = values - jnp.mean(values, axis=-1, keepdims=True)
    inverse = lax.rsqrt(jnp.mean(center * center, axis=-1, keepdims=True) + epsilon)
    return (center * inverse, inverse)


def norm_back(normed, inverse, grad):
    inner = (
        grad
        - jnp.mean(grad, axis=-1, keepdims=True)
        - normed * jnp.mean(grad * normed, axis=-1, keepdims=True)
    )
    return inverse * inner


def dot(a, b, ca, cb):
    return lax.dot_general(a, b, (((ca,), (cb,)), ((), ())), preferred_element_type=F32)


def doc_layout(lengths, places):
    ends = jnp.cumsum(lengths)
    starts = ends - lengths
    segment = jnp.sum((places[:, None] >= ends[None, :]).astype(jnp.int32), axis=1)
    member = segment[:, None] == jnp.arange(lengths.shape[0], dtype=jnp.int32)[None, :]
    offset = places - jnp.sum(jnp.where(member, starts[None, :], 0), axis=1)
    return (segment, offset)


def rope_tables(offset, head_dim):
    half = head_dim // 2
    freq = theta_base ** (-2.0 * jnp.arange(half, dtype=F32) / head_dim)
    angle = offset.astype(F32)[:, None] * freq[None, :]
    return (jnp.cos(angle)[None], jnp.sin(angle)[None])


def rotate(values, cosine, sine):
    half = values.shape[-1] // 2
    first = values[..., :half]
    second = values[..., half:]
    return jnp.concatenate(
        [first * cosine - second * sine, second * cosine + first * sine], axis=-1
    )


def split_heads(values):
    tokens, width = values.shape
    return jnp.transpose(values.reshape(tokens, width // HEAD_DIM, HEAD_DIM), (1, 0, 2))


def join_heads(values):
    heads, tokens, size = values.shape
    return jnp.transpose(values, (1, 0, 2)).reshape(tokens, heads * size)


def whereabouts():
    place = lax.axis_index("shard")
    core, col, row = lax.rem(place, 2), lax.rem(place // 2, 2), place // 4
    across, along = place + 2 - 4 * col, place + 4 - 8 * row
    return place, place + 1 - 2 * core, across, along, across + 4 - 8 * row


def whereabouts_of_mate():
    me, mate, across, along, far = whereabouts()
    shift = mate - me
    return across + shift, along + shift, far + shift


def tile_loop(rows, columns, size, step, narrow=None):
    narrow = narrow or size
    across = columns // narrow

    def one(i, carry):
        step(
            pl.ds(pl.multiple_of((i // across) * size, size), size),
            pl.ds(pl.multiple_of(lax.rem(i, across) * narrow, narrow), narrow),
        )
        return carry

    lax.fori_loop(0, (rows // size) * across, one, 0)


def product(a, b, ca, cb):
    return lax.dot_general(a, b, (((ca,), (cb,)), ((), ())), preferred_element_type=F32)


def ffn_tile(normed, dy, w_gate, w_up, w_down, hidden, grad_gate, grad_up, rows, columns):
    gate = product(normed[rows, :], w_gate[columns, :], 1, 1)
    up = product(normed[rows, :], w_up[columns, :], 1, 1)
    grad = product(dy[rows, :], w_down[:, columns], 1, 0)
    sigma = 0.5 + 0.5 * jnp.tanh(0.5 * gate)
    silu = gate * sigma
    hidden[rows, columns] = (silu * up).astype(BF)
    grad_gate[rows, columns] = (grad * (up * (sigma + silu * (1.0 - sigma)))).astype(BF)
    grad_up[rows, columns] = (grad * silu).astype(BF)


def block_rows(slot, tokens, part=0):
    size = tokens // 2
    if part:
        return pl.ds(pl.multiple_of(slot * tokens + (part - 1) * size, size), size)
    return pl.ds(pl.multiple_of(slot * tokens, tokens), tokens)


class Gather:
    def __init__(self, block, out, sent, came):
        self.block, self.out, self.sent, self.came = block, out, sent, came
        self.tokens = block.shape[0]
        self.replica = lax.axis_index("replica")
        self.me, self.mate, self.across, self.along, self.far = whereabouts()
        self.sends = []

    def move(self, k, slot, part, device, first=False):
        tokens = self.tokens
        local = pl.ds((part - 1) * (tokens // 2) if part else 0, tokens // 2 if part else tokens)
        rows = block_rows(slot, tokens, part)
        return pltpu.make_async_remote_copy(
            src_ref=self.block.at[local] if first else self.out.at[rows],
            dst_ref=self.out.at[rows],
            send_sem=self.sent.at[k],
            recv_sem=self.came.at[k],
            device_id=(self.replica, device),
            device_id_type=MESH,
        )

    def start(self, *moves):
        for one in moves:
            self.move(*one).start()
            self.sends.append(one)

    def came_in(self, *moves):
        for k, slot, part in moves:
            self.move(k, slot, part, self.mate).wait_recv()

    def firsts(self):
        me = self.me
        return (
            (1, me, 1, self.across, True),
            (3, me, 2, self.along, True),
            (0, me, 0, self.mate, True),
            (2, me, 2, self.across, True),
            (4, me, 1, self.along, True),
        )

    def one(self):
        self.start(*self.firsts())

    def two(self):
        self.came_in((1, self.across, 1))
        self.start((5, self.across, 1, self.along), (6, self.across, 1, self.mate))
        self.came_in((3, self.along, 2))
        self.start((7, self.along, 2, self.across), (8, self.along, 2, self.mate))

    def three(self):
        self.came_in((2, self.across, 2))
        self.start((9, self.across, 2, self.mate))
        self.came_in((4, self.along, 1))
        self.start((10, self.along, 1, self.mate))

    def four(self):
        self.came_in((5, self.far, 1))
        self.start((11, self.far, 1, self.mate))
        self.came_in((7, self.far, 2))
        self.start((12, self.far, 2, self.mate))

    def finish(self):
        across, along, far = whereabouts_of_mate()
        self.came_in(
            (0, self.mate, 0), (6, across, 1), (8, along, 2), (9, across, 2), (10, along, 1),
            (11, far, 1), (12, far, 2),
        )

    def drain(self):
        for one in self.sends:
            self.move(*one).wait_send()


class Scatter:
    def __init__(self, parts, buffers, sent, came):
        self.parts = parts
        self.pair, self.sums, self.by_far, self.by_side = buffers
        self.sent, self.came = sent, came
        self.tokens = self.pair.shape[1]
        self.replica = lax.axis_index("replica")
        me, mate, across, along, far = whereabouts()
        self.mine, self.shift, self.mate = (me, across, along, far), mate - me, mate
        low, high = pl.ds(0, self.tokens // 2), pl.ds(self.tokens // 2, self.tokens // 2)
        self.low, self.high = low, high
        sums, by_far, by_side = self.sums, self.by_far, self.by_side
        self.swaps = [
            self.move(k, parts.at[block_rows(self.mine[k] + self.shift, self.tokens)], self.pair.at[k], mate)
            for k in range(4)
        ]
        self.far_low = self.move(4, sums.at[2, low], by_far.at[0], across)
        self.far_high = self.move(5, sums.at[2, high], by_far.at[1], along)
        self.across_low = self.move(6, sums.at[0, low], by_side.at[0, low], across)
        self.along_high = self.move(7, sums.at[1, high], by_side.at[1, high], along)
        self.along_low = self.move(8, sums.at[1, low], by_side.at[1, low], along)
        self.across_high = self.move(9, sums.at[0, high], by_side.at[0, high], across)

    def move(self, k, src, dst, device):
        return pltpu.make_async_remote_copy(
            src_ref=src,
            dst_ref=dst,
            send_sem=self.sent.at[k],
            recv_sem=self.came.at[k],
            device_id=(self.replica, device),
            device_id_type=MESH,
        )

    def swap(self, *which):
        for k in which:
            self.swaps[k].start()

    def pair_sum(self, k):
        self.swaps[k].wait_recv()
        own = self.parts[block_rows(self.mine[k], self.tokens), :].astype(F32)
        self.sums[k - 1] = (own + self.pair[k].astype(F32)).astype(BF)

    def send_far(self):
        self.pair_sum(3)
        self.far_low.start()
        self.far_high.start()

    def send_near(self):
        self.pair_sum(1)
        self.across_low.start()
        self.pair_sum(2)
        self.along_high.start()

    def send_rest(self):
        low, high, sums = self.low, self.high, self.sums
        self.far_low.wait_recv()
        sums[1, low] = (sums[1, low].astype(F32) + self.by_far[0].astype(F32)).astype(BF)
        self.along_low.start()
        self.far_high.wait_recv()
        sums[0, high] = (sums[0, high].astype(F32) + self.by_far[1].astype(F32)).astype(BF)
        self.across_high.start()

    def total(self):
        self.swaps[0].wait_recv()
        own = self.parts[block_rows(self.mine[0], self.tokens), :].astype(F32)
        own = own + self.pair[0].astype(F32)
        for copy in (self.across_low, self.along_high, self.along_low, self.across_high):
            copy.wait_recv()
        return own + (self.by_side[0].astype(F32) + self.by_side[1].astype(F32))

    def drain(self):
        for copy in (
            *self.swaps, self.far_low, self.far_high, self.across_low, self.along_high,
            self.along_low, self.across_high,
        ):
            copy.wait_send()


class Line:
    def __init__(self, own, slots, sent, came):
        self.own, self.slots, self.sent, self.came = own, slots, sent, came
        self.replica, self.me = lax.axis_index("replica"), lax.axis_index("shard")
        self.replicas = lax.axis_size("replica")

    def move(self, way, i, slot, first):
        target = self.replica + (1 if way == 0 else -1)
        return pltpu.make_async_remote_copy(
            src_ref=self.own if first else self.slots(slot),
            dst_ref=self.slots(slot),
            send_sem=self.sent.at[way, i],
            recv_sem=self.came.at[way, i],
            device_id=(target, self.me),
            device_id_type=MESH,
        )

    def source(self, way, i):
        return self.replica - i if way == 0 else self.replica + i

    def has(self, way, i):
        return self.replica >= i if way == 0 else self.replica + i < self.replicas

    def can_send(self, way):
        return self.replica + 1 < self.replicas if way == 0 else self.replica >= 1

    def start(self):
        for way in (0, 1):

            @pl.when(self.can_send(way))
            def _(way=way):
                self.move(way, 0, self.replica, True).start()

    def step(self, i):
        for way in (0, 1):

            @pl.when(self.has(way, i))
            def _(way=way):
                self.move(way, i - 1, self.source(way, i), False).wait_recv()
                if i < self.replicas - 1:

                    @pl.when(self.can_send(way))
                    def _():
                        self.move(way, i, self.source(way, i), False).start()

    def drain(self):
        for way in (0, 1):
            for i in range(self.replicas - 1):

                @pl.when(self.has(way, i) & self.can_send(way))
                def _(way=way, i=i):
                    self.move(way, i, self.source(way, i), i == 0).wait_send()


class Hop:
    def __init__(self, k, source, landing, sent, came):
        self.k, self.source, self.landing, self.sent, self.came = k, source, landing, sent, came
        self.replica, self.me = lax.axis_index("replica"), lax.axis_index("shard")
        self.replicas = lax.axis_size("replica")

    def move(self, way):
        return pltpu.make_async_remote_copy(
            src_ref=self.source(way),
            dst_ref=self.landing.at[way],
            send_sem=self.sent.at[way],
            recv_sem=self.came.at[way],
            device_id=(self.replica + (1 if way == 0 else -1), self.me),
            device_id_type=MESH,
        )

    def sends(self, way):
        last = self.replicas - 1
        if way == 0:
            return (self.replica >= self.k - 1) & (self.replica < last)
        return (self.replica <= self.replicas - self.k) & (self.replica > 0)

    def receives(self, way):
        return self.replica >= self.k if way == 0 else self.replica < self.replicas - self.k

    def start(self):
        for way in (0, 1):

            @pl.when(self.sends(way))
            def _(way=way):
                self.move(way).start()

    def arrive(self):
        for way in (0, 1):

            @pl.when(self.receives(way))
            def _(way=way):
                self.move(way).wait_recv()

    def drain(self):
        for way in (0, 1):

            @pl.when(self.sends(way))
            def _(way=way):
                self.move(way).wait_send()


def greet_all(barrier):
    replica, replicas = lax.axis_index("replica"), lax.axis_size("replica")
    me, groups = lax.axis_index("shard"), lax.axis_size("shard")
    for i in range(1, groups):
        device = lax.rem(me + i, groups)
        pl.semaphore_signal(barrier, inc=1, device_id=(replica, device), device_id_type=MESH)

    @pl.when(replica >= 1)
    def _():
        pl.semaphore_signal(barrier, inc=1, device_id=(replica - 1, me), device_id_type=MESH)

    @pl.when(replica + 1 < replicas)
    def _():
        pl.semaphore_signal(barrier, inc=1, device_id=(replica + 1, me), device_id_type=MESH)

    edge = (replica == 0) | (replica == replicas - 1)

    @pl.when(edge)
    def _():
        pl.semaphore_wait(barrier, groups)

    @pl.when(jnp.logical_not(edge))
    def _():
        pl.semaphore_wait(barrier, groups + 1)


def rotate_head(values, cosine, sine):
    return values * cosine + pltpu.roll(values, values.shape[-1] // 2, 1) * sine


def key_reach(first, step, sequence):
    low = max(0, (first + 1 - sequence // 2) // 128 * 128)
    return low, pl.ds(low, first + step - low)


def allowed_bias(start, first, step, low):
    shape = (step, first + step - low)
    key_place = lax.broadcasted_iota(jnp.int32, shape, 1) + low
    query_place = lax.broadcasted_iota(jnp.int32, shape, 0) + first
    return jnp.where((key_place <= query_place) & (key_place >= start), 0.0, masked)


def head_scores(query, keys, bias):
    return product(query, keys, 1, 1) * (1.0 / math.sqrt(HEAD_DIM)) + bias


def fill_tables(lengths, frequency, cosine, sine, start):
    shape = start.shape
    place = lax.broadcasted_iota(jnp.int32, shape, 0)
    begin = jnp.zeros(shape, jnp.int32)
    end = 0
    for i in range(lengths.shape[1] - 1):
        end = end + lengths[0, i]
        begin = jnp.where(place >= end, end, begin)
    start[...] = begin
    angle = (place - begin).astype(F32) * frequency[...]
    lane = lax.broadcasted_iota(jnp.int32, shape, 1)
    cosine[...] = jnp.cos(angle)
    sine[...] = jnp.where(lane < shape[1] // 2, -1.0, 1.0) * jnp.sin(angle)


def front_kernel(
    lengths, frequency, x_own, dy_own, w_query, w_key, w_value, w_out, w_gate, w_up, w_down,
    n1_out, query_out, key_out, value_out, attn_out, attn_b_out, out_columns_out, down_parts,
    down_columns_out, hidden_out, grad_gate_out, grad_up_out, middle_out, n2_out, dy_out, n2_hopped,
    grad_out, grad_all_out, dy_hopped, passed, cosine_out, sine_out, start_out,
    n1, n2, dy, query, key, value, attn, attn_b, out_columns, gate_w, up_w, down_w,
    hidden, grad_gate, grad_up, parts, pair, sums, by_far, by_side, middle, normed, n2_own, grad_own, n1_own, cosine, sine, start,
    load_sem, save_sem, gather_sent, gather_came, scatter_sent, scatter_came,
    swap_sent, swap_came, line_sent, line_came, down_sent, down_came, pass_sem,
):
    replica = lax.axis_index("replica")
    replicas = lax.axis_size("replica")
    me = lax.axis_index("shard")
    groups = lax.axis_size("shard")
    tokens, width = x_own.shape
    sequence = n1.shape[0]
    saves = []

    def save(src, dst):
        copy = pltpu.make_async_copy(src, dst, save_sem.at[len(saves)])
        copy.start()
        saves.append(copy)

    def exchange(which, source, target):
        copies = []
        for i in range(1, groups):
            device = lax.rem(me + i, groups)
            copies.append(
                pltpu.make_async_remote_copy(
                    src_ref=source(device),
                    dst_ref=target,
                    send_sem=swap_sent.at[which, i],
                    recv_sem=swap_came.at[which, i],
                    device_id=(replica, device),
                    device_id_type=MESH,
                )
            )
        return copies

    gate_load = pltpu.make_async_copy(w_gate, gate_w, load_sem.at[0])
    up_load = pltpu.make_async_copy(w_up, up_w, load_sem.at[1])
    gate_load.start()
    up_load.start()
    own_rows = block_rows(me, tokens)
    x = x_own[...].astype(F32)
    center = x - jnp.mean(x, axis=-1, keepdims=True)
    inverse = lax.rsqrt(jnp.mean(center * center, axis=-1, keepdims=True) + epsilon)
    n1_own[...] = (center * inverse).astype(BF)
    own_n1 = pltpu.make_async_copy(n1_own, n1.at[own_rows], load_sem.at[2])
    own_dy = pltpu.make_async_copy(dy_own, dy.at[own_rows], load_sem.at[3])
    own_n1.start()
    own_dy.start()

    greet_all(pltpu.get_barrier_semaphore())
    n1_gather = Gather(n1_own, n1, gather_sent.at[0], gather_came.at[0])
    dy_gather = Gather(dy_own, dy, gather_sent.at[1], gather_came.at[1])
    n2_gather = Gather(n2_own, n2, gather_sent.at[2], gather_came.at[2])
    grad_gather = Gather(grad_own, grad_all_out, gather_sent.at[3], gather_came.at[3])
    half = sequence // 2
    dy_half = dy.at[pl.ds(pl.multiple_of(lax.rem(me, 2) * half, half), half)]
    n2_hop = Hop(1, lambda way: n2_own, n2_hopped, line_sent.at[0], line_came.at[0])
    dy_hop = Hop(1, lambda way: dy_half, dy_hopped, line_sent.at[1], line_came.at[1])
    passing = [
        pltpu.make_async_remote_copy(
            src_ref=src,
            dst_ref=passed.at[way],
            send_sem=pass_sem.at[0, way],
            recv_sem=pass_sem.at[1, way],
            device_id=(replica + (1 if way == 0 else -1), me),
            device_id_type=MESH,
        )
        for way in (0, 1)
        for src in (dy_own, passed.at[way])
    ]
    last = replicas - 1

    def passes(way, k):
        return replica == (k if way == 0 else last - k)

    def pass_on(k):
        for way in (0, 1):

            @pl.when(passes(way, k))
            def _(way=way):
                if k:
                    passing[2 * way].wait_recv()
                if k < 2:
                    passing[2 * way + (1 if k else 0)].start()

    down_line = Line(
        down_parts.at[replica], lambda s: down_parts.at[s], down_sent, down_came
    )
    buffers = (pair, sums, by_far, by_side)

    n1_gather.one()
    pass_on(0)
    fill_tables(lengths, frequency, cosine, sine, start)
    save(cosine, cosine_out)
    save(sine, sine_out)
    save(start, start_out)
    n1_gather.two()
    n1_gather.three()
    wide = w_out.shape[0]
    mine = pl.ds(pl.multiple_of(me * wide, wide), wide)
    part = down_parts.shape[2]

    def down_block(device):
        column = (device * replicas + replica) * part
        return w_down.at[:, pl.ds(pl.multiple_of(column, part), part)]

    def out_block(device):
        return w_out.at[:, pl.ds(pl.multiple_of(device * wide, wide), wide)]

    down_swaps = exchange(1, down_block, down_parts.at[replica, mine])
    out_swaps = exchange(0, out_block, out_columns.at[mine])
    own_down = pltpu.make_async_copy(down_block(me), down_parts.at[replica, mine], load_sem.at[5])
    own_down.start()
    own_out = pltpu.make_async_copy(out_block(me), out_columns.at[mine], load_sem.at[4])
    own_out.start()
    for copy in down_swaps + out_swaps:
        copy.start()
    pass_on(1)
    n1_gather.four()
    own_n1.wait()
    n1_gather.finish()
    save(n1, n1_out)

    heads = query.shape[1] // HEAD_DIM
    def projections(i, carry):
        rows = pl.ds(pl.multiple_of(i * 512, 512), 512)
        for weight, target in ((w_query, query), (w_key, key), (w_value, value)):
            values = product(n1[rows, :], weight[...], 1, 1)
            for head in range(heads):
                lanes = pl.ds(head * HEAD_DIM, HEAD_DIM)
                piece = values[:, head * HEAD_DIM : (head + 1) * HEAD_DIM]
                if target is not value:
                    piece = rotate_head(piece, cosine[rows, :], sine[rows, :])
                target[rows, lanes] = piece.astype(BF)
        return carry

    lax.fori_loop(0, sequence // 512, projections, 0)
    save(query, query_out)
    save(key, key_out)
    save(value, value_out)
    own_down.wait()
    for copy in down_swaps:
        copy.wait_recv()
    down_line.start()
    step = 256
    for first in range(0, sequence, step):
        rows = pl.ds(first, step)
        low, reach = key_reach(first, step, sequence)
        bias = allowed_bias(start[rows, 0:1], first, step, low)
        for head in range(heads):
            lanes = pl.ds(head * HEAD_DIM, HEAD_DIM)
            scores = head_scores(query[rows, lanes], key[reach, lanes], bias)
            weights = jnp.exp(scores - jnp.max(scores, axis=-1, keepdims=True))
            total = jnp.sum(weights, axis=-1, keepdims=True)
            result = product(weights.astype(BF), value[reach, lanes], 1, 0) / total
            attn[rows, lanes] = result
            attn_b[rows, lanes] = result.astype(BF)
    pass_on(2)
    save(attn, attn_out)
    save(attn_b, attn_b_out)

    own_out.wait()
    for copy in out_swaps:
        copy.wait_recv()
    save(out_columns, out_columns_out)

    def spread(rows, columns):
        parts[rows, columns] = product(attn_b[rows, :], out_columns[columns, :], 1, 1).astype(BF)

    tile_loop(sequence, width, 512, spread)
    scatter = Scatter(parts, buffers, scatter_sent.at[0], scatter_came.at[0])
    scatter.swap(3, 1, 2, 0)
    scatter.send_far()
    scatter.send_near()
    down_line.step(1)
    scatter.send_rest()
    middle[...] = x_own[...].astype(F32) + scatter.total()
    scatter.drain()
    save(middle, middle_out)
    center = middle[...] - jnp.mean(middle[...], axis=-1, keepdims=True)
    inverse = lax.rsqrt(jnp.mean(center * center, axis=-1, keepdims=True) + epsilon)
    normed[...] = center * inverse
    n2_own[...] = normed[...].astype(BF)
    n2_gather.one()
    own_n2 = pltpu.make_async_copy(n2_own, n2.at[own_rows], load_sem.at[6])
    own_n2.start()
    n2_gather.two()
    n2_gather.three()
    dy_gather.one()
    down_line.step(2)
    n2_hop.start()
    n2_gather.four()
    own_n2.wait()
    n2_gather.finish()
    save(n2, n2_out)
    gate_load.wait()
    up_load.wait()
    row = me // (groups // 2)

    def feed_forward(base):
        def forward(rows, columns):
            rows = pl.ds(pl.multiple_of(base, half), half)
            gate = product(n2[rows, :], gate_w[columns, :], 1, 1)
            up = product(n2[rows, :], up_w[columns, :], 1, 1)
            sigma = 0.5 + 0.5 * jnp.tanh(0.5 * gate)
            silu = gate * sigma
            hidden[rows, columns] = (silu * up).astype(BF)
            grad_gate[rows, columns] = (up * (sigma + silu * (1.0 - sigma))).astype(BF)
            grad_up[rows, columns] = silu.astype(BF)

        tile_loop(half, gate_w.shape[0], half, forward, 256)

    def both_forward(i, carry):
        feed_forward((1 - row + i * (2 * row - 1)) * half)

        @pl.when(i == 0)
        def _():
            dy_gather.two()
            dy_gather.three()

        return carry

    lax.fori_loop(0, 2, both_forward, 0)
    dy_gather.four()
    own_dy.wait()
    dy_gather.finish()
    save(dy, dy_out)
    save(hidden, hidden_out)
    dy_hop.start()
    down_line.step(3)
    down_loads = []
    for r in range(replicas):
        down_loads.append(
            pltpu.make_async_copy(
                down_parts.at[r], down_w.at[:, pl.ds(r * part, part)], load_sem.at[7 + r]
            )
        )
        down_loads[-1].start()
    for copy in down_loads:
        copy.wait()
    save(down_w, down_columns_out)

    back = Scatter(parts, buffers, scatter_sent.at[1], scatter_came.at[1])

    def feed(base):
        def grads(rows, columns):
            rows = pl.ds(pl.multiple_of(base, half), half)
            grad = product(dy[rows, :], down_w[:, columns], 1, 0)
            grad_gate[rows, columns] = (grad * grad_gate[rows, columns].astype(F32)).astype(BF)
            grad_up[rows, columns] = (grad * grad_up[rows, columns].astype(F32)).astype(BF)

        tile_loop(half, gate_w.shape[0], half, grads)

        def backward(rows, columns):
            rows = pl.ds(pl.multiple_of(base, half), half)
            value = product(grad_gate[rows, :], gate_w[:, columns], 1, 0)
            value = value + product(grad_up[rows, :], up_w[:, columns], 1, 0)
            parts[rows, columns] = value.astype(BF)

        tile_loop(half, width, half, backward)

    def both_back(i, carry):
        feed((1 - row + i * (2 * row - 1)) * half)

        @pl.when(i == 0)
        def _():
            back.swap(3, 2)
            back.send_far()

        return carry

    lax.fori_loop(0, 2, both_back, 0)
    save(grad_gate, grad_gate_out)
    save(grad_up, grad_up_out)
    back.swap(1, 0)
    back.send_near()
    back.send_rest()
    inner = back.total()
    back.drain()
    inner = (
        inner
        - jnp.mean(inner, axis=-1, keepdims=True)
        - normed[...] * jnp.mean(inner * normed[...], axis=-1, keepdims=True)
    )
    center = middle[...] - jnp.mean(middle[...], axis=-1, keepdims=True)
    inverse = lax.rsqrt(jnp.mean(center * center, axis=-1, keepdims=True) + epsilon)
    normed[...] = dy_own[...].astype(F32) + inverse * inner
    grad_own[...] = normed[...].astype(BF)
    grad_gather.one()
    save(normed, grad_out)
    save(grad_own, grad_all_out.at[own_rows])
    grad_gather.two()
    grad_gather.three()
    grad_gather.four()
    grad_gather.finish()
    for way in (0, 1):

        @pl.when(passes(way, 0) | passes(way, 1))
        def _(way=way):
            passing[2 * way].wait_send()

    n2_hop.arrive()
    dy_hop.arrive()
    for copy in saves:
        copy.wait()
    for copy in out_swaps + down_swaps:
        copy.wait_send()
    for user in (n1_gather, n2_gather, dy_gather, grad_gather, down_line, n2_hop, dy_hop):
        user.drain()


def front(lengths, frequency, x_own, dy_own, w_query, w_key, w_value, w_out, w_gate, w_up, w_down):
    groups, replicas = lax.axis_size("shard"), lax.axis_size("replica")
    tokens, width = x_own.shape
    sequence = tokens * groups
    wide, columns = w_query.shape[0], w_gate.shape[0]
    anywhere, vmem = pl.BlockSpec(memory_space=pl.ANY), pl.BlockSpec(memory_space=VMEM)

    def shape(dims, kind=BF):
        return jax.ShapeDtypeStruct(dims, kind)

    outs = (
        shape((sequence, width)),
        shape((sequence, wide)),
        shape((sequence, wide)),
        shape((sequence, wide)),
        shape((sequence, wide), F32),
        shape((sequence, wide)),
        shape((width, wide)),
        shape((replicas, width, columns // replicas)),
        shape((width, columns)),
        shape((sequence, columns)),
        shape((sequence, columns)),
        shape((sequence, columns)),
        shape((tokens, width), F32),
        shape((sequence, width)),
        shape((sequence, width)),
        shape((2, tokens, width)),
        shape((tokens, width), F32),
        shape((sequence, width)),
        shape((2, sequence // 2, width)),
        shape((2, tokens, width)),
        shape((sequence, HEAD_DIM), F32),
        shape((sequence, HEAD_DIM), F32),
        shape((sequence, HEAD_DIM), jnp.int32),
    )
    dma = pltpu.SemaphoreType.DMA
    return pl.pallas_call(
        front_kernel,
        out_shape=outs,
        in_specs=[pl.BlockSpec(memory_space=pltpu.SMEM)] + [vmem] * 6 + [anywhere] * 4,
        out_specs=(anywhere,) * len(outs),
        scratch_shapes=[
            pltpu.VMEM((sequence, width), BF),
            pltpu.VMEM((sequence, width), BF),
            pltpu.VMEM((sequence, width), BF),
            pltpu.VMEM((sequence, wide), BF),
            pltpu.VMEM((sequence, wide), BF),
            pltpu.VMEM((sequence, wide), BF),
            pltpu.VMEM((sequence, wide), F32),
            pltpu.VMEM((sequence, wide), BF),
            pltpu.VMEM((width, wide), BF),
            pltpu.VMEM((columns, width), BF),
            pltpu.VMEM((columns, width), BF),
            pltpu.VMEM((width, columns), BF),
            pltpu.VMEM((sequence, columns), BF),
            pltpu.VMEM((sequence, columns), BF),
            pltpu.VMEM((sequence, columns), BF),
            pltpu.VMEM((sequence, width), BF),
            pltpu.VMEM((4, tokens, width), BF),
            pltpu.VMEM((3, tokens, width), BF),
            pltpu.VMEM((2, tokens // 2, width), BF),
            pltpu.VMEM((2, tokens, width), BF),
            pltpu.VMEM((tokens, width), F32),
            pltpu.VMEM((tokens, width), F32),
            pltpu.VMEM((tokens, width), BF),
            pltpu.VMEM((tokens, width), BF),
            pltpu.VMEM((tokens, width), BF),
            pltpu.VMEM((sequence, HEAD_DIM), F32),
            pltpu.VMEM((sequence, HEAD_DIM), F32),
            pltpu.VMEM((sequence, HEAD_DIM), jnp.int32),
            dma((7 + replicas,)),
            dma((24,)),
            dma((4, 13)),
            dma((4, 13)),
            dma((2, 10)),
            dma((2, 10)),
            dma((2, groups)),
            dma((2, groups)),
            dma((2, 2)),
            dma((2, 2)),
            dma((2, replicas)),
            dma((2, replicas)),
            dma((2, 2)),
        ],
        compiler_params=pltpu.CompilerParams(
            collective_id=3, has_side_effects=True, vmem_limit_bytes=67043328
        ),
        cost_estimate=pl.CostEstimate(
            flops=12 * sequence * width * columns, bytes_accessed=64 * 1024 * 1024, transcendentals=0
        ),
        name="front",
    )(lengths, frequency, x_own, dy_own, w_query, w_key, w_value, w_out, w_gate, w_up, w_down)


def back_kernel(
    x_own, start, cosine, sine, hidden_in, down_in, grad_in, out_columns_in, attn_b_in, attn_in,
    query_in, key_in, value_in, n1_in, w_query, w_key, w_value, n2_near, dy_near, middle, grad_middle,
    layer_out, input_grad, attn_part, out_grad_out, n2_hopped, dy_hopped, near_all,
    hidden, down_w, grad, out_columns, attn_b, attn, query, key, value, n1, weights,
    grad_attn, key_grad, value_grad, columns_grad, out_grad, rows_grad, parts,
    pair, sums, by_far, by_side, pair2, sums2, by_far2, by_side2,
    load_sem, save_sem, scatter_sent, scatter_came, line_sent, line_came,
    gather_sent, gather_came,
):
    sequence, width = n1.shape
    me = lax.axis_index("shard")
    near_half = x_own.shape[0] // 2
    near_block = n2_near.at[1 - lax.rem(lax.axis_index("replica"), 2), pl.ds(0, near_half)]
    near = Gather(near_block, near_all, gather_sent, gather_came)
    wide = query.shape[1]
    heads = wide // HEAD_DIM
    pairs = (
        (hidden_in, hidden), (down_in, down_w), (grad_in, grad), (out_columns_in, out_columns),
        (attn_b_in, attn_b), (attn_in, attn), (query_in, query), (key_in, key), (value_in, value),
        (n1_in, n1), (w_query, weights.at[pl.ds(0, wide)]), (w_key, weights.at[pl.ds(wide, wide)]),
        (w_value, weights.at[pl.ds(2 * wide, wide)]),
    )
    loads = [
        pltpu.make_async_copy(src, dst, load_sem.at[i]) for i, (src, dst) in enumerate(pairs)
    ]
    for copy in loads:
        copy.start()
    greet_all(pltpu.get_barrier_semaphore())
    hops = (
        Hop(2, lambda way: n2_near.at[way], n2_hopped, line_sent.at[0], line_came.at[0]),
        Hop(2, lambda way: dy_near.at[way], dy_hopped, line_sent.at[1], line_came.at[1]),
    )
    for hop in hops:
        hop.start()
    loads[0].wait()
    loads[1].wait()

    def mix(rows, columns):
        parts[rows, columns] = product(hidden[rows, :], down_w[columns, :], 1, 1).astype(BF)

    tile_loop(sequence, width, 512, mix)
    mixed = Scatter(parts, (pair, sums, by_far, by_side), scatter_sent.at[0], scatter_came.at[0])
    mixed.swap(3, 1, 2, 0)

    for copy in loads[2:6]:
        copy.wait()
    mixed.send_far()
    mixed.send_near()
    near.one()
    own_near = pltpu.make_async_copy(near_block, near_all.at[block_rows(me, near.tokens)], save_sem.at[2])
    own_near.start()

    def out_step(i, carry):
        rows = pl.ds(pl.multiple_of(i * 512, 512), 512)
        out_grad[rows, :] = product(grad[:, rows], attn_b[...], 0, 0).astype(BF)
        return carry

    lax.fori_loop(0, width // 512, out_step, 0)
    out_save = pltpu.make_async_copy(out_grad, out_grad_out, save_sem.at[0])
    out_save.start()

    def attn_step(i, carry):
        rows = pl.ds(pl.multiple_of(i * 512, 512), 512)
        grad_attn[rows, :] = product(grad[rows, :], out_columns[...], 1, 0).astype(BF)
        return carry

    lax.fori_loop(0, sequence // 512, attn_step, 0)
    for copy in loads[6:]:
        copy.wait()
    mixed.send_rest()

    near.two()
    step = 256
    for first in range(sequence - step, -1, -step):
        if first == sequence - 2 * step:
            near.three()
        if first == sequence - 3 * step:
            near.four()
        rows = pl.ds(first, step)
        low, upto = key_reach(first, step, sequence)
        bias = allowed_bias(start[rows, 0:1], first, step, low)
        for head in range(heads):
            lanes = pl.ds(head * HEAD_DIM, HEAD_DIM)
            query_piece, grad_piece = query[rows, lanes], grad_attn[rows, lanes]
            scores = head_scores(query_piece, key[upto, lanes], bias)
            probs = jnp.exp(scores - jnp.max(scores, axis=-1, keepdims=True))
            probs = probs / jnp.sum(probs, axis=-1, keepdims=True)
            delta = jnp.sum(grad_piece.astype(F32) * attn[rows, lanes], axis=-1, keepdims=True)
            grad_probs = product(grad_piece, value[upto, lanes], 1, 1)
            grad_scores = (probs * (grad_probs - delta)).astype(BF)
            query_grad = product(grad_scores, key[upto, lanes], 1, 0) * (1.0 / math.sqrt(HEAD_DIM))
            query_grad = rotate_head(query_grad, cosine[rows, :], -sine[rows, :])
            columns_grad[rows, lanes] = query_grad.astype(BF)
            key_part = product(grad_scores, query_piece, 0, 0)
            value_part = product(probs.astype(BF), grad_piece, 0, 0)
            if first == sequence - step:
                key_grad[upto, lanes] = key_part
                value_grad[upto, lanes] = value_part
                if low:
                    key_grad[pl.ds(0, low), lanes] = jnp.zeros((low, HEAD_DIM), F32)
                    value_grad[pl.ds(0, low), lanes] = jnp.zeros((low, HEAD_DIM), F32)
            else:
                key_grad[upto, lanes] += key_part
                value_grad[upto, lanes] += value_part
    for head in range(heads):
        lanes = pl.ds(head * HEAD_DIM, HEAD_DIM)
        piece = key_grad[:, lanes] * (1.0 / math.sqrt(HEAD_DIM))
        piece = rotate_head(piece, cosine[...], -sine[...])
        columns_grad[:, pl.ds(wide + head * HEAD_DIM, HEAD_DIM)] = piece.astype(BF)
        columns_grad[:, pl.ds(2 * wide + head * HEAD_DIM, HEAD_DIM)] = value_grad[:, lanes].astype(BF)

    layer_out[...] = (middle[...] + mixed.total()).astype(BF)
    mixed.drain()

    def back(rows, columns):
        parts[rows, columns] = product(columns_grad[rows, :], weights[:, columns], 1, 0).astype(BF)

    tile_loop(sequence, width, 512, back)
    last = Scatter(parts, (pair2, sums2, by_far2, by_side2), scatter_sent.at[1], scatter_came.at[1])
    last.swap(3, 1, 2, 0)
    last.send_far()
    last.send_near()

    def collect(rows, columns):
        rows_grad[rows, columns] = product(columns_grad[:, rows], n1[:, columns], 0, 0).astype(BF)

    tile_loop(3 * wide, width, 256, collect, 512)
    rows_save = pltpu.make_async_copy(rows_grad, attn_part, save_sem.at[1])
    rows_save.start()
    last.send_rest()
    x = x_own[...].astype(F32)
    center = x - jnp.mean(x, axis=-1, keepdims=True)
    inverse = lax.rsqrt(jnp.mean(center * center, axis=-1, keepdims=True) + epsilon)
    inner = last.total()
    normed = center * inverse
    inner = (
        inner
        - jnp.mean(inner, axis=-1, keepdims=True)
        - normed * jnp.mean(inner * normed, axis=-1, keepdims=True)
    )
    input_grad[...] = grad_middle[...] + inverse * inner
    last.drain()
    out_save.wait()
    rows_save.wait()
    own_near.wait()
    near.finish()
    near.drain()
    for hop in hops:
        hop.arrive()
        hop.drain()


def back(x_own, start, cosine, sine, hidden, down, grad, out_columns, attn_b, attn, query, key, value, n1,
         w_query, w_key, w_value, n2_near, dy_near, middle, grad_middle):
    groups = lax.axis_size("shard")
    tokens, width = x_own.shape
    sequence = tokens * groups
    wide, columns = query.shape[1], hidden.shape[1]
    anywhere, vmem = pl.BlockSpec(memory_space=pl.ANY), pl.BlockSpec(memory_space=VMEM)
    dma = pltpu.SemaphoreType.DMA
    buffers = [
        pltpu.VMEM((4, tokens, width), BF),
        pltpu.VMEM((3, tokens, width), BF),
        pltpu.VMEM((2, tokens // 2, width), BF),
        pltpu.VMEM((2, tokens, width), BF),
    ]
    return pl.pallas_call(
        back_kernel,
        out_shape=(
            jax.ShapeDtypeStruct((tokens, width), BF),
            jax.ShapeDtypeStruct((tokens, width), F32),
            jax.ShapeDtypeStruct((3 * wide, width), BF),
            jax.ShapeDtypeStruct((width, wide), BF),
            jax.ShapeDtypeStruct(n2_near.shape, BF),
            jax.ShapeDtypeStruct(dy_near.shape, BF),
            jax.ShapeDtypeStruct((sequence // 2, width), BF),
        ),
        in_specs=[vmem] * 4 + [anywhere] * 15 + [vmem] * 2,
        out_specs=(vmem, vmem) + (anywhere,) * 5,
        scratch_shapes=[
            pltpu.VMEM((sequence, columns), BF),
            pltpu.VMEM((width, columns), BF),
            pltpu.VMEM((sequence, width), BF),
            pltpu.VMEM((width, wide), BF),
            pltpu.VMEM((sequence, wide), BF),
            pltpu.VMEM((sequence, wide), F32),
            pltpu.VMEM((sequence, wide), BF),
            pltpu.VMEM((sequence, wide), BF),
            pltpu.VMEM((sequence, wide), BF),
            pltpu.VMEM((sequence, width), BF),
            pltpu.VMEM((3 * wide, width), BF),
            pltpu.VMEM((sequence, wide), BF),
            pltpu.VMEM((sequence, wide), F32),
            pltpu.VMEM((sequence, wide), F32),
            pltpu.VMEM((sequence, 3 * wide), BF),
            pltpu.VMEM((width, wide), BF),
            pltpu.VMEM((3 * wide, width), BF),
            pltpu.VMEM((sequence, width), BF),
            *buffers,
            *buffers,
            dma((13,)),
            dma((3,)),
            dma((2, 10)),
            dma((2, 10)),
            dma((2, 2)),
            dma((2, 2)),
            dma((13,)),
            dma((13,)),
        ],
        compiler_params=pltpu.CompilerParams(
            collective_id=4, has_side_effects=True, vmem_limit_bytes=67043328
        ),
        cost_estimate=pl.CostEstimate(
            flops=24 * sequence * width * wide, bytes_accessed=48 * 1024 * 1024, transcendentals=0
        ),
        name="back",
    )(x_own, start, cosine, sine, hidden, down, grad, out_columns, attn_b, attn, query, key, value, n1,
      w_query, w_key, w_value, n2_near, dy_near, middle, grad_middle)


def every_kernel(
    near_all, n2_one, n2_two, dy_one, dy_two, passed, own_normed, own_dy, own_hidden, own_grad_gate, own_grad_up,
    attn_part, out_part,
    w_gate, w_up, w_down,
    both_out, out_down, out_attn, landed, kept, dy_other,
    out_rows, n2_three, near_rest, passed_three,
    normed, dy, hidden, grads, gate_w, up_w, down_w, down, totals, first_sum, second_sum, stage,
    load_sem, keep_sem, gather_sent, gather_came, line_sent, line_came, line_own, swap_sent, swap_came,
    out_sem, pair_sem, out_swap_sem, hop_sent, hop_came, near_sem,
):
    replica = lax.axis_index("replica")
    replicas = lax.axis_size("replica")
    me = lax.axis_index("shard")
    groups = lax.axis_size("shard")
    tokens = n2_one.shape[1]
    sequence, width = normed.shape
    half = sequence // 2
    columns = hidden.shape[1]
    grad_gate, grad_up = grads.at[0], grads.at[1]
    inner = (replica == 1) | (replica == 2)
    outer = (replica == 0) | (replica == 3)
    beside = replica + 1 - 2 * lax.rem(replica, 2)
    facing = 3 - replica
    chunks, depth = first_sum.shape[0], first_sum.shape[1]

    def piece(c):
        return pl.ds(c * depth, depth)

    def line_move(kind, c, src, dst, target):
        return pltpu.make_async_remote_copy(
            src_ref=src,
            dst_ref=dst,
            send_sem=line_sent.at[kind, c],
            recv_sem=line_came.at[kind, c],
            device_id=(target, me),
            device_id_type=MESH,
        )

    attn_chunks = attn_part.shape[0] // depth

    def own_chunk(c):
        return attn_part.at[piece(c)] if c < attn_chunks else out_rows.at[piece(c - attn_chunks)]

    def inward(c):
        return line_move(0, c, own_chunk(c), first_sum.at[c], beside)

    def middle(c):
        return line_move(1, c, first_sum.at[c], second_sum.at[c], facing)

    def outward(c):
        return line_move(2, c, second_sum.at[c], out_attn.at[piece(c)], beside)

    def keep(c):
        return pltpu.make_async_copy(second_sum.at[c], out_attn.at[piece(c)], line_own.at[c])

    def stage_load(c):
        return pltpu.make_async_copy(own_chunk(c), stage, keep_sem.at[2, 0])

    def half_sums(*which):
        @pl.when(inner)
        def _():
            for c in which:
                stage_load(c).wait()
                inward(c).wait_recv()
                first_sum[c] = (stage[...].astype(F32) + first_sum[c].astype(F32)).astype(BF)
                middle(c).start()
                if c + 1 < chunks:
                    stage_load(c + 1).start()

    def full_sums(*which):
        @pl.when(inner)
        def _():
            for c in which:
                middle(c).wait_recv()
                second_sum[c] = (first_sum[c].astype(F32) + second_sum[c].astype(F32)).astype(BF)
                outward(c).start()
                keep(c).start()

    core = lax.rem(me, 2)
    mate = me + 1 - 2 * core
    low_side, high_side = 1 - lax.rem(replica, 2), 1 - replica // 2
    hop = Hop(3, lambda way: n2_two.at[way], n2_three, hop_sent.at[0], hop_came.at[0])
    dy_hop = Hop(3, lambda way: passed.at[way], passed_three, hop_sent.at[1], hop_came.at[1])
    far_dy = passed_three.at[high_side]
    last_dy = Gather(far_dy, landed.at[3], gather_sent.at[3], gather_came.at[3])

    def last_dy_one():
        dy_hop.arrive()
        last_dy.one()

    def in_outer(action):
        def act():
            @pl.when(outer)
            def _():
                action()

        return act

    n2_blocks = {1: n2_one.at[low_side], 2: n2_two.at[high_side]}
    dy_halves = {1: dy_one.at[low_side], 2: dy_two.at[high_side]}
    roles = ((inner, n2_one.at[high_side]), (outer, n2_three.at[high_side]))
    third = dy_one.at[high_side]

    near = Gather(
        n2_one.at[low_side, pl.ds(tokens // 2, tokens // 2)], near_rest, gather_sent.at[0], gather_came.at[0]
    )

    def gather_of(n, block):
        return Gather(block, landed.at[n - 1], gather_sent.at[n - 1], gather_came.at[n - 1])

    gathers = [gather_of(2, n2_blocks[2]), gather_of(3, roles[0][1])]

    def last_one():
        hop.arrive()
        for role, block in roles:

            @pl.when(role)
            def _(block=block):
                gather_of(3, block).one()

        gather = gathers[1]
        gather.sends.extend(gather.firsts())

    def pair_copy(n, source):
        return pltpu.make_async_remote_copy(
            src_ref=source,
            dst_ref=dy_other.at[n - 1],
            send_sem=pair_sem.at[0, n - 1],
            recv_sem=pair_sem.at[1, n - 1],
            device_id=(replica, mate),
            device_id_type=MESH,
        )

    def normed_loads(n, target, base, block=None):
        copies = []
        if n == 1:
            for i in range(groups):
                device = lax.rem(me + i, groups)
                small = block_rows(device, near.tokens)
                rest = near_rest.at[small] if i else near.block
                for k, source in enumerate((near_all.at[small], rest)):
                    rows = block_rows(device, tokens, k + 1)
                    copies.append(pltpu.make_async_copy(source, target.at[rows], near_sem.at[k, i]))
            return copies
        for i in range(groups):
            device = lax.rem(me + i, groups)
            rows = block_rows(device, tokens)
            source = (n2_blocks[n] if block is None else block) if i == 0 else landed.at[n - 1, rows]
            copies.append(pltpu.make_async_copy(source, target.at[rows], load_sem.at[base, i]))
        return copies

    def dy_loads(n, source=None):
        mine = dy.at[pl.ds(pl.multiple_of(core * half, half), half)]
        others = dy.at[pl.ds(pl.multiple_of((1 - core) * half, half), half)]
        return [
            pltpu.make_async_copy(dy_halves[n] if source is None else source, mine, load_sem.at[1, 0]),
            pltpu.make_async_copy(dy_other.at[n - 1], others, load_sem.at[1, 1]),
        ]

    def far_loads():
        copies = []
        for i in range(groups):
            rows = block_rows(lax.rem(me + i, groups), tokens)
            source = landed.at[3, rows] if i else far_dy
            copies.append(pltpu.make_async_copy(source, dy.at[rows], load_sem.at[1, i]))
        return copies

    wide = width // groups

    def out_move(i):
        device = lax.rem(me + i, groups)
        return pltpu.make_async_remote_copy(
            src_ref=out_part.at[pl.ds(pl.multiple_of(device * wide, wide), wide)],
            dst_ref=out_rows.at[:, pl.ds(pl.multiple_of(me * wide, wide), wide)],
            send_sem=out_swap_sem.at[0, i],
            recv_sem=out_swap_sem.at[1, i],
            device_id=(replica, device),
            device_id_type=MESH,
        )

    own_out = pltpu.make_async_copy(
        out_part.at[pl.ds(pl.multiple_of(me * wide, wide), wide)],
        out_rows.at[:, pl.ds(pl.multiple_of(me * wide, wide), wide)],
        out_swap_sem.at[0, 0],
    )

    def out_ready():
        own_out.wait()
        for i in range(1, groups):
            out_move(i).wait_recv()

        @pl.when(outer)
        def _():
            start_all([inward(c) for c in range(attn_chunks, chunks)])

    def keeps(n):
        return [
            pltpu.make_async_copy(grad_gate, kept.at[n - 1, 0], keep_sem.at[0, n]),
            pltpu.make_async_copy(grad_up, kept.at[n - 1, 1], keep_sem.at[1, n]),
        ]

    def start_all(copies):
        for copy in copies:
            copy.start()

    def wait_all(copies):
        for copy in copies:
            copy.wait()

    first = [
        pltpu.make_async_copy(own_hidden, hidden, load_sem.at[1, 1]),
        pltpu.make_async_copy(own_dy, dy, load_sem.at[1, 0]),
    ]
    weights = [
        pltpu.make_async_copy(w_gate, gate_w, load_sem.at[2, 0]),
        pltpu.make_async_copy(w_up, up_w, load_sem.at[2, 1]),
        pltpu.make_async_copy(w_down, down_w, load_sem.at[2, 2]),
    ]
    start_all(first + weights)
    barrier = pltpu.get_barrier_semaphore()
    for i in range(1, groups):
        device = lax.rem(me + i, groups)
        pl.semaphore_signal(barrier, inc=1, device_id=(replica, device), device_id_type=MESH)
    pl.semaphore_signal(barrier, inc=1, device_id=(beside, me), device_id_type=MESH)

    @pl.when(inner)
    def _():
        pl.semaphore_signal(barrier, inc=1, device_id=(facing, me), device_id_type=MESH)
        pl.semaphore_wait(barrier, groups + 1)

    @pl.when(outer)
    def _():
        pl.semaphore_wait(barrier, groups)

    further, last_normed = gathers
    near.one()
    pair_copy(1, dy_halves[1]).start()
    pair_copy(2, dy_halves[2]).start()
    own_out.start()
    hop.start()
    dy_hop.start()

    @pl.when(inner)
    def _():
        pair_copy(3, third).start()


    @pl.when(outer)
    def _():
        start_all([inward(c) for c in range(attn_chunks)])

    @pl.when(inner)
    def _():
        stage_load(0).start()

    def collect(out, left, right, add):
        def step(rows, cols):
            value = product(left[:, rows], right[:, cols], 0, 0)
            if add is None:
                out[rows, cols] = value
            elif add is True:
                out[rows, cols] += value

        tile_loop(out.shape[0], out.shape[1], 512, step)

    wait_all(first)
    near.two()
    further.one()
    collect(down, dy, hidden, None)
    pair_copy(1, dy_halves[1]).wait()
    pair_copy(2, dy_halves[2]).wait()
    start_all(dy_loads(1))
    near.three()
    near.four()
    near.finish()
    start_all(normed_loads(1, normed, 0))
    wait_all(weights)
    wait_all(normed_loads(1, normed, 0))
    wait_all(dy_loads(1))

    def out_starts():
        for i in range(1, groups):
            out_move(i).start()

    agenda = {
        (1, 0): (further.two,),
        (1, 2): (further.three,),
        (1, 3): (further.four, last_one),
        (1, 4): (lambda: half_sums(0),),
        (1, 5): (further.finish,),
        (1, 7): (last_normed.two,),
        (2, 0): (last_normed.three, in_outer(last_dy_one)),
        (2, 1): (lambda: full_sums(0),),
        (2, 2): (last_normed.four,),
        (2, 4): (lambda: half_sums(2), in_outer(last_dy.two)),
        (2, 5): (lambda: full_sums(1),),
        (2, 7): (in_outer(last_dy.three), out_starts),
        (3, 0): (lambda: full_sums(2),),
        (3, 4): (lambda: half_sums(4),),
        (3, 6): (lambda: full_sums(3),),
        (3, 7): (out_ready,),
    }

    def after_down(n):
        wait_all(keeps(n))
        if n == 1:
            half_sums(1)
            start_all(dy_loads(2))
            wait_all(normed_loads(2, normed, 0))
            wait_all(dy_loads(2))
        else:
            half_sums(3)

            @pl.when(inner)
            def _():
                pair_copy(3, third).wait()
                start_all(dy_loads(3, third))
                wait_all(normed_loads(3, normed, 0, roles[0][1]))
                wait_all(dy_loads(3, third))

            @pl.when(outer)
            def _():
                last_dy.four()
                last_dy.finish()
                start_all(far_loads())
                wait_all(normed_loads(3, normed, 0, roles[1][1]))
                wait_all(far_loads())

    def sequence_step(n, carry):
        narrow = 256
        across = columns // narrow

        def one_tile(i, carry):
            ffn_tile(
                normed, dy, gate_w, up_w, down_w, hidden, grad_gate, grad_up,
                pl.ds(pl.multiple_of((i // across) * 512, 512), 512),
                pl.ds(pl.multiple_of(lax.rem(i, across) * narrow, narrow), narrow),
            )
            for (when, tile), actions in agenda.items():

                @pl.when((n == when) & (i == tile))
                def _(actions=actions):
                    for action in actions:
                        action()

            return carry

        lax.fori_loop(0, (sequence // 512) * across, one_tile, 0)
        for k in (1, 2):

            @pl.when(n == k)
            def _(k=k):
                start_all(keeps(k))
                if k == 1:
                    start_all(normed_loads(2, normed, 0))
                else:
                    last_normed.finish()
                    for role, block in roles:

                        @pl.when(role)
                        def _(block=block):
                            start_all(normed_loads(3, normed, 0, block))

        @pl.when(n < 3)
        def _():
            collect(down, dy, hidden, True)

        for k in (1, 2):

            @pl.when(n == k)
            def _(k=k):
                after_down(k)

        return carry

    lax.fori_loop(1, 4, sequence_step, 0)
    one_gate, one_up = up_w.at[:, pl.ds(0, columns)], up_w.at[:, pl.ds(columns, columns)]
    one_loads = normed_loads(1, gate_w, 2) + [
        pltpu.make_async_copy(kept.at[0, 0], one_gate, keep_sem.at[0, 0]),
        pltpu.make_async_copy(kept.at[0, 1], one_up, keep_sem.at[1, 0]),
    ]
    start_all(one_loads)

    wide = width // groups
    _, _, across_device, along_device, far_device = whereabouts()

    def down_move(send_index, recv_index, row, sender, device):
        return pltpu.make_async_remote_copy(
            src_ref=down_w.at[pl.ds(pl.multiple_of(row, wide), wide)],
            dst_ref=out_down.at[:, pl.ds(pl.multiple_of(sender * columns, columns), columns)],
            send_sem=swap_sent.at[send_index],
            recv_sem=swap_came.at[recv_index],
            device_id=(replica, device),
            device_id_type=MESH,
        )

    def chip_of(i):
        chip = jnp.where(i == 0, far_device, jnp.where(i == 1, across_device, along_device))
        return jnp.where(i == 3, me, chip) // 2

    def out_sends(i, k):
        return down_move(2 * i + k, 2 * i + core, (2 * i + k) * wide, me, chip_of(i) * 2 + k)

    def finish_down(i, carry):
        rows = pl.ds(pl.multiple_of(chip_of(i) * 2 * wide, 2 * wide), 2 * wide)

        def column_step(j, carry):
            cols = pl.ds(pl.multiple_of(j * 512, 512), 512)
            down[rows, cols] += product(dy[:, rows], hidden[:, cols], 0, 0)
            return carry

        lax.fori_loop(0, columns // 512, column_step, 0)
        down_w[pl.ds(pl.multiple_of(i * 2 * wide, 2 * wide), 2 * wide), :] = down[rows, :].astype(BF)

        @pl.when(i < 3)
        def _():
            out_sends(i, 0).start()
            out_sends(i, 1).start()

        return carry

    lax.fori_loop(0, 4, finish_down, 0)
    swaps = [out_sends(i, k) for i in range(3) for k in range(2)]
    arrivals = []
    for i in range(3):
        for k in range(2):
            peer = chip_of(i) * 2 + k
            arrivals.append(down_move(2 * i + k, 2 * i + k, (2 * i + k) * wide, peer, peer))
    swaps.append(down_move(6, 6, (6 + lax.rem(mate, 2)) * wide, me, mate))
    swaps[-1].start()
    arrivals.append(down_move(6, 6, 6 * wide, mate, mate))
    own_slab = pltpu.make_async_copy(
        down_w.at[pl.ds(pl.multiple_of((6 + core) * wide, wide), wide)],
        out_down.at[:, pl.ds(pl.multiple_of(me * columns, columns), columns)],
        keep_sem.at[2, 1],
    )
    own_slab.start()
    two_gate = pltpu.make_async_copy(kept.at[1, 0], hidden, keep_sem.at[0, 3])
    two_gate.start()
    full_sums(4)
    half_sums(5)
    wait_all(one_loads)
    two_loads = normed_loads(2, dy, 0)
    start_all(two_loads)

    two_up = pltpu.make_async_copy(kept.at[1, 1], hidden, keep_sem.at[1, 3])
    own_loads = [
        pltpu.make_async_copy(own_normed, normed, load_sem.at[2, 0]),
        pltpu.make_async_copy(own_grad_gate, one_gate, load_sem.at[2, 1]),
        pltpu.make_async_copy(own_grad_up, one_up, load_sem.at[2, 2]),
    ]

    def one_rows(u, rows):
        return up_w[:, pl.ds(pl.multiple_of(u * columns + rows.start, 512), 512)]

    def two_passes(u, carry):
        def newest(rows, cols):
            value = product(grads[u, :, rows], normed[:, cols], 0, 0)
            totals[u, rows, cols] = value + product(one_rows(u, rows), gate_w[:, cols], 0, 0)

        tile_loop(columns, width, 512, newest)

        @pl.when(u == 0)
        def _():
            half_sums(6)
            wait_all(two_loads)
            two_gate.wait()

        @pl.when(u == 1)
        def _():
            start_all(own_loads)
            full_sums(6)
            two_up.wait()

        def older(rows, cols):
            totals[u, rows, cols] += product(hidden[:, rows], dy[:, cols], 0, 0)

        tile_loop(columns, width, 512, older)

        @pl.when(u == 0)
        def _():
            two_up.start()
            full_sums(5)
            half_sums(7)

        return carry

    lax.fori_loop(0, 2, two_passes, 0)
    full_sums(7)
    wait_all(own_loads)

    def out_save(i):
        u, rows = i // (columns // 512), pl.ds(pl.multiple_of(lax.rem(i, columns // 512) * 512, 512), 512)
        return pltpu.make_async_copy(totals.at[u, rows], both_out.at[u, rows], out_sem.at[i])

    def last_rows(i, carry):
        u, rows = i // (columns // 512), pl.ds(pl.multiple_of(lax.rem(i, columns // 512) * 512, 512), 512)

        def column_step(j, carry):
            cols = pl.ds(pl.multiple_of(j * 512, 512), 512)
            totals[u, rows, cols] += product(one_rows(u, rows), normed[:, cols], 0, 0)
            return carry

        lax.fori_loop(0, width // 512, column_step, 0)
        out_save(i).start()
        return carry

    lax.fori_loop(0, 2 * (columns // 512), last_rows, 0)
    out_saves = [out_save(i) for i in range(2 * (columns // 512))]

    @pl.when(outer)
    def _():
        for c in range(chunks):
            inward(c).wait_send()
            outward(c).wait_recv()

    @pl.when(inner)
    def _():
        for c in range(chunks):
            middle(c).wait_send()
            outward(c).wait_send()
            keep(c).wait()

    for copy in swaps:
        copy.wait_send()
    for copy in arrivals:
        copy.wait_recv()
    own_slab.wait()
    for i in range(1, groups):
        out_move(i).wait_send()
    hop.drain()

    @pl.when(outer)
    def _():
        last_dy.drain()

    wait_all(out_saves)
    dy_hop.drain()
    near.drain()
    for gather in gathers:
        gather.drain()


def ffn_grads(near_all, n2_one, n2_two, dy_one, dy_two, passed, n2, dy_all, own, attn_part, out_part, w_gate, w_up, w_down_columns):
    _, tokens, width = n2_one.shape
    sequence = n2.shape[0]
    groups = sequence // tokens
    columns = w_gate.shape[0]
    chunks = 8
    attn_rows = attn_part.shape[0] + out_part.shape[1]
    depth = attn_rows // chunks
    anywhere = pl.BlockSpec(memory_space=pl.ANY)
    dma = pltpu.SemaphoreType.DMA
    out = pl.pallas_call(
        every_kernel,
        out_shape=(
            jax.ShapeDtypeStruct((2, columns, width), F32),
            jax.ShapeDtypeStruct((width // groups, columns * groups), BF),
            jax.ShapeDtypeStruct((attn_rows, width), BF),
            jax.ShapeDtypeStruct((4, sequence, width), BF),
            jax.ShapeDtypeStruct((2, 2, sequence, columns), BF),
            jax.ShapeDtypeStruct((3, sequence // 2, width), BF),
            jax.ShapeDtypeStruct((out_part.shape[1], width), BF),
            jax.ShapeDtypeStruct(n2_two.shape, BF),
            jax.ShapeDtypeStruct((sequence // 2, width), BF),
            jax.ShapeDtypeStruct(passed.shape, BF),
        ),
        in_specs=[anywhere] * 16,
        out_specs=(anywhere,) * 10,
        scratch_shapes=[
            pltpu.VMEM((sequence, width), BF),
            pltpu.VMEM((sequence, width), BF),
            pltpu.VMEM((sequence, columns), BF),
            pltpu.VMEM((2, sequence, columns), BF),
            pltpu.VMEM((columns, width), BF),
            pltpu.VMEM((columns, width), BF),
            pltpu.VMEM((width, columns), BF),
            pltpu.VMEM((width, columns), F32),
            pltpu.VMEM((2, columns, width), F32),
            pltpu.VMEM((chunks, depth, width), BF),
            pltpu.VMEM((chunks, depth, width), BF),
            pltpu.VMEM((depth, width), BF),
            dma((3, groups)),
            dma((3, 4)),
            dma((4, 13)),
            dma((4, 13)),
            dma((3, chunks)),
            dma((3, chunks)),
            dma((chunks,)),
            dma((groups,)),
            dma((groups,)),
            dma((2 * (columns // 512),)),
            dma((2, 3)),
            dma((2, groups)),
            dma((2, 2)),
            dma((2, 2)),
            dma((2, groups)),
        ],
        compiler_params=pltpu.CompilerParams(
            collective_id=2, has_side_effects=True, vmem_limit_bytes=67043328
        ),
        cost_estimate=pl.CostEstimate(
            flops=42 * sequence * width * columns, bytes_accessed=80 * 1024 * 1024, transcendentals=0
        ),
        name="ffn_grads",
    )(near_all, n2_one, n2_two, dy_one, dy_two, passed, n2, dy_all, *own, attn_part, out_part, w_gate, w_up, w_down_columns)
    return out[:3]


def gather_tokens(values):
    return lax.all_gather(values, "shard", axis=0, tiled=True)


def scatter_tokens(partial):
    return lax.psum_scatter(
        partial.astype(BF), "shard", scatter_dimension=0, tiled=True
    ).astype(F32)


def rows_to_columns(weight):
    return lax.all_to_all(weight, "shard", split_axis=1, concat_axis=0, tiled=True)


def columns_to_rows(grad):
    return lax.all_to_all(grad, "shard", split_axis=0, concat_axis=1, tiled=True)


def replica_sum(part):
    return lax.psum(part.astype(BF), "replica")


def general_body(hidden_in, cotangent, doc_lengths, w_query, w_key, w_value, w_out, w_gate, w_up, w_down):
    x = hidden_in[0].astype(F32)
    dyb = cotangent[0]
    tokens_here = x.shape[0]
    groups = lax.axis_size("shard")
    seq_length = tokens_here * groups
    factor = 1.0 / math.sqrt(HEAD_DIM)
    places = jnp.arange(seq_length, dtype=jnp.int32)
    segment, offset = doc_layout(doc_lengths[0], places)
    cosine, sine = rope_tables(offset, HEAD_DIM)
    allowed = ((segment[:, None] == segment[None, :]) & (places[None, :] <= places[:, None]))[None]

    normed_one, inverse_one = normalize(x)
    n1 = gather_tokens(normed_one.astype(BF))
    w_out_columns = rows_to_columns(w_out)
    query = rotate(split_heads(dot(n1, w_query, 1, 1)), cosine, sine).astype(BF)
    keys = rotate(split_heads(dot(n1, w_key, 1, 1)), cosine, sine).astype(BF)
    values = split_heads(dot(n1, w_value, 1, 1)).astype(BF)
    scores = factor * jnp.einsum("hqe,hke->hqk", query, keys, preferred_element_type=F32)
    scores = jnp.where(allowed, scores, masked)
    top = jnp.max(scores, axis=-1, keepdims=True)
    weights = jnp.where(allowed, jnp.exp(scores - top), 0.0)
    total = jnp.sum(weights, axis=-1, keepdims=True)
    log_total = top + jnp.log(total)
    attn = jnp.einsum("hqk,hke->hqe", weights.astype(BF), values, preferred_element_type=F32) / total
    out_b = join_heads(attn).astype(BF)
    middle = x + scatter_tokens(dot(out_b, w_out_columns, 1, 1))

    normed_two, inverse_two = normalize(middle)
    n2 = gather_tokens(normed_two.astype(BF))
    dy_all = gather_tokens(dyb)
    w_down_columns = rows_to_columns(w_down)
    gate = dot(n2, w_gate, 1, 1)
    up = dot(n2, w_up, 1, 1)
    sigma = jax.nn.sigmoid(gate)
    silu = gate * sigma
    hidden = (silu * up).astype(BF)
    grad_down = columns_to_rows(replica_sum(dot(dy_all, hidden, 0, 0)))
    grad_hidden = dot(dy_all, w_down_columns, 1, 0)
    grad_gate_b = (grad_hidden * up * sigma * (1.0 + gate * (1.0 - sigma))).astype(BF)
    grad_up_b = (grad_hidden * silu).astype(BF)
    grad_gate = replica_sum(dot(grad_gate_b, n2, 0, 0).astype(BF))
    grad_up = replica_sum(dot(grad_up_b, n2, 0, 0).astype(BF))
    grad_normed_two = scatter_tokens(dot(grad_gate_b, w_gate, 1, 0) + dot(grad_up_b, w_up, 1, 0))
    mixed = scatter_tokens(dot(hidden, w_down_columns, 1, 1))
    layer_out = (middle + mixed).astype(BF)
    grad_middle = dyb.astype(F32) + norm_back(normed_two, inverse_two, grad_normed_two)

    grad_middle_all = gather_tokens(grad_middle.astype(BF))
    grad_out = columns_to_rows(replica_sum(dot(grad_middle_all, out_b, 0, 0).astype(BF)))
    grad_attn = split_heads(dot(grad_middle_all, w_out_columns, 1, 0)).astype(BF)
    delta = jnp.sum(grad_attn.astype(F32) * attn, axis=-1, keepdims=True)
    probs = jnp.where(allowed, jnp.exp(scores - log_total), 0.0)
    grad_probs = jnp.einsum("hqe,hke->hqk", grad_attn, values, preferred_element_type=F32)
    grad_scores = (probs * (grad_probs - delta)).astype(BF)
    query_grad = factor * jnp.einsum("hqk,hke->hqe", grad_scores, keys, preferred_element_type=F32)
    key_grad = factor * jnp.einsum("hqk,hqe->hke", grad_scores, query, preferred_element_type=F32)
    value_grad = jnp.einsum("hqk,hqe->hke", probs.astype(BF), grad_attn, preferred_element_type=F32)
    query_grad = join_heads(rotate(query_grad, cosine, -sine)).astype(BF)
    key_grad = join_heads(rotate(key_grad, cosine, -sine)).astype(BF)
    value_grad = join_heads(value_grad).astype(BF)
    grad_query = replica_sum(dot(query_grad, n1, 0, 0).astype(BF))
    grad_key = replica_sum(dot(key_grad, n1, 0, 0).astype(BF))
    grad_value = replica_sum(dot(value_grad, n1, 0, 0).astype(BF))
    grad_normed_one = scatter_tokens(
        dot(query_grad, w_query, 1, 0) + dot(key_grad, w_key, 1, 0) + dot(value_grad, w_value, 1, 0)
    )
    grad_in = grad_middle + norm_back(normed_one, inverse_one, grad_normed_one)
    return (
        layer_out[None],
        grad_in[None],
        grad_query.astype(F32),
        grad_key.astype(F32),
        grad_value.astype(F32),
        grad_out.astype(F32),
        grad_gate.astype(F32),
        grad_up.astype(F32),
        grad_down.astype(F32),
    )


def body(hidden_in, cotangent, doc_lengths, w_query, w_key, w_value, w_out, w_gate, w_up, w_down):
    x_own, dy_own = hidden_in[0], cotangent[0]
    half = HEAD_DIM // 2
    frequency = theta_base ** (-2.0 * (np.arange(HEAD_DIM) % half) / HEAD_DIM)
    (
        n1, query, key, value, attn, attn_b, out_columns, _, down_columns,
        hidden, grad_gate_b, grad_up_b, middle, n2, dy, n2_one, grad_middle, grad_all, dy_one, passed,
        cosine, sine, start,
    ) = front(
        doc_lengths, jnp.asarray(frequency[None], F32), x_own, dy_own,
        w_query, w_key, w_value, w_out, w_gate, w_up, w_down,
    )
    layer_out, grad_in, attn_part, out_part, n2_two, dy_two, near_all = back(
        x_own, start, cosine, sine, hidden, down_columns, grad_all, out_columns, attn_b, attn,
        query, key, value, n1, w_query, w_key, w_value, n2_one, dy_one, middle, grad_middle,
    )
    grad_both, grad_down, attn_sum = ffn_grads(
        near_all, n2_one, n2_two, dy_one, dy_two, passed, n2, dy, (hidden, grad_gate_b, grad_up_b),
        attn_part, out_part, w_gate, w_up, down_columns,
    )
    grad_query, grad_key, grad_value, grad_out = jnp.split(attn_sum.astype(F32), 4, axis=0)
    return (
        layer_out[None],
        grad_in[None],
        grad_query,
        grad_key,
        grad_value,
        grad_out,
        grad_both[0],
        grad_both[1],
        grad_down.astype(F32),
    )


def solution(mesh):
    rows = P("shard", None)
    tokens = P("replica", "shard", None)
    in_specs = (tokens, tokens, P("replica", None)) + (rows,) * 7
    out_specs = (tokens, tokens) + (rows,) * 7
    local = body if mesh.shape["shard"] == 8 and mesh.shape["replica"] == 4 else general_body
    return jax.shard_map(local, mesh=mesh, in_specs=in_specs, out_specs=out_specs, check_vma=False)
```

```python
import functools
import math

import jax
import jax.numpy as jnp
import numpy as np
from jax import lax
from jax.experimental import pallas as pl
from jax.experimental.pallas import tpu as pltpu
from jax.sharding import PartitionSpec as P

HEAD_DIM = 128

epsilon = 1e-05
theta_base = 10000.0
masked = -1e30
BF = jnp.bfloat16
F32 = jnp.float32
MESH = pl.DeviceIdType.MESH
VMEM = pltpu.VMEM


def normalize(values):
    center = values - jnp.mean(values, axis=-1, keepdims=True)
    inverse = lax.rsqrt(jnp.mean(center * center, axis=-1, keepdims=True) + epsilon)
    return (center * inverse, inverse)


def norm_back(normed, inverse, grad):
    inner = (
        grad
        - jnp.mean(grad, axis=-1, keepdims=True)
        - normed * jnp.mean(grad * normed, axis=-1, keepdims=True)
    )
    return inverse * inner


def dot(a, b, ca, cb):
    return lax.dot_general(a, b, (((ca,), (cb,)), ((), ())), preferred_element_type=F32)


def doc_layout(lengths, places):
    ends = jnp.cumsum(lengths)
    starts = ends - lengths
    segment = jnp.sum((places[:, None] >= ends[None, :]).astype(jnp.int32), axis=1)
    member = segment[:, None] == jnp.arange(lengths.shape[0], dtype=jnp.int32)[None, :]
    offset = places - jnp.sum(jnp.where(member, starts[None, :], 0), axis=1)
    return (segment, offset)


def rope_tables(offset, head_dim):
    half = head_dim // 2
    freq = theta_base ** (-2.0 * jnp.arange(half, dtype=F32) / head_dim)
    angle = offset.astype(F32)[:, None] * freq[None, :]
    return (jnp.cos(angle)[None], jnp.sin(angle)[None])


def rotate(values, cosine, sine):
    half = values.shape[-1] // 2
    first = values[..., :half]
    second = values[..., half:]
    return jnp.concatenate(
        [first * cosine - second * sine, second * cosine + first * sine], axis=-1
    )


def split_heads(values):
    tokens, width = values.shape
    return jnp.transpose(values.reshape(tokens, width // HEAD_DIM, HEAD_DIM), (1, 0, 2))


def join_heads(values):
    heads, tokens, size = values.shape
    return jnp.transpose(values, (1, 0, 2)).reshape(tokens, heads * size)


def whereabouts():
    place = lax.axis_index("shard")
    core, col, row = lax.rem(place, 2), lax.rem(place // 2, 2), place // 4
    across, along = place + 2 - 4 * col, place + 4 - 8 * row
    return place, place + 1 - 2 * core, across, along, across + 4 - 8 * row


def whereabouts_of_mate():
    me, mate, across, along, far = whereabouts()
    shift = mate - me
    return across + shift, along + shift, far + shift


def tile_loop(rows, columns, size, step, narrow=None):
    narrow = narrow or size
    across = columns // narrow

    def one(i, carry):
        step(
            pl.ds(pl.multiple_of((i // across) * size, size), size),
            pl.ds(pl.multiple_of(lax.rem(i, across) * narrow, narrow), narrow),
        )
        return carry

    lax.fori_loop(0, (rows // size) * across, one, 0)


def product(a, b, ca, cb):
    return lax.dot_general(a, b, (((ca,), (cb,)), ((), ())), preferred_element_type=F32)


def ffn_tile(normed, dy, w_gate, w_up, w_down, hidden, grad_gate, grad_up, rows, columns):
    gate = product(normed[rows, :], w_gate[columns, :], 1, 1)
    up = product(normed[rows, :], w_up[columns, :], 1, 1)
    grad = product(dy[rows, :], w_down[:, columns], 1, 0)
    sigma = 0.5 + 0.5 * jnp.tanh(0.5 * gate)
    silu = gate * sigma
    hidden[rows, columns] = (silu * up).astype(BF)
    grad_gate[rows, columns] = (grad * (up * (sigma + silu * (1.0 - sigma)))).astype(BF)
    grad_up[rows, columns] = (grad * silu).astype(BF)


def block_rows(slot, tokens, part=0):
    size = tokens // 2
    if part:
        return pl.ds(pl.multiple_of(slot * tokens + (part - 1) * size, size), size)
    return pl.ds(pl.multiple_of(slot * tokens, tokens), tokens)


class Gather:
    def __init__(self, block, out, sent, came):
        self.block, self.out, self.sent, self.came = block, out, sent, came
        self.tokens = block.shape[0]
        self.replica = lax.axis_index("replica")
        self.me, self.mate, self.across, self.along, self.far = whereabouts()
        self.sends = []

    def move(self, k, slot, part, device, first=False):
        tokens = self.tokens
        local = pl.ds((part - 1) * (tokens // 2) if part else 0, tokens // 2 if part else tokens)
        rows = block_rows(slot, tokens, part)
        return pltpu.make_async_remote_copy(
            src_ref=self.block.at[local] if first else self.out.at[rows],
            dst_ref=self.out.at[rows],
            send_sem=self.sent.at[k],
            recv_sem=self.came.at[k],
            device_id=(self.replica, device),
            device_id_type=MESH,
        )

    def start(self, *moves):
        for one in moves:
            self.move(*one).start()
            self.sends.append(one)

    def came_in(self, *moves):
        for k, slot, part in moves:
            self.move(k, slot, part, self.mate).wait_recv()

    def firsts(self):
        me = self.me
        return (
            (1, me, 1, self.across, True),
            (3, me, 2, self.along, True),
            (0, me, 0, self.mate, True),
            (2, me, 2, self.across, True),
            (4, me, 1, self.along, True),
        )

    def one(self):
        self.start(*self.firsts())

    def two(self):
        self.came_in((1, self.across, 1))
        self.start((5, self.across, 1, self.along), (6, self.across, 1, self.mate))
        self.came_in((3, self.along, 2))
        self.start((7, self.along, 2, self.across), (8, self.along, 2, self.mate))

    def three(self):
        self.came_in((2, self.across, 2))
        self.start((9, self.across, 2, self.mate))
        self.came_in((4, self.along, 1))
        self.start((10, self.along, 1, self.mate))

    def four(self):
        self.came_in((5, self.far, 1))
        self.start((11, self.far, 1, self.mate))
        self.came_in((7, self.far, 2))
        self.start((12, self.far, 2, self.mate))

    def finish_near(self):
        across, _, _ = whereabouts_of_mate()
        self.came_in((0, self.mate, 0), (6, across, 1), (9, across, 2))

    def finish_far(self):
        _, along, far = whereabouts_of_mate()
        self.came_in((8, along, 2), (10, along, 1), (11, far, 1), (12, far, 2))

    def finish(self):
        self.finish_near()
        self.finish_far()

    def drain(self):
        for one in self.sends:
            self.move(*one).wait_send()


class Scatter:
    def __init__(self, parts, buffers, sent, came):
        self.parts = parts
        self.pair, self.sums, self.by_far, self.by_side = buffers
        self.sent, self.came = sent, came
        self.tokens = self.pair.shape[1]
        self.replica = lax.axis_index("replica")
        me, mate, across, along, far = whereabouts()
        self.mine, self.shift, self.mate = (me, across, along, far), mate - me, mate
        low, high = pl.ds(0, self.tokens // 2), pl.ds(self.tokens // 2, self.tokens // 2)
        self.low, self.high = low, high
        sums, by_far, by_side = self.sums, self.by_far, self.by_side
        self.swaps = [
            self.move(k, parts.at[block_rows(self.mine[k] + self.shift, self.tokens)], self.pair.at[k], mate)
            for k in range(4)
        ]
        self.far_low = self.move(4, sums.at[2, low], by_far.at[0], across)
        self.far_high = self.move(5, sums.at[2, high], by_far.at[1], along)
        self.across_low = self.move(6, sums.at[0, low], by_side.at[0, low], across)
        self.along_high = self.move(7, sums.at[1, high], by_side.at[1, high], along)
        self.along_low = self.move(8, sums.at[1, low], by_side.at[1, low], along)
        self.across_high = self.move(9, sums.at[0, high], by_side.at[0, high], across)

    def move(self, k, src, dst, device):
        return pltpu.make_async_remote_copy(
            src_ref=src,
            dst_ref=dst,
            send_sem=self.sent.at[k],
            recv_sem=self.came.at[k],
            device_id=(self.replica, device),
            device_id_type=MESH,
        )

    def swap(self, *which):
        for k in which:
            self.swaps[k].start()

    def pair_sum(self, k):
        self.swaps[k].wait_recv()
        own = self.parts[block_rows(self.mine[k], self.tokens), :].astype(F32)
        self.sums[k - 1] = (own + self.pair[k].astype(F32)).astype(BF)

    def send_far(self):
        self.pair_sum(3)
        self.far_low.start()
        self.far_high.start()

    def send_near(self):
        self.pair_sum(1)
        self.across_low.start()
        self.pair_sum(2)
        self.along_high.start()

    def send_rest(self):
        low, high, sums = self.low, self.high, self.sums
        self.far_low.wait_recv()
        sums[1, low] = (sums[1, low].astype(F32) + self.by_far[0].astype(F32)).astype(BF)
        self.along_low.start()
        self.far_high.wait_recv()
        sums[0, high] = (sums[0, high].astype(F32) + self.by_far[1].astype(F32)).astype(BF)
        self.across_high.start()

    def total(self):
        self.swaps[0].wait_recv()
        own = self.parts[block_rows(self.mine[0], self.tokens), :].astype(F32)
        own = own + self.pair[0].astype(F32)
        for copy in (self.across_low, self.along_high, self.along_low, self.across_high):
            copy.wait_recv()
        return own + (self.by_side[0].astype(F32) + self.by_side[1].astype(F32))

    def drain(self):
        for copy in (
            *self.swaps, self.far_low, self.far_high, self.across_low, self.along_high,
            self.along_low, self.across_high,
        ):
            copy.wait_send()


class Line:
    def __init__(self, own, slots, sent, came):
        self.own, self.slots, self.sent, self.came = own, slots, sent, came
        self.replica, self.me = lax.axis_index("replica"), lax.axis_index("shard")
        self.replicas = lax.axis_size("replica")

    def move(self, way, i, slot, first):
        target = self.replica + (1 if way == 0 else -1)
        return pltpu.make_async_remote_copy(
            src_ref=self.own if first else self.slots(slot),
            dst_ref=self.slots(slot),
            send_sem=self.sent.at[way, i],
            recv_sem=self.came.at[way, i],
            device_id=(target, self.me),
            device_id_type=MESH,
        )

    def source(self, way, i):
        return self.replica - i if way == 0 else self.replica + i

    def has(self, way, i):
        return self.replica >= i if way == 0 else self.replica + i < self.replicas

    def can_send(self, way):
        return self.replica + 1 < self.replicas if way == 0 else self.replica >= 1

    def start(self):
        for way in (0, 1):

            @pl.when(self.can_send(way))
            def _(way=way):
                self.move(way, 0, self.replica, True).start()

    def step(self, i):
        for way in (0, 1):

            @pl.when(self.has(way, i))
            def _(way=way):
                self.move(way, i - 1, self.source(way, i), False).wait_recv()
                if i < self.replicas - 1:

                    @pl.when(self.can_send(way))
                    def _():
                        self.move(way, i, self.source(way, i), False).start()

    def drain(self):
        for way in (0, 1):
            for i in range(self.replicas - 1):

                @pl.when(self.has(way, i) & self.can_send(way))
                def _(way=way, i=i):
                    self.move(way, i, self.source(way, i), i == 0).wait_send()


class Hop:
    def __init__(self, k, source, landing, sent, came):
        self.k, self.source, self.landing, self.sent, self.came = k, source, landing, sent, came
        self.replica, self.me = lax.axis_index("replica"), lax.axis_index("shard")
        self.replicas = lax.axis_size("replica")

    def move(self, way):
        return pltpu.make_async_remote_copy(
            src_ref=self.source(way),
            dst_ref=self.landing.at[way],
            send_sem=self.sent.at[way],
            recv_sem=self.came.at[way],
            device_id=(self.replica + (1 if way == 0 else -1), self.me),
            device_id_type=MESH,
        )

    def sends(self, way):
        last = self.replicas - 1
        if way == 0:
            return (self.replica >= self.k - 1) & (self.replica < last)
        return (self.replica <= self.replicas - self.k) & (self.replica > 0)

    def receives(self, way):
        return self.replica >= self.k if way == 0 else self.replica < self.replicas - self.k

    def start(self):
        for way in (0, 1):

            @pl.when(self.sends(way))
            def _(way=way):
                self.move(way).start()

    def arrive(self):
        for way in (0, 1):

            @pl.when(self.receives(way))
            def _(way=way):
                self.move(way).wait_recv()

    def drain(self):
        for way in (0, 1):

            @pl.when(self.sends(way))
            def _(way=way):
                self.move(way).wait_send()


def greet_all(barrier):
    replica, replicas = lax.axis_index("replica"), lax.axis_size("replica")
    me, groups = lax.axis_index("shard"), lax.axis_size("shard")
    for i in range(1, groups):
        device = lax.rem(me + i, groups)
        pl.semaphore_signal(barrier, inc=1, device_id=(replica, device), device_id_type=MESH)

    @pl.when(replica >= 1)
    def _():
        pl.semaphore_signal(barrier, inc=1, device_id=(replica - 1, me), device_id_type=MESH)

    @pl.when(replica + 1 < replicas)
    def _():
        pl.semaphore_signal(barrier, inc=1, device_id=(replica + 1, me), device_id_type=MESH)

    edge = (replica == 0) | (replica == replicas - 1)

    @pl.when(edge)
    def _():
        pl.semaphore_wait(barrier, groups)

    @pl.when(jnp.logical_not(edge))
    def _():
        pl.semaphore_wait(barrier, groups + 1)


def rotate_head(values, cosine, sine):
    return values * cosine + pltpu.roll(values, values.shape[-1] // 2, 1) * sine


def key_reach(first, step, sequence):
    low = max(0, (first + 1 - sequence // 2) // 128 * 128)
    return low, pl.ds(low, first + step - low)


def allowed_bias(start, first, step, low):
    shape = (step, first + step - low)
    key_place = lax.broadcasted_iota(jnp.int32, shape, 1) + low
    query_place = lax.broadcasted_iota(jnp.int32, shape, 0) + first
    return jnp.where((key_place <= query_place) & (key_place >= start), 0.0, masked)


def head_scores(query, keys, bias):
    return product(query, keys, 1, 1) * (1.0 / math.sqrt(HEAD_DIM)) + bias


def fill_tables(lengths, frequency, cosine, sine, start):
    shape = start.shape
    place = lax.broadcasted_iota(jnp.int32, shape, 0)
    begin = jnp.zeros(shape, jnp.int32)
    end = 0
    for i in range(lengths.shape[1] - 1):
        end = end + lengths[0, i]
        begin = jnp.where(place >= end, end, begin)
    start[...] = begin
    angle = (place - begin).astype(F32) * frequency[...]
    lane = lax.broadcasted_iota(jnp.int32, shape, 1)
    cosine[...] = jnp.cos(angle)
    sine[...] = jnp.where(lane < shape[1] // 2, -1.0, 1.0) * jnp.sin(angle)


def front_kernel(
    lengths, frequency, x_own, dy_own, w_query, w_key, w_value, w_out, w_gate, w_up, w_down,
    n1_out, query_out, key_out, value_out, attn_out, attn_b_out, out_columns_out, down_parts,
    down_columns_out, hidden_out, grad_gate_out, grad_up_out, middle_out, n2_out, dy_out, n2_hopped,
    grad_out, grad_all_out, dy_hopped, passed, cosine_out, sine_out, start_out,
    n1, n2, dy, query, key, value, attn, attn_b, out_columns, gate_w, up_w, down_w,
    hidden, grad_gate, grad_up, parts, pair, sums, by_far, by_side, middle, normed, n2_own, grad_own, n1_own, cosine, sine, start,
    load_sem, save_sem, gather_sent, gather_came, scatter_sent, scatter_came,
    swap_sent, swap_came, line_sent, line_came, down_sent, down_came, pass_sem,
):
    replica = lax.axis_index("replica")
    replicas = lax.axis_size("replica")
    me = lax.axis_index("shard")
    groups = lax.axis_size("shard")
    tokens, width = x_own.shape
    sequence = n1.shape[0]
    saves = []

    def save(src, dst):
        copy = pltpu.make_async_copy(src, dst, save_sem.at[len(saves)])
        copy.start()
        saves.append(copy)

    def exchange(which, source, target):
        copies = []
        for i in range(1, groups):
            device = lax.rem(me + i, groups)
            copies.append(
                pltpu.make_async_remote_copy(
                    src_ref=source(device),
                    dst_ref=target,
                    send_sem=swap_sent.at[which, i],
                    recv_sem=swap_came.at[which, i],
                    device_id=(replica, device),
                    device_id_type=MESH,
                )
            )
        return copies

    gate_load = pltpu.make_async_copy(w_gate, gate_w, load_sem.at[0])
    up_load = pltpu.make_async_copy(w_up, up_w, load_sem.at[1])
    gate_load.start()
    up_load.start()
    own_rows = block_rows(me, tokens)
    x = x_own[...].astype(F32)
    center = x - jnp.mean(x, axis=-1, keepdims=True)
    inverse = lax.rsqrt(jnp.mean(center * center, axis=-1, keepdims=True) + epsilon)
    n1_own[...] = (center * inverse).astype(BF)
    own_n1 = pltpu.make_async_copy(n1_own, n1.at[own_rows], load_sem.at[2])
    own_dy = pltpu.make_async_copy(dy_own, dy.at[own_rows], load_sem.at[3])
    own_n1.start()
    own_dy.start()

    greet_all(pltpu.get_barrier_semaphore())
    n1_gather = Gather(n1_own, n1, gather_sent.at[0], gather_came.at[0])
    dy_gather = Gather(dy_own, dy, gather_sent.at[1], gather_came.at[1])
    n2_gather = Gather(n2_own, n2, gather_sent.at[2], gather_came.at[2])
    grad_gather = Gather(grad_own, grad_all_out, gather_sent.at[3], gather_came.at[3])
    half = sequence // 2
    dy_half = dy.at[pl.ds(pl.multiple_of(lax.rem(me, 2) * half, half), half)]
    n2_hop = Hop(1, lambda way: n2_own, n2_hopped, line_sent.at[0], line_came.at[0])
    dy_hop = Hop(1, lambda way: dy_half, dy_hopped, line_sent.at[1], line_came.at[1])
    passing = [
        pltpu.make_async_remote_copy(
            src_ref=src,
            dst_ref=passed.at[way],
            send_sem=pass_sem.at[0, way],
            recv_sem=pass_sem.at[1, way],
            device_id=(replica + (1 if way == 0 else -1), me),
            device_id_type=MESH,
        )
        for way in (0, 1)
        for src in (dy_own, passed.at[way])
    ]
    last = replicas - 1

    def passes(way, k):
        return replica == (k if way == 0 else last - k)

    def pass_on(k):
        for way in (0, 1):

            @pl.when(passes(way, k))
            def _(way=way):
                if k:
                    passing[2 * way].wait_recv()
                if k < 2:
                    passing[2 * way + (1 if k else 0)].start()

    down_line = Line(
        down_parts.at[replica], lambda s: down_parts.at[s], down_sent, down_came
    )
    buffers = (pair, sums, by_far, by_side)

    n1_gather.one()
    pass_on(0)
    fill_tables(lengths, frequency, cosine, sine, start)
    save(cosine, cosine_out)
    save(sine, sine_out)
    save(start, start_out)
    n1_gather.two()
    n1_gather.three()
    wide = w_out.shape[0]
    mine = pl.ds(pl.multiple_of(me * wide, wide), wide)
    part = down_parts.shape[2]

    def down_block(device):
        column = (device * replicas + replica) * part
        return w_down.at[:, pl.ds(pl.multiple_of(column, part), part)]

    def out_block(device):
        return w_out.at[:, pl.ds(pl.multiple_of(device * wide, wide), wide)]

    down_swaps = exchange(1, down_block, down_parts.at[replica, mine])
    out_swaps = exchange(0, out_block, out_columns.at[mine])
    own_down = pltpu.make_async_copy(down_block(me), down_parts.at[replica, mine], load_sem.at[5])
    own_down.start()
    own_out = pltpu.make_async_copy(out_block(me), out_columns.at[mine], load_sem.at[4])
    own_out.start()
    for copy in down_swaps + out_swaps:
        copy.start()
    pass_on(1)
    own_n1.wait()
    n1_gather.finish_near()
    row = me // (groups // 2)

    def half_rows(i):
        return pl.ds(pl.multiple_of((row + i * (1 - 2 * row)) * half, half), half)


    heads = query.shape[1] // HEAD_DIM
    def projections(i, carry):
        rows = half_rows(i)
        for weight, target in ((w_query, query), (w_key, key), (w_value, value)):
            values = product(n1[rows, :], weight[...], 1, 1)
            for head in range(heads):
                lanes = pl.ds(head * HEAD_DIM, HEAD_DIM)
                piece = values[:, head * HEAD_DIM : (head + 1) * HEAD_DIM]
                if target is not value:
                    piece = rotate_head(piece, cosine[rows, :], sine[rows, :])
                target[rows, lanes] = piece.astype(BF)

        @pl.when(i == 0)
        def _():
            n1_gather.four()
            n1_gather.finish_far()

        return carry

    lax.fori_loop(0, 2, projections, 0)
    save(n1, n1_out)
    save(query, query_out)
    save(key, key_out)
    save(value, value_out)
    own_down.wait()
    for copy in down_swaps:
        copy.wait_recv()
    down_line.start()
    step = 256
    for first in range(0, sequence, step):
        rows = pl.ds(first, step)
        low, reach = key_reach(first, step, sequence)
        bias = allowed_bias(start[rows, 0:1], first, step, low)
        for head in range(heads):
            lanes = pl.ds(head * HEAD_DIM, HEAD_DIM)
            scores = head_scores(query[rows, lanes], key[reach, lanes], bias)
            weights = jnp.exp(scores - jnp.max(scores, axis=-1, keepdims=True))
            total = jnp.sum(weights, axis=-1, keepdims=True)
            result = product(weights.astype(BF), value[reach, lanes], 1, 0) / total
            attn[rows, lanes] = result
            attn_b[rows, lanes] = result.astype(BF)
    pass_on(2)
    save(attn, attn_out)
    save(attn_b, attn_b_out)

    own_out.wait()
    for copy in out_swaps:
        copy.wait_recv()
    save(out_columns, out_columns_out)

    scatter = Scatter(parts, buffers, scatter_sent.at[0], scatter_came.at[0])

    def spread(i, carry):
        def step(rows, columns):
            rows = half_rows(1 - i)
            parts[rows, columns] = product(attn_b[rows, :], out_columns[columns, :], 1, 1).astype(BF)

        tile_loop(half, width, half, step)

        @pl.when(i == 0)
        def _():
            scatter.swap(3, 2)

        return carry

    lax.fori_loop(0, 2, spread, 0)
    scatter.swap(1, 0)
    scatter.send_far()
    scatter.send_near()
    down_line.step(1)
    scatter.send_rest()
    middle[...] = x_own[...].astype(F32) + scatter.total()
    scatter.drain()
    save(middle, middle_out)
    center = middle[...] - jnp.mean(middle[...], axis=-1, keepdims=True)
    inverse = lax.rsqrt(jnp.mean(center * center, axis=-1, keepdims=True) + epsilon)
    normed[...] = center * inverse
    n2_own[...] = normed[...].astype(BF)
    n2_gather.one()
    own_n2 = pltpu.make_async_copy(n2_own, n2.at[own_rows], load_sem.at[6])
    own_n2.start()
    n2_gather.two()
    n2_gather.three()
    dy_gather.one()
    down_line.step(2)
    n2_hop.start()
    own_n2.wait()
    n2_gather.finish_near()
    gate_load.wait()
    up_load.wait()

    def feed_forward(i):
        def forward(rows, columns):
            rows = half_rows(i)
            gate = product(n2[rows, :], gate_w[columns, :], 1, 1)
            up = product(n2[rows, :], up_w[columns, :], 1, 1)
            sigma = 0.5 + 0.5 * jnp.tanh(0.5 * gate)
            silu = gate * sigma
            hidden[rows, columns] = (silu * up).astype(BF)
            grad_gate[rows, columns] = (up * (sigma + silu * (1.0 - sigma))).astype(BF)
            grad_up[rows, columns] = silu.astype(BF)

        tile_loop(half, gate_w.shape[0], half, forward, 256)

    def both_forward(i, carry):
        feed_forward(i)

        @pl.when(i == 0)
        def _():
            n2_gather.four()
            n2_gather.finish_far()
            dy_gather.two()

        return carry

    lax.fori_loop(0, 2, both_forward, 0)
    save(n2, n2_out)
    dy_gather.three()
    dy_gather.four()
    own_dy.wait()
    dy_gather.finish()
    save(dy, dy_out)
    save(hidden, hidden_out)
    dy_hop.start()
    down_line.step(3)
    down_loads = []
    for r in range(replicas):
        down_loads.append(
            pltpu.make_async_copy(
                down_parts.at[r], down_w.at[:, pl.ds(r * part, part)], load_sem.at[7 + r]
            )
        )
        down_loads[-1].start()
    for copy in down_loads:
        copy.wait()
    save(down_w, down_columns_out)

    back = Scatter(parts, buffers, scatter_sent.at[1], scatter_came.at[1])

    def feed(base):
        def grads(rows, columns):
            rows = pl.ds(pl.multiple_of(base, half), half)
            grad = product(dy[rows, :], down_w[:, columns], 1, 0)
            grad_gate[rows, columns] = (grad * grad_gate[rows, columns].astype(F32)).astype(BF)
            grad_up[rows, columns] = (grad * grad_up[rows, columns].astype(F32)).astype(BF)

        tile_loop(half, gate_w.shape[0], half, grads)

        def backward(rows, columns):
            rows = pl.ds(pl.multiple_of(base, half), half)
            value = product(grad_gate[rows, :], gate_w[:, columns], 1, 0)
            value = value + product(grad_up[rows, :], up_w[:, columns], 1, 0)
            parts[rows, columns] = value.astype(BF)

        tile_loop(half, width, half, backward)

    def both_back(i, carry):
        feed((1 - row + i * (2 * row - 1)) * half)

        @pl.when(i == 0)
        def _():
            back.swap(3, 2)
            back.send_far()

        return carry

    lax.fori_loop(0, 2, both_back, 0)
    save(grad_gate, grad_gate_out)
    save(grad_up, grad_up_out)
    back.swap(1, 0)
    back.send_near()
    back.send_rest()
    inner = back.total()
    back.drain()
    inner = (
        inner
        - jnp.mean(inner, axis=-1, keepdims=True)
        - normed[...] * jnp.mean(inner * normed[...], axis=-1, keepdims=True)
    )
    center = middle[...] - jnp.mean(middle[...], axis=-1, keepdims=True)
    inverse = lax.rsqrt(jnp.mean(center * center, axis=-1, keepdims=True) + epsilon)
    normed[...] = dy_own[...].astype(F32) + inverse * inner
    grad_own[...] = normed[...].astype(BF)
    grad_gather.one()
    save(normed, grad_out)
    save(grad_own, grad_all_out.at[own_rows])
    grad_gather.two()
    grad_gather.three()
    grad_gather.four()
    grad_gather.finish()
    for way in (0, 1):

        @pl.when(passes(way, 0) | passes(way, 1))
        def _(way=way):
            passing[2 * way].wait_send()

    n2_hop.arrive()
    dy_hop.arrive()
    for copy in saves:
        copy.wait()
    for copy in out_swaps + down_swaps:
        copy.wait_send()
    for user in (n1_gather, n2_gather, dy_gather, grad_gather, down_line, n2_hop, dy_hop):
        user.drain()


def front(lengths, frequency, x_own, dy_own, w_query, w_key, w_value, w_out, w_gate, w_up, w_down):
    groups, replicas = lax.axis_size("shard"), lax.axis_size("replica")
    tokens, width = x_own.shape
    sequence = tokens * groups
    wide, columns = w_query.shape[0], w_gate.shape[0]
    anywhere, vmem = pl.BlockSpec(memory_space=pl.ANY), pl.BlockSpec(memory_space=VMEM)

    def shape(dims, kind=BF):
        return jax.ShapeDtypeStruct(dims, kind)

    outs = (
        shape((sequence, width)),
        shape((sequence, wide)),
        shape((sequence, wide)),
        shape((sequence, wide)),
        shape((sequence, wide), F32),
        shape((sequence, wide)),
        shape((width, wide)),
        shape((replicas, width, columns // replicas)),
        shape((width, columns)),
        shape((sequence, columns)),
        shape((sequence, columns)),
        shape((sequence, columns)),
        shape((tokens, width), F32),
        shape((sequence, width)),
        shape((sequence, width)),
        shape((2, tokens, width)),
        shape((tokens, width), F32),
        shape((sequence, width)),
        shape((2, sequence // 2, width)),
        shape((2, tokens, width)),
        shape((sequence, HEAD_DIM), F32),
        shape((sequence, HEAD_DIM), F32),
        shape((sequence, HEAD_DIM), jnp.int32),
    )
    dma = pltpu.SemaphoreType.DMA
    return pl.pallas_call(
        front_kernel,
        out_shape=outs,
        in_specs=[pl.BlockSpec(memory_space=pltpu.SMEM)] + [vmem] * 6 + [anywhere] * 4,
        out_specs=(anywhere,) * len(outs),
        scratch_shapes=[
            pltpu.VMEM((sequence, width), BF),
            pltpu.VMEM((sequence, width), BF),
            pltpu.VMEM((sequence, width), BF),
            pltpu.VMEM((sequence, wide), BF),
            pltpu.VMEM((sequence, wide), BF),
            pltpu.VMEM((sequence, wide), BF),
            pltpu.VMEM((sequence, wide), F32),
            pltpu.VMEM((sequence, wide), BF),
            pltpu.VMEM((width, wide), BF),
            pltpu.VMEM((columns, width), BF),
            pltpu.VMEM((columns, width), BF),
            pltpu.VMEM((width, columns), BF),
            pltpu.VMEM((sequence, columns), BF),
            pltpu.VMEM((sequence, columns), BF),
            pltpu.VMEM((sequence, columns), BF),
            pltpu.VMEM((sequence, width), BF),
            pltpu.VMEM((4, tokens, width), BF),
            pltpu.VMEM((3, tokens, width), BF),
            pltpu.VMEM((2, tokens // 2, width), BF),
            pltpu.VMEM((2, tokens, width), BF),
            pltpu.VMEM((tokens, width), F32),
            pltpu.VMEM((tokens, width), F32),
            pltpu.VMEM((tokens, width), BF),
            pltpu.VMEM((tokens, width), BF),
            pltpu.VMEM((tokens, width), BF),
            pltpu.VMEM((sequence, HEAD_DIM), F32),
            pltpu.VMEM((sequence, HEAD_DIM), F32),
            pltpu.VMEM((sequence, HEAD_DIM), jnp.int32),
            dma((7 + replicas,)),
            dma((24,)),
            dma((4, 13)),
            dma((4, 13)),
            dma((2, 10)),
            dma((2, 10)),
            dma((2, groups)),
            dma((2, groups)),
            dma((2, 2)),
            dma((2, 2)),
            dma((2, replicas)),
            dma((2, replicas)),
            dma((2, 2)),
        ],
        compiler_params=pltpu.CompilerParams(
            collective_id=3, has_side_effects=True, vmem_limit_bytes=67043328
        ),
        cost_estimate=pl.CostEstimate(
            flops=12 * sequence * width * columns, bytes_accessed=64 * 1024 * 1024, transcendentals=0
        ),
        name="front",
    )(lengths, frequency, x_own, dy_own, w_query, w_key, w_value, w_out, w_gate, w_up, w_down)


def back_kernel(
    x_own, start, cosine, sine, hidden_in, down_in, grad_in, out_columns_in, attn_b_in, attn_in,
    query_in, key_in, value_in, n1_in, w_query, w_key, w_value, n2_near, dy_near, middle, grad_middle,
    layer_out, input_grad, attn_part, out_grad_out, n2_hopped, dy_hopped, near_all,
    hidden, down_w, grad, out_columns, attn_b, attn, query, key, value, n1, weights,
    grad_attn, key_grad, value_grad, columns_grad, out_grad, rows_grad, parts,
    pair, sums, by_far, by_side, pair2, sums2, by_far2, by_side2,
    load_sem, save_sem, scatter_sent, scatter_came, line_sent, line_came,
    gather_sent, gather_came,
):
    sequence, width = n1.shape
    me = lax.axis_index("shard")
    near_half = x_own.shape[0] // 2
    near_block = n2_near.at[1 - lax.rem(lax.axis_index("replica"), 2), pl.ds(0, near_half)]
    near = Gather(near_block, near_all, gather_sent, gather_came)
    wide = query.shape[1]
    heads = wide // HEAD_DIM
    pairs = (
        (hidden_in, hidden), (down_in, down_w), (grad_in, grad), (out_columns_in, out_columns),
        (attn_b_in, attn_b), (attn_in, attn), (query_in, query), (key_in, key), (value_in, value),
        (n1_in, n1), (w_query, weights.at[pl.ds(0, wide)]), (w_key, weights.at[pl.ds(wide, wide)]),
        (w_value, weights.at[pl.ds(2 * wide, wide)]),
    )
    loads = [
        pltpu.make_async_copy(src, dst, load_sem.at[i]) for i, (src, dst) in enumerate(pairs)
    ]
    for copy in loads[:2]:
        copy.start()
    greet_all(pltpu.get_barrier_semaphore())
    hops = (
        Hop(2, lambda way: n2_near.at[way], n2_hopped, line_sent.at[0], line_came.at[0]),
        Hop(2, lambda way: dy_near.at[way], dy_hopped, line_sent.at[1], line_came.at[1]),
    )
    for hop in hops:
        hop.start()
    loads[0].wait()
    loads[1].wait()
    for copy in loads[2:]:
        copy.start()

    mixed = Scatter(parts, (pair, sums, by_far, by_side), scatter_sent.at[0], scatter_came.at[0])
    half = sequence // 2
    row = me // (lax.axis_size("shard") // 2)

    def by_halves(scatter, tile):
        def one_half(i, carry):
            def step(rows, columns):
                rows = pl.ds(pl.multiple_of((1 - row + i * (2 * row - 1)) * half, half), half)
                parts[rows, columns] = tile(rows, columns).astype(BF)

            tile_loop(half, width, half, step)

            @pl.when(i == 0)
            def _():
                scatter.swap(3, 2)

            return carry

        lax.fori_loop(0, 2, one_half, 0)
        scatter.swap(1, 0)

    by_halves(mixed, lambda rows, columns: product(hidden[rows, :], down_w[columns, :], 1, 1))

    for copy in loads[2:6]:
        copy.wait()
    mixed.send_far()
    mixed.send_near()
    near.one()
    own_near = pltpu.make_async_copy(near_block, near_all.at[block_rows(me, near.tokens)], save_sem.at[2])
    own_near.start()

    def out_step(i, carry):
        rows = pl.ds(pl.multiple_of(i * 512, 512), 512)
        out_grad[rows, :] = product(grad[:, rows], attn_b[...], 0, 0).astype(BF)
        return carry

    lax.fori_loop(0, width // 512, out_step, 0)
    out_save = pltpu.make_async_copy(out_grad, out_grad_out, save_sem.at[0])
    out_save.start()

    def attn_step(i, carry):
        rows = pl.ds(pl.multiple_of(i * 512, 512), 512)
        grad_attn[rows, :] = product(grad[rows, :], out_columns[...], 1, 0).astype(BF)
        return carry

    lax.fori_loop(0, sequence // 512, attn_step, 0)
    for copy in loads[6:]:
        copy.wait()
    mixed.send_rest()

    near.two()
    step = 256
    for first in range(sequence - step, -1, -step):
        if first == sequence - 2 * step:
            near.three()
        if first == sequence - 3 * step:
            near.four()
        rows = pl.ds(first, step)
        low, upto = key_reach(first, step, sequence)
        bias = allowed_bias(start[rows, 0:1], first, step, low)
        for head in range(heads):
            lanes = pl.ds(head * HEAD_DIM, HEAD_DIM)
            query_piece, grad_piece = query[rows, lanes], grad_attn[rows, lanes]
            scores = head_scores(query_piece, key[upto, lanes], bias)
            probs = jnp.exp(scores - jnp.max(scores, axis=-1, keepdims=True))
            probs = probs / jnp.sum(probs, axis=-1, keepdims=True)
            delta = jnp.sum(grad_piece.astype(F32) * attn[rows, lanes], axis=-1, keepdims=True)
            grad_probs = product(grad_piece, value[upto, lanes], 1, 1)
            grad_scores = (probs * (grad_probs - delta)).astype(BF)
            query_grad = product(grad_scores, key[upto, lanes], 1, 0) * (1.0 / math.sqrt(HEAD_DIM))
            query_grad = rotate_head(query_grad, cosine[rows, :], -sine[rows, :])
            columns_grad[rows, lanes] = query_grad.astype(BF)
            key_part = product(grad_scores, query_piece, 0, 0)
            value_part = product(probs.astype(BF), grad_piece, 0, 0)
            if first == sequence - step:
                key_grad[upto, lanes] = key_part
                value_grad[upto, lanes] = value_part
                if low:
                    key_grad[pl.ds(0, low), lanes] = jnp.zeros((low, HEAD_DIM), F32)
                    value_grad[pl.ds(0, low), lanes] = jnp.zeros((low, HEAD_DIM), F32)
            else:
                key_grad[upto, lanes] += key_part
                value_grad[upto, lanes] += value_part
    for head in range(heads):
        lanes = pl.ds(head * HEAD_DIM, HEAD_DIM)
        piece = key_grad[:, lanes] * (1.0 / math.sqrt(HEAD_DIM))
        piece = rotate_head(piece, cosine[...], -sine[...])
        columns_grad[:, pl.ds(wide + head * HEAD_DIM, HEAD_DIM)] = piece.astype(BF)
        columns_grad[:, pl.ds(2 * wide + head * HEAD_DIM, HEAD_DIM)] = value_grad[:, lanes].astype(BF)

    layer_out[...] = (middle[...] + mixed.total()).astype(BF)
    mixed.drain()

    last = Scatter(parts, (pair2, sums2, by_far2, by_side2), scatter_sent.at[1], scatter_came.at[1])
    by_halves(last, lambda rows, columns: product(columns_grad[rows, :], weights[:, columns], 1, 0))
    last.send_far()
    last.send_near()

    def collect(rows, columns):
        rows_grad[rows, columns] = product(columns_grad[:, rows], n1[:, columns], 0, 0).astype(BF)

    tile_loop(3 * wide, width, 256, collect, 512)
    rows_save = pltpu.make_async_copy(rows_grad, attn_part, save_sem.at[1])
    rows_save.start()
    last.send_rest()
    x = x_own[...].astype(F32)
    center = x - jnp.mean(x, axis=-1, keepdims=True)
    inverse = lax.rsqrt(jnp.mean(center * center, axis=-1, keepdims=True) + epsilon)
    inner = last.total()
    normed = center * inverse
    inner = (
        inner
        - jnp.mean(inner, axis=-1, keepdims=True)
        - normed * jnp.mean(inner * normed, axis=-1, keepdims=True)
    )
    input_grad[...] = grad_middle[...] + inverse * inner
    last.drain()
    out_save.wait()
    rows_save.wait()
    own_near.wait()
    near.finish()
    near.drain()
    for hop in hops:
        hop.arrive()
        hop.drain()


def back(x_own, start, cosine, sine, hidden, down, grad, out_columns, attn_b, attn, query, key, value, n1,
         w_query, w_key, w_value, n2_near, dy_near, middle, grad_middle):
    groups = lax.axis_size("shard")
    tokens, width = x_own.shape
    sequence = tokens * groups
    wide, columns = query.shape[1], hidden.shape[1]
    anywhere, vmem = pl.BlockSpec(memory_space=pl.ANY), pl.BlockSpec(memory_space=VMEM)
    dma = pltpu.SemaphoreType.DMA
    buffers = [
        pltpu.VMEM((4, tokens, width), BF),
        pltpu.VMEM((3, tokens, width), BF),
        pltpu.VMEM((2, tokens // 2, width), BF),
        pltpu.VMEM((2, tokens, width), BF),
    ]
    return pl.pallas_call(
        back_kernel,
        out_shape=(
            jax.ShapeDtypeStruct((tokens, width), BF),
            jax.ShapeDtypeStruct((tokens, width), F32),
            jax.ShapeDtypeStruct((3 * wide, width), BF),
            jax.ShapeDtypeStruct((width, wide), BF),
            jax.ShapeDtypeStruct(n2_near.shape, BF),
            jax.ShapeDtypeStruct(dy_near.shape, BF),
            jax.ShapeDtypeStruct((sequence // 2, width), BF),
        ),
        in_specs=[vmem] * 4 + [anywhere] * 15 + [vmem] * 2,
        out_specs=(vmem, vmem) + (anywhere,) * 5,
        scratch_shapes=[
            pltpu.VMEM((sequence, columns), BF),
            pltpu.VMEM((width, columns), BF),
            pltpu.VMEM((sequence, width), BF),
            pltpu.VMEM((width, wide), BF),
            pltpu.VMEM((sequence, wide), BF),
            pltpu.VMEM((sequence, wide), F32),
            pltpu.VMEM((sequence, wide), BF),
            pltpu.VMEM((sequence, wide), BF),
            pltpu.VMEM((sequence, wide), BF),
            pltpu.VMEM((sequence, width), BF),
            pltpu.VMEM((3 * wide, width), BF),
            pltpu.VMEM((sequence, wide), BF),
            pltpu.VMEM((sequence, wide), F32),
            pltpu.VMEM((sequence, wide), F32),
            pltpu.VMEM((sequence, 3 * wide), BF),
            pltpu.VMEM((width, wide), BF),
            pltpu.VMEM((3 * wide, width), BF),
            pltpu.VMEM((sequence, width), BF),
            *buffers,
            *buffers,
            dma((13,)),
            dma((3,)),
            dma((2, 10)),
            dma((2, 10)),
            dma((2, 2)),
            dma((2, 2)),
            dma((13,)),
            dma((13,)),
        ],
        compiler_params=pltpu.CompilerParams(
            collective_id=4, has_side_effects=True, vmem_limit_bytes=67043328
        ),
        cost_estimate=pl.CostEstimate(
            flops=24 * sequence * width * wide, bytes_accessed=48 * 1024 * 1024, transcendentals=0
        ),
        name="back",
    )(x_own, start, cosine, sine, hidden, down, grad, out_columns, attn_b, attn, query, key, value, n1,
      w_query, w_key, w_value, n2_near, dy_near, middle, grad_middle)


def every_kernel(
    near_all, n2_one, n2_two, dy_one, dy_two, passed, own_normed, own_dy, own_hidden, own_grad_gate, own_grad_up,
    attn_part, out_part,
    w_gate, w_up, w_down,
    both_out, out_down, out_attn, landed, kept, dy_other,
    out_rows, n2_three, near_rest, passed_three,
    normed, dy, hidden, grads, gate_w, up_w, down_w, down, totals, first_sum, second_sum, stage,
    load_sem, keep_sem, gather_sent, gather_came, line_sent, line_came, line_own, swap_sent, swap_came,
    out_sem, pair_sem, out_swap_sem, hop_sent, hop_came, near_sem,
):
    replica = lax.axis_index("replica")
    replicas = lax.axis_size("replica")
    me = lax.axis_index("shard")
    groups = lax.axis_size("shard")
    tokens = n2_one.shape[1]
    sequence, width = normed.shape
    half = sequence // 2
    columns = hidden.shape[1]
    grad_gate, grad_up = grads.at[0], grads.at[1]
    inner = (replica == 1) | (replica == 2)
    outer = (replica == 0) | (replica == 3)
    beside = replica + 1 - 2 * lax.rem(replica, 2)
    facing = 3 - replica
    chunks, depth = first_sum.shape[0], first_sum.shape[1]

    def piece(c):
        return pl.ds(c * depth, depth)

    def line_move(kind, c, src, dst, target):
        return pltpu.make_async_remote_copy(
            src_ref=src,
            dst_ref=dst,
            send_sem=line_sent.at[kind, c],
            recv_sem=line_came.at[kind, c],
            device_id=(target, me),
            device_id_type=MESH,
        )

    attn_chunks = attn_part.shape[0] // depth

    def own_chunk(c):
        return attn_part.at[piece(c)] if c < attn_chunks else out_rows.at[piece(c - attn_chunks)]

    def inward(c):
        return line_move(0, c, own_chunk(c), first_sum.at[c], beside)

    def middle(c):
        return line_move(1, c, first_sum.at[c], second_sum.at[c], facing)

    def outward(c):
        return line_move(2, c, second_sum.at[c], out_attn.at[piece(c)], beside)

    def keep(c):
        return pltpu.make_async_copy(second_sum.at[c], out_attn.at[piece(c)], line_own.at[c])

    def stage_load(c):
        return pltpu.make_async_copy(own_chunk(c), stage, keep_sem.at[2, 0])

    def half_sums(*which):
        @pl.when(inner)
        def _():
            for c in which:
                stage_load(c).wait()
                inward(c).wait_recv()
                first_sum[c] = (stage[...].astype(F32) + first_sum[c].astype(F32)).astype(BF)
                middle(c).start()
                if c + 1 < chunks:
                    stage_load(c + 1).start()

    def full_sums(*which):
        @pl.when(inner)
        def _():
            for c in which:
                middle(c).wait_recv()
                second_sum[c] = (first_sum[c].astype(F32) + second_sum[c].astype(F32)).astype(BF)
                outward(c).start()
                keep(c).start()

    core = lax.rem(me, 2)
    mate = me + 1 - 2 * core
    low_side, high_side = 1 - lax.rem(replica, 2), 1 - replica // 2
    hop = Hop(3, lambda way: n2_two.at[way], n2_three, hop_sent.at[0], hop_came.at[0])
    dy_hop = Hop(3, lambda way: passed.at[way], passed_three, hop_sent.at[1], hop_came.at[1])
    far_dy = passed_three.at[high_side]
    last_dy = Gather(far_dy, landed.at[3], gather_sent.at[3], gather_came.at[3])

    def last_dy_one():
        dy_hop.arrive()
        last_dy.one()

    def in_outer(action):
        def act():
            @pl.when(outer)
            def _():
                action()

        return act

    n2_blocks = {1: n2_one.at[low_side], 2: n2_two.at[high_side]}
    dy_halves = {1: dy_one.at[low_side], 2: dy_two.at[high_side]}
    roles = ((inner, n2_one.at[high_side]), (outer, n2_three.at[high_side]))
    third = dy_one.at[high_side]

    near = Gather(
        n2_one.at[low_side, pl.ds(tokens // 2, tokens // 2)], near_rest, gather_sent.at[0], gather_came.at[0]
    )

    def gather_of(n, block):
        return Gather(block, landed.at[n - 1], gather_sent.at[n - 1], gather_came.at[n - 1])

    gathers = [gather_of(2, n2_blocks[2]), gather_of(3, roles[0][1])]

    def last_one():
        hop.arrive()
        for role, block in roles:

            @pl.when(role)
            def _(block=block):
                gather_of(3, block).one()

        gather = gathers[1]
        gather.sends.extend(gather.firsts())

    def pair_copy(n, source):
        return pltpu.make_async_remote_copy(
            src_ref=source,
            dst_ref=dy_other.at[n - 1],
            send_sem=pair_sem.at[0, n - 1],
            recv_sem=pair_sem.at[1, n - 1],
            device_id=(replica, mate),
            device_id_type=MESH,
        )

    def normed_loads(n, target, base, block=None):
        copies = []
        if n == 1:
            for i in range(groups):
                device = lax.rem(me + i, groups)
                small = block_rows(device, near.tokens)
                rest = near_rest.at[small] if i else near.block
                for k, source in enumerate((near_all.at[small], rest)):
                    rows = block_rows(device, tokens, k + 1)
                    copies.append(pltpu.make_async_copy(source, target.at[rows], near_sem.at[k, i]))
            return copies
        for i in range(groups):
            device = lax.rem(me + i, groups)
            rows = block_rows(device, tokens)
            source = (n2_blocks[n] if block is None else block) if i == 0 else landed.at[n - 1, rows]
            copies.append(pltpu.make_async_copy(source, target.at[rows], load_sem.at[base, i]))
        return copies

    def dy_loads(n, source=None):
        mine = dy.at[pl.ds(pl.multiple_of(core * half, half), half)]
        others = dy.at[pl.ds(pl.multiple_of((1 - core) * half, half), half)]
        return [
            pltpu.make_async_copy(dy_halves[n] if source is None else source, mine, load_sem.at[1, 0]),
            pltpu.make_async_copy(dy_other.at[n - 1], others, load_sem.at[1, 1]),
        ]

    def far_loads():
        copies = []
        for i in range(groups):
            rows = block_rows(lax.rem(me + i, groups), tokens)
            source = landed.at[3, rows] if i else far_dy
            copies.append(pltpu.make_async_copy(source, dy.at[rows], load_sem.at[1, i]))
        return copies

    wide = width // groups

    def out_move(i):
        device = lax.rem(me + i, groups)
        return pltpu.make_async_remote_copy(
            src_ref=out_part.at[pl.ds(pl.multiple_of(device * wide, wide), wide)],
            dst_ref=out_rows.at[:, pl.ds(pl.multiple_of(me * wide, wide), wide)],
            send_sem=out_swap_sem.at[0, i],
            recv_sem=out_swap_sem.at[1, i],
            device_id=(replica, device),
            device_id_type=MESH,
        )

    own_out = pltpu.make_async_copy(
        out_part.at[pl.ds(pl.multiple_of(me * wide, wide), wide)],
        out_rows.at[:, pl.ds(pl.multiple_of(me * wide, wide), wide)],
        out_swap_sem.at[0, 0],
    )

    def out_ready():
        own_out.wait()
        for i in range(1, groups):
            out_move(i).wait_recv()

        @pl.when(outer)
        def _():
            start_all([inward(c) for c in range(attn_chunks, chunks)])

    def keeps(n):
        return [
            pltpu.make_async_copy(grad_gate, kept.at[n - 1, 0], keep_sem.at[0, n]),
            pltpu.make_async_copy(grad_up, kept.at[n - 1, 1], keep_sem.at[1, n]),
        ]

    def start_all(copies):
        for copy in copies:
            copy.start()

    def wait_all(copies):
        for copy in copies:
            copy.wait()

    first = [
        pltpu.make_async_copy(own_hidden, hidden, load_sem.at[1, 1]),
        pltpu.make_async_copy(own_dy, dy, load_sem.at[1, 0]),
    ]
    weights = [
        pltpu.make_async_copy(w_gate, gate_w, load_sem.at[2, 0]),
        pltpu.make_async_copy(w_up, up_w, load_sem.at[2, 1]),
        pltpu.make_async_copy(w_down, down_w, load_sem.at[2, 2]),
    ]
    start_all(first)
    barrier = pltpu.get_barrier_semaphore()
    for i in range(1, groups):
        device = lax.rem(me + i, groups)
        pl.semaphore_signal(barrier, inc=1, device_id=(replica, device), device_id_type=MESH)
    pl.semaphore_signal(barrier, inc=1, device_id=(beside, me), device_id_type=MESH)

    @pl.when(inner)
    def _():
        pl.semaphore_signal(barrier, inc=1, device_id=(facing, me), device_id_type=MESH)
        pl.semaphore_wait(barrier, groups + 1)

    @pl.when(outer)
    def _():
        pl.semaphore_wait(barrier, groups)

    further, last_normed = gathers
    near.one()
    pair_copy(1, dy_halves[1]).start()
    pair_copy(2, dy_halves[2]).start()
    own_out.start()
    hop.start()
    dy_hop.start()

    @pl.when(inner)
    def _():
        pair_copy(3, third).start()


    @pl.when(outer)
    def _():
        start_all([inward(c) for c in range(attn_chunks)])

    @pl.when(inner)
    def _():
        stage_load(0).start()

    def collect(out, left, right, add):
        def step(rows, cols):
            value = product(left[:, rows], right[:, cols], 0, 0)
            if add is None:
                out[rows, cols] = value
            elif add is True:
                out[rows, cols] += value

        tile_loop(out.shape[0], out.shape[1], 512, step)

    wait_all(first)
    start_all(weights)
    near.two()
    further.one()
    collect(down, dy, hidden, None)
    pair_copy(1, dy_halves[1]).wait()
    pair_copy(2, dy_halves[2]).wait()
    start_all(dy_loads(1))
    near.three()
    near.four()
    near.finish()
    start_all(normed_loads(1, normed, 0))
    wait_all(weights)
    wait_all(normed_loads(1, normed, 0))
    wait_all(dy_loads(1))

    def out_starts():
        for i in range(1, groups):
            out_move(i).start()

    agenda = {
        (1, 0): (further.two,),
        (1, 2): (further.three,),
        (1, 3): (further.four, last_one),
        (1, 4): (lambda: half_sums(0),),
        (1, 5): (further.finish,),
        (1, 7): (last_normed.two,),
        (2, 0): (last_normed.three, in_outer(last_dy_one)),
        (2, 1): (lambda: full_sums(0),),
        (2, 2): (last_normed.four,),
        (2, 4): (lambda: half_sums(2), in_outer(last_dy.two)),
        (2, 5): (lambda: full_sums(1),),
        (2, 7): (in_outer(last_dy.three), out_starts),
        (3, 0): (lambda: full_sums(2),),
        (3, 4): (lambda: half_sums(4),),
        (3, 6): (lambda: full_sums(3),),
        (3, 7): (out_ready,),
    }

    def after_down(n):
        if n == 1:
            start_all(dy_loads(2))
            half_sums(1)
            wait_all(keeps(n))
            wait_all(normed_loads(2, normed, 0))
            wait_all(dy_loads(2))
        else:
            @pl.when(inner)
            def _():
                pair_copy(3, third).wait()
                start_all(dy_loads(3, third))
                half_sums(3)
                wait_all(keeps(n))
                wait_all(normed_loads(3, normed, 0, roles[0][1]))
                wait_all(dy_loads(3, third))

            @pl.when(outer)
            def _():
                last_dy.four()
                last_dy.finish()
                start_all(far_loads())
                wait_all(keeps(n))
                wait_all(normed_loads(3, normed, 0, roles[1][1]))
                wait_all(far_loads())

    def sequence_step(n, carry):
        narrow = 256
        across = columns // narrow

        def one_tile(i, carry):
            ffn_tile(
                normed, dy, gate_w, up_w, down_w, hidden, grad_gate, grad_up,
                pl.ds(pl.multiple_of((i // across) * 512, 512), 512),
                pl.ds(pl.multiple_of(lax.rem(i, across) * narrow, narrow), narrow),
            )
            for (when, tile), actions in agenda.items():

                @pl.when((n == when) & (i == tile))
                def _(actions=actions):
                    for action in actions:
                        action()

            return carry

        lax.fori_loop(0, (sequence // 512) * across, one_tile, 0)
        for k in (1, 2):

            @pl.when(n == k)
            def _(k=k):
                start_all(keeps(k))
                if k == 1:
                    start_all(normed_loads(2, normed, 0))
                else:
                    last_normed.finish()
                    for role, block in roles:

                        @pl.when(role)
                        def _(block=block):
                            start_all(normed_loads(3, normed, 0, block))

        @pl.when(n < 3)
        def _():
            collect(down, dy, hidden, True)

        for k in (1, 2):

            @pl.when(n == k)
            def _(k=k):
                after_down(k)

        return carry

    lax.fori_loop(1, 4, sequence_step, 0)
    one_gate, one_up = up_w.at[:, pl.ds(0, columns)], up_w.at[:, pl.ds(columns, columns)]
    one_loads = normed_loads(1, gate_w, 2) + [
        pltpu.make_async_copy(kept.at[0, 0], one_gate, keep_sem.at[0, 0]),
        pltpu.make_async_copy(kept.at[0, 1], one_up, keep_sem.at[1, 0]),
    ]
    start_all(one_loads)

    wide = width // groups
    _, _, across_device, along_device, far_device = whereabouts()

    def down_move(send_index, recv_index, row, sender, device):
        return pltpu.make_async_remote_copy(
            src_ref=down_w.at[pl.ds(pl.multiple_of(row, wide), wide)],
            dst_ref=out_down.at[:, pl.ds(pl.multiple_of(sender * columns, columns), columns)],
            send_sem=swap_sent.at[send_index],
            recv_sem=swap_came.at[recv_index],
            device_id=(replica, device),
            device_id_type=MESH,
        )

    def chip_of(i):
        chip = jnp.where(i == 0, far_device, jnp.where(i == 1, across_device, along_device))
        return jnp.where(i == 3, me, chip) // 2

    def out_sends(i, k):
        return down_move(2 * i + k, 2 * i + core, (2 * i + k) * wide, me, chip_of(i) * 2 + k)

    def finish_down(i, carry):
        rows = pl.ds(pl.multiple_of(chip_of(i) * 2 * wide, 2 * wide), 2 * wide)

        def column_step(j, carry):
            cols = pl.ds(pl.multiple_of(j * 512, 512), 512)
            down[rows, cols] += product(dy[:, rows], hidden[:, cols], 0, 0)
            return carry

        lax.fori_loop(0, columns // 512, column_step, 0)
        down_w[pl.ds(pl.multiple_of(i * 2 * wide, 2 * wide), 2 * wide), :] = down[rows, :].astype(BF)

        @pl.when(i < 3)
        def _():
            out_sends(i, 0).start()
            out_sends(i, 1).start()

        return carry

    lax.fori_loop(0, 4, finish_down, 0)
    swaps = [out_sends(i, k) for i in range(3) for k in range(2)]
    arrivals = []
    for i in range(3):
        for k in range(2):
            peer = chip_of(i) * 2 + k
            arrivals.append(down_move(2 * i + k, 2 * i + k, (2 * i + k) * wide, peer, peer))
    swaps.append(down_move(6, 6, (6 + lax.rem(mate, 2)) * wide, me, mate))
    swaps[-1].start()
    arrivals.append(down_move(6, 6, 6 * wide, mate, mate))
    own_slab = pltpu.make_async_copy(
        down_w.at[pl.ds(pl.multiple_of((6 + core) * wide, wide), wide)],
        out_down.at[:, pl.ds(pl.multiple_of(me * columns, columns), columns)],
        keep_sem.at[2, 1],
    )
    own_slab.start()
    two_gate = pltpu.make_async_copy(kept.at[1, 0], hidden, keep_sem.at[0, 3])
    two_gate.start()
    full_sums(4)
    half_sums(5)
    wait_all(one_loads)
    two_loads = normed_loads(2, dy, 0)
    start_all(two_loads)

    two_up = pltpu.make_async_copy(kept.at[1, 1], hidden, keep_sem.at[1, 3])
    own_loads = [
        pltpu.make_async_copy(own_normed, normed, load_sem.at[2, 0]),
        pltpu.make_async_copy(own_grad_gate, one_gate, load_sem.at[2, 1]),
        pltpu.make_async_copy(own_grad_up, one_up, load_sem.at[2, 2]),
    ]

    def one_rows(u, rows):
        return up_w[:, pl.ds(pl.multiple_of(u * columns + rows.start, 512), 512)]

    def two_passes(u, carry):
        def newest(rows, cols):
            value = product(grads[u, :, rows], normed[:, cols], 0, 0)
            totals[u, rows, cols] = value + product(one_rows(u, rows), gate_w[:, cols], 0, 0)

        tile_loop(columns, width, 512, newest)

        @pl.when(u == 0)
        def _():
            half_sums(6)
            wait_all(two_loads)
            two_gate.wait()

        @pl.when(u == 1)
        def _():
            start_all(own_loads)
            full_sums(6)
            two_up.wait()

        def older(rows, cols):
            totals[u, rows, cols] += product(hidden[:, rows], dy[:, cols], 0, 0)

        tile_loop(columns, width, 512, older)

        @pl.when(u == 0)
        def _():
            two_up.start()
            full_sums(5)
            half_sums(7)

        return carry

    lax.fori_loop(0, 2, two_passes, 0)
    full_sums(7)
    wait_all(own_loads)

    def out_save(i):
        u, rows = i // (columns // 512), pl.ds(pl.multiple_of(lax.rem(i, columns // 512) * 512, 512), 512)
        return pltpu.make_async_copy(totals.at[u, rows], both_out.at[u, rows], out_sem.at[i])

    def last_rows(i, carry):
        u, rows = i // (columns // 512), pl.ds(pl.multiple_of(lax.rem(i, columns // 512) * 512, 512), 512)

        def column_step(j, carry):
            cols = pl.ds(pl.multiple_of(j * 512, 512), 512)
            totals[u, rows, cols] += product(one_rows(u, rows), normed[:, cols], 0, 0)
            return carry

        lax.fori_loop(0, width // 512, column_step, 0)
        out_save(i).start()
        return carry

    lax.fori_loop(0, 2 * (columns // 512), last_rows, 0)
    out_saves = [out_save(i) for i in range(2 * (columns // 512))]

    @pl.when(outer)
    def _():
        for c in range(chunks):
            inward(c).wait_send()
            outward(c).wait_recv()

    @pl.when(inner)
    def _():
        for c in range(chunks):
            middle(c).wait_send()
            outward(c).wait_send()
            keep(c).wait()

    for copy in swaps:
        copy.wait_send()
    for copy in arrivals:
        copy.wait_recv()
    own_slab.wait()
    for i in range(1, groups):
        out_move(i).wait_send()
    hop.drain()

    @pl.when(outer)
    def _():
        last_dy.drain()

    wait_all(out_saves)
    dy_hop.drain()
    near.drain()
    for gather in gathers:
        gather.drain()


def ffn_grads(near_all, n2_one, n2_two, dy_one, dy_two, passed, n2, dy_all, own, attn_part, out_part, w_gate, w_up, w_down_columns):
    _, tokens, width = n2_one.shape
    sequence = n2.shape[0]
    groups = sequence // tokens
    columns = w_gate.shape[0]
    chunks = 8
    attn_rows = attn_part.shape[0] + out_part.shape[1]
    depth = attn_rows // chunks
    anywhere = pl.BlockSpec(memory_space=pl.ANY)
    dma = pltpu.SemaphoreType.DMA
    out = pl.pallas_call(
        every_kernel,
        out_shape=(
            jax.ShapeDtypeStruct((2, columns, width), F32),
            jax.ShapeDtypeStruct((width // groups, columns * groups), BF),
            jax.ShapeDtypeStruct((attn_rows, width), BF),
            jax.ShapeDtypeStruct((4, sequence, width), BF),
            jax.ShapeDtypeStruct((2, 2, sequence, columns), BF),
            jax.ShapeDtypeStruct((3, sequence // 2, width), BF),
            jax.ShapeDtypeStruct((out_part.shape[1], width), BF),
            jax.ShapeDtypeStruct(n2_two.shape, BF),
            jax.ShapeDtypeStruct((sequence // 2, width), BF),
            jax.ShapeDtypeStruct(passed.shape, BF),
        ),
        in_specs=[anywhere] * 16,
        out_specs=(anywhere,) * 10,
        scratch_shapes=[
            pltpu.VMEM((sequence, width), BF),
            pltpu.VMEM((sequence, width), BF),
            pltpu.VMEM((sequence, columns), BF),
            pltpu.VMEM((2, sequence, columns), BF),
            pltpu.VMEM((columns, width), BF),
            pltpu.VMEM((columns, width), BF),
            pltpu.VMEM((width, columns), BF),
            pltpu.VMEM((width, columns), F32),
            pltpu.VMEM((2, columns, width), F32),
            pltpu.VMEM((chunks, depth, width), BF),
            pltpu.VMEM((chunks, depth, width), BF),
            pltpu.VMEM((depth, width), BF),
            dma((3, groups)),
            dma((3, 4)),
            dma((4, 13)),
            dma((4, 13)),
            dma((3, chunks)),
            dma((3, chunks)),
            dma((chunks,)),
            dma((groups,)),
            dma((groups,)),
            dma((2 * (columns // 512),)),
            dma((2, 3)),
            dma((2, groups)),
            dma((2, 2)),
            dma((2, 2)),
            dma((2, groups)),
        ],
        compiler_params=pltpu.CompilerParams(
            collective_id=2, has_side_effects=True, vmem_limit_bytes=67043328
        ),
        cost_estimate=pl.CostEstimate(
            flops=42 * sequence * width * columns, bytes_accessed=80 * 1024 * 1024, transcendentals=0
        ),
        name="ffn_grads",
    )(near_all, n2_one, n2_two, dy_one, dy_two, passed, n2, dy_all, *own, attn_part, out_part, w_gate, w_up, w_down_columns)
    return out[:3]


def gather_tokens(values):
    return lax.all_gather(values, "shard", axis=0, tiled=True)


def scatter_tokens(partial):
    return lax.psum_scatter(
        partial.astype(BF), "shard", scatter_dimension=0, tiled=True
    ).astype(F32)


def rows_to_columns(weight):
    return lax.all_to_all(weight, "shard", split_axis=1, concat_axis=0, tiled=True)


def columns_to_rows(grad):
    return lax.all_to_all(grad, "shard", split_axis=0, concat_axis=1, tiled=True)


def replica_sum(part):
    return lax.psum(part.astype(BF), "replica")


def general_body(hidden_in, cotangent, doc_lengths, w_query, w_key, w_value, w_out, w_gate, w_up, w_down):
    x = hidden_in[0].astype(F32)
    dyb = cotangent[0]
    tokens_here = x.shape[0]
    groups = lax.axis_size("shard")
    seq_length = tokens_here * groups
    factor = 1.0 / math.sqrt(HEAD_DIM)
    places = jnp.arange(seq_length, dtype=jnp.int32)
    segment, offset = doc_layout(doc_lengths[0], places)
    cosine, sine = rope_tables(offset, HEAD_DIM)
    allowed = ((segment[:, None] == segment[None, :]) & (places[None, :] <= places[:, None]))[None]

    normed_one, inverse_one = normalize(x)
    n1 = gather_tokens(normed_one.astype(BF))
    w_out_columns = rows_to_columns(w_out)
    query = rotate(split_heads(dot(n1, w_query, 1, 1)), cosine, sine).astype(BF)
    keys = rotate(split_heads(dot(n1, w_key, 1, 1)), cosine, sine).astype(BF)
    values = split_heads(dot(n1, w_value, 1, 1)).astype(BF)
    scores = factor * jnp.einsum("hqe,hke->hqk", query, keys, preferred_element_type=F32)
    scores = jnp.where(allowed, scores, masked)
    top = jnp.max(scores, axis=-1, keepdims=True)
    weights = jnp.where(allowed, jnp.exp(scores - top), 0.0)
    total = jnp.sum(weights, axis=-1, keepdims=True)
    log_total = top + jnp.log(total)
    attn = jnp.einsum("hqk,hke->hqe", weights.astype(BF), values, preferred_element_type=F32) / total
    out_b = join_heads(attn).astype(BF)
    middle = x + scatter_tokens(dot(out_b, w_out_columns, 1, 1))

    normed_two, inverse_two = normalize(middle)
    n2 = gather_tokens(normed_two.astype(BF))
    dy_all = gather_tokens(dyb)
    w_down_columns = rows_to_columns(w_down)
    gate = dot(n2, w_gate, 1, 1)
    up = dot(n2, w_up, 1, 1)
    sigma = jax.nn.sigmoid(gate)
    silu = gate * sigma
    hidden = (silu * up).astype(BF)
    grad_down = columns_to_rows(replica_sum(dot(dy_all, hidden, 0, 0)))
    grad_hidden = dot(dy_all, w_down_columns, 1, 0)
    grad_gate_b = (grad_hidden * up * sigma * (1.0 + gate * (1.0 - sigma))).astype(BF)
    grad_up_b = (grad_hidden * silu).astype(BF)
    grad_gate = replica_sum(dot(grad_gate_b, n2, 0, 0).astype(BF))
    grad_up = replica_sum(dot(grad_up_b, n2, 0, 0).astype(BF))
    grad_normed_two = scatter_tokens(dot(grad_gate_b, w_gate, 1, 0) + dot(grad_up_b, w_up, 1, 0))
    mixed = scatter_tokens(dot(hidden, w_down_columns, 1, 1))
    layer_out = (middle + mixed).astype(BF)
    grad_middle = dyb.astype(F32) + norm_back(normed_two, inverse_two, grad_normed_two)

    grad_middle_all = gather_tokens(grad_middle.astype(BF))
    grad_out = columns_to_rows(replica_sum(dot(grad_middle_all, out_b, 0, 0).astype(BF)))
    grad_attn = split_heads(dot(grad_middle_all, w_out_columns, 1, 0)).astype(BF)
    delta = jnp.sum(grad_attn.astype(F32) * attn, axis=-1, keepdims=True)
    probs = jnp.where(allowed, jnp.exp(scores - log_total), 0.0)
    grad_probs = jnp.einsum("hqe,hke->hqk", grad_attn, values, preferred_element_type=F32)
    grad_scores = (probs * (grad_probs - delta)).astype(BF)
    query_grad = factor * jnp.einsum("hqk,hke->hqe", grad_scores, keys, preferred_element_type=F32)
    key_grad = factor * jnp.einsum("hqk,hqe->hke", grad_scores, query, preferred_element_type=F32)
    value_grad = jnp.einsum("hqk,hqe->hke", probs.astype(BF), grad_attn, preferred_element_type=F32)
    query_grad = join_heads(rotate(query_grad, cosine, -sine)).astype(BF)
    key_grad = join_heads(rotate(key_grad, cosine, -sine)).astype(BF)
    value_grad = join_heads(value_grad).astype(BF)
    grad_query = replica_sum(dot(query_grad, n1, 0, 0).astype(BF))
    grad_key = replica_sum(dot(key_grad, n1, 0, 0).astype(BF))
    grad_value = replica_sum(dot(value_grad, n1, 0, 0).astype(BF))
    grad_normed_one = scatter_tokens(
        dot(query_grad, w_query, 1, 0) + dot(key_grad, w_key, 1, 0) + dot(value_grad, w_value, 1, 0)
    )
    grad_in = grad_middle + norm_back(normed_one, inverse_one, grad_normed_one)
    return (
        layer_out[None],
        grad_in[None],
        grad_query.astype(F32),
        grad_key.astype(F32),
        grad_value.astype(F32),
        grad_out.astype(F32),
        grad_gate.astype(F32),
        grad_up.astype(F32),
        grad_down.astype(F32),
    )


def body(hidden_in, cotangent, doc_lengths, w_query, w_key, w_value, w_out, w_gate, w_up, w_down):
    x_own, dy_own = hidden_in[0], cotangent[0]
    half = HEAD_DIM // 2
    frequency = theta_base ** (-2.0 * (np.arange(HEAD_DIM) % half) / HEAD_DIM)
    (
        n1, query, key, value, attn, attn_b, out_columns, _, down_columns,
        hidden, grad_gate_b, grad_up_b, middle, n2, dy, n2_one, grad_middle, grad_all, dy_one, passed,
        cosine, sine, start,
    ) = front(
        doc_lengths, jnp.asarray(frequency[None], F32), x_own, dy_own,
        w_query, w_key, w_value, w_out, w_gate, w_up, w_down,
    )
    layer_out, grad_in, attn_part, out_part, n2_two, dy_two, near_all = back(
        x_own, start, cosine, sine, hidden, down_columns, grad_all, out_columns, attn_b, attn,
        query, key, value, n1, w_query, w_key, w_value, n2_one, dy_one, middle, grad_middle,
    )
    grad_both, grad_down, attn_sum = ffn_grads(
        near_all, n2_one, n2_two, dy_one, dy_two, passed, n2, dy, (hidden, grad_gate_b, grad_up_b),
        attn_part, out_part, w_gate, w_up, down_columns,
    )
    grad_query, grad_key, grad_value, grad_out = jnp.split(attn_sum.astype(F32), 4, axis=0)
    return (
        layer_out[None],
        grad_in[None],
        grad_query,
        grad_key,
        grad_value,
        grad_out,
        grad_both[0],
        grad_both[1],
        grad_down.astype(F32),
    )


def solution(mesh):
    rows = P("shard", None)
    tokens = P("replica", "shard", None)
    in_specs = (tokens, tokens, P("replica", None)) + (rows,) * 7
    out_specs = (tokens, tokens) + (rows,) * 7
    local = body if mesh.shape["shard"] == 8 and mesh.shape["replica"] == 4 else general_body
    return jax.shard_map(local, mesh=mesh, in_specs=in_specs, out_specs=out_specs, check_vma=False)
```

```python
import functools
import math

import jax
import jax.numpy as jnp
import numpy as np
from jax import lax
from jax.experimental import pallas as pl
from jax.experimental.pallas import tpu as pltpu
from jax.sharding import PartitionSpec as P

HEAD_DIM = 128

epsilon = 1e-05
theta_base = 10000.0
masked = -1e30
BF = jnp.bfloat16
F32 = jnp.float32
MESH = pl.DeviceIdType.MESH
VMEM = pltpu.VMEM


def normalize(values):
    center = values - jnp.mean(values, axis=-1, keepdims=True)
    inverse = lax.rsqrt(jnp.mean(center * center, axis=-1, keepdims=True) + epsilon)
    return (center * inverse, inverse)


def norm_back(normed, inverse, grad):
    inner = (
        grad
        - jnp.mean(grad, axis=-1, keepdims=True)
        - normed * jnp.mean(grad * normed, axis=-1, keepdims=True)
    )
    return inverse * inner


def dot(a, b, ca, cb):
    return lax.dot_general(a, b, (((ca,), (cb,)), ((), ())), preferred_element_type=F32)


def doc_layout(lengths, places):
    ends = jnp.cumsum(lengths)
    starts = ends - lengths
    segment = jnp.sum((places[:, None] >= ends[None, :]).astype(jnp.int32), axis=1)
    member = segment[:, None] == jnp.arange(lengths.shape[0], dtype=jnp.int32)[None, :]
    offset = places - jnp.sum(jnp.where(member, starts[None, :], 0), axis=1)
    return (segment, offset)


def rope_tables(offset, head_dim):
    half = head_dim // 2
    freq = theta_base ** (-2.0 * jnp.arange(half, dtype=F32) / head_dim)
    angle = offset.astype(F32)[:, None] * freq[None, :]
    return (jnp.cos(angle)[None], jnp.sin(angle)[None])


def rotate(values, cosine, sine):
    half = values.shape[-1] // 2
    first = values[..., :half]
    second = values[..., half:]
    return jnp.concatenate(
        [first * cosine - second * sine, second * cosine + first * sine], axis=-1
    )


def split_heads(values):
    tokens, width = values.shape
    return jnp.transpose(values.reshape(tokens, width // HEAD_DIM, HEAD_DIM), (1, 0, 2))


def join_heads(values):
    heads, tokens, size = values.shape
    return jnp.transpose(values, (1, 0, 2)).reshape(tokens, heads * size)


def whereabouts():
    place = lax.axis_index("shard")
    core, col, row = lax.rem(place, 2), lax.rem(place // 2, 2), place // 4
    across, along = place + 2 - 4 * col, place + 4 - 8 * row
    return place, place + 1 - 2 * core, across, along, across + 4 - 8 * row


def whereabouts_of_mate():
    me, mate, across, along, far = whereabouts()
    shift = mate - me
    return across + shift, along + shift, far + shift


def tile_loop(rows, columns, size, step, narrow=None):
    narrow = narrow or size
    across = columns // narrow

    def one(i, carry):
        step(
            pl.ds(pl.multiple_of((i // across) * size, size), size),
            pl.ds(pl.multiple_of(lax.rem(i, across) * narrow, narrow), narrow),
        )
        return carry

    lax.fori_loop(0, (rows // size) * across, one, 0)


def product(a, b, ca, cb):
    return lax.dot_general(a, b, (((ca,), (cb,)), ((), ())), preferred_element_type=F32)


def ffn_tile(normed, dy, w_gate, w_up, w_down, hidden, grad_gate, grad_up, rows, columns):
    gate = product(normed[rows, :], w_gate[columns, :], 1, 1)
    up = product(normed[rows, :], w_up[columns, :], 1, 1)
    grad = product(dy[rows, :], w_down[:, columns], 1, 0)
    sigma = 0.5 + 0.5 * jnp.tanh(0.5 * gate)
    silu = gate * sigma
    hidden[rows, columns] = (silu * up).astype(BF)
    grad_gate[rows, columns] = (grad * (up * (sigma + silu * (1.0 - sigma)))).astype(BF)
    grad_up[rows, columns] = (grad * silu).astype(BF)


def block_rows(slot, tokens, part=0):
    size = tokens // 2
    if part:
        return pl.ds(pl.multiple_of(slot * tokens + (part - 1) * size, size), size)
    return pl.ds(pl.multiple_of(slot * tokens, tokens), tokens)


class Gather:
    def __init__(self, block, out, sent, came):
        self.block, self.out, self.sent, self.came = block, out, sent, came
        self.tokens = block.shape[0]
        self.replica = lax.axis_index("replica")
        self.me, self.mate, self.across, self.along, self.far = whereabouts()
        self.sends = []

    def move(self, k, slot, part, device, first=False):
        tokens = self.tokens
        local = pl.ds((part - 1) * (tokens // 2) if part else 0, tokens // 2 if part else tokens)
        rows = block_rows(slot, tokens, part)
        return pltpu.make_async_remote_copy(
            src_ref=self.block.at[local] if first else self.out.at[rows],
            dst_ref=self.out.at[rows],
            send_sem=self.sent.at[k],
            recv_sem=self.came.at[k],
            device_id=(self.replica, device),
            device_id_type=MESH,
        )

    def start(self, *moves):
        for one in moves:
            self.move(*one).start()
            self.sends.append(one)

    def came_in(self, *moves):
        for k, slot, part in moves:
            self.move(k, slot, part, self.mate).wait_recv()

    def firsts(self):
        me = self.me
        return (
            (1, me, 1, self.across, True),
            (3, me, 2, self.along, True),
            (0, me, 0, self.mate, True),
            (2, me, 2, self.across, True),
            (4, me, 1, self.along, True),
        )

    def one(self):
        self.start(*self.firsts())

    def two(self):
        self.came_in((1, self.across, 1))
        self.start((5, self.across, 1, self.along), (6, self.across, 1, self.mate))
        self.came_in((3, self.along, 2))
        self.start((7, self.along, 2, self.across), (8, self.along, 2, self.mate))

    def three(self):
        self.came_in((2, self.across, 2))
        self.start((9, self.across, 2, self.mate))
        self.came_in((4, self.along, 1))
        self.start((10, self.along, 1, self.mate))

    def four(self):
        self.came_in((5, self.far, 1))
        self.start((11, self.far, 1, self.mate))
        self.came_in((7, self.far, 2))
        self.start((12, self.far, 2, self.mate))

    def finish_near(self):
        across, _, _ = whereabouts_of_mate()
        self.came_in((0, self.mate, 0), (6, across, 1), (9, across, 2))

    def finish_far(self):
        _, along, far = whereabouts_of_mate()
        self.came_in((8, along, 2), (10, along, 1), (11, far, 1), (12, far, 2))

    def finish(self):
        self.finish_near()
        self.finish_far()

    def drain(self):
        for one in self.sends:
            self.move(*one).wait_send()


class Scatter:
    def __init__(self, parts, buffers, sent, came):
        self.parts = parts
        self.pair, self.sums, self.by_far, self.by_side = buffers
        self.sent, self.came = sent, came
        self.tokens = self.pair.shape[1]
        self.replica = lax.axis_index("replica")
        me, mate, across, along, far = whereabouts()
        self.mine, self.shift, self.mate = (me, across, along, far), mate - me, mate
        low, high = pl.ds(0, self.tokens // 2), pl.ds(self.tokens // 2, self.tokens // 2)
        self.low, self.high = low, high
        sums, by_far, by_side = self.sums, self.by_far, self.by_side
        self.swaps = [
            self.move(k, parts.at[block_rows(self.mine[k] + self.shift, self.tokens)], self.pair.at[k], mate)
            for k in range(4)
        ]
        self.far_low = self.move(4, sums.at[2, low], by_far.at[0], across)
        self.far_high = self.move(5, sums.at[2, high], by_far.at[1], along)
        self.across_low = self.move(6, sums.at[0, low], by_side.at[0, low], across)
        self.along_high = self.move(7, sums.at[1, high], by_side.at[1, high], along)
        self.along_low = self.move(8, sums.at[1, low], by_side.at[1, low], along)
        self.across_high = self.move(9, sums.at[0, high], by_side.at[0, high], across)

    def move(self, k, src, dst, device):
        return pltpu.make_async_remote_copy(
            src_ref=src,
            dst_ref=dst,
            send_sem=self.sent.at[k],
            recv_sem=self.came.at[k],
            device_id=(self.replica, device),
            device_id_type=MESH,
        )

    def swap(self, *which):
        for k in which:
            self.swaps[k].start()

    def pair_sum(self, k):
        self.swaps[k].wait_recv()
        own = self.parts[block_rows(self.mine[k], self.tokens), :].astype(F32)
        self.sums[k - 1] = (own + self.pair[k].astype(F32)).astype(BF)

    def send_far(self):
        self.pair_sum(3)
        self.far_low.start()
        self.far_high.start()

    def send_near(self):
        self.pair_sum(1)
        self.across_low.start()
        self.pair_sum(2)
        self.along_high.start()

    def send_rest(self):
        low, high, sums = self.low, self.high, self.sums
        self.far_low.wait_recv()
        sums[1, low] = (sums[1, low].astype(F32) + self.by_far[0].astype(F32)).astype(BF)
        self.along_low.start()
        self.far_high.wait_recv()
        sums[0, high] = (sums[0, high].astype(F32) + self.by_far[1].astype(F32)).astype(BF)
        self.across_high.start()

    def total(self):
        self.swaps[0].wait_recv()
        own = self.parts[block_rows(self.mine[0], self.tokens), :].astype(F32)
        own = own + self.pair[0].astype(F32)
        for copy in (self.across_low, self.along_high, self.along_low, self.across_high):
            copy.wait_recv()
        return own + (self.by_side[0].astype(F32) + self.by_side[1].astype(F32))

    def drain(self):
        for copy in (
            *self.swaps, self.far_low, self.far_high, self.across_low, self.along_high,
            self.along_low, self.across_high,
        ):
            copy.wait_send()


class Line:
    def __init__(self, own, slots, sent, came):
        self.own, self.slots, self.sent, self.came = own, slots, sent, came
        self.replica, self.me = lax.axis_index("replica"), lax.axis_index("shard")
        self.replicas = lax.axis_size("replica")

    def move(self, way, i, slot, first):
        target = self.replica + (1 if way == 0 else -1)
        return pltpu.make_async_remote_copy(
            src_ref=self.own if first else self.slots(slot),
            dst_ref=self.slots(slot),
            send_sem=self.sent.at[way, i],
            recv_sem=self.came.at[way, i],
            device_id=(target, self.me),
            device_id_type=MESH,
        )

    def source(self, way, i):
        return self.replica - i if way == 0 else self.replica + i

    def has(self, way, i):
        return self.replica >= i if way == 0 else self.replica + i < self.replicas

    def can_send(self, way):
        return self.replica + 1 < self.replicas if way == 0 else self.replica >= 1

    def start(self):
        for way in (0, 1):

            @pl.when(self.can_send(way))
            def _(way=way):
                self.move(way, 0, self.replica, True).start()

    def step(self, i):
        for way in (0, 1):

            @pl.when(self.has(way, i))
            def _(way=way):
                self.move(way, i - 1, self.source(way, i), False).wait_recv()
                if i < self.replicas - 1:

                    @pl.when(self.can_send(way))
                    def _():
                        self.move(way, i, self.source(way, i), False).start()

    def drain(self):
        for way in (0, 1):
            for i in range(self.replicas - 1):

                @pl.when(self.has(way, i) & self.can_send(way))
                def _(way=way, i=i):
                    self.move(way, i, self.source(way, i), i == 0).wait_send()


class Hop:
    def __init__(self, k, source, landing, sent, came):
        self.k, self.source, self.landing, self.sent, self.came = k, source, landing, sent, came
        self.replica, self.me = lax.axis_index("replica"), lax.axis_index("shard")
        self.replicas = lax.axis_size("replica")

    def move(self, way):
        return pltpu.make_async_remote_copy(
            src_ref=self.source(way),
            dst_ref=self.landing.at[way],
            send_sem=self.sent.at[way],
            recv_sem=self.came.at[way],
            device_id=(self.replica + (1 if way == 0 else -1), self.me),
            device_id_type=MESH,
        )

    def sends(self, way):
        last = self.replicas - 1
        if way == 0:
            return (self.replica >= self.k - 1) & (self.replica < last)
        return (self.replica <= self.replicas - self.k) & (self.replica > 0)

    def receives(self, way):
        return self.replica >= self.k if way == 0 else self.replica < self.replicas - self.k

    def start(self):
        for way in (0, 1):

            @pl.when(self.sends(way))
            def _(way=way):
                self.move(way).start()

    def arrive(self):
        for way in (0, 1):

            @pl.when(self.receives(way))
            def _(way=way):
                self.move(way).wait_recv()

    def drain(self):
        for way in (0, 1):

            @pl.when(self.sends(way))
            def _(way=way):
                self.move(way).wait_send()


def greet_all(barrier):
    replica, replicas = lax.axis_index("replica"), lax.axis_size("replica")
    me, groups = lax.axis_index("shard"), lax.axis_size("shard")
    for i in range(1, groups):
        device = lax.rem(me + i, groups)
        pl.semaphore_signal(barrier, inc=1, device_id=(replica, device), device_id_type=MESH)

    @pl.when(replica >= 1)
    def _():
        pl.semaphore_signal(barrier, inc=1, device_id=(replica - 1, me), device_id_type=MESH)

    @pl.when(replica + 1 < replicas)
    def _():
        pl.semaphore_signal(barrier, inc=1, device_id=(replica + 1, me), device_id_type=MESH)

    edge = (replica == 0) | (replica == replicas - 1)

    @pl.when(edge)
    def _():
        pl.semaphore_wait(barrier, groups)

    @pl.when(jnp.logical_not(edge))
    def _():
        pl.semaphore_wait(barrier, groups + 1)


def rotate_head(values, cosine, sine):
    return values * cosine + pltpu.roll(values, values.shape[-1] // 2, 1) * sine


def key_reach(first, step, sequence):
    low = max(0, (first + 1 - sequence // 2) // 128 * 128)
    return low, pl.ds(low, first + step - low)


def allowed_bias(start, first, step, low):
    shape = (step, first + step - low)
    key_place = lax.broadcasted_iota(jnp.int32, shape, 1) + low
    query_place = lax.broadcasted_iota(jnp.int32, shape, 0) + first
    return jnp.where((key_place <= query_place) & (key_place >= start), 0.0, masked)


def head_scores(query, keys, bias):
    return product(query, keys, 1, 1) * (1.0 / math.sqrt(HEAD_DIM)) + bias


def fill_tables(lengths, frequency, cosine, sine, start):
    shape = start.shape
    place = lax.broadcasted_iota(jnp.int32, shape, 0)
    begin = jnp.zeros(shape, jnp.int32)
    end = 0
    for i in range(lengths.shape[1] - 1):
        end = end + lengths[0, i]
        begin = jnp.where(place >= end, end, begin)
    start[...] = begin
    angle = (place - begin).astype(F32) * frequency[...]
    lane = lax.broadcasted_iota(jnp.int32, shape, 1)
    cosine[...] = jnp.cos(angle)
    sine[...] = jnp.where(lane < shape[1] // 2, -1.0, 1.0) * jnp.sin(angle)


def front_kernel(
    lengths, frequency, x_own, dy_own, w_query, w_key, w_value, w_out, w_gate, w_up, w_down,
    n1_out, query_out, key_out, value_out, attn_out, attn_b_out, out_columns_out, down_parts,
    down_columns_out, hidden_out, grad_gate_out, grad_up_out, middle_out, n2_out, dy_out, n2_hopped,
    grad_out, grad_all_out, dy_hopped, passed, cosine_out, sine_out, start_out,
    n1, n2, dy, query, key, value, attn, attn_b, out_columns, gate_w, up_w, down_w,
    hidden, grad_gate, grad_up, parts, pair, sums, by_far, by_side, middle, normed, n2_own, grad_own, n1_own, cosine, sine, start,
    load_sem, save_sem, gather_sent, gather_came, scatter_sent, scatter_came,
    swap_sent, swap_came, line_sent, line_came, down_sent, down_came, pass_sem,
):
    replica = lax.axis_index("replica")
    replicas = lax.axis_size("replica")
    me = lax.axis_index("shard")
    groups = lax.axis_size("shard")
    tokens, width = x_own.shape
    sequence = n1.shape[0]
    saves = []

    def save(src, dst):
        copy = pltpu.make_async_copy(src, dst, save_sem.at[len(saves)])
        copy.start()
        saves.append(copy)

    def exchange(which, source, target):
        copies = []
        for i in range(1, groups):
            device = lax.rem(me + i, groups)
            copies.append(
                pltpu.make_async_remote_copy(
                    src_ref=source(device),
                    dst_ref=target,
                    send_sem=swap_sent.at[which, i],
                    recv_sem=swap_came.at[which, i],
                    device_id=(replica, device),
                    device_id_type=MESH,
                )
            )
        return copies

    gate_load = pltpu.make_async_copy(w_gate, gate_w, load_sem.at[0])
    up_load = pltpu.make_async_copy(w_up, up_w, load_sem.at[1])
    gate_load.start()
    up_load.start()
    own_rows = block_rows(me, tokens)
    x = x_own[...].astype(F32)
    center = x - jnp.mean(x, axis=-1, keepdims=True)
    inverse = lax.rsqrt(jnp.mean(center * center, axis=-1, keepdims=True) + epsilon)
    n1_own[...] = (center * inverse).astype(BF)
    own_n1 = pltpu.make_async_copy(n1_own, n1.at[own_rows], load_sem.at[2])
    own_dy = pltpu.make_async_copy(dy_own, dy.at[own_rows], load_sem.at[3])
    own_n1.start()
    own_dy.start()

    greet_all(pltpu.get_barrier_semaphore())
    n1_gather = Gather(n1_own, n1, gather_sent.at[0], gather_came.at[0])
    dy_gather = Gather(dy_own, dy, gather_sent.at[1], gather_came.at[1])
    n2_gather = Gather(n2_own, n2, gather_sent.at[2], gather_came.at[2])
    grad_gather = Gather(grad_own, grad_all_out, gather_sent.at[3], gather_came.at[3])
    half = sequence // 2
    dy_half = dy.at[pl.ds(pl.multiple_of(lax.rem(me, 2) * half, half), half)]
    n2_hop = Hop(1, lambda way: n2_own, n2_hopped, line_sent.at[0], line_came.at[0])
    dy_hop = Hop(1, lambda way: dy_half, dy_hopped, line_sent.at[1], line_came.at[1])
    passing = [
        pltpu.make_async_remote_copy(
            src_ref=src,
            dst_ref=passed.at[way],
            send_sem=pass_sem.at[0, way],
            recv_sem=pass_sem.at[1, way],
            device_id=(replica + (1 if way == 0 else -1), me),
            device_id_type=MESH,
        )
        for way in (0, 1)
        for src in (dy_own, passed.at[way])
    ]
    last = replicas - 1

    def passes(way, k):
        return replica == (k if way == 0 else last - k)

    def pass_on(k):
        for way in (0, 1):

            @pl.when(passes(way, k))
            def _(way=way):
                if k:
                    passing[2 * way].wait_recv()
                if k < 2:
                    passing[2 * way + (1 if k else 0)].start()

    down_line = Line(
        down_parts.at[replica], lambda s: down_parts.at[s], down_sent, down_came
    )
    buffers = (pair, sums, by_far, by_side)

    n1_gather.one()
    pass_on(0)
    fill_tables(lengths, frequency, cosine, sine, start)
    save(cosine, cosine_out)
    save(sine, sine_out)
    save(start, start_out)
    n1_gather.two()
    n1_gather.three()
    wide = w_out.shape[0]
    mine = pl.ds(pl.multiple_of(me * wide, wide), wide)
    part = down_parts.shape[2]

    def down_block(device):
        column = (device * replicas + replica) * part
        return w_down.at[:, pl.ds(pl.multiple_of(column, part), part)]

    def out_block(device):
        return w_out.at[:, pl.ds(pl.multiple_of(device * wide, wide), wide)]

    down_swaps = exchange(1, down_block, down_parts.at[replica, mine])
    out_swaps = exchange(0, out_block, out_columns.at[mine])
    own_down = pltpu.make_async_copy(down_block(me), down_parts.at[replica, mine], load_sem.at[5])
    own_down.start()
    own_out = pltpu.make_async_copy(out_block(me), out_columns.at[mine], load_sem.at[4])
    own_out.start()
    for copy in down_swaps + out_swaps:
        copy.start()
    pass_on(1)
    own_n1.wait()
    n1_gather.finish_near()
    row = me // (groups // 2)

    def half_rows(i):
        return pl.ds(pl.multiple_of((row + i * (1 - 2 * row)) * half, half), half)


    heads = query.shape[1] // HEAD_DIM
    def projections(i, carry):
        rows = half_rows(i)
        for weight, target in ((w_query, query), (w_key, key), (w_value, value)):
            values = product(n1[rows, :], weight[...], 1, 1)
            for head in range(heads):
                lanes = pl.ds(head * HEAD_DIM, HEAD_DIM)
                piece = values[:, head * HEAD_DIM : (head + 1) * HEAD_DIM]
                if target is not value:
                    piece = rotate_head(piece, cosine[rows, :], sine[rows, :])
                target[rows, lanes] = piece.astype(BF)

        @pl.when(i == 0)
        def _():
            n1_gather.four()
            n1_gather.finish_far()

        return carry

    lax.fori_loop(0, 2, projections, 0)
    save(n1, n1_out)
    save(query, query_out)
    save(key, key_out)
    save(value, value_out)
    own_down.wait()
    for copy in down_swaps:
        copy.wait_recv()
    down_line.start()
    step = 256
    for first in range(0, sequence, step):
        rows = pl.ds(first, step)
        low, reach = key_reach(first, step, sequence)
        bias = allowed_bias(start[rows, 0:1], first, step, low)
        for head in range(heads):
            lanes = pl.ds(head * HEAD_DIM, HEAD_DIM)
            scores = head_scores(query[rows, lanes], key[reach, lanes], bias)
            weights = jnp.exp(scores - jnp.max(scores, axis=-1, keepdims=True))
            total = jnp.sum(weights, axis=-1, keepdims=True)
            result = product(weights.astype(BF), value[reach, lanes], 1, 0) / total
            attn[rows, lanes] = result
            attn_b[rows, lanes] = result.astype(BF)
    pass_on(2)
    save(attn, attn_out)
    save(attn_b, attn_b_out)

    own_out.wait()
    for copy in out_swaps:
        copy.wait_recv()
    save(out_columns, out_columns_out)

    scatter = Scatter(parts, buffers, scatter_sent.at[0], scatter_came.at[0])

    def spread(i, carry):
        def step(rows, columns):
            rows = half_rows(1 - i)
            parts[rows, columns] = product(attn_b[rows, :], out_columns[columns, :], 1, 1).astype(BF)

        tile_loop(half, width, half, step)

        @pl.when(i == 0)
        def _():
            scatter.swap(3, 2)

        return carry

    lax.fori_loop(0, 2, spread, 0)
    scatter.swap(1, 0)
    scatter.send_far()
    scatter.send_near()
    down_line.step(1)
    scatter.send_rest()
    middle[...] = x_own[...].astype(F32) + scatter.total()
    scatter.drain()
    save(middle, middle_out)
    center = middle[...] - jnp.mean(middle[...], axis=-1, keepdims=True)
    inverse = lax.rsqrt(jnp.mean(center * center, axis=-1, keepdims=True) + epsilon)
    normed[...] = center * inverse
    n2_own[...] = normed[...].astype(BF)
    n2_gather.one()
    own_n2 = pltpu.make_async_copy(n2_own, n2.at[own_rows], load_sem.at[6])
    own_n2.start()
    n2_gather.two()
    n2_gather.three()
    dy_gather.one()
    down_line.step(2)
    n2_hop.start()
    own_n2.wait()
    n2_gather.finish_near()
    gate_load.wait()
    up_load.wait()

    def feed_forward(i):
        def forward(rows, columns):
            rows = half_rows(i)
            gate = product(n2[rows, :], gate_w[columns, :], 1, 1)
            up = product(n2[rows, :], up_w[columns, :], 1, 1)
            sigma = 0.5 + 0.5 * jnp.tanh(0.5 * gate)
            silu = gate * sigma
            hidden[rows, columns] = (silu * up).astype(BF)
            grad_gate[rows, columns] = (up * (sigma + silu * (1.0 - sigma))).astype(BF)
            grad_up[rows, columns] = silu.astype(BF)

        tile_loop(half, gate_w.shape[0], half, forward, 256)

    def both_forward(i, carry):
        feed_forward(i)

        @pl.when(i == 0)
        def _():
            n2_gather.four()
            n2_gather.finish_far()
            dy_gather.two()

        return carry

    lax.fori_loop(0, 2, both_forward, 0)
    save(n2, n2_out)
    dy_gather.three()
    dy_gather.four()
    own_dy.wait()
    dy_gather.finish()
    save(dy, dy_out)
    save(hidden, hidden_out)
    dy_hop.start()
    down_line.step(3)
    down_loads = []
    for r in range(replicas):
        down_loads.append(
            pltpu.make_async_copy(
                down_parts.at[r], down_w.at[:, pl.ds(r * part, part)], load_sem.at[7 + r]
            )
        )
        down_loads[-1].start()
    for copy in down_loads:
        copy.wait()
    save(down_w, down_columns_out)

    back = Scatter(parts, buffers, scatter_sent.at[1], scatter_came.at[1])

    def feed(base):
        def grads(rows, columns):
            rows = pl.ds(pl.multiple_of(base, half), half)
            grad = product(dy[rows, :], down_w[:, columns], 1, 0)
            grad_gate[rows, columns] = (grad * grad_gate[rows, columns].astype(F32)).astype(BF)
            grad_up[rows, columns] = (grad * grad_up[rows, columns].astype(F32)).astype(BF)

        tile_loop(half, gate_w.shape[0], half, grads)

        def backward(rows, columns):
            rows = pl.ds(pl.multiple_of(base, half), half)
            value = product(grad_gate[rows, :], gate_w[:, columns], 1, 0)
            value = value + product(grad_up[rows, :], up_w[:, columns], 1, 0)
            parts[rows, columns] = value.astype(BF)

        tile_loop(half, width, half, backward)

    def both_back(i, carry):
        feed((1 - row + i * (2 * row - 1)) * half)

        @pl.when(i == 0)
        def _():
            back.swap(3, 2)
            back.send_far()

        return carry

    lax.fori_loop(0, 2, both_back, 0)
    save(grad_gate, grad_gate_out)
    save(grad_up, grad_up_out)
    back.swap(1, 0)
    back.send_near()
    back.send_rest()
    inner = back.total()
    back.drain()
    inner = (
        inner
        - jnp.mean(inner, axis=-1, keepdims=True)
        - normed[...] * jnp.mean(inner * normed[...], axis=-1, keepdims=True)
    )
    center = middle[...] - jnp.mean(middle[...], axis=-1, keepdims=True)
    inverse = lax.rsqrt(jnp.mean(center * center, axis=-1, keepdims=True) + epsilon)
    normed[...] = dy_own[...].astype(F32) + inverse * inner
    grad_own[...] = normed[...].astype(BF)
    grad_gather.one()
    save(normed, grad_out)
    save(grad_own, grad_all_out.at[own_rows])
    grad_gather.two()
    grad_gather.three()
    grad_gather.four()
    grad_gather.finish()
    for way in (0, 1):

        @pl.when(passes(way, 0) | passes(way, 1))
        def _(way=way):
            passing[2 * way].wait_send()

    n2_hop.arrive()
    dy_hop.arrive()
    for copy in saves:
        copy.wait()
    for copy in out_swaps + down_swaps:
        copy.wait_send()
    for user in (n1_gather, n2_gather, dy_gather, grad_gather, down_line, n2_hop, dy_hop):
        user.drain()


def front(lengths, frequency, x_own, dy_own, w_query, w_key, w_value, w_out, w_gate, w_up, w_down):
    groups, replicas = lax.axis_size("shard"), lax.axis_size("replica")
    tokens, width = x_own.shape
    sequence = tokens * groups
    wide, columns = w_query.shape[0], w_gate.shape[0]
    anywhere, vmem = pl.BlockSpec(memory_space=pl.ANY), pl.BlockSpec(memory_space=VMEM)

    def shape(dims, kind=BF):
        return jax.ShapeDtypeStruct(dims, kind)

    outs = (
        shape((sequence, width)),
        shape((sequence, wide)),
        shape((sequence, wide)),
        shape((sequence, wide)),
        shape((sequence, wide), F32),
        shape((sequence, wide)),
        shape((width, wide)),
        shape((replicas, width, columns // replicas)),
        shape((width, columns)),
        shape((sequence, columns)),
        shape((sequence, columns)),
        shape((sequence, columns)),
        shape((tokens, width), F32),
        shape((sequence, width)),
        shape((sequence, width)),
        shape((2, tokens, width)),
        shape((tokens, width), F32),
        shape((sequence, width)),
        shape((2, sequence // 2, width)),
        shape((2, tokens, width)),
        shape((sequence, HEAD_DIM), F32),
        shape((sequence, HEAD_DIM), F32),
        shape((sequence, HEAD_DIM), jnp.int32),
    )
    dma = pltpu.SemaphoreType.DMA
    return pl.pallas_call(
        front_kernel,
        out_shape=outs,
        in_specs=[pl.BlockSpec(memory_space=pltpu.SMEM)] + [vmem] * 6 + [anywhere] * 4,
        out_specs=(anywhere,) * len(outs),
        scratch_shapes=[
            pltpu.VMEM((sequence, width), BF),
            pltpu.VMEM((sequence, width), BF),
            pltpu.VMEM((sequence, width), BF),
            pltpu.VMEM((sequence, wide), BF),
            pltpu.VMEM((sequence, wide), BF),
            pltpu.VMEM((sequence, wide), BF),
            pltpu.VMEM((sequence, wide), F32),
            pltpu.VMEM((sequence, wide), BF),
            pltpu.VMEM((width, wide), BF),
            pltpu.VMEM((columns, width), BF),
            pltpu.VMEM((columns, width), BF),
            pltpu.VMEM((width, columns), BF),
            pltpu.VMEM((sequence, columns), BF),
            pltpu.VMEM((sequence, columns), BF),
            pltpu.VMEM((sequence, columns), BF),
            pltpu.VMEM((sequence, width), BF),
            pltpu.VMEM((4, tokens, width), BF),
            pltpu.VMEM((3, tokens, width), BF),
            pltpu.VMEM((2, tokens // 2, width), BF),
            pltpu.VMEM((2, tokens, width), BF),
            pltpu.VMEM((tokens, width), F32),
            pltpu.VMEM((tokens, width), F32),
            pltpu.VMEM((tokens, width), BF),
            pltpu.VMEM((tokens, width), BF),
            pltpu.VMEM((tokens, width), BF),
            pltpu.VMEM((sequence, HEAD_DIM), F32),
            pltpu.VMEM((sequence, HEAD_DIM), F32),
            pltpu.VMEM((sequence, HEAD_DIM), jnp.int32),
            dma((7 + replicas,)),
            dma((24,)),
            dma((4, 13)),
            dma((4, 13)),
            dma((2, 10)),
            dma((2, 10)),
            dma((2, groups)),
            dma((2, groups)),
            dma((2, 2)),
            dma((2, 2)),
            dma((2, replicas)),
            dma((2, replicas)),
            dma((2, 2)),
        ],
        compiler_params=pltpu.CompilerParams(
            collective_id=3, has_side_effects=True, vmem_limit_bytes=67043328
        ),
        cost_estimate=pl.CostEstimate(
            flops=12 * sequence * width * columns, bytes_accessed=64 * 1024 * 1024, transcendentals=0
        ),
        name="front",
    )(lengths, frequency, x_own, dy_own, w_query, w_key, w_value, w_out, w_gate, w_up, w_down)


def back_kernel(
    x_own, start, cosine, sine, hidden_in, down_in, grad_in, out_columns_in, attn_b_in, attn_in,
    query_in, key_in, value_in, n1_in, w_query, w_key, w_value, n2_near, dy_near, middle, grad_middle,
    layer_out, input_grad, attn_part, out_grad_out, n2_hopped, dy_hopped, near_all,
    hidden, down_w, grad, out_columns, attn_b, attn, query, key, value, n1, weights,
    grad_attn, key_grad, value_grad, columns_grad, out_grad, rows_grad, parts,
    pair, sums, by_far, by_side, pair2, sums2, by_far2, by_side2,
    load_sem, save_sem, scatter_sent, scatter_came, line_sent, line_came,
    gather_sent, gather_came,
):
    sequence, width = n1.shape
    me = lax.axis_index("shard")
    near_half = x_own.shape[0] // 2
    near_block = n2_near.at[1 - lax.rem(lax.axis_index("replica"), 2), pl.ds(0, near_half)]
    near = Gather(near_block, near_all, gather_sent, gather_came)
    wide = query.shape[1]
    heads = wide // HEAD_DIM
    pairs = (
        (hidden_in, hidden), (down_in, down_w), (grad_in, grad), (out_columns_in, out_columns),
        (attn_b_in, attn_b), (attn_in, attn), (query_in, query), (key_in, key), (value_in, value),
        (n1_in, n1), (w_query, weights.at[pl.ds(0, wide)]), (w_key, weights.at[pl.ds(wide, wide)]),
        (w_value, weights.at[pl.ds(2 * wide, wide)]),
    )
    loads = [
        pltpu.make_async_copy(src, dst, load_sem.at[i]) for i, (src, dst) in enumerate(pairs)
    ]
    for copy in loads[:2]:
        copy.start()
    greet_all(pltpu.get_barrier_semaphore())
    hops = (
        Hop(2, lambda way: n2_near.at[way], n2_hopped, line_sent.at[0], line_came.at[0]),
        Hop(2, lambda way: dy_near.at[way], dy_hopped, line_sent.at[1], line_came.at[1]),
    )
    for hop in hops:
        hop.start()
    near.one()
    own_near = pltpu.make_async_copy(near_block, near_all.at[block_rows(me, near.tokens)], save_sem.at[2])
    own_near.start()
    loads[0].wait()
    loads[1].wait()
    for copy in loads[2:]:
        copy.start()

    mixed = Scatter(parts, (pair, sums, by_far, by_side), scatter_sent.at[0], scatter_came.at[0])
    half = sequence // 2
    row = me // (lax.axis_size("shard") // 2)

    def by_halves(scatter, tile):
        def one_half(i, carry):
            def step(rows, columns):
                rows = pl.ds(pl.multiple_of((1 - row + i * (2 * row - 1)) * half, half), half)
                parts[rows, columns] = tile(rows, columns).astype(BF)

            tile_loop(half, width, half, step)

            @pl.when(i == 0)
            def _():
                scatter.swap(3, 2)

            return carry

        lax.fori_loop(0, 2, one_half, 0)
        scatter.swap(1, 0)

    by_halves(mixed, lambda rows, columns: product(hidden[rows, :], down_w[columns, :], 1, 1))

    for copy in loads[2:6]:
        copy.wait()
    near.two()
    mixed.send_far()
    mixed.send_near()
    near.three()

    def out_step(i, carry):
        rows = pl.ds(pl.multiple_of(i * 512, 512), 512)
        out_grad[rows, :] = product(grad[:, rows], attn_b[...], 0, 0).astype(BF)
        return carry

    lax.fori_loop(0, width // 512, out_step, 0)
    out_save = pltpu.make_async_copy(out_grad, out_grad_out, save_sem.at[0])
    out_save.start()

    def attn_step(i, carry):
        rows = pl.ds(pl.multiple_of(i * 512, 512), 512)
        grad_attn[rows, :] = product(grad[rows, :], out_columns[...], 1, 0).astype(BF)
        return carry

    lax.fori_loop(0, sequence // 512, attn_step, 0)
    for copy in loads[6:]:
        copy.wait()
    mixed.send_rest()

    near.four()
    step = 256
    for first in range(sequence - step, -1, -step):
        rows = pl.ds(first, step)
        low, upto = key_reach(first, step, sequence)
        bias = allowed_bias(start[rows, 0:1], first, step, low)
        for head in range(heads):
            lanes = pl.ds(head * HEAD_DIM, HEAD_DIM)
            query_piece, grad_piece = query[rows, lanes], grad_attn[rows, lanes]
            scores = head_scores(query_piece, key[upto, lanes], bias)
            probs = jnp.exp(scores - jnp.max(scores, axis=-1, keepdims=True))
            probs = probs / jnp.sum(probs, axis=-1, keepdims=True)
            delta = jnp.sum(grad_piece.astype(F32) * attn[rows, lanes], axis=-1, keepdims=True)
            grad_probs = product(grad_piece, value[upto, lanes], 1, 1)
            grad_scores = (probs * (grad_probs - delta)).astype(BF)
            query_grad = product(grad_scores, key[upto, lanes], 1, 0) * (1.0 / math.sqrt(HEAD_DIM))
            query_grad = rotate_head(query_grad, cosine[rows, :], -sine[rows, :])
            columns_grad[rows, lanes] = query_grad.astype(BF)
            key_part = product(grad_scores, query_piece, 0, 0)
            value_part = product(probs.astype(BF), grad_piece, 0, 0)
            if first == sequence - step:
                key_grad[upto, lanes] = key_part
                value_grad[upto, lanes] = value_part
                if low:
                    key_grad[pl.ds(0, low), lanes] = jnp.zeros((low, HEAD_DIM), F32)
                    value_grad[pl.ds(0, low), lanes] = jnp.zeros((low, HEAD_DIM), F32)
            else:
                key_grad[upto, lanes] += key_part
                value_grad[upto, lanes] += value_part
    for head in range(heads):
        lanes = pl.ds(head * HEAD_DIM, HEAD_DIM)
        piece = key_grad[:, lanes] * (1.0 / math.sqrt(HEAD_DIM))
        piece = rotate_head(piece, cosine[...], -sine[...])
        columns_grad[:, pl.ds(wide + head * HEAD_DIM, HEAD_DIM)] = piece.astype(BF)
        columns_grad[:, pl.ds(2 * wide + head * HEAD_DIM, HEAD_DIM)] = value_grad[:, lanes].astype(BF)

    layer_out[...] = (middle[...] + mixed.total()).astype(BF)
    mixed.drain()

    last = Scatter(parts, (pair2, sums2, by_far2, by_side2), scatter_sent.at[1], scatter_came.at[1])
    by_halves(last, lambda rows, columns: product(columns_grad[rows, :], weights[:, columns], 1, 0))
    last.send_far()
    last.send_near()

    def collect(rows, columns):
        rows_grad[rows, columns] = product(columns_grad[:, rows], n1[:, columns], 0, 0).astype(BF)

    tile_loop(3 * wide, width, 256, collect, 512)
    rows_save = pltpu.make_async_copy(rows_grad, attn_part, save_sem.at[1])
    rows_save.start()
    last.send_rest()
    x = x_own[...].astype(F32)
    center = x - jnp.mean(x, axis=-1, keepdims=True)
    inverse = lax.rsqrt(jnp.mean(center * center, axis=-1, keepdims=True) + epsilon)
    inner = last.total()
    normed = center * inverse
    inner = (
        inner
        - jnp.mean(inner, axis=-1, keepdims=True)
        - normed * jnp.mean(inner * normed, axis=-1, keepdims=True)
    )
    input_grad[...] = grad_middle[...] + inverse * inner
    last.drain()
    out_save.wait()
    rows_save.wait()
    own_near.wait()
    near.finish()
    near.drain()
    for hop in hops:
        hop.arrive()
        hop.drain()


def back(x_own, start, cosine, sine, hidden, down, grad, out_columns, attn_b, attn, query, key, value, n1,
         w_query, w_key, w_value, n2_near, dy_near, middle, grad_middle):
    groups = lax.axis_size("shard")
    tokens, width = x_own.shape
    sequence = tokens * groups
    wide, columns = query.shape[1], hidden.shape[1]
    anywhere, vmem = pl.BlockSpec(memory_space=pl.ANY), pl.BlockSpec(memory_space=VMEM)
    dma = pltpu.SemaphoreType.DMA
    buffers = [
        pltpu.VMEM((4, tokens, width), BF),
        pltpu.VMEM((3, tokens, width), BF),
        pltpu.VMEM((2, tokens // 2, width), BF),
        pltpu.VMEM((2, tokens, width), BF),
    ]
    return pl.pallas_call(
        back_kernel,
        out_shape=(
            jax.ShapeDtypeStruct((tokens, width), BF),
            jax.ShapeDtypeStruct((tokens, width), F32),
            jax.ShapeDtypeStruct((3 * wide, width), BF),
            jax.ShapeDtypeStruct((width, wide), BF),
            jax.ShapeDtypeStruct(n2_near.shape, BF),
            jax.ShapeDtypeStruct(dy_near.shape, BF),
            jax.ShapeDtypeStruct((sequence // 2, width), BF),
        ),
        in_specs=[vmem] * 4 + [anywhere] * 15 + [vmem] * 2,
        out_specs=(vmem, vmem) + (anywhere,) * 5,
        scratch_shapes=[
            pltpu.VMEM((sequence, columns), BF),
            pltpu.VMEM((width, columns), BF),
            pltpu.VMEM((sequence, width), BF),
            pltpu.VMEM((width, wide), BF),
            pltpu.VMEM((sequence, wide), BF),
            pltpu.VMEM((sequence, wide), F32),
            pltpu.VMEM((sequence, wide), BF),
            pltpu.VMEM((sequence, wide), BF),
            pltpu.VMEM((sequence, wide), BF),
            pltpu.VMEM((sequence, width), BF),
            pltpu.VMEM((3 * wide, width), BF),
            pltpu.VMEM((sequence, wide), BF),
            pltpu.VMEM((sequence, wide), F32),
            pltpu.VMEM((sequence, wide), F32),
            pltpu.VMEM((sequence, 3 * wide), BF),
            pltpu.VMEM((width, wide), BF),
            pltpu.VMEM((3 * wide, width), BF),
            pltpu.VMEM((sequence, width), BF),
            *buffers,
            *buffers,
            dma((13,)),
            dma((3,)),
            dma((2, 10)),
            dma((2, 10)),
            dma((2, 2)),
            dma((2, 2)),
            dma((13,)),
            dma((13,)),
        ],
        compiler_params=pltpu.CompilerParams(
            collective_id=4, has_side_effects=True, vmem_limit_bytes=67043328
        ),
        cost_estimate=pl.CostEstimate(
            flops=24 * sequence * width * wide, bytes_accessed=48 * 1024 * 1024, transcendentals=0
        ),
        name="back",
    )(x_own, start, cosine, sine, hidden, down, grad, out_columns, attn_b, attn, query, key, value, n1,
      w_query, w_key, w_value, n2_near, dy_near, middle, grad_middle)


def every_kernel(
    near_all, n2_one, n2_two, dy_one, dy_two, passed, own_normed, own_dy, own_hidden, own_grad_gate, own_grad_up,
    attn_part, out_part,
    w_gate, w_up, w_down,
    both_out, out_down, out_attn, landed, kept, dy_other,
    out_rows, n2_three, near_rest, passed_three,
    normed, dy, hidden, grads, gate_w, up_w, down_w, down, totals, first_sum, second_sum, stage,
    load_sem, keep_sem, gather_sent, gather_came, line_sent, line_came, line_own, swap_sent, swap_came,
    out_sem, pair_sem, out_swap_sem, hop_sent, hop_came, near_sem,
):
    replica = lax.axis_index("replica")
    replicas = lax.axis_size("replica")
    me = lax.axis_index("shard")
    groups = lax.axis_size("shard")
    tokens = n2_one.shape[1]
    sequence, width = normed.shape
    half = sequence // 2
    columns = hidden.shape[1]
    grad_gate, grad_up = grads.at[0], grads.at[1]
    inner = (replica == 1) | (replica == 2)
    outer = (replica == 0) | (replica == 3)
    beside = replica + 1 - 2 * lax.rem(replica, 2)
    facing = 3 - replica
    chunks, depth = first_sum.shape[0], first_sum.shape[1]

    def piece(c):
        return pl.ds(c * depth, depth)

    def line_move(kind, c, src, dst, target):
        return pltpu.make_async_remote_copy(
            src_ref=src,
            dst_ref=dst,
            send_sem=line_sent.at[kind, c],
            recv_sem=line_came.at[kind, c],
            device_id=(target, me),
            device_id_type=MESH,
        )

    attn_chunks = attn_part.shape[0] // depth

    def own_chunk(c):
        return attn_part.at[piece(c)] if c < attn_chunks else out_rows.at[piece(c - attn_chunks)]

    def inward(c):
        return line_move(0, c, own_chunk(c), first_sum.at[c], beside)

    def middle(c):
        return line_move(1, c, first_sum.at[c], second_sum.at[c], facing)

    def outward(c):
        return line_move(2, c, second_sum.at[c], out_attn.at[piece(c)], beside)

    def keep(c):
        return pltpu.make_async_copy(second_sum.at[c], out_attn.at[piece(c)], line_own.at[c])

    def stage_load(c):
        return pltpu.make_async_copy(own_chunk(c), stage, keep_sem.at[2, 0])

    def half_sums(*which):
        @pl.when(inner)
        def _():
            for c in which:
                stage_load(c).wait()
                inward(c).wait_recv()
                first_sum[c] = (stage[...].astype(F32) + first_sum[c].astype(F32)).astype(BF)
                middle(c).start()
                if c + 1 < chunks:
                    stage_load(c + 1).start()

    def full_sums(*which):
        @pl.when(inner)
        def _():
            for c in which:
                middle(c).wait_recv()
                second_sum[c] = (first_sum[c].astype(F32) + second_sum[c].astype(F32)).astype(BF)
                outward(c).start()
                keep(c).start()

    core = lax.rem(me, 2)
    mate = me + 1 - 2 * core
    low_side, high_side = 1 - lax.rem(replica, 2), 1 - replica // 2
    hop = Hop(3, lambda way: n2_two.at[way], n2_three, hop_sent.at[0], hop_came.at[0])
    dy_hop = Hop(3, lambda way: passed.at[way], passed_three, hop_sent.at[1], hop_came.at[1])
    far_dy = passed_three.at[high_side]
    last_dy = Gather(far_dy, landed.at[3], gather_sent.at[3], gather_came.at[3])

    def last_dy_one():
        dy_hop.arrive()
        last_dy.one()

    def in_outer(action):
        def act():
            @pl.when(outer)
            def _():
                action()

        return act

    n2_blocks = {1: n2_one.at[low_side], 2: n2_two.at[high_side]}
    dy_halves = {1: dy_one.at[low_side], 2: dy_two.at[high_side]}
    roles = ((inner, n2_one.at[high_side]), (outer, n2_three.at[high_side]))
    third = dy_one.at[high_side]

    near = Gather(
        n2_one.at[low_side, pl.ds(tokens // 2, tokens // 2)], near_rest, gather_sent.at[0], gather_came.at[0]
    )

    def gather_of(n, block):
        return Gather(block, landed.at[n - 1], gather_sent.at[n - 1], gather_came.at[n - 1])

    gathers = [gather_of(2, n2_blocks[2]), gather_of(3, roles[0][1])]

    def last_one():
        hop.arrive()
        for role, block in roles:

            @pl.when(role)
            def _(block=block):
                gather_of(3, block).one()

        gather = gathers[1]
        gather.sends.extend(gather.firsts())

    def pair_copy(n, source):
        return pltpu.make_async_remote_copy(
            src_ref=source,
            dst_ref=dy_other.at[n - 1],
            send_sem=pair_sem.at[0, n - 1],
            recv_sem=pair_sem.at[1, n - 1],
            device_id=(replica, mate),
            device_id_type=MESH,
        )

    def normed_loads(n, target, base, block=None):
        copies = []
        if n == 1:
            for i in range(groups):
                device = lax.rem(me + i, groups)
                small = block_rows(device, near.tokens)
                rest = near_rest.at[small] if i else near.block
                for k, source in enumerate((near_all.at[small], rest)):
                    rows = block_rows(device, tokens, k + 1)
                    copies.append(pltpu.make_async_copy(source, target.at[rows], near_sem.at[k, i]))
            return copies
        for i in range(groups):
            device = lax.rem(me + i, groups)
            rows = block_rows(device, tokens)
            source = (n2_blocks[n] if block is None else block) if i == 0 else landed.at[n - 1, rows]
            copies.append(pltpu.make_async_copy(source, target.at[rows], load_sem.at[base, i]))
        return copies

    def dy_loads(n, source=None):
        mine = dy.at[pl.ds(pl.multiple_of(core * half, half), half)]
        others = dy.at[pl.ds(pl.multiple_of((1 - core) * half, half), half)]
        return [
            pltpu.make_async_copy(dy_halves[n] if source is None else source, mine, load_sem.at[1, 0]),
            pltpu.make_async_copy(dy_other.at[n - 1], others, load_sem.at[1, 1]),
        ]

    def far_loads():
        copies = []
        for i in range(groups):
            rows = block_rows(lax.rem(me + i, groups), tokens)
            source = landed.at[3, rows] if i else far_dy
            copies.append(pltpu.make_async_copy(source, dy.at[rows], load_sem.at[1, i]))
        return copies

    wide = width // groups

    def out_move(i):
        device = lax.rem(me + i, groups)
        return pltpu.make_async_remote_copy(
            src_ref=out_part.at[pl.ds(pl.multiple_of(device * wide, wide), wide)],
            dst_ref=out_rows.at[:, pl.ds(pl.multiple_of(me * wide, wide), wide)],
            send_sem=out_swap_sem.at[0, i],
            recv_sem=out_swap_sem.at[1, i],
            device_id=(replica, device),
            device_id_type=MESH,
        )

    own_out = pltpu.make_async_copy(
        out_part.at[pl.ds(pl.multiple_of(me * wide, wide), wide)],
        out_rows.at[:, pl.ds(pl.multiple_of(me * wide, wide), wide)],
        out_swap_sem.at[0, 0],
    )

    def out_ready():
        own_out.wait()
        for i in range(1, groups):
            out_move(i).wait_recv()

        @pl.when(outer)
        def _():
            start_all([inward(c) for c in range(attn_chunks, chunks)])

    def keeps(n):
        return [
            pltpu.make_async_copy(grad_gate, kept.at[n - 1, 0], keep_sem.at[0, n]),
            pltpu.make_async_copy(grad_up, kept.at[n - 1, 1], keep_sem.at[1, n]),
        ]

    def start_all(copies):
        for copy in copies:
            copy.start()

    def wait_all(copies):
        for copy in copies:
            copy.wait()

    first = [
        pltpu.make_async_copy(own_hidden, hidden, load_sem.at[1, 1]),
        pltpu.make_async_copy(own_dy, dy, load_sem.at[1, 0]),
    ]
    weights = [
        pltpu.make_async_copy(w_gate, gate_w, load_sem.at[2, 0]),
        pltpu.make_async_copy(w_up, up_w, load_sem.at[2, 1]),
        pltpu.make_async_copy(w_down, down_w, load_sem.at[2, 2]),
    ]
    start_all(first)
    barrier = pltpu.get_barrier_semaphore()
    for i in range(1, groups):
        device = lax.rem(me + i, groups)
        pl.semaphore_signal(barrier, inc=1, device_id=(replica, device), device_id_type=MESH)
    pl.semaphore_signal(barrier, inc=1, device_id=(beside, me), device_id_type=MESH)

    @pl.when(inner)
    def _():
        pl.semaphore_signal(barrier, inc=1, device_id=(facing, me), device_id_type=MESH)
        pl.semaphore_wait(barrier, groups + 1)

    @pl.when(outer)
    def _():
        pl.semaphore_wait(barrier, groups)

    further, last_normed = gathers
    near.one()
    pair_copy(1, dy_halves[1]).start()
    pair_copy(2, dy_halves[2]).start()
    own_out.start()
    hop.start()
    dy_hop.start()

    @pl.when(inner)
    def _():
        pair_copy(3, third).start()


    @pl.when(outer)
    def _():
        start_all([inward(c) for c in range(attn_chunks)])

    @pl.when(inner)
    def _():
        stage_load(0).start()

    def collect(out, left, right, add):
        def step(rows, cols):
            value = product(left[:, rows], right[:, cols], 0, 0)
            if add is None:
                out[rows, cols] = value
            elif add is True:
                out[rows, cols] += value

        tile_loop(out.shape[0], out.shape[1], 512, step)

    wait_all(first)
    start_all(weights)
    near.two()
    further.one()
    collect(down, dy, hidden, None)
    pair_copy(1, dy_halves[1]).wait()
    pair_copy(2, dy_halves[2]).wait()
    start_all(dy_loads(1))
    near.three()
    near.four()
    near.finish()
    start_all(normed_loads(1, normed, 0))
    wait_all(weights)
    wait_all(normed_loads(1, normed, 0))
    wait_all(dy_loads(1))

    def out_starts():
        for i in range(1, groups):
            out_move(i).start()

    agenda = {
        (1, 0): (further.two,),
        (1, 2): (further.three,),
        (1, 3): (further.four, last_one),
        (1, 4): (lambda: half_sums(0),),
        (1, 5): (further.finish,),
        (1, 7): (last_normed.two,),
        (2, 0): (last_normed.three, in_outer(last_dy_one)),
        (2, 1): (lambda: full_sums(0),),
        (2, 2): (last_normed.four,),
        (2, 4): (lambda: half_sums(2), in_outer(last_dy.two)),
        (2, 5): (lambda: full_sums(1),),
        (2, 7): (in_outer(last_dy.three), out_starts),
        (3, 0): (lambda: full_sums(2),),
        (3, 4): (lambda: half_sums(4),),
        (3, 6): (lambda: full_sums(3),),
        (3, 7): (out_ready,),
    }

    def after_down(n):
        if n == 1:
            start_all(dy_loads(2))
            half_sums(1)
            wait_all(keeps(n))
            wait_all(normed_loads(2, normed, 0))
            wait_all(dy_loads(2))
        else:
            @pl.when(inner)
            def _():
                pair_copy(3, third).wait()
                start_all(dy_loads(3, third))
                half_sums(3)
                wait_all(keeps(n))
                wait_all(normed_loads(3, normed, 0, roles[0][1]))
                wait_all(dy_loads(3, third))

            @pl.when(outer)
            def _():
                last_dy.four()
                last_dy.finish()
                start_all(far_loads())
                wait_all(keeps(n))
                wait_all(normed_loads(3, normed, 0, roles[1][1]))
                wait_all(far_loads())

    def sequence_step(n, carry):
        narrow = 256
        across = columns // narrow

        def one_tile(i, carry):
            ffn_tile(
                normed, dy, gate_w, up_w, down_w, hidden, grad_gate, grad_up,
                pl.ds(pl.multiple_of((i // across) * 512, 512), 512),
                pl.ds(pl.multiple_of(lax.rem(i, across) * narrow, narrow), narrow),
            )
            for (when, tile), actions in agenda.items():

                @pl.when((n == when) & (i == tile))
                def _(actions=actions):
                    for action in actions:
                        action()

            return carry

        lax.fori_loop(0, (sequence // 512) * across, one_tile, 0)
        for k in (1, 2):

            @pl.when(n == k)
            def _(k=k):
                start_all(keeps(k))
                if k == 1:
                    start_all(normed_loads(2, normed, 0))
                else:
                    last_normed.finish()
                    for role, block in roles:

                        @pl.when(role)
                        def _(block=block):
                            start_all(normed_loads(3, normed, 0, block))

        @pl.when(n < 3)
        def _():
            collect(down, dy, hidden, True)

        for k in (1, 2):

            @pl.when(n == k)
            def _(k=k):
                after_down(k)

        return carry

    lax.fori_loop(1, 4, sequence_step, 0)
    one_gate, one_up = up_w.at[:, pl.ds(0, columns)], up_w.at[:, pl.ds(columns, columns)]
    one_loads = normed_loads(1, gate_w, 2) + [
        pltpu.make_async_copy(kept.at[0, 0], one_gate, keep_sem.at[0, 0]),
        pltpu.make_async_copy(kept.at[0, 1], one_up, keep_sem.at[1, 0]),
    ]
    start_all(one_loads)

    wide = width // groups
    _, _, across_device, along_device, far_device = whereabouts()

    def down_move(send_index, recv_index, row, sender, device):
        return pltpu.make_async_remote_copy(
            src_ref=down_w.at[pl.ds(pl.multiple_of(row, wide), wide)],
            dst_ref=out_down.at[:, pl.ds(pl.multiple_of(sender * columns, columns), columns)],
            send_sem=swap_sent.at[send_index],
            recv_sem=swap_came.at[recv_index],
            device_id=(replica, device),
            device_id_type=MESH,
        )

    def chip_of(i):
        chip = jnp.where(i == 0, far_device, jnp.where(i == 1, across_device, along_device))
        return jnp.where(i == 3, me, chip) // 2

    def out_sends(i, k):
        return down_move(2 * i + k, 2 * i + core, (2 * i + k) * wide, me, chip_of(i) * 2 + k)

    def finish_down(i, carry):
        rows = pl.ds(pl.multiple_of(chip_of(i) * 2 * wide, 2 * wide), 2 * wide)

        def column_step(j, carry):
            cols = pl.ds(pl.multiple_of(j * 512, 512), 512)
            down[rows, cols] += product(dy[:, rows], hidden[:, cols], 0, 0)
            return carry

        lax.fori_loop(0, columns // 512, column_step, 0)
        down_w[pl.ds(pl.multiple_of(i * 2 * wide, 2 * wide), 2 * wide), :] = down[rows, :].astype(BF)

        @pl.when(i < 3)
        def _():
            out_sends(i, 0).start()
            out_sends(i, 1).start()

        return carry

    lax.fori_loop(0, 4, finish_down, 0)
    swaps = [out_sends(i, k) for i in range(3) for k in range(2)]
    arrivals = []
    for i in range(3):
        for k in range(2):
            peer = chip_of(i) * 2 + k
            arrivals.append(down_move(2 * i + k, 2 * i + k, (2 * i + k) * wide, peer, peer))
    swaps.append(down_move(6, 6, (6 + lax.rem(mate, 2)) * wide, me, mate))
    swaps[-1].start()
    arrivals.append(down_move(6, 6, 6 * wide, mate, mate))
    own_slab = pltpu.make_async_copy(
        down_w.at[pl.ds(pl.multiple_of((6 + core) * wide, wide), wide)],
        out_down.at[:, pl.ds(pl.multiple_of(me * columns, columns), columns)],
        keep_sem.at[2, 1],
    )
    own_slab.start()
    two_gate = pltpu.make_async_copy(kept.at[1, 0], hidden, keep_sem.at[0, 3])
    two_gate.start()
    full_sums(4)
    half_sums(5)
    wait_all(one_loads)
    two_loads = normed_loads(2, dy, 0)
    start_all(two_loads)

    two_up = pltpu.make_async_copy(kept.at[1, 1], hidden, keep_sem.at[1, 3])
    own_loads = [
        pltpu.make_async_copy(own_normed, normed, load_sem.at[2, 0]),
        pltpu.make_async_copy(own_grad_gate, one_gate, load_sem.at[2, 1]),
        pltpu.make_async_copy(own_grad_up, one_up, load_sem.at[2, 2]),
    ]

    def one_rows(u, rows):
        return up_w[:, pl.ds(pl.multiple_of(u * columns + rows.start, 512), 512)]

    def two_passes(u, carry):
        def newest(rows, cols):
            value = product(grads[u, :, rows], normed[:, cols], 0, 0)
            totals[u, rows, cols] = value + product(one_rows(u, rows), gate_w[:, cols], 0, 0)

        tile_loop(columns, width, 512, newest)

        @pl.when(u == 0)
        def _():
            half_sums(6)
            wait_all(two_loads)
            two_gate.wait()

        @pl.when(u == 1)
        def _():
            start_all(own_loads)
            full_sums(6)
            two_up.wait()

        def older(rows, cols):
            totals[u, rows, cols] += product(hidden[:, rows], dy[:, cols], 0, 0)

        tile_loop(columns, width, 512, older)

        @pl.when(u == 0)
        def _():
            two_up.start()
            full_sums(5)
            half_sums(7)

        return carry

    lax.fori_loop(0, 2, two_passes, 0)
    full_sums(7)
    wait_all(own_loads)

    def out_save(i):
        u, rows = i // (columns // 512), pl.ds(pl.multiple_of(lax.rem(i, columns // 512) * 512, 512), 512)
        return pltpu.make_async_copy(totals.at[u, rows], both_out.at[u, rows], out_sem.at[i])

    def last_rows(i, carry):
        u, rows = i // (columns // 512), pl.ds(pl.multiple_of(lax.rem(i, columns // 512) * 512, 512), 512)

        def column_step(j, carry):
            cols = pl.ds(pl.multiple_of(j * 512, 512), 512)
            totals[u, rows, cols] += product(one_rows(u, rows), normed[:, cols], 0, 0)
            return carry

        lax.fori_loop(0, width // 512, column_step, 0)
        out_save(i).start()
        return carry

    lax.fori_loop(0, 2 * (columns // 512), last_rows, 0)
    out_saves = [out_save(i) for i in range(2 * (columns // 512))]

    @pl.when(outer)
    def _():
        for c in range(chunks):
            inward(c).wait_send()
            outward(c).wait_recv()

    @pl.when(inner)
    def _():
        for c in range(chunks):
            middle(c).wait_send()
            outward(c).wait_send()
            keep(c).wait()

    for copy in swaps:
        copy.wait_send()
    for copy in arrivals:
        copy.wait_recv()
    own_slab.wait()
    for i in range(1, groups):
        out_move(i).wait_send()
    hop.drain()

    @pl.when(outer)
    def _():
        last_dy.drain()

    wait_all(out_saves)
    dy_hop.drain()
    near.drain()
    for gather in gathers:
        gather.drain()


def ffn_grads(near_all, n2_one, n2_two, dy_one, dy_two, passed, n2, dy_all, own, attn_part, out_part, w_gate, w_up, w_down_columns):
    _, tokens, width = n2_one.shape
    sequence = n2.shape[0]
    groups = sequence // tokens
    columns = w_gate.shape[0]
    chunks = 8
    attn_rows = attn_part.shape[0] + out_part.shape[1]
    depth = attn_rows // chunks
    anywhere = pl.BlockSpec(memory_space=pl.ANY)
    dma = pltpu.SemaphoreType.DMA
    out = pl.pallas_call(
        every_kernel,
        out_shape=(
            jax.ShapeDtypeStruct((2, columns, width), F32),
            jax.ShapeDtypeStruct((width // groups, columns * groups), BF),
            jax.ShapeDtypeStruct((attn_rows, width), BF),
            jax.ShapeDtypeStruct((4, sequence, width), BF),
            jax.ShapeDtypeStruct((2, 2, sequence, columns), BF),
            jax.ShapeDtypeStruct((3, sequence // 2, width), BF),
            jax.ShapeDtypeStruct((out_part.shape[1], width), BF),
            jax.ShapeDtypeStruct(n2_two.shape, BF),
            jax.ShapeDtypeStruct((sequence // 2, width), BF),
            jax.ShapeDtypeStruct(passed.shape, BF),
        ),
        in_specs=[anywhere] * 16,
        out_specs=(anywhere,) * 10,
        scratch_shapes=[
            pltpu.VMEM((sequence, width), BF),
            pltpu.VMEM((sequence, width), BF),
            pltpu.VMEM((sequence, columns), BF),
            pltpu.VMEM((2, sequence, columns), BF),
            pltpu.VMEM((columns, width), BF),
            pltpu.VMEM((columns, width), BF),
            pltpu.VMEM((width, columns), BF),
            pltpu.VMEM((width, columns), F32),
            pltpu.VMEM((2, columns, width), F32),
            pltpu.VMEM((chunks, depth, width), BF),
            pltpu.VMEM((chunks, depth, width), BF),
            pltpu.VMEM((depth, width), BF),
            dma((3, groups)),
            dma((3, 4)),
            dma((4, 13)),
            dma((4, 13)),
            dma((3, chunks)),
            dma((3, chunks)),
            dma((chunks,)),
            dma((groups,)),
            dma((groups,)),
            dma((2 * (columns // 512),)),
            dma((2, 3)),
            dma((2, groups)),
            dma((2, 2)),
            dma((2, 2)),
            dma((2, groups)),
        ],
        compiler_params=pltpu.CompilerParams(
            collective_id=2, has_side_effects=True, vmem_limit_bytes=67043328
        ),
        cost_estimate=pl.CostEstimate(
            flops=42 * sequence * width * columns, bytes_accessed=80 * 1024 * 1024, transcendentals=0
        ),
        name="ffn_grads",
    )(near_all, n2_one, n2_two, dy_one, dy_two, passed, n2, dy_all, *own, attn_part, out_part, w_gate, w_up, w_down_columns)
    return out[:3]


def gather_tokens(values):
    return lax.all_gather(values, "shard", axis=0, tiled=True)


def scatter_tokens(partial):
    return lax.psum_scatter(
        partial.astype(BF), "shard", scatter_dimension=0, tiled=True
    ).astype(F32)


def rows_to_columns(weight):
    return lax.all_to_all(weight, "shard", split_axis=1, concat_axis=0, tiled=True)


def columns_to_rows(grad):
    return lax.all_to_all(grad, "shard", split_axis=0, concat_axis=1, tiled=True)


def replica_sum(part):
    return lax.psum(part.astype(BF), "replica")


def general_body(hidden_in, cotangent, doc_lengths, w_query, w_key, w_value, w_out, w_gate, w_up, w_down):
    x = hidden_in[0].astype(F32)
    dyb = cotangent[0]
    tokens_here = x.shape[0]
    groups = lax.axis_size("shard")
    seq_length = tokens_here * groups
    factor = 1.0 / math.sqrt(HEAD_DIM)
    places = jnp.arange(seq_length, dtype=jnp.int32)
    segment, offset = doc_layout(doc_lengths[0], places)
    cosine, sine = rope_tables(offset, HEAD_DIM)
    allowed = ((segment[:, None] == segment[None, :]) & (places[None, :] <= places[:, None]))[None]

    normed_one, inverse_one = normalize(x)
    n1 = gather_tokens(normed_one.astype(BF))
    w_out_columns = rows_to_columns(w_out)
    query = rotate(split_heads(dot(n1, w_query, 1, 1)), cosine, sine).astype(BF)
    keys = rotate(split_heads(dot(n1, w_key, 1, 1)), cosine, sine).astype(BF)
    values = split_heads(dot(n1, w_value, 1, 1)).astype(BF)
    scores = factor * jnp.einsum("hqe,hke->hqk", query, keys, preferred_element_type=F32)
    scores = jnp.where(allowed, scores, masked)
    top = jnp.max(scores, axis=-1, keepdims=True)
    weights = jnp.where(allowed, jnp.exp(scores - top), 0.0)
    total = jnp.sum(weights, axis=-1, keepdims=True)
    log_total = top + jnp.log(total)
    attn = jnp.einsum("hqk,hke->hqe", weights.astype(BF), values, preferred_element_type=F32) / total
    out_b = join_heads(attn).astype(BF)
    middle = x + scatter_tokens(dot(out_b, w_out_columns, 1, 1))

    normed_two, inverse_two = normalize(middle)
    n2 = gather_tokens(normed_two.astype(BF))
    dy_all = gather_tokens(dyb)
    w_down_columns = rows_to_columns(w_down)
    gate = dot(n2, w_gate, 1, 1)
    up = dot(n2, w_up, 1, 1)
    sigma = jax.nn.sigmoid(gate)
    silu = gate * sigma
    hidden = (silu * up).astype(BF)
    grad_down = columns_to_rows(replica_sum(dot(dy_all, hidden, 0, 0)))
    grad_hidden = dot(dy_all, w_down_columns, 1, 0)
    grad_gate_b = (grad_hidden * up * sigma * (1.0 + gate * (1.0 - sigma))).astype(BF)
    grad_up_b = (grad_hidden * silu).astype(BF)
    grad_gate = replica_sum(dot(grad_gate_b, n2, 0, 0).astype(BF))
    grad_up = replica_sum(dot(grad_up_b, n2, 0, 0).astype(BF))
    grad_normed_two = scatter_tokens(dot(grad_gate_b, w_gate, 1, 0) + dot(grad_up_b, w_up, 1, 0))
    mixed = scatter_tokens(dot(hidden, w_down_columns, 1, 1))
    layer_out = (middle + mixed).astype(BF)
    grad_middle = dyb.astype(F32) + norm_back(normed_two, inverse_two, grad_normed_two)

    grad_middle_all = gather_tokens(grad_middle.astype(BF))
    grad_out = columns_to_rows(replica_sum(dot(grad_middle_all, out_b, 0, 0).astype(BF)))
    grad_attn = split_heads(dot(grad_middle_all, w_out_columns, 1, 0)).astype(BF)
    delta = jnp.sum(grad_attn.astype(F32) * attn, axis=-1, keepdims=True)
    probs = jnp.where(allowed, jnp.exp(scores - log_total), 0.0)
    grad_probs = jnp.einsum("hqe,hke->hqk", grad_attn, values, preferred_element_type=F32)
    grad_scores = (probs * (grad_probs - delta)).astype(BF)
    query_grad = factor * jnp.einsum("hqk,hke->hqe", grad_scores, keys, preferred_element_type=F32)
    key_grad = factor * jnp.einsum("hqk,hqe->hke", grad_scores, query, preferred_element_type=F32)
    value_grad = jnp.einsum("hqk,hqe->hke", probs.astype(BF), grad_attn, preferred_element_type=F32)
    query_grad = join_heads(rotate(query_grad, cosine, -sine)).astype(BF)
    key_grad = join_heads(rotate(key_grad, cosine, -sine)).astype(BF)
    value_grad = join_heads(value_grad).astype(BF)
    grad_query = replica_sum(dot(query_grad, n1, 0, 0).astype(BF))
    grad_key = replica_sum(dot(key_grad, n1, 0, 0).astype(BF))
    grad_value = replica_sum(dot(value_grad, n1, 0, 0).astype(BF))
    grad_normed_one = scatter_tokens(
        dot(query_grad, w_query, 1, 0) + dot(key_grad, w_key, 1, 0) + dot(value_grad, w_value, 1, 0)
    )
    grad_in = grad_middle + norm_back(normed_one, inverse_one, grad_normed_one)
    return (
        layer_out[None],
        grad_in[None],
        grad_query.astype(F32),
        grad_key.astype(F32),
        grad_value.astype(F32),
        grad_out.astype(F32),
        grad_gate.astype(F32),
        grad_up.astype(F32),
        grad_down.astype(F32),
    )


def body(hidden_in, cotangent, doc_lengths, w_query, w_key, w_value, w_out, w_gate, w_up, w_down):
    x_own, dy_own = hidden_in[0], cotangent[0]
    half = HEAD_DIM // 2
    frequency = theta_base ** (-2.0 * (np.arange(HEAD_DIM) % half) / HEAD_DIM)
    (
        n1, query, key, value, attn, attn_b, out_columns, _, down_columns,
        hidden, grad_gate_b, grad_up_b, middle, n2, dy, n2_one, grad_middle, grad_all, dy_one, passed,
        cosine, sine, start,
    ) = front(
        doc_lengths, jnp.asarray(frequency[None], F32), x_own, dy_own,
        w_query, w_key, w_value, w_out, w_gate, w_up, w_down,
    )
    layer_out, grad_in, attn_part, out_part, n2_two, dy_two, near_all = back(
        x_own, start, cosine, sine, hidden, down_columns, grad_all, out_columns, attn_b, attn,
        query, key, value, n1, w_query, w_key, w_value, n2_one, dy_one, middle, grad_middle,
    )
    grad_both, grad_down, attn_sum = ffn_grads(
        near_all, n2_one, n2_two, dy_one, dy_two, passed, n2, dy, (hidden, grad_gate_b, grad_up_b),
        attn_part, out_part, w_gate, w_up, down_columns,
    )
    grad_query, grad_key, grad_value, grad_out = jnp.split(attn_sum.astype(F32), 4, axis=0)
    return (
        layer_out[None],
        grad_in[None],
        grad_query,
        grad_key,
        grad_value,
        grad_out,
        grad_both[0],
        grad_both[1],
        grad_down.astype(F32),
    )


def solution(mesh):
    rows = P("shard", None)
    tokens = P("replica", "shard", None)
    in_specs = (tokens, tokens, P("replica", None)) + (rows,) * 7
    out_specs = (tokens, tokens) + (rows,) * 7
    local = body if mesh.shape["shard"] == 8 and mesh.shape["replica"] == 4 else general_body
    return jax.shard_map(local, mesh=mesh, in_specs=in_specs, out_specs=out_specs, check_vma=False)
```

```python
import functools
import math

import jax
import jax.numpy as jnp
import numpy as np
from jax import lax
from jax.experimental import pallas as pl
from jax.experimental.pallas import tpu as pltpu
from jax.sharding import PartitionSpec as P

HEAD_DIM = 128

epsilon = 1e-05
theta_base = 10000.0
masked = -1e30
BF = jnp.bfloat16
F32 = jnp.float32
MESH = pl.DeviceIdType.MESH
VMEM = pltpu.VMEM


def normalize(values):
    center = values - jnp.mean(values, axis=-1, keepdims=True)
    inverse = lax.rsqrt(jnp.mean(center * center, axis=-1, keepdims=True) + epsilon)
    return (center * inverse, inverse)


def norm_back(normed, inverse, grad):
    inner = (
        grad
        - jnp.mean(grad, axis=-1, keepdims=True)
        - normed * jnp.mean(grad * normed, axis=-1, keepdims=True)
    )
    return inverse * inner


def dot(a, b, ca, cb):
    return lax.dot_general(a, b, (((ca,), (cb,)), ((), ())), preferred_element_type=F32)


def doc_layout(lengths, places):
    ends = jnp.cumsum(lengths)
    starts = ends - lengths
    segment = jnp.sum((places[:, None] >= ends[None, :]).astype(jnp.int32), axis=1)
    member = segment[:, None] == jnp.arange(lengths.shape[0], dtype=jnp.int32)[None, :]
    offset = places - jnp.sum(jnp.where(member, starts[None, :], 0), axis=1)
    return (segment, offset)


def rope_tables(offset, head_dim):
    half = head_dim // 2
    freq = theta_base ** (-2.0 * jnp.arange(half, dtype=F32) / head_dim)
    angle = offset.astype(F32)[:, None] * freq[None, :]
    return (jnp.cos(angle)[None], jnp.sin(angle)[None])


def rotate(values, cosine, sine):
    half = values.shape[-1] // 2
    first = values[..., :half]
    second = values[..., half:]
    return jnp.concatenate(
        [first * cosine - second * sine, second * cosine + first * sine], axis=-1
    )


def split_heads(values):
    tokens, width = values.shape
    return jnp.transpose(values.reshape(tokens, width // HEAD_DIM, HEAD_DIM), (1, 0, 2))


def join_heads(values):
    heads, tokens, size = values.shape
    return jnp.transpose(values, (1, 0, 2)).reshape(tokens, heads * size)


def whereabouts():
    place = lax.axis_index("shard")
    core, col, row = lax.rem(place, 2), lax.rem(place // 2, 2), place // 4
    across, along = place + 2 - 4 * col, place + 4 - 8 * row
    return place, place + 1 - 2 * core, across, along, across + 4 - 8 * row


def whereabouts_of_mate():
    me, mate, across, along, far = whereabouts()
    shift = mate - me
    return across + shift, along + shift, far + shift


def tile_loop(rows, columns, size, step, narrow=None):
    narrow = narrow or size
    across = columns // narrow

    def one(i, carry):
        step(
            pl.ds(pl.multiple_of((i // across) * size, size), size),
            pl.ds(pl.multiple_of(lax.rem(i, across) * narrow, narrow), narrow),
        )
        return carry

    lax.fori_loop(0, (rows // size) * across, one, 0)


def product(a, b, ca, cb):
    return lax.dot_general(a, b, (((ca,), (cb,)), ((), ())), preferred_element_type=F32)


def ffn_tile(normed, dy, w_gate, w_up, w_down, hidden, grad_gate, grad_up, rows, columns):
    gate = product(normed[rows, :], w_gate[columns, :], 1, 1)
    up = product(normed[rows, :], w_up[columns, :], 1, 1)
    grad = product(dy[rows, :], w_down[:, columns], 1, 0)
    sigma = 0.5 + 0.5 * jnp.tanh(0.5 * gate)
    silu = gate * sigma
    hidden[rows, columns] = (silu * up).astype(BF)
    grad_gate[rows, columns] = (grad * (up * (sigma + silu * (1.0 - sigma)))).astype(BF)
    grad_up[rows, columns] = (grad * silu).astype(BF)


def block_rows(slot, tokens, part=0):
    size = tokens // 2
    if part:
        return pl.ds(pl.multiple_of(slot * tokens + (part - 1) * size, size), size)
    return pl.ds(pl.multiple_of(slot * tokens, tokens), tokens)


class Gather:
    def __init__(self, block, out, sent, came):
        self.block, self.out, self.sent, self.came = block, out, sent, came
        self.tokens = block.shape[0]
        self.replica = lax.axis_index("replica")
        self.me, self.mate, self.across, self.along, self.far = whereabouts()
        self.sends = []

    def move(self, k, slot, part, device, first=False):
        tokens = self.tokens
        local = pl.ds((part - 1) * (tokens // 2) if part else 0, tokens // 2 if part else tokens)
        rows = block_rows(slot, tokens, part)
        return pltpu.make_async_remote_copy(
            src_ref=self.block.at[local] if first else self.out.at[rows],
            dst_ref=self.out.at[rows],
            send_sem=self.sent.at[k],
            recv_sem=self.came.at[k],
            device_id=(self.replica, device),
            device_id_type=MESH,
        )

    def start(self, *moves):
        for one in moves:
            self.move(*one).start()
            self.sends.append(one)

    def came_in(self, *moves):
        for k, slot, part in moves:
            self.move(k, slot, part, self.mate).wait_recv()

    def firsts(self):
        me = self.me
        return (
            (1, me, 1, self.across, True),
            (3, me, 2, self.along, True),
            (0, me, 0, self.mate, True),
            (2, me, 2, self.across, True),
            (4, me, 1, self.along, True),
        )

    def one(self):
        self.start(*self.firsts())

    def two(self):
        self.came_in((1, self.across, 1))
        self.start((5, self.across, 1, self.along), (6, self.across, 1, self.mate))
        self.came_in((3, self.along, 2))
        self.start((7, self.along, 2, self.across), (8, self.along, 2, self.mate))

    def three(self):
        self.came_in((2, self.across, 2))
        self.start((9, self.across, 2, self.mate))
        self.came_in((4, self.along, 1))
        self.start((10, self.along, 1, self.mate))

    def four(self):
        self.came_in((5, self.far, 1))
        self.start((11, self.far, 1, self.mate))
        self.came_in((7, self.far, 2))
        self.start((12, self.far, 2, self.mate))

    def finish_near(self):
        across, _, _ = whereabouts_of_mate()
        self.came_in((0, self.mate, 0), (6, across, 1), (9, across, 2))

    def finish_far(self):
        _, along, far = whereabouts_of_mate()
        self.came_in((8, along, 2), (10, along, 1), (11, far, 1), (12, far, 2))

    def finish(self):
        self.finish_near()
        self.finish_far()

    def drain(self):
        for one in self.sends:
            self.move(*one).wait_send()


class Scatter:
    def __init__(self, parts, buffers, sent, came):
        self.parts = parts
        self.pair, self.sums, self.by_far, self.by_side = buffers
        self.sent, self.came = sent, came
        self.tokens = self.pair.shape[1]
        self.replica = lax.axis_index("replica")
        me, mate, across, along, far = whereabouts()
        self.mine, self.shift, self.mate = (me, across, along, far), mate - me, mate
        low, high = pl.ds(0, self.tokens // 2), pl.ds(self.tokens // 2, self.tokens // 2)
        self.low, self.high = low, high
        sums, by_far, by_side = self.sums, self.by_far, self.by_side
        self.swaps = [
            self.move(k, parts.at[block_rows(self.mine[k] + self.shift, self.tokens)], self.pair.at[k], mate)
            for k in range(4)
        ]
        self.far_low = self.move(4, sums.at[2, low], by_far.at[0], across)
        self.far_high = self.move(5, sums.at[2, high], by_far.at[1], along)
        self.across_low = self.move(6, sums.at[0, low], by_side.at[0, low], across)
        self.along_high = self.move(7, sums.at[1, high], by_side.at[1, high], along)
        self.along_low = self.move(8, sums.at[1, low], by_side.at[1, low], along)
        self.across_high = self.move(9, sums.at[0, high], by_side.at[0, high], across)

    def move(self, k, src, dst, device):
        return pltpu.make_async_remote_copy(
            src_ref=src,
            dst_ref=dst,
            send_sem=self.sent.at[k],
            recv_sem=self.came.at[k],
            device_id=(self.replica, device),
            device_id_type=MESH,
        )

    def swap(self, *which):
        for k in which:
            self.swaps[k].start()

    def pair_sum(self, k):
        self.swaps[k].wait_recv()
        own = self.parts[block_rows(self.mine[k], self.tokens), :].astype(F32)
        self.sums[k - 1] = (own + self.pair[k].astype(F32)).astype(BF)

    def send_far(self):
        self.pair_sum(3)
        self.far_low.start()
        self.far_high.start()

    def send_near(self):
        self.pair_sum(1)
        self.across_low.start()
        self.pair_sum(2)
        self.along_high.start()

    def send_rest(self):
        low, high, sums = self.low, self.high, self.sums
        self.far_low.wait_recv()
        sums[1, low] = (sums[1, low].astype(F32) + self.by_far[0].astype(F32)).astype(BF)
        self.along_low.start()
        self.far_high.wait_recv()
        sums[0, high] = (sums[0, high].astype(F32) + self.by_far[1].astype(F32)).astype(BF)
        self.across_high.start()

    def total(self):
        self.swaps[0].wait_recv()
        own = self.parts[block_rows(self.mine[0], self.tokens), :].astype(F32)
        own = own + self.pair[0].astype(F32)
        for copy in (self.across_low, self.along_high, self.along_low, self.across_high):
            copy.wait_recv()
        return own + (self.by_side[0].astype(F32) + self.by_side[1].astype(F32))

    def drain(self):
        for copy in (
            *self.swaps, self.far_low, self.far_high, self.across_low, self.along_high,
            self.along_low, self.across_high,
        ):
            copy.wait_send()


class Line:
    def __init__(self, own, slots, sent, came):
        self.own, self.slots, self.sent, self.came = own, slots, sent, came
        self.replica, self.me = lax.axis_index("replica"), lax.axis_index("shard")
        self.replicas = lax.axis_size("replica")

    def move(self, way, i, slot, first):
        target = self.replica + (1 if way == 0 else -1)
        return pltpu.make_async_remote_copy(
            src_ref=self.own if first else self.slots(slot),
            dst_ref=self.slots(slot),
            send_sem=self.sent.at[way, i],
            recv_sem=self.came.at[way, i],
            device_id=(target, self.me),
            device_id_type=MESH,
        )

    def source(self, way, i):
        return self.replica - i if way == 0 else self.replica + i

    def has(self, way, i):
        return self.replica >= i if way == 0 else self.replica + i < self.replicas

    def can_send(self, way):
        return self.replica + 1 < self.replicas if way == 0 else self.replica >= 1

    def start(self):
        for way in (0, 1):

            @pl.when(self.can_send(way))
            def _(way=way):
                self.move(way, 0, self.replica, True).start()

    def step(self, i):
        for way in (0, 1):

            @pl.when(self.has(way, i))
            def _(way=way):
                self.move(way, i - 1, self.source(way, i), False).wait_recv()
                if i < self.replicas - 1:

                    @pl.when(self.can_send(way))
                    def _():
                        self.move(way, i, self.source(way, i), False).start()

    def drain(self):
        for way in (0, 1):
            for i in range(self.replicas - 1):

                @pl.when(self.has(way, i) & self.can_send(way))
                def _(way=way, i=i):
                    self.move(way, i, self.source(way, i), i == 0).wait_send()


class Hop:
    def __init__(self, k, source, landing, sent, came):
        self.k, self.source, self.landing, self.sent, self.came = k, source, landing, sent, came
        self.replica, self.me = lax.axis_index("replica"), lax.axis_index("shard")
        self.replicas = lax.axis_size("replica")

    def move(self, way):
        return pltpu.make_async_remote_copy(
            src_ref=self.source(way),
            dst_ref=self.landing.at[way],
            send_sem=self.sent.at[way],
            recv_sem=self.came.at[way],
            device_id=(self.replica + (1 if way == 0 else -1), self.me),
            device_id_type=MESH,
        )

    def sends(self, way):
        last = self.replicas - 1
        if way == 0:
            return (self.replica >= self.k - 1) & (self.replica < last)
        return (self.replica <= self.replicas - self.k) & (self.replica > 0)

    def receives(self, way):
        return self.replica >= self.k if way == 0 else self.replica < self.replicas - self.k

    def start(self):
        for way in (0, 1):

            @pl.when(self.sends(way))
            def _(way=way):
                self.move(way).start()

    def arrive(self):
        for way in (0, 1):

            @pl.when(self.receives(way))
            def _(way=way):
                self.move(way).wait_recv()

    def drain(self):
        for way in (0, 1):

            @pl.when(self.sends(way))
            def _(way=way):
                self.move(way).wait_send()


def greet_all(barrier):
    replica, replicas = lax.axis_index("replica"), lax.axis_size("replica")
    me, groups = lax.axis_index("shard"), lax.axis_size("shard")
    for i in range(1, groups):
        device = lax.rem(me + i, groups)
        pl.semaphore_signal(barrier, inc=1, device_id=(replica, device), device_id_type=MESH)

    @pl.when(replica >= 1)
    def _():
        pl.semaphore_signal(barrier, inc=1, device_id=(replica - 1, me), device_id_type=MESH)

    @pl.when(replica + 1 < replicas)
    def _():
        pl.semaphore_signal(barrier, inc=1, device_id=(replica + 1, me), device_id_type=MESH)

    edge = (replica == 0) | (replica == replicas - 1)

    @pl.when(edge)
    def _():
        pl.semaphore_wait(barrier, groups)

    @pl.when(jnp.logical_not(edge))
    def _():
        pl.semaphore_wait(barrier, groups + 1)


def rotate_head(values, cosine, sine):
    return values * cosine + pltpu.roll(values, values.shape[-1] // 2, 1) * sine


def key_reach(first, step, sequence):
    low = max(0, (first + 1 - sequence // 2) // 128 * 128)
    return low, pl.ds(low, first + step - low)


def allowed_bias(start, first, step, low):
    shape = (step, first + step - low)
    key_place = lax.broadcasted_iota(jnp.int32, shape, 1) + low
    query_place = lax.broadcasted_iota(jnp.int32, shape, 0) + first
    return jnp.where((key_place <= query_place) & (key_place >= start), 0.0, masked)


def head_scores(query, keys, bias):
    return product(query, keys, 1, 1) * (1.0 / math.sqrt(HEAD_DIM)) + bias


def fill_tables(lengths, frequency, cosine, sine, start):
    shape = start.shape
    place = lax.broadcasted_iota(jnp.int32, shape, 0)
    begin = jnp.zeros(shape, jnp.int32)
    end = 0
    for i in range(lengths.shape[1] - 1):
        end = end + lengths[0, i]
        begin = jnp.where(place >= end, end, begin)
    start[...] = begin
    angle = (place - begin).astype(F32) * frequency[...]
    lane = lax.broadcasted_iota(jnp.int32, shape, 1)
    cosine[...] = jnp.cos(angle)
    sine[...] = jnp.where(lane < shape[1] // 2, -1.0, 1.0) * jnp.sin(angle)


def front_kernel(
    lengths, frequency, x_own, dy_own, w_query, w_key, w_value, w_out, w_gate, w_up, w_down,
    n1_out, query_out, key_out, value_out, attn_out, attn_b_out, out_columns_out, down_parts,
    down_columns_out, hidden_out, grad_gate_out, grad_up_out, middle_out, n2_out, dy_out, n2_hopped,
    grad_out, grad_all_out, dy_hopped, passed, cosine_out, sine_out, start_out,
    n1, n2, dy, query, key, value, attn, attn_b, out_columns, gate_w, up_w, down_w,
    hidden, grad_gate, grad_up, parts, pair, sums, by_far, by_side, middle, normed, n2_own, grad_own, n1_own, cosine, sine, start,
    load_sem, save_sem, gather_sent, gather_came, scatter_sent, scatter_came,
    swap_sent, swap_came, line_sent, line_came, down_sent, down_came, pass_sem,
):
    replica = lax.axis_index("replica")
    replicas = lax.axis_size("replica")
    me = lax.axis_index("shard")
    groups = lax.axis_size("shard")
    tokens, width = x_own.shape
    sequence = n1.shape[0]
    saves = []

    def save(src, dst):
        copy = pltpu.make_async_copy(src, dst, save_sem.at[len(saves)])
        copy.start()
        saves.append(copy)

    def exchange(which, source, target):
        copies = []
        for i in range(1, groups):
            device = lax.rem(me + i, groups)
            copies.append(
                pltpu.make_async_remote_copy(
                    src_ref=source(device),
                    dst_ref=target,
                    send_sem=swap_sent.at[which, i],
                    recv_sem=swap_came.at[which, i],
                    device_id=(replica, device),
                    device_id_type=MESH,
                )
            )
        return copies

    gate_load = pltpu.make_async_copy(w_gate, gate_w, load_sem.at[0])
    up_load = pltpu.make_async_copy(w_up, up_w, load_sem.at[1])
    gate_load.start()
    up_load.start()
    own_rows = block_rows(me, tokens)
    x = x_own[...].astype(F32)
    center = x - jnp.mean(x, axis=-1, keepdims=True)
    inverse = lax.rsqrt(jnp.mean(center * center, axis=-1, keepdims=True) + epsilon)
    n1_own[...] = (center * inverse).astype(BF)
    own_n1 = pltpu.make_async_copy(n1_own, n1.at[own_rows], load_sem.at[2])
    own_dy = pltpu.make_async_copy(dy_own, dy.at[own_rows], load_sem.at[3])
    own_n1.start()
    own_dy.start()

    greet_all(pltpu.get_barrier_semaphore())
    n1_gather = Gather(n1_own, n1, gather_sent.at[0], gather_came.at[0])
    dy_gather = Gather(dy_own, dy, gather_sent.at[1], gather_came.at[1])
    n2_gather = Gather(n2_own, n2, gather_sent.at[2], gather_came.at[2])
    grad_gather = Gather(grad_own, grad_all_out, gather_sent.at[3], gather_came.at[3])
    half = sequence // 2
    dy_half = dy.at[pl.ds(pl.multiple_of(lax.rem(me, 2) * half, half), half)]
    n2_hop = Hop(1, lambda way: n2_own, n2_hopped, line_sent.at[0], line_came.at[0])
    dy_hop = Hop(1, lambda way: dy_half, dy_hopped, line_sent.at[1], line_came.at[1])
    passing = [
        pltpu.make_async_remote_copy(
            src_ref=src,
            dst_ref=passed.at[way],
            send_sem=pass_sem.at[0, way],
            recv_sem=pass_sem.at[1, way],
            device_id=(replica + (1 if way == 0 else -1), me),
            device_id_type=MESH,
        )
        for way in (0, 1)
        for src in (dy_own, passed.at[way])
    ]
    last = replicas - 1

    def passes(way, k):
        return replica == (k if way == 0 else last - k)

    def pass_on(k):
        for way in (0, 1):

            @pl.when(passes(way, k))
            def _(way=way):
                if k:
                    passing[2 * way].wait_recv()
                if k < 2:
                    passing[2 * way + (1 if k else 0)].start()

    down_line = Line(
        down_parts.at[replica], lambda s: down_parts.at[s], down_sent, down_came
    )
    buffers = (pair, sums, by_far, by_side)

    n1_gather.one()
    pass_on(0)
    fill_tables(lengths, frequency, cosine, sine, start)
    save(cosine, cosine_out)
    save(sine, sine_out)
    save(start, start_out)
    n1_gather.two()
    n1_gather.three()
    wide = w_out.shape[0]
    mine = pl.ds(pl.multiple_of(me * wide, wide), wide)
    part = down_parts.shape[2]

    def down_block(device):
        column = (device * replicas + replica) * part
        return w_down.at[:, pl.ds(pl.multiple_of(column, part), part)]

    def out_block(device):
        return w_out.at[:, pl.ds(pl.multiple_of(device * wide, wide), wide)]

    down_swaps = exchange(1, down_block, down_parts.at[replica, mine])
    out_swaps = exchange(0, out_block, out_columns.at[mine])
    own_down = pltpu.make_async_copy(down_block(me), down_parts.at[replica, mine], load_sem.at[5])
    own_down.start()
    own_out = pltpu.make_async_copy(out_block(me), out_columns.at[mine], load_sem.at[4])
    own_out.start()
    for copy in down_swaps + out_swaps:
        copy.start()
    pass_on(1)
    own_n1.wait()
    n1_gather.finish_near()
    row = me // (groups // 2)

    def half_rows(i):
        return pl.ds(pl.multiple_of((row + i * (1 - 2 * row)) * half, half), half)


    heads = query.shape[1] // HEAD_DIM
    def projections(i, carry):
        rows = half_rows(i)
        for weight, target in ((w_query, query), (w_key, key), (w_value, value)):
            values = product(n1[rows, :], weight[...], 1, 1)
            for head in range(heads):
                lanes = pl.ds(head * HEAD_DIM, HEAD_DIM)
                piece = values[:, head * HEAD_DIM : (head + 1) * HEAD_DIM]
                if target is not value:
                    piece = rotate_head(piece, cosine[rows, :], sine[rows, :])
                target[rows, lanes] = piece.astype(BF)

        @pl.when(i == 0)
        def _():
            n1_gather.four()
            n1_gather.finish_far()

        return carry

    lax.fori_loop(0, 2, projections, 0)
    save(n1, n1_out)
    save(query, query_out)
    save(key, key_out)
    save(value, value_out)
    own_down.wait()
    for copy in down_swaps:
        copy.wait_recv()
    down_line.start()
    step = 256
    for first in range(0, sequence, step):
        rows = pl.ds(first, step)
        low, reach = key_reach(first, step, sequence)
        bias = allowed_bias(start[rows, 0:1], first, step, low)
        for head in range(heads):
            lanes = pl.ds(head * HEAD_DIM, HEAD_DIM)
            scores = head_scores(query[rows, lanes], key[reach, lanes], bias)
            weights = jnp.exp(scores - jnp.max(scores, axis=-1, keepdims=True))
            total = jnp.sum(weights, axis=-1, keepdims=True)
            result = product(weights.astype(BF), value[reach, lanes], 1, 0) / total
            attn[rows, lanes] = result
            attn_b[rows, lanes] = result.astype(BF)
    pass_on(2)
    save(attn, attn_out)
    save(attn_b, attn_b_out)

    own_out.wait()
    for copy in out_swaps:
        copy.wait_recv()
    save(out_columns, out_columns_out)

    scatter = Scatter(parts, buffers, scatter_sent.at[0], scatter_came.at[0])

    def spread(i, carry):
        def step(rows, columns):
            rows = half_rows(1 - i)
            parts[rows, columns] = product(attn_b[rows, :], out_columns[columns, :], 1, 1).astype(BF)

        tile_loop(half, width, half, step)

        @pl.when(i == 0)
        def _():
            scatter.swap(3, 2)

        return carry

    lax.fori_loop(0, 2, spread, 0)
    scatter.swap(1, 0)
    scatter.send_far()
    scatter.send_near()
    down_line.step(1)
    scatter.send_rest()
    middle[...] = x_own[...].astype(F32) + scatter.total()
    scatter.drain()
    save(middle, middle_out)
    center = middle[...] - jnp.mean(middle[...], axis=-1, keepdims=True)
    inverse = lax.rsqrt(jnp.mean(center * center, axis=-1, keepdims=True) + epsilon)
    normed[...] = center * inverse
    n2_own[...] = normed[...].astype(BF)
    n2_gather.one()
    own_n2 = pltpu.make_async_copy(n2_own, n2.at[own_rows], load_sem.at[6])
    own_n2.start()
    n2_gather.two()
    n2_gather.three()
    dy_gather.one()
    down_line.step(2)
    n2_hop.start()
    own_n2.wait()
    n2_gather.finish_near()
    gate_load.wait()
    up_load.wait()

    def feed_forward(i):
        def forward(rows, columns):
            rows = half_rows(i)
            gate = product(n2[rows, :], gate_w[columns, :], 1, 1)
            up = product(n2[rows, :], up_w[columns, :], 1, 1)
            sigma = 0.5 + 0.5 * jnp.tanh(0.5 * gate)
            silu = gate * sigma
            hidden[rows, columns] = (silu * up).astype(BF)
            grad_gate[rows, columns] = (up * (sigma + silu * (1.0 - sigma))).astype(BF)
            grad_up[rows, columns] = silu.astype(BF)

        tile_loop(half, gate_w.shape[0], half, forward, 256)

    def both_forward(i, carry):
        feed_forward(i)

        @pl.when(i == 0)
        def _():
            n2_gather.four()
            n2_gather.finish_far()
            dy_gather.two()

        return carry

    lax.fori_loop(0, 2, both_forward, 0)
    save(n2, n2_out)
    dy_gather.three()
    dy_gather.four()
    own_dy.wait()
    dy_gather.finish()
    save(dy, dy_out)
    save(hidden, hidden_out)
    dy_hop.start()
    down_line.step(3)
    down_loads = []
    for r in range(replicas):
        down_loads.append(
            pltpu.make_async_copy(
                down_parts.at[r], down_w.at[:, pl.ds(r * part, part)], load_sem.at[7 + r]
            )
        )
        down_loads[-1].start()
    for copy in down_loads:
        copy.wait()
    save(down_w, down_columns_out)

    back = Scatter(parts, buffers, scatter_sent.at[1], scatter_came.at[1])

    def feed(base, i):
        def grads(rows, columns):
            rows = pl.ds(pl.multiple_of(base, half), half)
            grad = product(dy[rows, :], down_w[:, columns], 1, 0)
            grad_gate[rows, columns] = (grad * grad_gate[rows, columns].astype(F32)).astype(BF)
            grad_up[rows, columns] = (grad * grad_up[rows, columns].astype(F32)).astype(BF)

        tile_loop(half, gate_w.shape[0], half, grads)

        @pl.when(i == 1)
        def _():
            back.send_far()

        def backward(rows, columns):
            rows = pl.ds(pl.multiple_of(base, half), half)
            value = product(grad_gate[rows, :], gate_w[:, columns], 1, 0)
            value = value + product(grad_up[rows, :], up_w[:, columns], 1, 0)
            parts[rows, columns] = value.astype(BF)

        tile_loop(half, width, half, backward)

    def both_back(i, carry):
        feed((1 - row + i * (2 * row - 1)) * half, i)

        @pl.when(i == 0)
        def _():
            back.swap(3, 2)

        return carry

    lax.fori_loop(0, 2, both_back, 0)
    save(grad_gate, grad_gate_out)
    save(grad_up, grad_up_out)
    back.swap(1, 0)
    back.send_near()
    back.send_rest()
    inner = back.total()
    back.drain()
    inner = (
        inner
        - jnp.mean(inner, axis=-1, keepdims=True)
        - normed[...] * jnp.mean(inner * normed[...], axis=-1, keepdims=True)
    )
    center = middle[...] - jnp.mean(middle[...], axis=-1, keepdims=True)
    inverse = lax.rsqrt(jnp.mean(center * center, axis=-1, keepdims=True) + epsilon)
    normed[...] = dy_own[...].astype(F32) + inverse * inner
    grad_own[...] = normed[...].astype(BF)
    grad_gather.one()
    save(normed, grad_out)
    save(grad_own, grad_all_out.at[own_rows])
    grad_gather.two()
    grad_gather.three()
    grad_gather.four()
    grad_gather.finish()
    for way in (0, 1):

        @pl.when(passes(way, 0) | passes(way, 1))
        def _(way=way):
            passing[2 * way].wait_send()

    n2_hop.arrive()
    dy_hop.arrive()
    for copy in saves:
        copy.wait()
    for copy in out_swaps + down_swaps:
        copy.wait_send()
    for user in (n1_gather, n2_gather, dy_gather, grad_gather, down_line, n2_hop, dy_hop):
        user.drain()


def front(lengths, frequency, x_own, dy_own, w_query, w_key, w_value, w_out, w_gate, w_up, w_down):
    groups, replicas = lax.axis_size("shard"), lax.axis_size("replica")
    tokens, width = x_own.shape
    sequence = tokens * groups
    wide, columns = w_query.shape[0], w_gate.shape[0]
    anywhere, vmem = pl.BlockSpec(memory_space=pl.ANY), pl.BlockSpec(memory_space=VMEM)

    def shape(dims, kind=BF):
        return jax.ShapeDtypeStruct(dims, kind)

    outs = (
        shape((sequence, width)),
        shape((sequence, wide)),
        shape((sequence, wide)),
        shape((sequence, wide)),
        shape((sequence, wide), F32),
        shape((sequence, wide)),
        shape((width, wide)),
        shape((replicas, width, columns // replicas)),
        shape((width, columns)),
        shape((sequence, columns)),
        shape((sequence, columns)),
        shape((sequence, columns)),
        shape((tokens, width), F32),
        shape((sequence, width)),
        shape((sequence, width)),
        shape((2, tokens, width)),
        shape((tokens, width), F32),
        shape((sequence, width)),
        shape((2, sequence // 2, width)),
        shape((2, tokens, width)),
        shape((sequence, HEAD_DIM), F32),
        shape((sequence, HEAD_DIM), F32),
        shape((sequence, HEAD_DIM), jnp.int32),
    )
    dma = pltpu.SemaphoreType.DMA
    return pl.pallas_call(
        front_kernel,
        out_shape=outs,
        in_specs=[pl.BlockSpec(memory_space=pltpu.SMEM)] + [vmem] * 6 + [anywhere] * 4,
        out_specs=(anywhere,) * len(outs),
        scratch_shapes=[
            pltpu.VMEM((sequence, width), BF),
            pltpu.VMEM((sequence, width), BF),
            pltpu.VMEM((sequence, width), BF),
            pltpu.VMEM((sequence, wide), BF),
            pltpu.VMEM((sequence, wide), BF),
            pltpu.VMEM((sequence, wide), BF),
            pltpu.VMEM((sequence, wide), F32),
            pltpu.VMEM((sequence, wide), BF),
            pltpu.VMEM((width, wide), BF),
            pltpu.VMEM((columns, width), BF),
            pltpu.VMEM((columns, width), BF),
            pltpu.VMEM((width, columns), BF),
            pltpu.VMEM((sequence, columns), BF),
            pltpu.VMEM((sequence, columns), BF),
            pltpu.VMEM((sequence, columns), BF),
            pltpu.VMEM((sequence, width), BF),
            pltpu.VMEM((4, tokens, width), BF),
            pltpu.VMEM((3, tokens, width), BF),
            pltpu.VMEM((2, tokens // 2, width), BF),
            pltpu.VMEM((2, tokens, width), BF),
            pltpu.VMEM((tokens, width), F32),
            pltpu.VMEM((tokens, width), F32),
            pltpu.VMEM((tokens, width), BF),
            pltpu.VMEM((tokens, width), BF),
            pltpu.VMEM((tokens, width), BF),
            pltpu.VMEM((sequence, HEAD_DIM), F32),
            pltpu.VMEM((sequence, HEAD_DIM), F32),
            pltpu.VMEM((sequence, HEAD_DIM), jnp.int32),
            dma((7 + replicas,)),
            dma((24,)),
            dma((4, 13)),
            dma((4, 13)),
            dma((2, 10)),
            dma((2, 10)),
            dma((2, groups)),
            dma((2, groups)),
            dma((2, 2)),
            dma((2, 2)),
            dma((2, replicas)),
            dma((2, replicas)),
            dma((2, 2)),
        ],
        compiler_params=pltpu.CompilerParams(
            collective_id=3, has_side_effects=True, vmem_limit_bytes=67043328
        ),
        cost_estimate=pl.CostEstimate(
            flops=12 * sequence * width * columns, bytes_accessed=64 * 1024 * 1024, transcendentals=0
        ),
        name="front",
    )(lengths, frequency, x_own, dy_own, w_query, w_key, w_value, w_out, w_gate, w_up, w_down)


def back_kernel(
    x_own, start, cosine, sine, hidden_in, down_in, grad_in, out_columns_in, attn_b_in, attn_in,
    query_in, key_in, value_in, n1_in, w_query, w_key, w_value, n2_near, dy_near, middle, grad_middle,
    layer_out, input_grad, attn_part, out_grad_out, n2_hopped, dy_hopped, near_all,
    hidden, down_w, grad, out_columns, attn_b, attn, query, key, value, n1, weights,
    grad_attn, key_grad, value_grad, columns_grad, out_grad, rows_grad, parts,
    pair, sums, by_far, by_side, pair2, sums2, by_far2, by_side2,
    load_sem, save_sem, scatter_sent, scatter_came, line_sent, line_came,
    gather_sent, gather_came,
):
    sequence, width = n1.shape
    me = lax.axis_index("shard")
    near_half = x_own.shape[0] // 2
    near_block = n2_near.at[1 - lax.rem(lax.axis_index("replica"), 2), pl.ds(0, near_half)]
    near = Gather(near_block, near_all, gather_sent, gather_came)
    wide = query.shape[1]
    heads = wide // HEAD_DIM
    pairs = (
        (hidden_in, hidden), (down_in, down_w), (grad_in, grad), (out_columns_in, out_columns),
        (attn_b_in, attn_b), (attn_in, attn), (query_in, query), (key_in, key), (value_in, value),
        (n1_in, n1), (w_query, weights.at[pl.ds(0, wide)]), (w_key, weights.at[pl.ds(wide, wide)]),
        (w_value, weights.at[pl.ds(2 * wide, wide)]),
    )
    loads = [
        pltpu.make_async_copy(src, dst, load_sem.at[i]) for i, (src, dst) in enumerate(pairs)
    ]
    for copy in loads[:2]:
        copy.start()
    greet_all(pltpu.get_barrier_semaphore())
    hops = (
        Hop(2, lambda way: n2_near.at[way], n2_hopped, line_sent.at[0], line_came.at[0]),
        Hop(2, lambda way: dy_near.at[way], dy_hopped, line_sent.at[1], line_came.at[1]),
    )
    for hop in hops:
        hop.start()
    near.one()
    own_near = pltpu.make_async_copy(near_block, near_all.at[block_rows(me, near.tokens)], save_sem.at[2])
    own_near.start()
    loads[0].wait()
    loads[1].wait()
    for copy in loads[2:]:
        copy.start()

    mixed = Scatter(parts, (pair, sums, by_far, by_side), scatter_sent.at[0], scatter_came.at[0])
    half = sequence // 2
    row = me // (lax.axis_size("shard") // 2)

    def by_halves(scatter, tile):
        def one_half(i, carry):
            def step(rows, columns):
                rows = pl.ds(pl.multiple_of((1 - row + i * (2 * row - 1)) * half, half), half)
                parts[rows, columns] = tile(rows, columns).astype(BF)

            tile_loop(half, width, half, step)

            @pl.when(i == 0)
            def _():
                scatter.swap(3, 2)

            return carry

        lax.fori_loop(0, 2, one_half, 0)
        scatter.swap(1, 0)

    by_halves(mixed, lambda rows, columns: product(hidden[rows, :], down_w[columns, :], 1, 1))

    for copy in loads[2:6]:
        copy.wait()
    near.two()
    mixed.send_far()
    mixed.send_near()
    near.three()

    def out_step(i, carry):
        rows = pl.ds(pl.multiple_of(i * 512, 512), 512)
        out_grad[rows, :] = product(grad[:, rows], attn_b[...], 0, 0).astype(BF)
        return carry

    lax.fori_loop(0, width // 512, out_step, 0)
    out_save = pltpu.make_async_copy(out_grad, out_grad_out, save_sem.at[0])
    out_save.start()

    def attn_step(i, carry):
        rows = pl.ds(pl.multiple_of(i * 512, 512), 512)
        grad_attn[rows, :] = product(grad[rows, :], out_columns[...], 1, 0).astype(BF)
        return carry

    lax.fori_loop(0, sequence // 512, attn_step, 0)
    for copy in loads[6:]:
        copy.wait()
    mixed.send_rest()

    near.four()
    step = 256
    for first in range(sequence - step, -1, -step):
        rows = pl.ds(first, step)
        low, upto = key_reach(first, step, sequence)
        bias = allowed_bias(start[rows, 0:1], first, step, low)
        for head in range(heads):
            lanes = pl.ds(head * HEAD_DIM, HEAD_DIM)
            query_piece, grad_piece = query[rows, lanes], grad_attn[rows, lanes]
            scores = head_scores(query_piece, key[upto, lanes], bias)
            probs = jnp.exp(scores - jnp.max(scores, axis=-1, keepdims=True))
            probs = probs / jnp.sum(probs, axis=-1, keepdims=True)
            delta = jnp.sum(grad_piece.astype(F32) * attn[rows, lanes], axis=-1, keepdims=True)
            grad_probs = product(grad_piece, value[upto, lanes], 1, 1)
            grad_scores = (probs * (grad_probs - delta)).astype(BF)
            query_grad = product(grad_scores, key[upto, lanes], 1, 0) * (1.0 / math.sqrt(HEAD_DIM))
            query_grad = rotate_head(query_grad, cosine[rows, :], -sine[rows, :])
            columns_grad[rows, lanes] = query_grad.astype(BF)
            key_part = product(grad_scores, query_piece, 0, 0)
            value_part = product(probs.astype(BF), grad_piece, 0, 0)
            if first == sequence - step:
                key_grad[upto, lanes] = key_part
                value_grad[upto, lanes] = value_part
                if low:
                    key_grad[pl.ds(0, low), lanes] = jnp.zeros((low, HEAD_DIM), F32)
                    value_grad[pl.ds(0, low), lanes] = jnp.zeros((low, HEAD_DIM), F32)
            else:
                key_grad[upto, lanes] += key_part
                value_grad[upto, lanes] += value_part
    for head in range(heads):
        lanes = pl.ds(head * HEAD_DIM, HEAD_DIM)
        piece = key_grad[:, lanes] * (1.0 / math.sqrt(HEAD_DIM))
        piece = rotate_head(piece, cosine[...], -sine[...])
        columns_grad[:, pl.ds(wide + head * HEAD_DIM, HEAD_DIM)] = piece.astype(BF)
        columns_grad[:, pl.ds(2 * wide + head * HEAD_DIM, HEAD_DIM)] = value_grad[:, lanes].astype(BF)

    layer_out[...] = (middle[...] + mixed.total()).astype(BF)
    mixed.drain()

    last = Scatter(parts, (pair2, sums2, by_far2, by_side2), scatter_sent.at[1], scatter_came.at[1])
    by_halves(last, lambda rows, columns: product(columns_grad[rows, :], weights[:, columns], 1, 0))
    last.send_far()
    last.send_near()

    def collect(rows, columns):
        rows_grad[rows, columns] = product(columns_grad[:, rows], n1[:, columns], 0, 0).astype(BF)

    tile_loop(3 * wide, width, 256, collect, 512)
    rows_save = pltpu.make_async_copy(rows_grad, attn_part, save_sem.at[1])
    rows_save.start()
    last.send_rest()
    x = x_own[...].astype(F32)
    center = x - jnp.mean(x, axis=-1, keepdims=True)
    inverse = lax.rsqrt(jnp.mean(center * center, axis=-1, keepdims=True) + epsilon)
    inner = last.total()
    normed = center * inverse
    inner = (
        inner
        - jnp.mean(inner, axis=-1, keepdims=True)
        - normed * jnp.mean(inner * normed, axis=-1, keepdims=True)
    )
    input_grad[...] = grad_middle[...] + inverse * inner
    last.drain()
    out_save.wait()
    rows_save.wait()
    own_near.wait()
    near.finish()
    near.drain()
    for hop in hops:
        hop.arrive()
        hop.drain()


def back(x_own, start, cosine, sine, hidden, down, grad, out_columns, attn_b, attn, query, key, value, n1,
         w_query, w_key, w_value, n2_near, dy_near, middle, grad_middle):
    groups = lax.axis_size("shard")
    tokens, width = x_own.shape
    sequence = tokens * groups
    wide, columns = query.shape[1], hidden.shape[1]
    anywhere, vmem = pl.BlockSpec(memory_space=pl.ANY), pl.BlockSpec(memory_space=VMEM)
    dma = pltpu.SemaphoreType.DMA
    buffers = [
        pltpu.VMEM((4, tokens, width), BF),
        pltpu.VMEM((3, tokens, width), BF),
        pltpu.VMEM((2, tokens // 2, width), BF),
        pltpu.VMEM((2, tokens, width), BF),
    ]
    return pl.pallas_call(
        back_kernel,
        out_shape=(
            jax.ShapeDtypeStruct((tokens, width), BF),
            jax.ShapeDtypeStruct((tokens, width), F32),
            jax.ShapeDtypeStruct((3 * wide, width), BF),
            jax.ShapeDtypeStruct((width, wide), BF),
            jax.ShapeDtypeStruct(n2_near.shape, BF),
            jax.ShapeDtypeStruct(dy_near.shape, BF),
            jax.ShapeDtypeStruct((sequence // 2, width), BF),
        ),
        in_specs=[vmem] * 4 + [anywhere] * 15 + [vmem] * 2,
        out_specs=(vmem, vmem) + (anywhere,) * 5,
        scratch_shapes=[
            pltpu.VMEM((sequence, columns), BF),
            pltpu.VMEM((width, columns), BF),
            pltpu.VMEM((sequence, width), BF),
            pltpu.VMEM((width, wide), BF),
            pltpu.VMEM((sequence, wide), BF),
            pltpu.VMEM((sequence, wide), F32),
            pltpu.VMEM((sequence, wide), BF),
            pltpu.VMEM((sequence, wide), BF),
            pltpu.VMEM((sequence, wide), BF),
            pltpu.VMEM((sequence, width), BF),
            pltpu.VMEM((3 * wide, width), BF),
            pltpu.VMEM((sequence, wide), BF),
            pltpu.VMEM((sequence, wide), F32),
            pltpu.VMEM((sequence, wide), F32),
            pltpu.VMEM((sequence, 3 * wide), BF),
            pltpu.VMEM((width, wide), BF),
            pltpu.VMEM((3 * wide, width), BF),
            pltpu.VMEM((sequence, width), BF),
            *buffers,
            *buffers,
            dma((13,)),
            dma((3,)),
            dma((2, 10)),
            dma((2, 10)),
            dma((2, 2)),
            dma((2, 2)),
            dma((13,)),
            dma((13,)),
        ],
        compiler_params=pltpu.CompilerParams(
            collective_id=4, has_side_effects=True, vmem_limit_bytes=67043328
        ),
        cost_estimate=pl.CostEstimate(
            flops=24 * sequence * width * wide, bytes_accessed=48 * 1024 * 1024, transcendentals=0
        ),
        name="back",
    )(x_own, start, cosine, sine, hidden, down, grad, out_columns, attn_b, attn, query, key, value, n1,
      w_query, w_key, w_value, n2_near, dy_near, middle, grad_middle)


def every_kernel(
    near_all, n2_one, n2_two, dy_one, dy_two, passed, own_normed, own_dy, own_hidden, own_grad_gate, own_grad_up,
    attn_part, out_part,
    w_gate, w_up, w_down,
    both_out, out_down, out_attn, landed, kept, dy_other,
    out_rows, n2_three, near_rest, passed_three,
    normed, dy, hidden, grads, gate_w, up_w, down_w, down, totals, first_sum, second_sum, stage,
    load_sem, keep_sem, gather_sent, gather_came, line_sent, line_came, line_own, swap_sent, swap_came,
    out_sem, pair_sem, out_swap_sem, hop_sent, hop_came, near_sem,
):
    replica = lax.axis_index("replica")
    replicas = lax.axis_size("replica")
    me = lax.axis_index("shard")
    groups = lax.axis_size("shard")
    tokens = n2_one.shape[1]
    sequence, width = normed.shape
    half = sequence // 2
    columns = hidden.shape[1]
    grad_gate, grad_up = grads.at[0], grads.at[1]
    inner = (replica == 1) | (replica == 2)
    outer = (replica == 0) | (replica == 3)
    beside = replica + 1 - 2 * lax.rem(replica, 2)
    facing = 3 - replica
    chunks, depth = first_sum.shape[0], first_sum.shape[1]

    def piece(c):
        return pl.ds(c * depth, depth)

    def line_move(kind, c, src, dst, target):
        return pltpu.make_async_remote_copy(
            src_ref=src,
            dst_ref=dst,
            send_sem=line_sent.at[kind, c],
            recv_sem=line_came.at[kind, c],
            device_id=(target, me),
            device_id_type=MESH,
        )

    attn_chunks = attn_part.shape[0] // depth

    def own_chunk(c):
        return attn_part.at[piece(c)] if c < attn_chunks else out_rows.at[piece(c - attn_chunks)]

    def inward(c):
        return line_move(0, c, own_chunk(c), first_sum.at[c], beside)

    def middle(c):
        return line_move(1, c, first_sum.at[c], second_sum.at[c], facing)

    def outward(c):
        return line_move(2, c, second_sum.at[c], out_attn.at[piece(c)], beside)

    def keep(c):
        return pltpu.make_async_copy(second_sum.at[c], out_attn.at[piece(c)], line_own.at[c])

    def stage_load(c):
        return pltpu.make_async_copy(own_chunk(c), stage, keep_sem.at[2, 0])

    def half_sums(*which):
        @pl.when(inner)
        def _():
            for c in which:
                stage_load(c).wait()
                inward(c).wait_recv()
                first_sum[c] = (stage[...].astype(F32) + first_sum[c].astype(F32)).astype(BF)
                middle(c).start()
                if c + 1 < chunks:
                    stage_load(c + 1).start()

    def full_sums(*which):
        @pl.when(inner)
        def _():
            for c in which:
                middle(c).wait_recv()
                second_sum[c] = (first_sum[c].astype(F32) + second_sum[c].astype(F32)).astype(BF)
                outward(c).start()
                keep(c).start()

    core = lax.rem(me, 2)
    mate = me + 1 - 2 * core
    low_side, high_side = 1 - lax.rem(replica, 2), 1 - replica // 2
    hop = Hop(3, lambda way: n2_two.at[way], n2_three, hop_sent.at[0], hop_came.at[0])
    dy_hop = Hop(3, lambda way: passed.at[way], passed_three, hop_sent.at[1], hop_came.at[1])
    far_dy = passed_three.at[high_side]
    last_dy = Gather(far_dy, landed.at[3], gather_sent.at[3], gather_came.at[3])

    def last_dy_one():
        dy_hop.arrive()
        last_dy.one()

    def in_outer(action):
        def act():
            @pl.when(outer)
            def _():
                action()

        return act

    n2_blocks = {1: n2_one.at[low_side], 2: n2_two.at[high_side]}
    dy_halves = {1: dy_one.at[low_side], 2: dy_two.at[high_side]}
    roles = ((inner, n2_one.at[high_side]), (outer, n2_three.at[high_side]))
    third = dy_one.at[high_side]

    near = Gather(
        n2_one.at[low_side, pl.ds(tokens // 2, tokens // 2)], near_rest, gather_sent.at[0], gather_came.at[0]
    )

    def gather_of(n, block):
        return Gather(block, landed.at[n - 1], gather_sent.at[n - 1], gather_came.at[n - 1])

    gathers = [gather_of(2, n2_blocks[2]), gather_of(3, roles[0][1])]

    def last_one():
        hop.arrive()
        for role, block in roles:

            @pl.when(role)
            def _(block=block):
                gather_of(3, block).one()

        gather = gathers[1]
        gather.sends.extend(gather.firsts())

    def pair_copy(n, source):
        return pltpu.make_async_remote_copy(
            src_ref=source,
            dst_ref=dy_other.at[n - 1],
            send_sem=pair_sem.at[0, n - 1],
            recv_sem=pair_sem.at[1, n - 1],
            device_id=(replica, mate),
            device_id_type=MESH,
        )

    def normed_loads(n, target, base, block=None):
        copies = []
        if n == 1:
            for i in range(groups):
                device = lax.rem(me + i, groups)
                small = block_rows(device, near.tokens)
                rest = near_rest.at[small] if i else near.block
                for k, source in enumerate((near_all.at[small], rest)):
                    rows = block_rows(device, tokens, k + 1)
                    copies.append(pltpu.make_async_copy(source, target.at[rows], near_sem.at[k, i]))
            return copies
        for i in range(groups):
            device = lax.rem(me + i, groups)
            rows = block_rows(device, tokens)
            source = (n2_blocks[n] if block is None else block) if i == 0 else landed.at[n - 1, rows]
            copies.append(pltpu.make_async_copy(source, target.at[rows], load_sem.at[base, i]))
        return copies

    def dy_loads(n, source=None):
        mine = dy.at[pl.ds(pl.multiple_of(core * half, half), half)]
        others = dy.at[pl.ds(pl.multiple_of((1 - core) * half, half), half)]
        return [
            pltpu.make_async_copy(dy_halves[n] if source is None else source, mine, load_sem.at[1, 0]),
            pltpu.make_async_copy(dy_other.at[n - 1], others, load_sem.at[1, 1]),
        ]

    def far_loads():
        copies = []
        for i in range(groups):
            rows = block_rows(lax.rem(me + i, groups), tokens)
            source = landed.at[3, rows] if i else far_dy
            copies.append(pltpu.make_async_copy(source, dy.at[rows], load_sem.at[1, i]))
        return copies

    wide = width // groups

    def out_move(i):
        device = lax.rem(me + i, groups)
        return pltpu.make_async_remote_copy(
            src_ref=out_part.at[pl.ds(pl.multiple_of(device * wide, wide), wide)],
            dst_ref=out_rows.at[:, pl.ds(pl.multiple_of(me * wide, wide), wide)],
            send_sem=out_swap_sem.at[0, i],
            recv_sem=out_swap_sem.at[1, i],
            device_id=(replica, device),
            device_id_type=MESH,
        )

    own_out = pltpu.make_async_copy(
        out_part.at[pl.ds(pl.multiple_of(me * wide, wide), wide)],
        out_rows.at[:, pl.ds(pl.multiple_of(me * wide, wide), wide)],
        out_swap_sem.at[0, 0],
    )

    def out_ready():
        own_out.wait()
        for i in range(1, groups):
            out_move(i).wait_recv()

        @pl.when(outer)
        def _():
            start_all([inward(c) for c in range(attn_chunks, chunks)])

    def keeps(n):
        return [
            pltpu.make_async_copy(grad_gate, kept.at[n - 1, 0], keep_sem.at[0, n]),
            pltpu.make_async_copy(grad_up, kept.at[n - 1, 1], keep_sem.at[1, n]),
        ]

    def start_all(copies):
        for copy in copies:
            copy.start()

    def wait_all(copies):
        for copy in copies:
            copy.wait()

    first = [
        pltpu.make_async_copy(own_hidden, hidden, load_sem.at[1, 1]),
        pltpu.make_async_copy(own_dy, dy, load_sem.at[1, 0]),
    ]
    weights = [
        pltpu.make_async_copy(w_gate, gate_w, load_sem.at[2, 0]),
        pltpu.make_async_copy(w_up, up_w, load_sem.at[2, 1]),
        pltpu.make_async_copy(w_down, down_w, load_sem.at[2, 2]),
    ]
    start_all(first)
    barrier = pltpu.get_barrier_semaphore()
    for i in range(1, groups):
        device = lax.rem(me + i, groups)
        pl.semaphore_signal(barrier, inc=1, device_id=(replica, device), device_id_type=MESH)
    pl.semaphore_signal(barrier, inc=1, device_id=(beside, me), device_id_type=MESH)

    @pl.when(inner)
    def _():
        pl.semaphore_signal(barrier, inc=1, device_id=(facing, me), device_id_type=MESH)
        pl.semaphore_wait(barrier, groups + 1)

    @pl.when(outer)
    def _():
        pl.semaphore_wait(barrier, groups)

    further, last_normed = gathers
    near.one()
    pair_copy(1, dy_halves[1]).start()
    pair_copy(2, dy_halves[2]).start()
    own_out.start()
    hop.start()
    dy_hop.start()

    @pl.when(inner)
    def _():
        pair_copy(3, third).start()


    @pl.when(outer)
    def _():
        start_all([inward(c) for c in range(attn_chunks)])

    @pl.when(inner)
    def _():
        stage_load(0).start()

    def collect(out, left, right, add):
        def step(rows, cols):
            value = product(left[:, rows], right[:, cols], 0, 0)
            if add is None:
                out[rows, cols] = value
            elif add is True:
                out[rows, cols] += value

        tile_loop(out.shape[0], out.shape[1], 512, step)

    wait_all(first)
    start_all(weights)
    near.two()
    further.one()
    collect(down, dy, hidden, None)
    pair_copy(1, dy_halves[1]).wait()
    pair_copy(2, dy_halves[2]).wait()
    start_all(dy_loads(1))
    near.three()
    near.four()
    near.finish()
    start_all(normed_loads(1, normed, 0))
    wait_all(weights)
    wait_all(normed_loads(1, normed, 0))
    wait_all(dy_loads(1))

    def out_starts():
        for i in range(1, groups):
            out_move(i).start()

    agenda = {
        (1, 0): (further.two,),
        (1, 2): (further.three,),
        (1, 3): (further.four, last_one),
        (1, 4): (lambda: half_sums(0),),
        (1, 5): (further.finish,),
        (1, 7): (last_normed.two,),
        (2, 0): (last_normed.three, in_outer(last_dy_one)),
        (2, 1): (lambda: full_sums(0),),
        (2, 2): (last_normed.four,),
        (2, 4): (lambda: half_sums(2), in_outer(last_dy.two)),
        (2, 5): (lambda: full_sums(1),),
        (2, 7): (in_outer(last_dy.three), out_starts),
        (3, 0): (lambda: full_sums(2),),
        (3, 4): (lambda: half_sums(4),),
        (3, 6): (lambda: full_sums(3),),
        (3, 7): (out_ready,),
    }

    def after_down(n):
        if n == 1:
            start_all(dy_loads(2))
            half_sums(1)
            wait_all(keeps(n))
            wait_all(normed_loads(2, normed, 0))
            wait_all(dy_loads(2))
        else:
            @pl.when(inner)
            def _():
                pair_copy(3, third).wait()
                start_all(dy_loads(3, third))
                half_sums(3)
                wait_all(keeps(n))
                wait_all(normed_loads(3, normed, 0, roles[0][1]))
                wait_all(dy_loads(3, third))

            @pl.when(outer)
            def _():
                last_dy.four()
                last_dy.finish()
                start_all(far_loads())
                wait_all(keeps(n))
                wait_all(normed_loads(3, normed, 0, roles[1][1]))
                wait_all(far_loads())

    def sequence_step(n, carry):
        narrow = 256
        across = columns // narrow

        def one_tile(i, carry):
            ffn_tile(
                normed, dy, gate_w, up_w, down_w, hidden, grad_gate, grad_up,
                pl.ds(pl.multiple_of((i // across) * 512, 512), 512),
                pl.ds(pl.multiple_of(lax.rem(i, across) * narrow, narrow), narrow),
            )
            for (when, tile), actions in agenda.items():

                @pl.when((n == when) & (i == tile))
                def _(actions=actions):
                    for action in actions:
                        action()

            return carry

        lax.fori_loop(0, (sequence // 512) * across, one_tile, 0)
        for k in (1, 2):

            @pl.when(n == k)
            def _(k=k):
                start_all(keeps(k))
                if k == 1:
                    start_all(normed_loads(2, normed, 0))
                else:
                    last_normed.finish()
                    for role, block in roles:

                        @pl.when(role)
                        def _(block=block):
                            start_all(normed_loads(3, normed, 0, block))

        @pl.when(n < 3)
        def _():
            collect(down, dy, hidden, True)

        for k in (1, 2):

            @pl.when(n == k)
            def _(k=k):
                after_down(k)

        return carry

    lax.fori_loop(1, 4, sequence_step, 0)
    one_gate, one_up = up_w.at[:, pl.ds(0, columns)], up_w.at[:, pl.ds(columns, columns)]
    one_loads = normed_loads(1, gate_w, 2) + [
        pltpu.make_async_copy(kept.at[0, 0], one_gate, keep_sem.at[0, 0]),
        pltpu.make_async_copy(kept.at[0, 1], one_up, keep_sem.at[1, 0]),
    ]
    start_all(one_loads)

    wide = width // groups
    _, _, across_device, along_device, far_device = whereabouts()

    def down_move(send_index, recv_index, row, sender, device):
        return pltpu.make_async_remote_copy(
            src_ref=down_w.at[pl.ds(pl.multiple_of(row, wide), wide)],
            dst_ref=out_down.at[:, pl.ds(pl.multiple_of(sender * columns, columns), columns)],
            send_sem=swap_sent.at[send_index],
            recv_sem=swap_came.at[recv_index],
            device_id=(replica, device),
            device_id_type=MESH,
        )

    def chip_of(i):
        chip = jnp.where(i == 0, far_device, jnp.where(i == 1, across_device, along_device))
        return jnp.where(i == 3, me, chip) // 2

    def out_sends(i, k):
        return down_move(2 * i + k, 2 * i + core, (2 * i + k) * wide, me, chip_of(i) * 2 + k)

    def finish_down(i, carry):
        rows = pl.ds(pl.multiple_of(chip_of(i) * 2 * wide, 2 * wide), 2 * wide)

        def column_step(j, carry):
            cols = pl.ds(pl.multiple_of(j * 512, 512), 512)
            down[rows, cols] += product(dy[:, rows], hidden[:, cols], 0, 0)
            return carry

        lax.fori_loop(0, columns // 512, column_step, 0)
        down_w[pl.ds(pl.multiple_of(i * 2 * wide, 2 * wide), 2 * wide), :] = down[rows, :].astype(BF)

        @pl.when(i < 3)
        def _():
            out_sends(i, 0).start()
            out_sends(i, 1).start()

        return carry

    lax.fori_loop(0, 4, finish_down, 0)
    swaps = [out_sends(i, k) for i in range(3) for k in range(2)]
    arrivals = []
    for i in range(3):
        for k in range(2):
            peer = chip_of(i) * 2 + k
            arrivals.append(down_move(2 * i + k, 2 * i + k, (2 * i + k) * wide, peer, peer))
    swaps.append(down_move(6, 6, (6 + lax.rem(mate, 2)) * wide, me, mate))
    swaps[-1].start()
    arrivals.append(down_move(6, 6, 6 * wide, mate, mate))
    own_slab = pltpu.make_async_copy(
        down_w.at[pl.ds(pl.multiple_of((6 + core) * wide, wide), wide)],
        out_down.at[:, pl.ds(pl.multiple_of(me * columns, columns), columns)],
        keep_sem.at[2, 1],
    )
    own_slab.start()
    two_gate = pltpu.make_async_copy(kept.at[1, 0], hidden, keep_sem.at[0, 3])
    two_gate.start()
    full_sums(4)
    half_sums(5)
    wait_all(one_loads)
    two_loads = normed_loads(2, dy, 0)
    start_all(two_loads)

    two_up = pltpu.make_async_copy(kept.at[1, 1], hidden, keep_sem.at[1, 3])
    own_loads = [
        pltpu.make_async_copy(own_normed, normed, load_sem.at[2, 0]),
        pltpu.make_async_copy(own_grad_gate, one_gate, load_sem.at[2, 1]),
        pltpu.make_async_copy(own_grad_up, one_up, load_sem.at[2, 2]),
    ]

    def one_rows(u, rows):
        return up_w[:, pl.ds(pl.multiple_of(u * columns + rows.start, 512), 512)]

    def two_passes(u, carry):
        def newest(rows, cols):
            value = product(grads[u, :, rows], normed[:, cols], 0, 0)
            totals[u, rows, cols] = value + product(one_rows(u, rows), gate_w[:, cols], 0, 0)

        tile_loop(columns, width, 512, newest)

        @pl.when(u == 0)
        def _():
            half_sums(6)
            wait_all(two_loads)
            two_gate.wait()

        @pl.when(u == 1)
        def _():
            start_all(own_loads)
            full_sums(6)
            two_up.wait()

        def older(rows, cols):
            totals[u, rows, cols] += product(hidden[:, rows], dy[:, cols], 0, 0)

        tile_loop(columns, width, 512, older)

        @pl.when(u == 0)
        def _():
            two_up.start()
            full_sums(5)
            half_sums(7)

        return carry

    lax.fori_loop(0, 2, two_passes, 0)
    full_sums(7)
    wait_all(own_loads)

    def out_save(i):
        u, rows = i // (columns // 512), pl.ds(pl.multiple_of(lax.rem(i, columns // 512) * 512, 512), 512)
        return pltpu.make_async_copy(totals.at[u, rows], both_out.at[u, rows], out_sem.at[i])

    def last_rows(i, carry):
        u, rows = i // (columns // 512), pl.ds(pl.multiple_of(lax.rem(i, columns // 512) * 512, 512), 512)

        def column_step(j, carry):
            cols = pl.ds(pl.multiple_of(j * 512, 512), 512)
            totals[u, rows, cols] += product(one_rows(u, rows), normed[:, cols], 0, 0)
            return carry

        lax.fori_loop(0, width // 512, column_step, 0)
        out_save(i).start()
        return carry

    lax.fori_loop(0, 2 * (columns // 512), last_rows, 0)
    out_saves = [out_save(i) for i in range(2 * (columns // 512))]

    @pl.when(outer)
    def _():
        for c in range(chunks):
            inward(c).wait_send()
            outward(c).wait_recv()

    @pl.when(inner)
    def _():
        for c in range(chunks):
            middle(c).wait_send()
            outward(c).wait_send()
            keep(c).wait()

    for copy in swaps:
        copy.wait_send()
    for copy in arrivals:
        copy.wait_recv()
    own_slab.wait()
    for i in range(1, groups):
        out_move(i).wait_send()
    hop.drain()

    @pl.when(outer)
    def _():
        last_dy.drain()

    wait_all(out_saves)
    dy_hop.drain()
    near.drain()
    for gather in gathers:
        gather.drain()


def ffn_grads(near_all, n2_one, n2_two, dy_one, dy_two, passed, n2, dy_all, own, attn_part, out_part, w_gate, w_up, w_down_columns):
    _, tokens, width = n2_one.shape
    sequence = n2.shape[0]
    groups = sequence // tokens
    columns = w_gate.shape[0]
    chunks = 8
    attn_rows = attn_part.shape[0] + out_part.shape[1]
    depth = attn_rows // chunks
    anywhere = pl.BlockSpec(memory_space=pl.ANY)
    dma = pltpu.SemaphoreType.DMA
    out = pl.pallas_call(
        every_kernel,
        out_shape=(
            jax.ShapeDtypeStruct((2, columns, width), F32),
            jax.ShapeDtypeStruct((width // groups, columns * groups), BF),
            jax.ShapeDtypeStruct((attn_rows, width), BF),
            jax.ShapeDtypeStruct((4, sequence, width), BF),
            jax.ShapeDtypeStruct((2, 2, sequence, columns), BF),
            jax.ShapeDtypeStruct((3, sequence // 2, width), BF),
            jax.ShapeDtypeStruct((out_part.shape[1], width), BF),
            jax.ShapeDtypeStruct(n2_two.shape, BF),
            jax.ShapeDtypeStruct((sequence // 2, width), BF),
            jax.ShapeDtypeStruct(passed.shape, BF),
        ),
        in_specs=[anywhere] * 16,
        out_specs=(anywhere,) * 10,
        scratch_shapes=[
            pltpu.VMEM((sequence, width), BF),
            pltpu.VMEM((sequence, width), BF),
            pltpu.VMEM((sequence, columns), BF),
            pltpu.VMEM((2, sequence, columns), BF),
            pltpu.VMEM((columns, width), BF),
            pltpu.VMEM((columns, width), BF),
            pltpu.VMEM((width, columns), BF),
            pltpu.VMEM((width, columns), F32),
            pltpu.VMEM((2, columns, width), F32),
            pltpu.VMEM((chunks, depth, width), BF),
            pltpu.VMEM((chunks, depth, width), BF),
            pltpu.VMEM((depth, width), BF),
            dma((3, groups)),
            dma((3, 4)),
            dma((4, 13)),
            dma((4, 13)),
            dma((3, chunks)),
            dma((3, chunks)),
            dma((chunks,)),
            dma((groups,)),
            dma((groups,)),
            dma((2 * (columns // 512),)),
            dma((2, 3)),
            dma((2, groups)),
            dma((2, 2)),
            dma((2, 2)),
            dma((2, groups)),
        ],
        compiler_params=pltpu.CompilerParams(
            collective_id=2, has_side_effects=True, vmem_limit_bytes=67043328
        ),
        cost_estimate=pl.CostEstimate(
            flops=42 * sequence * width * columns, bytes_accessed=80 * 1024 * 1024, transcendentals=0
        ),
        name="ffn_grads",
    )(near_all, n2_one, n2_two, dy_one, dy_two, passed, n2, dy_all, *own, attn_part, out_part, w_gate, w_up, w_down_columns)
    return out[:3]


def gather_tokens(values):
    return lax.all_gather(values, "shard", axis=0, tiled=True)


def scatter_tokens(partial):
    return lax.psum_scatter(
        partial.astype(BF), "shard", scatter_dimension=0, tiled=True
    ).astype(F32)


def rows_to_columns(weight):
    return lax.all_to_all(weight, "shard", split_axis=1, concat_axis=0, tiled=True)


def columns_to_rows(grad):
    return lax.all_to_all(grad, "shard", split_axis=0, concat_axis=1, tiled=True)


def replica_sum(part):
    return lax.psum(part.astype(BF), "replica")


def general_body(hidden_in, cotangent, doc_lengths, w_query, w_key, w_value, w_out, w_gate, w_up, w_down):
    x = hidden_in[0].astype(F32)
    dyb = cotangent[0]
    tokens_here = x.shape[0]
    groups = lax.axis_size("shard")
    seq_length = tokens_here * groups
    factor = 1.0 / math.sqrt(HEAD_DIM)
    places = jnp.arange(seq_length, dtype=jnp.int32)
    segment, offset = doc_layout(doc_lengths[0], places)
    cosine, sine = rope_tables(offset, HEAD_DIM)
    allowed = ((segment[:, None] == segment[None, :]) & (places[None, :] <= places[:, None]))[None]

    normed_one, inverse_one = normalize(x)
    n1 = gather_tokens(normed_one.astype(BF))
    w_out_columns = rows_to_columns(w_out)
    query = rotate(split_heads(dot(n1, w_query, 1, 1)), cosine, sine).astype(BF)
    keys = rotate(split_heads(dot(n1, w_key, 1, 1)), cosine, sine).astype(BF)
    values = split_heads(dot(n1, w_value, 1, 1)).astype(BF)
    scores = factor * jnp.einsum("hqe,hke->hqk", query, keys, preferred_element_type=F32)
    scores = jnp.where(allowed, scores, masked)
    top = jnp.max(scores, axis=-1, keepdims=True)
    weights = jnp.where(allowed, jnp.exp(scores - top), 0.0)
    total = jnp.sum(weights, axis=-1, keepdims=True)
    log_total = top + jnp.log(total)
    attn = jnp.einsum("hqk,hke->hqe", weights.astype(BF), values, preferred_element_type=F32) / total
    out_b = join_heads(attn).astype(BF)
    middle = x + scatter_tokens(dot(out_b, w_out_columns, 1, 1))

    normed_two, inverse_two = normalize(middle)
    n2 = gather_tokens(normed_two.astype(BF))
    dy_all = gather_tokens(dyb)
    w_down_columns = rows_to_columns(w_down)
    gate = dot(n2, w_gate, 1, 1)
    up = dot(n2, w_up, 1, 1)
    sigma = jax.nn.sigmoid(gate)
    silu = gate * sigma
    hidden = (silu * up).astype(BF)
    grad_down = columns_to_rows(replica_sum(dot(dy_all, hidden, 0, 0)))
    grad_hidden = dot(dy_all, w_down_columns, 1, 0)
    grad_gate_b = (grad_hidden * up * sigma * (1.0 + gate * (1.0 - sigma))).astype(BF)
    grad_up_b = (grad_hidden * silu).astype(BF)
    grad_gate = replica_sum(dot(grad_gate_b, n2, 0, 0).astype(BF))
    grad_up = replica_sum(dot(grad_up_b, n2, 0, 0).astype(BF))
    grad_normed_two = scatter_tokens(dot(grad_gate_b, w_gate, 1, 0) + dot(grad_up_b, w_up, 1, 0))
    mixed = scatter_tokens(dot(hidden, w_down_columns, 1, 1))
    layer_out = (middle + mixed).astype(BF)
    grad_middle = dyb.astype(F32) + norm_back(normed_two, inverse_two, grad_normed_two)

    grad_middle_all = gather_tokens(grad_middle.astype(BF))
    grad_out = columns_to_rows(replica_sum(dot(grad_middle_all, out_b, 0, 0).astype(BF)))
    grad_attn = split_heads(dot(grad_middle_all, w_out_columns, 1, 0)).astype(BF)
    delta = jnp.sum(grad_attn.astype(F32) * attn, axis=-1, keepdims=True)
    probs = jnp.where(allowed, jnp.exp(scores - log_total), 0.0)
    grad_probs = jnp.einsum("hqe,hke->hqk", grad_attn, values, preferred_element_type=F32)
    grad_scores = (probs * (grad_probs - delta)).astype(BF)
    query_grad = factor * jnp.einsum("hqk,hke->hqe", grad_scores, keys, preferred_element_type=F32)
    key_grad = factor * jnp.einsum("hqk,hqe->hke", grad_scores, query, preferred_element_type=F32)
    value_grad = jnp.einsum("hqk,hqe->hke", probs.astype(BF), grad_attn, preferred_element_type=F32)
    query_grad = join_heads(rotate(query_grad, cosine, -sine)).astype(BF)
    key_grad = join_heads(rotate(key_grad, cosine, -sine)).astype(BF)
    value_grad = join_heads(value_grad).astype(BF)
    grad_query = replica_sum(dot(query_grad, n1, 0, 0).astype(BF))
    grad_key = replica_sum(dot(key_grad, n1, 0, 0).astype(BF))
    grad_value = replica_sum(dot(value_grad, n1, 0, 0).astype(BF))
    grad_normed_one = scatter_tokens(
        dot(query_grad, w_query, 1, 0) + dot(key_grad, w_key, 1, 0) + dot(value_grad, w_value, 1, 0)
    )
    grad_in = grad_middle + norm_back(normed_one, inverse_one, grad_normed_one)
    return (
        layer_out[None],
        grad_in[None],
        grad_query.astype(F32),
        grad_key.astype(F32),
        grad_value.astype(F32),
        grad_out.astype(F32),
        grad_gate.astype(F32),
        grad_up.astype(F32),
        grad_down.astype(F32),
    )


def body(hidden_in, cotangent, doc_lengths, w_query, w_key, w_value, w_out, w_gate, w_up, w_down):
    x_own, dy_own = hidden_in[0], cotangent[0]
    half = HEAD_DIM // 2
    frequency = theta_base ** (-2.0 * (np.arange(HEAD_DIM) % half) / HEAD_DIM)
    (
        n1, query, key, value, attn, attn_b, out_columns, _, down_columns,
        hidden, grad_gate_b, grad_up_b, middle, n2, dy, n2_one, grad_middle, grad_all, dy_one, passed,
        cosine, sine, start,
    ) = front(
        doc_lengths, jnp.asarray(frequency[None], F32), x_own, dy_own,
        w_query, w_key, w_value, w_out, w_gate, w_up, w_down,
    )
    layer_out, grad_in, attn_part, out_part, n2_two, dy_two, near_all = back(
        x_own, start, cosine, sine, hidden, down_columns, grad_all, out_columns, attn_b, attn,
        query, key, value, n1, w_query, w_key, w_value, n2_one, dy_one, middle, grad_middle,
    )
    grad_both, grad_down, attn_sum = ffn_grads(
        near_all, n2_one, n2_two, dy_one, dy_two, passed, n2, dy, (hidden, grad_gate_b, grad_up_b),
        attn_part, out_part, w_gate, w_up, down_columns,
    )
    grad_query, grad_key, grad_value, grad_out = jnp.split(attn_sum.astype(F32), 4, axis=0)
    return (
        layer_out[None],
        grad_in[None],
        grad_query,
        grad_key,
        grad_value,
        grad_out,
        grad_both[0],
        grad_both[1],
        grad_down.astype(F32),
    )


def solution(mesh):
    rows = P("shard", None)
    tokens = P("replica", "shard", None)
    in_specs = (tokens, tokens, P("replica", None)) + (rows,) * 7
    out_specs = (tokens, tokens) + (rows,) * 7
    local = body if mesh.shape["shard"] == 8 and mesh.shape["replica"] == 4 else general_body
    return jax.shard_map(local, mesh=mesh, in_specs=in_specs, out_specs=out_specs, check_vma=False)
```
